32 devices in a mesh: dp: 8 (over z, x), tensor: 4 (over y, core).
Axes of the slice: x: 2, y: 2, z: 4, core: 2. Of those that a mesh axis runs over, the one named last changes fastest.
Arguments:
- inputs: bfloat16 [16384, 1280], P(('dp', 'tensor')), may hold values from -6 to 6
- cotangent: bfloat16 [16384, 1280], P(('dp', 'tensor')), may hold values from -6 to 6
- adapter_choice_per_tree: int32 [8], P('dp'), may hold values from 0 to 7
- segment_lengths: int32 [8, 13], P('dp'), may hold values from 1 to 768, 2048 in all within a row
- segment_parents: int32 [8, 13], P('dp'), may hold values from 0 to 4, as said below
- norm_gain_rows: float32 [2, 1280], replicated, may hold values from 0.25 to 1.75
- query_dimension_scale: float32 [80], replicated, may hold values from 0.5 to 2
- attention_weights: bfloat16 [3, 1280, 1280], P(None, 'dp', 'tensor'), may hold values from -0.15625 to 0.15625
- output_weight: bfloat16 [1280, 1280], P('dp', 'tensor'), may hold values from -4 to 4
- feedforward_weights: bfloat16 [2, 1280, 1280], P(None, 'dp', 'tensor'), may hold values from -0.15625 to 0.15625
- adapter_first_input: bfloat16 [4, 8, 1280, 16], replicated, may hold values from -0.15625 to 0.15625
- adapter_second_attention: bfloat16 [3, 8, 16, 1280], replicated, may hold values from -1.5 to 1.5
- adapter_second_up: bfloat16 [8, 16, 1280], replicated, may hold values from -1.5 to 1.5
- adapter_first_output: bfloat16 [8, 1280, 16], replicated, may hold values from -4 to 4
- adapter_first_down: bfloat16 [8, 1280, 16], replicated, may hold values from -0.15625 to 0.15625
- adapter_second_residual: bfloat16 [2, 8, 16, 1280], replicated, may hold values from -1.5 to 1.5
Outputs:
- output: bfloat16 [16384, 1280], P(('dp', 'tensor'))
- input_grad: float32 [16384, 1280], P(('dp', 'tensor'))
- grad_lora_a_in: float32 [4, 8, 1280, 16], replicated
- grad_lora_b_qkv: float32 [3, 8, 16, 1280], replicated
- grad_lora_b_up: float32 [8, 16, 1280], replicated
- grad_lora_a_out: float32 [8, 1280, 16], replicated
- grad_lora_a_down: float32 [8, 1280, 16], replicated
- grad_lora_b_res: float32 [2, 8, 16, 1280], replicated
The draws below stay inside these ranges and needn't reach their ends.
Inputs may be any that keep to these rules, and one draw needn't show every extreme that they name: `segment_lengths`: each row lists a tree's 13 segment lengths in token order (trunk, four branches, eight leaves) and sums to 2048; the longest segment of each tree has exactly 768 tokens. `segment_parents`: segment 0 is the trunk and is its own parent; segments 1 to 4 are branches with parent 0; segments 5 to 12 are leaves, exactly two under each branch, in drawn order.
All inputs are finite; a program needn't handle non-finite values.
Results may differ from the reference program's by a relative error of at most 0.015.
Values may be sent and summed in bfloat16 or wider, within the bound.
A program may use at most 192 MiB of HBM per device.

```python
import math
import jax
import jax.numpy as jnp
import numpy as np
from jax import lax

MODEL_WIDTH = 1280
HEADS = 16
HEAD_DIM = 80
HIDDEN_UNITS = 1280
ADAPTER_RANK = 16
ADAPTER_COUNT = 8
SEGS = 13
TOK_DEV = 512
TREE = 2048
TREES = 8
TOKENS = 16384
N_DP = 8
N_TENSOR = 4


def draw_segment_parents(key, part):

    def one_tree(tree_key):
        order = jax.random.permutation(tree_key, 8).astype(jnp.int32)
        leaves = 1 + order % 4
        return jnp.concatenate([jnp.zeros((5,), jnp.int32), leaves.astype(jnp.int32)])
    return jax.vmap(one_tree)(jax.random.split(key, TREES))


def set_ends(values, stream_key, smallest, top_value):
    longest = values.shape.index(max(values.shape))
    spots = []
    for shift in (0, 1):
        where = [jax.random.randint(jax.random.fold_in(stream_key, axis), (), 0, length) for axis, length in enumerate(values.shape)]
        where[longest] = (where[longest] + shift) % values.shape[longest]
        spots.append(tuple(where))
    return values.at[spots[0]].set(smallest).at[spots[1]].set(top_value)


def levels(own_key, extent, pieces, least, high):
    level, own = 1.0, jax.random.fold_in(own_key, 6)
    for dim, blocks in pieces:
        steps = jnp.exp(jax.random.uniform(jax.random.fold_in(own, dim), (blocks,), jnp.float32, least / len(pieces), high / len(pieces)))
        level = level * jnp.repeat(steps, extent[dim] // blocks).reshape([-1 if axis == dim else 1 for axis in range(len(extent))])
    return level


def profile(count, total, reach, lean):
    portions = [(1 << 20) // math.isqrt(standing ** lean) + 1 for standing in range(2, count + 1)]
    surplus, given = total - reach - (count - 1), [1] * (count - 1)
    while surplus > 0:
        movable = [i for i in range(count - 1) if given[i] < reach]
        pool, remaining = sum([portions[i] for i in movable]), surplus
        for i in movable:
            more = min(reach - given[i], max(1, remaining * portions[i] // pool), surplus)
            given[i] = given[i] + more
            surplus = surplus - more
    return np.array([reach] + given)


def uneven(own_key, number_of, total, most, lean):
    if number_of == 2:
        one = jax.random.randint(own_key, (), max(1, total - most), min(most, total - 1) + 1)
        return jnp.stack([one, total - one])
    sizes = jnp.asarray(profile(number_of, total, most, lean), jnp.int32)
    twos = (number_of - 1) // 2
    donor, sink = sizes[1:1 + 2 * twos:2], sizes[2:2 + 2 * twos:2]
    margin = jnp.minimum(donor - 1, most - sink)
    passed = jax.random.randint(jax.random.fold_in(own_key, 1), (twos,), 0, 1 << 20) % (margin + 1)
    sizes = sizes.at[1:1 + 2 * twos:2].set(donor - passed).at[2:2 + 2 * twos:2].set(sink + passed)
    return sizes[jax.random.permutation(jax.random.fold_in(own_key, 2), number_of)]


def noise(rng, extent, spread, reach, cuts=(), kind=jnp.bfloat16):
    values = spread * jax.random.normal(rng, extent, jnp.float32)
    if cuts:
        values = values * levels(rng, extent, cuts, -0.22, 0.18)
    return jnp.clip(values, -reach, reach).astype(kind)


def setup_inputs(seed: int = 0) -> dict:
    seeds = jax.random.split(jax.random.key(seed), 17)
    inputs = noise(seeds[0], (TOKENS, MODEL_WIDTH), 1.0, 6.0, ((0, 32),))
    cotangent = noise(seeds[1], (TOKENS, MODEL_WIDTH), 1.0, 6.0, ((0, 32),))
    adapter_choice_per_tree = set_ends(jax.random.randint(seeds[2], (TREES,), 0, ADAPTER_COUNT), jax.random.fold_in(seeds[2], 1), 0, ADAPTER_COUNT - 1).astype(jnp.int32)
    segment_lengths = jax.vmap(lambda own: uneven(own, SEGS, TREE, TREE * 3 // 8, 2))(jax.random.split(seeds[3], TREES)).reshape((TREES, SEGS)).astype(jnp.int32)
    segment_parents = draw_segment_parents(jax.random.fold_in(seeds[16], 71), 0)
    norm_gain_rows = jnp.clip(1.0 + 0.15 * jax.random.normal(seeds[5], (2, MODEL_WIDTH), jnp.float32), 0.25, 1.75)
    query_dimension_scale = jnp.clip(jnp.exp(jax.random.uniform(seeds[6], (HEAD_DIM,), jnp.float32, math.log(0.5), math.log(2.0))), 0.5, 2.0)
    attention_weights = noise(seeds[7], (3, MODEL_WIDTH, MODEL_WIDTH), MODEL_WIDTH ** -0.5, 0.15625, ((1, 8), (2, 4)))
    output_weight = noise(seeds[8], (MODEL_WIDTH, MODEL_WIDTH), (max(1, MODEL_WIDTH // 512)) ** -0.5, 4.0, ((0, 8), (1, 4)))
    feedforward_weights = noise(seeds[9], (2, MODEL_WIDTH, HIDDEN_UNITS), MODEL_WIDTH ** -0.5, 0.15625, ((1, 8), (2, 4)))
    adapter_first_input = noise(seeds[10], (4, ADAPTER_COUNT, MODEL_WIDTH, ADAPTER_RANK), MODEL_WIDTH ** -0.5, 0.15625)
    adapter_second_attention = noise(seeds[11], (3, ADAPTER_COUNT, ADAPTER_RANK, MODEL_WIDTH), ADAPTER_RANK ** -0.5, 1.5)
    adapter_second_up = noise(seeds[12], (ADAPTER_COUNT, ADAPTER_RANK, HIDDEN_UNITS), ADAPTER_RANK ** -0.5, 1.5)
    adapter_first_output = noise(seeds[13], (ADAPTER_COUNT, MODEL_WIDTH, ADAPTER_RANK), (max(1, MODEL_WIDTH // 512)) ** -0.5, 4.0)
    adapter_first_down = noise(seeds[14], (ADAPTER_COUNT, HIDDEN_UNITS, ADAPTER_RANK), HIDDEN_UNITS ** -0.5, 0.15625)
    adapter_second_residual = noise(seeds[15], (2, ADAPTER_COUNT, ADAPTER_RANK, MODEL_WIDTH), ADAPTER_RANK ** -0.5, 1.5)
    return {"inputs": inputs, "cotangent": cotangent, "adapter_choice_per_tree": adapter_choice_per_tree, "segment_lengths": segment_lengths, "segment_parents": segment_parents, "norm_gain_rows": norm_gain_rows, "query_dimension_scale": query_dimension_scale, "attention_weights": attention_weights, "output_weight": output_weight, "feedforward_weights": feedforward_weights, "adapter_first_input": adapter_first_input, "adapter_second_attention": adapter_second_attention, "adapter_second_up": adapter_second_up, "adapter_first_output": adapter_first_output, "adapter_first_down": adapter_first_down, "adapter_second_residual": adapter_second_residual}


@jax.custom_vjp
def low(v):
    return lax.optimization_barrier(v.astype(jnp.bfloat16)).astype(jnp.float32)

@jax.custom_vjp
def lowrank_backward(v):
    return v

def low_keep(v):
    return (low(v), None)

def low_pass(kept, grad):
    return (grad,)

def back_keep(v):
    return (v, None)

def back_low(kept, grad):
    return (low(grad),)
low.defvjp(low_keep, low_pass)
lowrank_backward.defvjp(back_keep, back_low)
adapter_scale = 0.5
epsilon = 1e-06
highest_precision = lax.Precision.HIGHEST
masked_value = -1e+30

def precise_product(first_term, second_term):
    return jnp.dot(first_term, second_term, precision=highest_precision, preferred_element_type=jnp.float32)

def rms_norm(token_rows, gain_row):
    return token_rows * lax.rsqrt(lax.optimization_barrier(jnp.mean(token_rows * token_rows, axis=-1, keepdims=True)) + epsilon) * gain_row

def silu_act(values_in):
    return values_in / (1.0 + jnp.exp(-values_in))

def ancestry(parents):
    seg_count = parents.shape[0]
    indices = jnp.arange(seg_count, dtype=jnp.int32)
    parent_hot = (parents[:, None] == indices[None, :]).astype(jnp.float32)
    grand_hot = precise_product(parent_hot, parent_hot)
    return jnp.maximum(jnp.maximum(parent_hot, grand_hot), jnp.eye(seg_count, dtype=jnp.float32))

def token_hot(lengths, tree_len):
    seg_ends = jnp.cumsum(lengths).astype(jnp.int32)
    positions = jnp.arange(tree_len, dtype=jnp.int32)
    seg_ids = lax.optimization_barrier(jnp.sum((positions[:, None] >= seg_ends[None, :]).astype(jnp.int32), axis=1)).astype(jnp.int32)
    indices = jnp.arange(lengths.shape[0], dtype=jnp.int32)
    return (seg_ids, (seg_ids[:, None] == indices[None, :]).astype(jnp.float32))

def allowed_block(seg_ids, seg_hot, reach_table, block_start, block_rows):
    query_hot = lax.dynamic_slice_in_dim(seg_hot, block_start, block_rows, 0)
    query_ids = lax.dynamic_slice_in_dim(seg_ids, block_start, block_rows, 0)
    linked = precise_product(precise_product(query_hot, reach_table), seg_hot.T) > 0.5
    query_pos = block_start + jnp.arange(block_rows, dtype=jnp.int32)
    key_pos = jnp.arange(seg_ids.shape[0], dtype=jnp.int32)
    causal = (query_ids[:, None] != seg_ids[None, :]) | (key_pos[None, :] <= query_pos[:, None])
    return linked & causal

def attention(queries, key_heads, values, seg_ids, seg_hot, reach_table):
    tree_len = key_heads.shape[0]
    block_rows = min(512, tree_len)

    def one_block(block_start):
        block_q = lax.dynamic_slice_in_dim(queries, block_start, block_rows, 0)
        scores = lowrank_backward(jnp.einsum('qhd,khd->hqk', block_q, key_heads, precision=highest_precision))
        allowed = allowed_block(seg_ids, seg_hot, reach_table, block_start, block_rows)
        scores = jnp.where(allowed[None], scores, masked_value)
        row_max = lax.optimization_barrier(jnp.max(scores, axis=-1, keepdims=True))
        weights = jnp.exp(scores - row_max)
        row_probs = weights / lax.optimization_barrier(jnp.sum(weights, axis=-1, keepdims=True))
        return jnp.einsum('hqk,khd->qhd', low(row_probs), values, precision=highest_precision)
    block_starts = jnp.arange(tree_len // block_rows, dtype=jnp.int32) * block_rows
    mixed_output = lax.map(jax.checkpoint(one_block), block_starts)
    return mixed_output.reshape(tree_len, HEADS * HEAD_DIM)

def tree_forward(token_rows, adapter_input, frozen, selected_index, seg_ids, seg_hot, reach_table):
    adapter_input_delta, adapter_attention_delta, adapter_up_delta, adapter_output_delta, adapter_down_delta, adapter_residual_delta = [lax.dynamic_index_in_dim(table_input, selected_index, gather_along_axis, keepdims=False) for table_input, gather_along_axis in zip(adapter_input, (1, 1, 0, 0, 0, 1))]
    norm_gain_rows, query_dimension_scale, attention_weights, output_weight, feedforward_weights = frozen
    tree_len = token_rows.shape[0]
    shape_heads = (tree_len, HEADS, HEAD_DIM)
    normed_input = low(rms_norm(token_rows, norm_gain_rows[0]))
    lowrank_attention = jnp.einsum('ny,qyf->qnf', normed_input, adapter_input_delta[:3], precision=highest_precision)
    unscaled_projection = jnp.einsum('td,sdc->stc', normed_input, attention_weights, precision=highest_precision)
    unscaled_projection = unscaled_projection + adapter_scale * jnp.einsum('jlh,jhx->jlx', lowrank_attention, adapter_attention_delta, precision=highest_precision)
    scale_row = jnp.tile(query_dimension_scale, HEADS) / math.sqrt(HEAD_DIM)
    queries = low(lowrank_backward(unscaled_projection[0]) * scale_row).reshape(shape_heads)
    key_heads = low(lowrank_backward(unscaled_projection[1])).reshape(shape_heads)
    values = low(lowrank_backward(unscaled_projection[2])).reshape(shape_heads)
    mixed_output = low(lowrank_backward(attention(queries, key_heads, values, seg_ids, seg_hot, reach_table)))
    attention_output = jnp.einsum('tc,dc->td', mixed_output, output_weight, precision=highest_precision)
    attention_output = lowrank_backward(attention_output + adapter_scale * precise_product(precise_product(mixed_output, adapter_output_delta), adapter_residual_delta[0]))
    middle = token_rows + attention_output
    hidden_input = low(rms_norm(middle, norm_gain_rows[1]))
    up_projection = precise_product(hidden_input, feedforward_weights[0]) + adapter_scale * precise_product(precise_product(hidden_input, adapter_input_delta[3]), adapter_up_delta)
    hidden_activation = low(silu_act(lowrank_backward(up_projection)))
    down_projection = jnp.einsum('tf,df->td', hidden_activation, feedforward_weights[1], precision=highest_precision)
    down_projection = lowrank_backward(down_projection + adapter_scale * precise_product(precise_product(hidden_activation, adapter_down_delta), adapter_residual_delta[1]))
    return middle + down_projection

def reference(inputs, cotangent, adapter_choice_per_tree, segment_lengths, segment_parents, norm_gain_rows, query_dimension_scale, attention_weights, output_weight, feedforward_weights, adapter_first_input, adapter_second_attention, adapter_second_up, adapter_first_output, adapter_first_down, adapter_second_residual):
    tree_len = TOK_DEV * N_TENSOR
    adapter_tables = tuple((table_input.astype(jnp.float32) for table_input in (adapter_first_input, adapter_second_attention, adapter_second_up, adapter_first_output, adapter_first_down, adapter_second_residual)))
    frozen = (norm_gain_rows.astype(jnp.float32), query_dimension_scale.astype(jnp.float32), attention_weights.astype(jnp.float32), output_weight.astype(jnp.float32), feedforward_weights.astype(jnp.float32))
    tree_rows = inputs.astype(jnp.float32).reshape(N_DP, tree_len, MODEL_WIDTH)
    tree_cot = cotangent.astype(jnp.float32).reshape(N_DP, tree_len, MODEL_WIDTH)

    def per_tree(totals, tree_items):
        token_rows, tree_grad, selected_index, lengths, parents = tree_items
        seg_ids, seg_hot = token_hot(lengths, tree_len)
        reach_table = ancestry(parents)

        def forward(rows_in, adapter_input):
            return tree_forward(rows_in, adapter_input, frozen, selected_index, seg_ids, seg_hot, reach_table)
        tree_out, pullback = jax.vjp(forward, token_rows, adapter_tables)
        grad_rows, grad_adapt = pullback(tree_grad)
        totals = jax.tree.map(lambda first_term, second_term: first_term + second_term, totals, grad_adapt)
        return (totals, (tree_out, grad_rows))
    start_totals = jax.tree.map(jnp.zeros_like, adapter_tables)
    totals, (tree_outs, tree_grads) = lax.scan(per_tree, start_totals, (tree_rows, tree_cot, adapter_choice_per_tree, segment_lengths, segment_parents))
    output = tree_outs.reshape(N_DP * tree_len, MODEL_WIDTH).astype(jnp.bfloat16)
    input_grad = tree_grads.reshape(N_DP * tree_len, MODEL_WIDTH)
    return (output, input_grad, totals[0], totals[1], totals[2], totals[3], totals[4], totals[5])
```

```python
import functools
import math

import jax
import jax.numpy as jnp
from jax import lax
from jax.experimental import pallas as pl
from jax.experimental.pallas import tpu as pltpu
from jax.sharding import PartitionSpec as P

F32, BF16 = jnp.float32, jnp.bfloat16
BIG = 1e30
BLK = 256
HD = 80

def dot(a, b):
    return lax.dot_general(a, b, (((1,), (0,)), ((), ())), preferred_element_type=F32)
def dot_nt(a, b):
    return lax.dot_general(a, b, (((1,), (1,)), ((), ())), preferred_element_type=F32)
def dot_tn(a, b):
    return lax.dot_general(a, b, (((0,), (0,)), ((), ())), preferred_element_type=F32)

def project(b, x_ref, wp_ref, a_ref, bp_ref, scale_ref, seg_ref, mq_ref, q_ref, qt_ref, k_ref, kt_ref, v_ref, vt_ref, rank_ref):
    rows = pl.ds(pl.multiple_of(b * BLK, BLK), BLK)
    xb = x_ref[rows, :]
    rank = dot_nt(xb, a_ref[...]).astype(BF16)
    rank_ref[rows, :] = rank
    lane = lax.broadcasted_iota(jnp.int32, (BLK, 128), 1)
    tok = (lax.broadcasted_iota(jnp.int32, (BLK, 128), 0) + b * BLK).astype(F32)
    hot = jnp.where((tok >= seg_ref[0:1, :]) & (tok < seg_ref[1:2, :]), 1.0, 0.0)
    qfeat = dot(hot.astype(BF16), mq_ref[...])
    kfeat = jnp.where((lane >= HD + 13) & (lane < HD + 16), 1.0, hot)
    vfeat = jnp.where(lane < HD + 2, 1.0, 0.0)
    heads = q_ref.shape[0]
    for s, (n_ref, t_ref, feat) in enumerate(((q_ref, qt_ref, qfeat), (k_ref, kt_ref, kfeat), (v_ref, vt_ref, vfeat))):
        y = dot(xb, wp_ref[s]) + dot(rank, bp_ref[s])
        if s == 0:
            y = y * scale_ref[...]
        for h in range(heads):
            yh = jnp.where(lane < HD, y[:, h * 128:(h + 1) * 128], feat)
            n_ref[h, rows, :] = yh.astype(BF16)
            yt = yh.T
            t_ref[h, :, rows] = yt[:t_ref.shape[1]].astype(BF16)

def attend_block(i, qt_ref, k_ref, vt_ref, m_ref, acc_ref, mixt_ref, mix_ref, count=None, jlist=None):
    heads = qt_ref.shape[0]
    cols = pl.ds(pl.multiple_of(i * BLK, BLK), BLK)
    m_ref[...] = jnp.full_like(m_ref, -3e38)
    acc_ref[...] = jnp.zeros_like(acc_ref)
    def step(j, diag):
        rows = pl.ds(pl.multiple_of(j * BLK, BLK), BLK)
        hs = range(heads)
        ss = [dot(k_ref[h, rows, :], qt_ref[h, :, cols]) for h in hs]
        if diag:
            low = lax.broadcasted_iota(jnp.int32, ss[0].shape, 0) <= lax.broadcasted_iota(jnp.int32, ss[0].shape, 1)
            ss = [jnp.where(low, s, -BIG) for s in ss]
        olds = [m_ref[h] for h in hs]
        news = [jnp.maximum(olds[h], jnp.max(ss[h], axis=0, keepdims=True)) for h in hs]
        ps = [jnp.exp(ss[h] - news[h]).astype(BF16) for h in hs]
        pv = [dot(vt_ref[h, :, rows], ps[h]) for h in hs]
        accs = [acc_ref[h] * jnp.exp(olds[h] - news[h]) + pv[h] for h in hs]
        for h in hs:
            acc_ref[h] = accs[h]
            m_ref[h] = news[h]
    if jlist is None:
        lax.fori_loop(0, i, lambda j, c: (step(j, False), c)[1], 0)
    else:
        lax.fori_loop(0, count, lambda n, c: (step(jlist(n), False), c)[1], 0)
    step(i, True)
    outs = []
    for h in range(heads):
        acc = acc_ref[h]
        l = acc[HD:HD + 1]
        o = acc[:HD] * (1.0 / l)
        lse = m_ref[h] + jnp.log(l)
        hi = (-lse).astype(BF16).astype(F32)
        mid = (-lse - hi).astype(BF16).astype(F32)
        lo = -lse - hi - mid
        r = lax.broadcasted_iota(jnp.int32, (16, BLK), 0)
        old = qt_ref[h, HD:HD + 16, cols].astype(F32)
        new = jnp.where(r == 13, hi, jnp.where(r == 14, mid, jnp.where(r == 15, lo, old)))
        qt_ref[h, HD:HD + 16, cols] = new.astype(BF16)
        outs.append(o)
    ot = jnp.concatenate(outs, axis=0)
    mixt_ref[:, cols] = ot.astype(BF16)
    mix_ref[cols, :] = ot.T.astype(BF16)

def seg_masks(len_ref, par_ref, segs, nblk):
    start, km, qm = 0, [0] * nblk, [0] * nblk
    for u in range(segs):
        end = start + len_ref[u]
        up = par_ref[u]
        anc = jnp.int32(1 << u) | (jnp.int32(1) << up) | (jnp.int32(1) << par_ref[up])
        for b in range(nblk):
            inside = (start < (b + 1) * BLK) & (end > b * BLK)
            km[b] = km[b] | jnp.where(inside, jnp.int32(1 << u), 0)
            qm[b] = qm[b] | jnp.where(inside, anc, 0)
        start = end
    return km, qm

def spread_heads(hcols, pad):
    c = lax.broadcasted_iota(jnp.int32, (hcols, pad), 0)
    l = lax.broadcasted_iota(jnp.int32, (hcols, pad), 1)
    return jnp.where(((l & 127) < HD) & ((l >> 7) * HD + (l & 127) == c), 1.0, 0.0).astype(BF16)


def fwd_kernel(x_ref, wq_ref, a_ref, b_ref, scale_ref, seg_ref, mq_ref,
               q_ref, qt_ref, k_ref, kt_ref, v_ref, rank_ref, mixt_ref, mix_ref, wp_ref, bp_ref,
               vt_ref, m_ref, acc_ref):
    sel = spread_heads(wq_ref.shape[2], wp_ref.shape[2])
    bp_ref[...] = jnp.zeros_like(bp_ref)
    for s in range(3):
        wp_ref[s] = dot(wq_ref[s], sel).astype(BF16)
        n = b_ref.shape[1]
        bp_ref[s, s * n:(s + 1) * n] = (0.5 * dot(b_ref[s], sel)).astype(BF16)
    nblk = x_ref.shape[0] // BLK
    lax.fori_loop(0, nblk, lambda b, c: (project(b, x_ref, wp_ref, a_ref, bp_ref, scale_ref, seg_ref, mq_ref, q_ref, qt_ref, k_ref, kt_ref, v_ref, vt_ref, rank_ref), c)[1], 0)
    lax.fori_loop(0, nblk, lambda i, c: (attend_block(i, qt_ref, k_ref, vt_ref, m_ref, acc_ref, mixt_ref, mix_ref), c)[1], 0)


def bwd_prep(b, dm_ref, mixt_ref, do_ref, dot_ref):
    rows = pl.ds(pl.multiple_of(b * BLK, BLK), BLK)
    heads = do_ref.shape[0]
    dt = dm_ref[rows, :].astype(F32).T
    prod = dt * mixt_ref[:, rows].astype(F32)
    r = lax.broadcasted_iota(jnp.int32, (16, BLK), 0)
    for h in range(heads):
        d = dt[h * HD:(h + 1) * HD]
        delta = -jnp.sum(prod[h * HD:(h + 1) * HD], axis=0, keepdims=True)
        hi = delta.astype(BF16).astype(F32)
        ext = jnp.where(r == 0, hi, jnp.where(r == 1, delta - hi, 0.0))
        full = jnp.concatenate([d, ext, jnp.zeros((32, BLK), F32)], axis=0)
        dot_ref[h, :, rows] = full.astype(BF16)
        do_ref[h, rows, :] = full.T.astype(BF16)

def bwd_pair(i, j, diag, q_ref, qt_ref, k_ref, kt_ref, v_ref, do_ref, dot_ref, dqt_ref, dk_ref, dv_ref):
    heads = q_ref.shape[0]
    cols = pl.ds(pl.multiple_of(i * BLK, BLK), BLK)
    rows = pl.ds(pl.multiple_of(j * BLK, BLK), BLK)
    hs = range(heads)
    ss = [dot(k_ref[h, rows, :], qt_ref[h, :, cols]) for h in hs]
    dps = [dot(v_ref[h, rows, :], dot_ref[h, :, cols]) for h in hs]
    if diag:
        low = lax.broadcasted_iota(jnp.int32, ss[0].shape, 0) <= lax.broadcasted_iota(jnp.int32, ss[0].shape, 1)
        ss = [jnp.where(low, s, -BIG) for s in ss]
    ps = [jnp.exp(s) for s in ss]
    dss = [(p * dp).astype(BF16) for p, dp in zip(ps, dps)]
    ps = [p.astype(BF16) for p in ps]
    dvs = [dot(ps[h], do_ref[h, cols, :]) for h in hs]
    dks = [dot(dss[h], q_ref[h, cols, :]) for h in hs]
    dqs = [dot(kt_ref[h, :, rows], dss[h]) for h in hs]
    for h in hs:
        dv_ref[h, rows, :] += dvs[h]
        dk_ref[h, rows, :] += dks[h]
        dqt_ref[h, :, cols] += dqs[h]

def bwd_kernel(len_ref, par_ref, dm_ref, mixt_ref, q_ref, qt_ref, k_ref, kt_ref, v_ref, scale_ref,
               dqo_ref, dko_ref, dvo_ref, do_ref, dot_ref, dqt_ref, dk_ref, dv_ref, list_ref):
    nblk = dm_ref.shape[0] // BLK
    heads = q_ref.shape[0]
    km, qm = seg_masks(len_ref, par_ref, len_ref.shape[0], nblk)
    n = jnp.int32(0)
    for j in range(nblk):
        for i in range(j + 1, nblk):
            list_ref[n] = jnp.int32(i * nblk + j)
            n = n + jnp.where((qm[i] & km[j]) != 0, 1, 0)
    dqt_ref[...] = jnp.zeros_like(dqt_ref)
    dk_ref[...] = jnp.zeros_like(dk_ref)
    dv_ref[...] = jnp.zeros_like(dv_ref)
    lax.fori_loop(0, nblk, lambda b, c: (bwd_prep(b, dm_ref, mixt_ref, do_ref, dot_ref), c)[1], 0)
    args = (q_ref, qt_ref, k_ref, kt_ref, v_ref, do_ref, dot_ref, dqt_ref, dk_ref, dv_ref)
    lax.fori_loop(0, nblk, lambda b, c: (bwd_pair(b, b, True, *args), c)[1], 0)
    def one(t, c):
        w = list_ref[t]
        bwd_pair(w // nblk, w % nblk, False, *args)
        return c
    lax.fori_loop(0, n, one, 0)
    lane = lax.broadcasted_iota(jnp.int32, (BLK, 128), 1)
    def finish(b, c):
        rows = pl.ds(pl.multiple_of(b * BLK, BLK), BLK)
        for h in range(heads):
            hl = slice(h * 128, (h + 1) * 128)
            dq = jnp.concatenate([dqt_ref[h, :, rows], jnp.zeros((48, BLK), F32)], axis=0).T
            dqo_ref[rows, hl] = (dq * scale_ref[:, hl]).astype(BF16)
            dko_ref[rows, hl] = jnp.where(lane < HD, dk_ref[h, rows, :], 0.0).astype(BF16)
            dvo_ref[rows, hl] = jnp.where(lane < HD, dv_ref[h, rows, :], 0.0).astype(BF16)
        return c
    lax.fori_loop(0, nblk, finish, 0)


MESH = pl.DeviceIdType.MESH


class Place:
    def __init__(self, ndp):
        self.d, self.t = lax.axis_index("dp"), lax.axis_index("tensor")
        self.line = ndp // 2
        self.p, self.par = self.d // 2, self.d % 2
        self.dx = self.d + 1 - 2 * self.par
        self.c, self.y = self.t % 2, self.t // 2
        self.t1 = self.t + 1 - 2 * self.c
        self.t2 = (self.t + 2) % 4
        self.t3 = (self.t1 + 2) % 4
        self.has_left, self.has_right = self.p > 0, self.p < self.line - 1


def signal(sem, d, t):
    pl.semaphore_signal(sem, inc=1, device_id=(d, t), device_id_type=MESH)


def remote(src, dst, send_sem, recv_sem, d, t):
    return pltpu.make_async_remote_copy(src_ref=src, dst_ref=dst, send_sem=send_sem, recv_sem=recv_sem, device_id=(d, t), device_id_type=MESH)


def greet(me, tensor=(), pair=False, line=False):
    bar = pltpu.get_barrier_semaphore()
    count = len(tensor) + (1 if pair else 0)
    for t in tensor:
        signal(bar, me.d, t)
    if pair:
        signal(bar, me.dx, me.t)
    if line:
        @pl.when(me.has_left)
        def _():
            signal(bar, me.d - 2, me.t)
        @pl.when(me.has_right)
        def _():
            signal(bar, me.d + 2, me.t)
        count = count + jnp.where(me.has_left, 1, 0) + jnp.where(me.has_right, 1, 0)
    pl.semaphore_wait(bar, count)


class PairLine:
    def __init__(self, me, own, buf, send, recv):
        self.me, self.own, self.buf, self.send, self.recv = me, own, buf, send, recv

    def copy(self, o, src, d, kind):
        return remote(src, self.buf.at[o], self.send.at[kind, o], self.recv.at[o], d, self.me.t)

    def start(self):
        me = self.me
        @pl.when(me.has_left)
        def _():
            self.copy(me.d, self.own, me.d - 2, 0).start()
        @pl.when(me.has_right)
        def _():
            self.copy(me.d, self.own, me.d + 2, 1).start()
        self.copy(me.d, self.own, me.dx, 2).start()

    def hop(self, k, then=None):
        me = self.me
        @pl.when(me.p - k >= 0)
        def _():
            o = me.d - 2 * k
            self.copy(o, self.buf.at[o], me.dx, 2).wait_recv()
            @pl.when(me.has_right)
            def _():
                self.copy(o, self.buf.at[o], me.d + 2, 1).start()
            self.copy(o, self.buf.at[o], me.dx, 2).start()
            if then is not None:
                then(o)
        @pl.when(me.p + k < me.line)
        def _():
            o = me.d + 2 * k
            self.copy(o, self.buf.at[o], me.dx, 2).wait_recv()
            @pl.when(me.has_left)
            def _():
                self.copy(o, self.buf.at[o], me.d - 2, 0).start()
            self.copy(o, self.buf.at[o], me.dx, 2).start()
            if then is not None:
                then(o)

    def pair_arrivals(self, then=None):
        def one(q, c):
            o = 2 * q + 1 - self.me.par
            self.copy(o, self.buf.at[o], self.me.dx, 2).wait_recv()
            if then is not None:
                then(o)
            return c
        lax.fori_loop(0, self.me.line, one, 0)

    def sent(self):
        me = self.me
        def one(q, c):
            o = 2 * q + me.par
            self.copy(o, self.buf.at[o], me.dx, 2).wait_send()
            @pl.when((q >= me.p) & me.has_left)
            def _():
                self.copy(o, self.buf.at[o], me.dx, 0).wait_send()
            @pl.when((q <= me.p) & me.has_right)
            def _():
                self.copy(o, self.buf.at[o], me.dx, 1).wait_send()
            return c
        lax.fori_loop(0, me.line, one, 0)


class FullGather:
    def __init__(self, me, own, buf, send, first, recv):
        self.me, self.own, self.buf, self.send, self.first, self.recv = me, own, buf, send, first, recv
        cut = own.shape[0] // 32 * 16
        self.parts = (pl.ds(0, cut), pl.ds(cut, own.shape[0] - cut))

    def copy(self, h, o, t, d2, t2, kind, own=False):
        rows = self.parts[h]
        src = self.own.at[rows] if own else self.buf.at[o, t, rows]
        sem = self.first.at[h] if kind == 4 else self.send.at[h, o, t, kind]
        return remote(src, self.buf.at[o, t, rows], sem, self.recv.at[h, o, t], d2, t2)

    def last(self, h):
        me = self.me
        return (me.d, me.t2) if h == 0 else (me.dx, me.t)

    def spread(self, h, o, t, left, right, own=False):
        me = self.me
        @pl.when(left)
        def _():
            self.copy(h, o, t, me.d - 2, me.t, 0, own).start()
        @pl.when(right)
        def _():
            self.copy(h, o, t, me.d + 2, me.t, 1, own).start()
        self.copy(h, o, t, *self.last(h), 2, own).start()
        self.copy(h, o, t, me.d, me.t1, 3, own).start()

    def start(self):
        me = self.me
        self.copy(0, me.d, me.t, me.dx, me.t, 4, True).start()
        self.copy(1, me.d, me.t, me.d, me.t2, 4, True).start()
        for h in range(2):
            self.spread(h, me.d, me.t, me.has_left, me.has_right, True)

    def arrived(self, h, o, t):
        self.copy(h, o, t, self.me.d, self.me.t1, 3).wait_recv()

    def firsts(self):
        me = self.me
        self.arrived(0, me.dx, me.t)
        self.spread(0, me.dx, me.t, me.has_left, me.has_right)
        self.arrived(1, me.d, me.t2)
        self.spread(1, me.d, me.t2, me.has_left, me.has_right)

    def streams(self, q):
        me = self.me
        return ((0, 2 * q + me.par, me.t), (0, 2 * q + 1 - me.par, me.t), (1, 2 * q + me.par, me.t), (1, 2 * q + me.par, me.t2))

    def hop(self, k):
        me = self.me
        @pl.when(me.p - k >= 0)
        def _():
            for h, o, t in self.streams(me.p - k):
                self.arrived(h, o, t)
                self.spread(h, o, t, False, me.has_right)
        @pl.when(me.p + k < me.line)
        def _():
            for h, o, t in self.streams(me.p + k):
                self.arrived(h, o, t)
                self.spread(h, o, t, me.has_left, False)

    def lasts(self):
        me = self.me
        def one(q, c):
            for h, o, t in ((0, 2 * q, me.t2), (0, 2 * q + 1, me.t2), (1, 2 * q + 1 - me.par, me.t), (1, 2 * q + 1 - me.par, me.t2)):
                self.arrived(h, o, t)
                self.copy(h, o, t, me.d, me.t1, 3).start()
            return c
        lax.fori_loop(0, me.line, one, 0)

    def finish(self):
        me = self.me
        def one(o, c):
            for h in range(2):
                self.arrived(h, o, me.t1)
                self.arrived(h, o, me.t3)
                for t in (me.t, me.t2):
                    self.copy(h, o, t, me.d, me.t1, 3).wait_send()
            return c
        lax.fori_loop(0, 2 * me.line, one, 0)
        def two(q, c):
            for h, o, t in self.streams(q):
                self.copy(h, o, t, me.d, me.t1, 2).wait_send()
                @pl.when((q >= me.p) & me.has_left)
                def _():
                    self.copy(h, o, t, me.d, me.t1, 0).wait_send()
                @pl.when((q <= me.p) & me.has_right)
                def _():
                    self.copy(h, o, t, me.d, me.t1, 1).wait_send()
            return c
        lax.fori_loop(0, me.line, two, 0)
        for h in range(2):
            self.copy(h, me.d, me.t, me.d, me.t1, 4).wait_send()


EPS = 1e-6


def gather_kernel(ndp, chunks, x_ref, gain_ref, choice_ref, a_ref, wo_ref, wf_ref, xo_ref, ao_ref, wout_ref, cho_ref,
                  xn_ref, aown_ref, wown_ref, ls, xs, xr, a_s, a_r, c_s, c_r, w_s, w_f, w_r):
    me = Place(ndp)
    rows_o = wo_ref.shape[0]
    loads = [pltpu.make_async_copy(a_ref, aown_ref, ls.at[0]), pltpu.make_async_copy(wo_ref, wown_ref.at[pl.ds(0, rows_o)], ls.at[1]),
             pltpu.make_async_copy(wf_ref, wown_ref.at[pl.ds(rows_o, wf_ref.shape[0])], ls.at[2])]
    for copy in loads:
        copy.start()
    x = x_ref[...].astype(F32)
    xn_ref[...] = (x * lax.rsqrt(jnp.mean(x * x, axis=-1, keepdims=True) + EPS) * gain_ref[0:1, :]).astype(BF16)
    greet(me, tensor=(me.t1, me.t2), pair=True, line=True)
    size = x_ref.shape[0] // chunks

    def xcopy(o, c, own, t, kind):
        rows = pl.ds(c * size, size)
        return remote(xn_ref.at[rows] if own else xo_ref.at[o, rows], xo_ref.at[o, rows], xs.at[kind, c], xr.at[o, c], me.d, t)

    for c in range(chunks):
        xcopy(me.t, c, True, me.t2, 0).start()
    for c in range(chunks):
        xcopy(me.t, c, True, me.t1, 1).start()
    for copy in loads:
        copy.wait()
    a = PairLine(me, aown_ref, ao_ref, a_s, a_r)
    ch = PairLine(me, choice_ref, cho_ref, c_s, c_r)
    w = FullGather(me, wown_ref, wout_ref, w_s, w_f, w_r)
    a.start()
    ch.start()
    w.start()
    mine = [pltpu.make_async_copy(xn_ref, xo_ref.at[me.t], ls.at[0]), pltpu.make_async_copy(aown_ref, ao_ref.at[me.d], ls.at[1]),
            pltpu.make_async_copy(wown_ref, wout_ref.at[me.d, me.t], ls.at[2]), pltpu.make_async_copy(choice_ref, cho_ref.at[me.d], ls.at[3])]
    for copy in mine:
        copy.start()
    w.firsts()

    def forward(c):
        xcopy(me.t2, c, False, me.t1, 2).wait_recv()
        xcopy(me.t2, c, False, me.t1, 2).start()

    forward(0)

    def hop(k, carry):
        a.hop(k)
        ch.hop(k)
        w.hop(k)
        return carry
    lax.fori_loop(1, me.line, hop, 0)
    for c in range(1, chunks):
        forward(c)
    w.lasts()
    a.pair_arrivals()
    ch.pair_arrivals()
    for c in range(chunks):
        xcopy(me.t1, c, False, me.t1, 2).wait_recv()
        xcopy(me.t3, c, False, me.t1, 2).wait_recv()
    w.finish()
    a.sent()
    ch.sent()
    for c in range(chunks):
        for kind in range(3):
            xcopy(me.t, c, True, me.t1, kind).wait_send()
    for copy in mine:
        copy.wait()


def swap_kernel(ndp, x_ref, o_ref, send, recv, ls):
    me = Place(ndp)
    greet(me, tensor=(me.t1, me.t2, me.t3))
    size = o_ref.shape[1]

    def copy(n, t):
        return remote(x_ref.at[pl.ds(pl.multiple_of(t * size, size), size)], o_ref.at[me.t], send.at[n], recv.at[me.t], me.d, t)

    own = pltpu.make_async_copy(x_ref.at[pl.ds(pl.multiple_of(me.t * size, size), size)], o_ref.at[me.t], ls.at[0])
    for n, t in enumerate((me.t3, me.t2, me.t1)):
        copy(n, t).start()
    own.start()
    for t in (me.t1, me.t2, me.t3):
        remote(o_ref.at[t], o_ref.at[t], send.at[0], recv.at[t], me.d, t).wait_recv()
    for n, t in enumerate((me.t3, me.t2, me.t1)):
        copy(n, t).wait_send()
    own.wait()


def sigmoid(v):
    return 1.0 / (1.0 + jnp.exp(-v))


def mid_kernel(x_ref, g_ref, mix4_ref, gain_ref, w_ref, at_ref, b_ref, out_ref, dmid_ref, dmix_ref, grads_ref,
               mix_ref, mid_ref, hid_ref, up_ref, act_ref, f_ref, low_ref):
    width = x_ref.shape[1]
    step = 256
    part = mix4_ref.shape[2]
    for t in range(mix4_ref.shape[0]):
        mix_ref[:, t * part:(t + 1) * part] = mix4_ref[t]

    def cols(n):
        return pl.ds(pl.multiple_of(n * step, step), step)

    def each(fn):
        lax.fori_loop(0, width // step, lambda n, c: (fn(cols(n)), c)[1], 0)

    gain = gain_ref[1:2, :]
    r_out = dot_nt(mix_ref[...], at_ref[0]).astype(BF16)

    def project_out(n):
        attn = dot_nt(mix_ref[...], w_ref[0, n, :]) + 0.5 * dot(r_out, b_ref[0, :, n])
        mid_ref[:, n] = x_ref[:, n].astype(F32) + attn
    each(project_out)
    middle = mid_ref[...]
    r = lax.rsqrt(jnp.mean(middle * middle, axis=-1, keepdims=True) + EPS)
    hid_ref[...] = (middle * r * gain).astype(BF16)
    r_up = dot_nt(hid_ref[...], at_ref[1]).astype(BF16)

    def up_step(n):
        up = dot(hid_ref[...], w_ref[1, :, n]) + 0.5 * dot(r_up, b_ref[1, :, n])
        up_ref[:, n] = up
        act_ref[:, n] = (up * sigmoid(up)).astype(BF16)
    each(up_step)
    r_down = dot_nt(act_ref[...], at_ref[2]).astype(BF16)

    def down_step(n):
        down = dot_nt(act_ref[...], w_ref[2, n, :]) + 0.5 * dot(r_down, b_ref[2, :, n])
        out_ref[:, n] = (mid_ref[:, n] + down).astype(BF16)
    each(down_step)
    grads_ref[5] = 0.5 * dot_tn(r_down, g_ref[...])
    dz_down = (0.5 * dot_nt(g_ref[...], b_ref[2])).astype(BF16)
    grads_ref[3] = dot_tn(dz_down, act_ref[...])

    def act_back(n):
        d_act = dot(g_ref[...], w_ref[2, :, n]) + dot(dz_down, at_ref[2, :, n])
        up = up_ref[:, n]
        sg = sigmoid(up)
        low_ref[:, n] = (d_act * sg * (1.0 + up * (1.0 - sg))).astype(BF16)
    each(act_back)
    dz_up = (0.5 * dot_nt(low_ref[...], b_ref[1])).astype(BF16)
    grads_ref[1] = 0.5 * dot_tn(r_up, low_ref[...])
    grads_ref[0] = dot_tn(dz_up, hid_ref[...])

    def hidden_back(n):
        f_ref[:, n] = (dot_nt(low_ref[...], w_ref[1, n, :]) + dot(dz_up, at_ref[1, :, n])) * gain_ref[1:2, n]
    each(hidden_back)
    gd = f_ref[...]
    middle = mid_ref[...]
    s = jnp.mean(middle * gd, axis=-1, keepdims=True)
    d_mid = g_ref[...].astype(F32) + r * gd - middle * (r * r * r * s)
    dmid_ref[...] = d_mid
    low_ref[...] = d_mid.astype(BF16)
    dz_out = (0.5 * dot_nt(low_ref[...], b_ref[0])).astype(BF16)
    grads_ref[4] = 0.5 * dot_tn(r_out, low_ref[...])
    grads_ref[2] = dot_tn(dz_out, mix_ref[...])

    def mixed_back(n):
        act_ref[:, n] = (dot(low_ref[...], w_ref[0, :, n]) + dot(dz_out, at_ref[0, :, n])).astype(BF16)
    each(mixed_back)
    for t in range(dmix_ref.shape[0]):
        dmix_ref[t] = act_ref[:, t * part:(t + 1) * part]


def finish_kernel(ndp, chunks, dq_ref, dk_ref, dv_ref, wp_ref, bp_ref, at_ref, xn_ref, rank_ref, x_ref, dmid_ref, gain_ref, gmid_ref,
                  ig_ref, gall_ref,
                  dn_ref, r1_ref, s2_ref, r2_ref, ga_ref, gb_ref, gp_ref, gr_ref, g2_ref, gown_ref,
                  s1s, s1r, s2s, s2r, g1s, g1r, gs, gr, fs, fr, ls):
    me = Place(ndp)
    tok = x_ref.shape[0]
    greet(me, tensor=(me.t1, me.t2), pair=True, line=True)
    ga_ref[...] = jnp.zeros_like(ga_ref)
    gb_ref[...] = jnp.zeros_like(gb_ref)

    def shard(t, slot):
        def half(b, c):
            rows = pl.ds(pl.multiple_of(t * tok + b * BLK, BLK), BLK)
            ds = [ref[rows, :] for ref in (dq_ref, dk_ref, dv_ref)]
            dz = sum(dot_nt(ds[s], bp_ref[s]) for s in range(3)).astype(BF16)
            dn = sum(dot_nt(ds[s], wp_ref[s]) for s in range(3)) + dot(dz, at_ref[...])
            dn_ref[slot, pl.ds(pl.multiple_of(b * BLK, BLK), BLK), :] = dn.astype(BF16)
            ga_ref[...] += dot_tn(dz, xn_ref[rows, :])
            for s in range(3):
                gb_ref[s] += dot_tn(rank_ref[rows, :], ds[s])
            return c
        lax.fori_loop(0, tok // BLK, half, 0)

    def one(slot):
        return remote(dn_ref.at[slot], r1_ref.at[slot], s1s.at[slot], s1r.at[slot], me.d, me.t1)

    shard(me.t3, 0)
    one(0).start()
    shard(me.t2, 2)
    one(0).wait_recv()
    s2_ref[...] = (dn_ref[2].astype(F32) + r1_ref[0].astype(F32)).astype(BF16)
    size = tok // chunks

    def two(c):
        rows = pl.ds(c * size, size)
        return remote(s2_ref.at[rows], r2_ref.at[rows], s2s.at[c], s2r.at[c], me.d, me.t2)

    two(0).start()
    shard(me.t1, 1)
    one(1).start()
    shard(me.t, 3)
    hd = gb_ref.shape[2]
    heads_cols = (hd // 128) * HD
    l = lax.broadcasted_iota(jnp.int32, (hd, at_ref.shape[1]), 0)
    col = lax.broadcasted_iota(jnp.int32, (hd, at_ref.shape[1]), 1)
    put = ((l & 127) < HD) & (me.t * heads_cols + (l >> 7) * HD + (l & 127) == col)
    put = jnp.where(put, 1.0, 0.0).astype(BF16)
    n16 = gb_ref.shape[1] // 3
    n48 = 3 * n16
    gp_ref[0, :n48] = ga_ref[...].astype(BF16)
    for s in range(3):
        gp_ref[0, n48 + s * n16:n48 + (s + 1) * n16] = dot((0.5 * gb_ref[s, s * n16:(s + 1) * n16]).astype(BF16), put).astype(BF16)
    gp_ref[1] = gmid_ref[...].astype(BF16)

    g1 = remote(gp_ref.at[1 - me.c], gr_ref.at[0], g1s.at[0], g1r.at[0], me.d, me.t1)
    g1.start()
    g1.wait_recv()
    g2_ref[...] = (gp_ref[me.c].astype(F32) + gr_ref[0].astype(F32)).astype(BF16)
    g2 = remote(g2_ref, gr_ref.at[1], g1s.at[1], g1r.at[1], me.d, me.t2)
    g2.start()
    for c in range(1, chunks):
        two(c).start()
    g2.wait_recv()
    gown_ref[...] = (g2_ref[...].astype(F32) + gr_ref[1].astype(F32)).astype(BF16)
    g = PairLine(me, gown_ref, gall_ref.at[me.c], gs, gr)
    g.start()

    def relay(o, own=False):
        return remote(gown_ref if own else gall_ref.at[me.c, o], gall_ref.at[me.c, o], fs.at[o], fr.at[o], me.d, me.t1)

    relay(me.d, True).start()
    keep = pltpu.make_async_copy(gown_ref, gall_ref.at[me.c, me.d], ls.at[0])
    keep.start()
    lax.fori_loop(1, me.line, lambda k, c: (g.hop(k, lambda o: relay(o).start()), c)[1], 0)
    g.pair_arrivals(lambda o: relay(o).start())
    one(1).wait_recv()
    for c in range(chunks):
        two(c).wait_recv()
        rows = pl.ds(c * size, size)
        dn = dn_ref[3, rows, :].astype(F32) + r1_ref[1, rows, :].astype(F32) + r2_ref[rows, :].astype(F32)
        x = x_ref[rows, :].astype(F32)
        r = lax.rsqrt(jnp.mean(x * x, axis=-1, keepdims=True) + EPS)
        gd = gain_ref[0:1, :] * dn
        ig_ref[rows, :] = dmid_ref[rows, :] + r * gd - x * (r * r * r * jnp.mean(x * gd, axis=-1, keepdims=True))
    def settle(o, c):
        remote(gown_ref, gall_ref.at[1 - me.c, o], fs.at[o], fr.at[o], me.d, me.t1).wait_recv()
        remote(gown_ref, gall_ref.at[1 - me.c, o], fs.at[o], fr.at[o], me.d, me.t1).wait_send()
        return c
    lax.fori_loop(0, ndp, settle, 0)
    g.sent()
    keep.wait()
    for slot in range(2):
        one(slot).wait_send()
    for c in range(chunks):
        two(c).wait_send()
    g1.wait_send()
    g2.wait_send()


def place_kernel(e_ref, g_ref, ain_ref, bqkv_ref, bup_ref, aout_ref, adown_ref, bres_ref):
    ndp = g_ref.shape[1]
    for ref in (ain_ref, bqkv_ref, bup_ref, aout_ref, adown_ref, bres_ref):
        ref[...] = jnp.zeros_like(ref)

    def add(d, c):
        e = e_ref[d]
        for n in range(3):
            ain_ref[n, e] += g_ref[0, d, n * 16:(n + 1) * 16, :].astype(F32)
            bqkv_ref[n, e] += g_ref[0, d, (3 + n) * 16:(4 + n) * 16, :].astype(F32)
        ain_ref[3, e] += g_ref[1, d, 0:16, :].astype(F32)
        bup_ref[e] += g_ref[1, d, 16:32, :].astype(F32)
        aout_ref[e] += g_ref[1, d, 32:48, :].astype(F32)
        adown_ref[e] += g_ref[1, d, 48:64, :].astype(F32)
        bres_ref[0, e] += g_ref[1, d, 64:80, :].astype(F32)
        bres_ref[1, e] += g_ref[1, d, 80:96, :].astype(F32)
        return c
    lax.fori_loop(0, ndp, add, 0)


VMEM = pltpu.VMEM
DMA = pltpu.SemaphoreType.DMA
IN_VMEM = pl.BlockSpec(memory_space=pltpu.VMEM)
IN_SMEM = pl.BlockSpec(memory_space=pltpu.SMEM)
IN_ANY = pl.BlockSpec(memory_space=pl.ANY)


def shape(*dims, dtype=BF16):
    return jax.ShapeDtypeStruct(dims, dtype)


def params(cid=None, limit=60 << 20):
    if cid is None:
        return pltpu.CompilerParams(vmem_limit_bytes=limit)
    return pltpu.CompilerParams(collective_id=cid, has_side_effects=True, vmem_limit_bytes=limit)


def local(
    inputs, cotangent, adapter_choice_per_tree, segment_lengths, segment_parents, norm_gain_rows, query_dimension_scale,
    attention_weights, output_weight, feedforward_weights, adapter_first_input, adapter_second_attention, adapter_second_up,
    adapter_first_output, adapter_first_down, adapter_second_residual,
):
    ndp, nt = lax.axis_size("dp"), lax.axis_size("tensor")
    tpos = lax.axis_index("tensor")
    tok, width = inputs.shape
    tree = tok * nt
    wrows, hcols = output_weight.shape
    heads = hcols // HD
    pad = heads * 128
    segs = segment_lengths.shape[1]
    rank = adapter_first_input.shape[3]
    nblk = tree // BLK
    e = adapter_choice_per_tree[0]
    lens, parents = segment_lengths[0], segment_parents[0]

    def pick(table, axis):
        return lax.dynamic_index_in_dim(table, e, axis, keepdims=False)

    a_in = pick(jnp.swapaxes(adapter_first_input, 2, 3), 1)
    b_attn = lax.dynamic_slice_in_dim(pick(adapter_second_attention, 1), tpos * hcols, hcols, 2)
    b_res = pick(adapter_second_residual, 1)
    at_qkv = a_in[:3].reshape(3 * rank, width)
    at_mid = jnp.stack([pick(jnp.swapaxes(adapter_first_output, 1, 2), 0), a_in[3], pick(jnp.swapaxes(adapter_first_down, 1, 2), 0)])
    b_mid = jnp.stack([b_res[0], pick(adapter_second_up, 0), b_res[1]])
    ends = jnp.cumsum(lens)
    lane = jnp.arange(128, dtype=jnp.int32) - HD
    spot = (lane[None, :] == jnp.arange(segs, dtype=jnp.int32)[:, None])
    seg = jnp.stack([jnp.sum(jnp.where(spot, (ends - lens)[:, None], 0), 0), jnp.sum(jnp.where(spot, ends[:, None], 0), 0)]
                    + [jnp.zeros((128,), jnp.int32)] * 6).astype(F32)
    idx = jnp.arange(segs, dtype=jnp.int32)
    grand = jnp.sum(jnp.where(parents[:, None] == idx[None, :], parents[None, :], 0), axis=1)
    reach = (idx[:, None] == idx[None, :]) | (parents[:, None] == idx[None, :]) | (grand[:, None] == idx[None, :])
    mq = jnp.pad(jnp.where(reach, 0.0, -BIG).astype(BF16), ((HD, 128 - HD - segs), (HD, 128 - HD - segs)))
    scale = jnp.pad(jnp.broadcast_to(query_dimension_scale[None, :] / math.sqrt(HD), (heads, HD)), ((0, 0), (0, 128 - HD))).reshape(1, pad)

    chunks = 4
    choice = jnp.full((8, 128), e, F32)
    wr = wrows * 3
    xn, wa, wall, choices = pl.pallas_call(
        functools.partial(gather_kernel, ndp, chunks),
        out_shape=[shape(nt, tok, width), shape(ndp, wr, hcols), shape(ndp, nt, wr, hcols), shape(ndp, 8, 128, dtype=F32)],
        in_specs=[IN_VMEM] * 3 + [IN_ANY] * 3, out_specs=[IN_ANY] * 4,
        scratch_shapes=[VMEM((tok, width), BF16), VMEM((wr, hcols), BF16), VMEM((wr, hcols), BF16), DMA((4,)),
                        DMA((3, chunks)), DMA((nt, chunks)), DMA((3, ndp)), DMA((ndp,)), DMA((3, ndp)), DMA((ndp,)),
                        DMA((2, ndp, nt, 4)), DMA((2,)), DMA((2, ndp, nt))],
        compiler_params=params(1), name="gather",
    )(inputs, norm_gain_rows, choice, attention_weights.reshape(wr, hcols), output_weight, feedforward_weights.reshape(2 * wrows, hcols))
    xn = xn.reshape(tree, width)
    wq = wa.reshape(ndp, 3, wrows, hcols).swapaxes(0, 1).reshape(3, width, hcols)
    wmid = wall.reshape(ndp, nt, 3, wrows, hcols).transpose(2, 0, 3, 1, 4).reshape(3, width, nt * hcols)

    q, qt, k, kt, v, ranks, mixt, mix, wp, bp = pl.pallas_call(
        fwd_kernel,
        out_shape=[shape(heads, tree, 128), shape(heads, 128, tree), shape(heads, tree, 128), shape(heads, HD, tree), shape(heads, tree, 128),
                   shape(tree, 3 * rank), shape(hcols, tree), shape(tree, hcols), shape(3, width, pad), shape(3, 3 * rank, pad)],
        in_specs=[IN_VMEM] * 7, out_specs=[IN_VMEM] * 10,
        scratch_shapes=[VMEM((heads, HD + 16, tree), BF16), VMEM((heads, 1, BLK), F32), VMEM((heads, HD + 16, BLK), F32)],
        compiler_params=params(), name="attend",
    )(xn, wq, at_qkv, b_attn, scale, seg, mq)

    def swap(x, cid):
        return pl.pallas_call(
            functools.partial(swap_kernel, ndp), out_shape=shape(nt, tok, hcols), in_specs=[IN_VMEM], out_specs=IN_ANY,
            scratch_shapes=[DMA((3,)), DMA((nt,)), DMA((1,))], compiler_params=params(cid), name="swap",
        )(x)

    mixed = swap(mix, 2)
    output, d_mid, d_mix, g_mid = pl.pallas_call(
        mid_kernel,
        out_shape=[shape(tok, width), shape(tok, width, dtype=F32), shape(nt, tok, hcols), shape(6, rank, width, dtype=F32)],
        in_specs=[IN_VMEM] * 7, out_specs=[IN_VMEM] * 4,
        scratch_shapes=[VMEM((tok, width), BF16), VMEM((tok, width), F32), VMEM((tok, width), BF16), VMEM((tok, width), F32),
                        VMEM((tok, width), BF16), VMEM((tok, width), F32), VMEM((tok, width), BF16)],
        compiler_params=params(), name="middle",
    )(inputs, cotangent, mixed, norm_gain_rows, wmid, at_mid, b_mid)
    d_mixed = swap(d_mix.reshape(nt * tok, hcols), 3).reshape(tree, hcols)

    dq, dk, dv = pl.pallas_call(
        bwd_kernel, out_shape=[shape(tree, pad)] * 3, in_specs=[IN_SMEM] * 2 + [IN_VMEM] * 8, out_specs=[IN_VMEM] * 3,
        scratch_shapes=[VMEM((heads, tree, 128), BF16), VMEM((heads, 128, tree), BF16), VMEM((heads, HD, tree), F32),
                        VMEM((heads, tree, 128), F32), VMEM((heads, tree, 128), F32), pltpu.SMEM((nblk * nblk,), jnp.int32)],
        compiler_params=params(limit=62 << 20), name="attend_back",
    )(lens, parents, d_mixed, mixt, q, qt, k, kt, v, scale)

    gr = 6 * rank
    input_grad, gathered = pl.pallas_call(
        functools.partial(finish_kernel, ndp, chunks),
        out_shape=[shape(tok, width, dtype=F32), shape(2, ndp, gr, width)],
        in_specs=[IN_VMEM] * 12, out_specs=[IN_VMEM, IN_ANY],
        scratch_shapes=[VMEM((4, tok, width), BF16), VMEM((2, tok, width), BF16), VMEM((tok, width), BF16), VMEM((tok, width), BF16),
                        VMEM((3 * rank, width), F32), VMEM((3, 3 * rank, pad), F32), VMEM((2, gr, width), BF16), VMEM((2, gr, width), BF16),
                        VMEM((gr, width), BF16), VMEM((gr, width), BF16),
                        DMA((2,)), DMA((2,)), DMA((chunks,)), DMA((chunks,)), DMA((2,)), DMA((2,)), DMA((3, ndp)), DMA((ndp,)),
                        DMA((ndp,)), DMA((ndp,)), DMA((1,))],
        compiler_params=params(4, 62 << 20), name="finish",
    )(dq, dk, dv, wp, bp, at_qkv, xn, ranks, inputs, d_mid, norm_gain_rows, g_mid.reshape(gr, width))

    count = adapter_first_input.shape[1]
    ga_in, gb_qkv, gb_up, ga_out, ga_down, gb_res = pl.pallas_call(
        place_kernel,
        out_shape=[shape(4, count, rank, width, dtype=F32), shape(3, count, rank, width, dtype=F32), shape(count, rank, width, dtype=F32),
                   shape(count, rank, width, dtype=F32), shape(count, rank, width, dtype=F32), shape(2, count, rank, width, dtype=F32)],
        in_specs=[IN_SMEM, IN_VMEM], out_specs=[IN_VMEM] * 6, compiler_params=params(), name="place",
    )(choices[:, 0, 0].astype(jnp.int32), gathered)
    return (output, input_grad, jnp.swapaxes(ga_in, 2, 3), gb_qkv, gb_up, jnp.swapaxes(ga_out, 1, 2), jnp.swapaxes(ga_down, 1, 2), gb_res)


def solution(mesh):
    tokens, weights = P(("dp", "tensor"), None), P(None, "dp", "tensor")
    in_specs = (tokens, tokens, P("dp"), P("dp", None), P("dp", None), P(), P(), weights, P("dp", "tensor"), weights) + (P(),) * 6
    out_specs = (tokens, tokens) + (P(),) * 6
    return jax.shard_map(local, mesh=mesh, in_specs=in_specs, out_specs=out_specs, check_vma=False)
```

```python
import functools
import math

import jax
import jax.numpy as jnp
from jax import lax
from jax.experimental import pallas as pl
from jax.experimental.pallas import tpu as pltpu
from jax.sharding import PartitionSpec as P

F32, BF16 = jnp.float32, jnp.bfloat16
BIG = 1e30
BLK = 256
HD = 80

def dot(a, b):
    return lax.dot_general(a, b, (((1,), (0,)), ((), ())), preferred_element_type=F32)
def dot_nt(a, b):
    return lax.dot_general(a, b, (((1,), (1,)), ((), ())), preferred_element_type=F32)
def dot_tn(a, b):
    return lax.dot_general(a, b, (((0,), (0,)), ((), ())), preferred_element_type=F32)

def project(b, x_ref, wp_ref, a_ref, bp_ref, scale_ref, seg_ref, mq_ref, q_ref, qt_ref, k_ref, kt_ref, v_ref, vt_ref, rank_ref):
    rows = pl.ds(pl.multiple_of(b * BLK, BLK), BLK)
    xb = x_ref[rows, :]
    rank = dot_nt(xb, a_ref[...]).astype(BF16)
    rank_ref[rows, :] = rank
    lane = lax.broadcasted_iota(jnp.int32, (BLK, 128), 1)
    tok = (lax.broadcasted_iota(jnp.int32, (BLK, 128), 0) + b * BLK).astype(F32)
    hot = jnp.where((tok >= seg_ref[0:1, :]) & (tok < seg_ref[1:2, :]), 1.0, 0.0)
    qfeat = dot(hot.astype(BF16), mq_ref[...])
    kfeat = jnp.where((lane >= HD + 13) & (lane < HD + 16), 1.0, hot)
    vfeat = jnp.where(lane < HD + 2, 1.0, 0.0)
    heads = q_ref.shape[0]
    for s, (n_ref, t_ref, feat) in enumerate(((q_ref, qt_ref, qfeat), (k_ref, kt_ref, kfeat), (v_ref, vt_ref, vfeat))):
        y = dot(xb, wp_ref[s]) + dot(rank, bp_ref[s])
        if s == 0:
            y = y * scale_ref[...]
        for h in range(heads):
            yh = jnp.where(lane < HD, y[:, h * 128:(h + 1) * 128], feat)
            n_ref[h, rows, :] = yh.astype(BF16)
            yt = yh.T
            t_ref[h, :, rows] = yt[:t_ref.shape[1]].astype(BF16)

def attend_block(i, qt_ref, k_ref, vt_ref, m_ref, acc_ref, mixt_ref, mix_ref, count=None, jlist=None):
    heads = qt_ref.shape[0]
    cols = pl.ds(pl.multiple_of(i * BLK, BLK), BLK)
    m_ref[...] = jnp.full_like(m_ref, -3e38)
    acc_ref[...] = jnp.zeros_like(acc_ref)
    def step(j, diag):
        rows = pl.ds(pl.multiple_of(j * BLK, BLK), BLK)
        hs = range(heads)
        ss = [dot(k_ref[h, rows, :], qt_ref[h, :, cols]) for h in hs]
        if diag:
            low = lax.broadcasted_iota(jnp.int32, ss[0].shape, 0) <= lax.broadcasted_iota(jnp.int32, ss[0].shape, 1)
            ss = [jnp.where(low, s, -BIG) for s in ss]
        olds = [m_ref[h] for h in hs]
        news = [jnp.maximum(olds[h], jnp.max(ss[h], axis=0, keepdims=True)) for h in hs]
        ps = [jnp.exp(ss[h] - news[h]).astype(BF16) for h in hs]
        pv = [dot(vt_ref[h, :, rows], ps[h]) for h in hs]
        accs = [acc_ref[h] * jnp.exp(olds[h] - news[h]) + pv[h] for h in hs]
        for h in hs:
            acc_ref[h] = accs[h]
            m_ref[h] = news[h]
    if jlist is None:
        lax.fori_loop(0, i, lambda j, c: (step(j, False), c)[1], 0)
    else:
        lax.fori_loop(0, count, lambda n, c: (step(jlist(n), False), c)[1], 0)
    step(i, True)
    outs = []
    for h in range(heads):
        acc = acc_ref[h]
        l = acc[HD:HD + 1]
        o = acc[:HD] * (1.0 / l)
        lse = m_ref[h] + jnp.log(l)
        hi = (-lse).astype(BF16).astype(F32)
        mid = (-lse - hi).astype(BF16).astype(F32)
        lo = -lse - hi - mid
        r = lax.broadcasted_iota(jnp.int32, (16, BLK), 0)
        old = qt_ref[h, HD:HD + 16, cols].astype(F32)
        new = jnp.where(r == 13, hi, jnp.where(r == 14, mid, jnp.where(r == 15, lo, old)))
        qt_ref[h, HD:HD + 16, cols] = new.astype(BF16)
        outs.append(o)
    ot = jnp.concatenate(outs, axis=0)
    mixt_ref[:, cols] = ot.astype(BF16)
    mix_ref[cols, :] = ot.T.astype(BF16)

def seg_masks(len_ref, par_ref, segs, nblk):
    start, km, qm = 0, [0] * nblk, [0] * nblk
    for u in range(segs):
        end = start + len_ref[u]
        up = par_ref[u]
        anc = jnp.int32(1 << u) | (jnp.int32(1) << up) | (jnp.int32(1) << par_ref[up])
        for b in range(nblk):
            inside = (start < (b + 1) * BLK) & (end > b * BLK)
            km[b] = km[b] | jnp.where(inside, jnp.int32(1 << u), 0)
            qm[b] = qm[b] | jnp.where(inside, anc, 0)
        start = end
    return km, qm

def spread_heads(hcols, pad):
    c = lax.broadcasted_iota(jnp.int32, (hcols, pad), 0)
    l = lax.broadcasted_iota(jnp.int32, (hcols, pad), 1)
    return jnp.where(((l & 127) < HD) & ((l >> 7) * HD + (l & 127) == c), 1.0, 0.0).astype(BF16)


def bwd_prep(b, dm_ref, mixt_ref, do_ref, dot_ref):
    rows = pl.ds(pl.multiple_of(b * BLK, BLK), BLK)
    heads = do_ref.shape[0]
    dt = dm_ref[rows, :].astype(F32).T
    prod = dt * mixt_ref[:, rows].astype(F32)
    r = lax.broadcasted_iota(jnp.int32, (16, BLK), 0)
    for h in range(heads):
        d = dt[h * HD:(h + 1) * HD]
        delta = -jnp.sum(prod[h * HD:(h + 1) * HD], axis=0, keepdims=True)
        hi = delta.astype(BF16).astype(F32)
        ext = jnp.where(r == 0, hi, jnp.where(r == 1, delta - hi, 0.0))
        full = jnp.concatenate([d, ext, jnp.zeros((32, BLK), F32)], axis=0)
        dot_ref[h, :, rows] = full.astype(BF16)
        do_ref[h, rows, :] = full.T.astype(BF16)

def bwd_pair(i, j, diag, q_ref, qt_ref, k_ref, kt_ref, v_ref, do_ref, dot_ref, dqt_ref, dk_ref, dv_ref):
    heads = q_ref.shape[0]
    cols = pl.ds(pl.multiple_of(i * BLK, BLK), BLK)
    rows = pl.ds(pl.multiple_of(j * BLK, BLK), BLK)
    hs = range(heads)
    ss = [dot(k_ref[h, rows, :], qt_ref[h, :, cols]) for h in hs]
    dps = [dot(v_ref[h, rows, :], dot_ref[h, :, cols]) for h in hs]
    if diag:
        low = lax.broadcasted_iota(jnp.int32, ss[0].shape, 0) <= lax.broadcasted_iota(jnp.int32, ss[0].shape, 1)
        ss = [jnp.where(low, s, -BIG) for s in ss]
    ps = [jnp.exp(s) for s in ss]
    dss = [(p * dp).astype(BF16) for p, dp in zip(ps, dps)]
    ps = [p.astype(BF16) for p in ps]
    dvs = [dot(ps[h], do_ref[h, cols, :]) for h in hs]
    dks = [dot(dss[h], q_ref[h, cols, :]) for h in hs]
    dqs = [dot(kt_ref[h, :, rows], dss[h]) for h in hs]
    for h in hs:
        dv_ref[h, rows, :] += dvs[h]
        dk_ref[h, rows, :] += dks[h]
        dqt_ref[h, :, cols] += dqs[h]

def bwd_kernel(len_ref, par_ref, dm_ref, mixt_ref, q_ref, qt_ref, k_ref, kt_ref, v_ref, scale_ref,
               dqo_ref, dko_ref, dvo_ref, do_ref, dot_ref, dqt_ref, dk_ref, dv_ref, list_ref):
    nblk = dm_ref.shape[0] // BLK
    heads = q_ref.shape[0]
    km, qm = seg_masks(len_ref, par_ref, len_ref.shape[0], nblk)
    n = jnp.int32(0)
    for j in range(nblk):
        for i in range(j + 1, nblk):
            list_ref[n] = jnp.int32(i * nblk + j)
            n = n + jnp.where((qm[i] & km[j]) != 0, 1, 0)
    dqt_ref[...] = jnp.zeros_like(dqt_ref)
    dk_ref[...] = jnp.zeros_like(dk_ref)
    dv_ref[...] = jnp.zeros_like(dv_ref)
    lax.fori_loop(0, nblk, lambda b, c: (bwd_prep(b, dm_ref, mixt_ref, do_ref, dot_ref), c)[1], 0)
    args = (q_ref, qt_ref, k_ref, kt_ref, v_ref, do_ref, dot_ref, dqt_ref, dk_ref, dv_ref)
    lax.fori_loop(0, nblk, lambda b, c: (bwd_pair(b, b, True, *args), c)[1], 0)
    def one(t, c):
        w = list_ref[t]
        bwd_pair(w // nblk, w % nblk, False, *args)
        return c
    lax.fori_loop(0, n, one, 0)
    lane = lax.broadcasted_iota(jnp.int32, (BLK, 128), 1)
    def finish(b, c):
        rows = pl.ds(pl.multiple_of(b * BLK, BLK), BLK)
        for h in range(heads):
            hl = slice(h * 128, (h + 1) * 128)
            dq = jnp.concatenate([dqt_ref[h, :, rows], jnp.zeros((48, BLK), F32)], axis=0).T
            dqo_ref[rows, hl] = (dq * scale_ref[:, hl]).astype(BF16)
            dko_ref[rows, hl] = jnp.where(lane < HD, dk_ref[h, rows, :], 0.0).astype(BF16)
            dvo_ref[rows, hl] = jnp.where(lane < HD, dv_ref[h, rows, :], 0.0).astype(BF16)
        return c
    lax.fori_loop(0, nblk, finish, 0)


MESH = pl.DeviceIdType.MESH


class Place:
    def __init__(self, ndp):
        self.d, self.t = lax.axis_index("dp"), lax.axis_index("tensor")
        self.line = ndp // 2
        self.p, self.par = self.d // 2, self.d % 2
        self.dx = self.d + 1 - 2 * self.par
        self.c, self.y = self.t % 2, self.t // 2
        self.t1 = self.t + 1 - 2 * self.c
        self.t2 = (self.t + 2) % 4
        self.t3 = (self.t1 + 2) % 4
        self.has_left, self.has_right = self.p > 0, self.p < self.line - 1


def signal(sem, d, t):
    pl.semaphore_signal(sem, inc=1, device_id=(d, t), device_id_type=MESH)


def remote(src, dst, send_sem, recv_sem, d, t):
    return pltpu.make_async_remote_copy(src_ref=src, dst_ref=dst, send_sem=send_sem, recv_sem=recv_sem, device_id=(d, t), device_id_type=MESH)


def greet(me, tensor=(), pair=False, line=False):
    bar = pltpu.get_barrier_semaphore()
    count = len(tensor) + (1 if pair else 0)
    for t in tensor:
        signal(bar, me.d, t)
    if pair:
        signal(bar, me.dx, me.t)
    if line:
        @pl.when(me.has_left)
        def _():
            signal(bar, me.d - 2, me.t)
        @pl.when(me.has_right)
        def _():
            signal(bar, me.d + 2, me.t)
        count = count + jnp.where(me.has_left, 1, 0) + jnp.where(me.has_right, 1, 0)
    pl.semaphore_wait(bar, count)


class PairLine:
    def __init__(self, me, own, buf, send, recv):
        self.me, self.own, self.buf, self.send, self.recv = me, own, buf, send, recv

    def copy(self, o, src, d, kind):
        return remote(src, self.buf.at[o], self.send.at[kind, o], self.recv.at[o], d, self.me.t)

    def start(self):
        me = self.me
        @pl.when(me.has_left)
        def _():
            self.copy(me.d, self.own, me.d - 2, 0).start()
        @pl.when(me.has_right)
        def _():
            self.copy(me.d, self.own, me.d + 2, 1).start()
        self.copy(me.d, self.own, me.dx, 2).start()

    def hop(self, k, then=None):
        me = self.me
        @pl.when(me.p - k >= 0)
        def _():
            o = me.d - 2 * k
            self.copy(o, self.buf.at[o], me.dx, 2).wait_recv()
            @pl.when(me.has_right)
            def _():
                self.copy(o, self.buf.at[o], me.d + 2, 1).start()
            self.copy(o, self.buf.at[o], me.dx, 2).start()
            if then is not None:
                then(o)
        @pl.when(me.p + k < me.line)
        def _():
            o = me.d + 2 * k
            self.copy(o, self.buf.at[o], me.dx, 2).wait_recv()
            @pl.when(me.has_left)
            def _():
                self.copy(o, self.buf.at[o], me.d - 2, 0).start()
            self.copy(o, self.buf.at[o], me.dx, 2).start()
            if then is not None:
                then(o)

    def pair_arrivals(self, then=None):
        def one(q, c):
            o = 2 * q + 1 - self.me.par
            self.copy(o, self.buf.at[o], self.me.dx, 2).wait_recv()
            if then is not None:
                then(o)
            return c
        lax.fori_loop(0, self.me.line, one, 0)

    def sent(self):
        me = self.me
        def one(q, c):
            o = 2 * q + me.par
            self.copy(o, self.buf.at[o], me.dx, 2).wait_send()
            @pl.when((q >= me.p) & me.has_left)
            def _():
                self.copy(o, self.buf.at[o], me.dx, 0).wait_send()
            @pl.when((q <= me.p) & me.has_right)
            def _():
                self.copy(o, self.buf.at[o], me.dx, 1).wait_send()
            return c
        lax.fori_loop(0, me.line, one, 0)


class FullGather:
    def __init__(self, me, own, buf, send, first, recv):
        self.me, self.own, self.buf, self.send, self.first, self.recv = me, own, buf, send, first, recv
        cut = own.shape[0] // 32 * 16
        self.parts = (pl.ds(0, cut), pl.ds(cut, own.shape[0] - cut))

    def copy(self, h, o, t, d2, t2, kind, own=False):
        rows = self.parts[h]
        src = self.own.at[rows] if own else self.buf.at[o, t, rows]
        sem = self.first.at[h] if kind == 4 else self.send.at[h, o, t, kind]
        return remote(src, self.buf.at[o, t, rows], sem, self.recv.at[h, o, t], d2, t2)

    def last(self, h):
        me = self.me
        return (me.d, me.t2) if h == 0 else (me.dx, me.t)

    def spread(self, h, o, t, left, right, own=False):
        me = self.me
        @pl.when(left)
        def _():
            self.copy(h, o, t, me.d - 2, me.t, 0, own).start()
        @pl.when(right)
        def _():
            self.copy(h, o, t, me.d + 2, me.t, 1, own).start()
        self.copy(h, o, t, *self.last(h), 2, own).start()
        self.copy(h, o, t, me.d, me.t1, 3, own).start()

    def start(self):
        me = self.me
        self.copy(0, me.d, me.t, me.dx, me.t, 4, True).start()
        self.copy(1, me.d, me.t, me.d, me.t2, 4, True).start()
        for h in range(2):
            self.spread(h, me.d, me.t, me.has_left, me.has_right, True)

    def arrived(self, h, o, t):
        self.copy(h, o, t, self.me.d, self.me.t1, 3).wait_recv()

    def firsts(self):
        me = self.me
        self.arrived(0, me.dx, me.t)
        self.spread(0, me.dx, me.t, me.has_left, me.has_right)
        self.arrived(1, me.d, me.t2)
        self.spread(1, me.d, me.t2, me.has_left, me.has_right)

    def streams(self, q):
        me = self.me
        return ((0, 2 * q + me.par, me.t), (0, 2 * q + 1 - me.par, me.t), (1, 2 * q + me.par, me.t), (1, 2 * q + me.par, me.t2))

    def hop(self, k):
        me = self.me
        @pl.when(me.p - k >= 0)
        def _():
            for h, o, t in self.streams(me.p - k):
                self.arrived(h, o, t)
                self.spread(h, o, t, False, me.has_right)
        @pl.when(me.p + k < me.line)
        def _():
            for h, o, t in self.streams(me.p + k):
                self.arrived(h, o, t)
                self.spread(h, o, t, me.has_left, False)

    def lasts(self):
        me = self.me
        def one(q, c):
            for h, o, t in ((0, 2 * q, me.t2), (0, 2 * q + 1, me.t2), (1, 2 * q + 1 - me.par, me.t), (1, 2 * q + 1 - me.par, me.t2)):
                self.arrived(h, o, t)
                self.copy(h, o, t, me.d, me.t1, 3).start()
            return c
        lax.fori_loop(0, me.line, one, 0)

    def finish(self):
        me = self.me
        def one(o, c):
            for h in range(2):
                self.arrived(h, o, me.t1)
                self.arrived(h, o, me.t3)
                for t in (me.t, me.t2):
                    self.copy(h, o, t, me.d, me.t1, 3).wait_send()
            return c
        lax.fori_loop(0, 2 * me.line, one, 0)
        def two(q, c):
            for h, o, t in self.streams(q):
                self.copy(h, o, t, me.d, me.t1, 2).wait_send()
                @pl.when((q >= me.p) & me.has_left)
                def _():
                    self.copy(h, o, t, me.d, me.t1, 0).wait_send()
                @pl.when((q <= me.p) & me.has_right)
                def _():
                    self.copy(h, o, t, me.d, me.t1, 1).wait_send()
            return c
        lax.fori_loop(0, me.line, two, 0)
        for h in range(2):
            self.copy(h, me.d, me.t, me.d, me.t1, 4).wait_send()


EPS = 1e-6


def forward_kernel(ndp, chunks, x_ref, gain_ref, choice_ref, at_ref, b_ref, scale_ref, seg_ref, mq_ref, a_ref, wo_ref, wf_ref,
                   wout_ref, cho_ref, mixed_ref, xno_ref, qo_ref, qto_ref, ko_ref, kto_ref, vo_ref, ranko_ref, mixto_ref, wpo_ref, bpo_ref,
                   aown_ref, wown_ref, xn_ref, wa_ref, wp_ref, bp_ref, q_ref, qt_ref, k_ref, kt_ref, v_ref, vt_ref, rank_ref, mixt_ref,
                   mix_ref, m_ref, acc_ref, ls, os, xs, xr, a_s, a_r, c_s, c_r, w_s, w_f, w_r, ms, mr):
    me = Place(ndp)
    tok, width = x_ref.shape
    rows_o = wo_ref.shape[0]
    loads = [pltpu.make_async_copy(a_ref, aown_ref, ls.at[0]), pltpu.make_async_copy(wo_ref, wown_ref.at[pl.ds(0, rows_o)], ls.at[1]),
             pltpu.make_async_copy(wf_ref, wown_ref.at[pl.ds(rows_o, wf_ref.shape[0])], ls.at[2])]
    for copy in loads:
        copy.start()
    x = x_ref[...].astype(F32)
    mine = pl.ds(pl.multiple_of(me.t * tok, tok), tok)
    xn_ref[mine, :] = (x * lax.rsqrt(jnp.mean(x * x, axis=-1, keepdims=True) + EPS) * gain_ref[0:1, :]).astype(BF16)
    greet(me, tensor=(me.t1, me.t2, me.t3), pair=True, line=True)
    size = tok // chunks

    def xcopy(o, c, t, kind):
        rows = pl.ds(pl.multiple_of(o * tok + c * size, size), size)
        return remote(xn_ref.at[rows], xn_ref.at[rows], xs.at[kind, c], xr.at[o, c], me.d, t)

    for c in range(chunks):
        xcopy(me.t, c, me.t2, 0).start()
    for c in range(chunks):
        xcopy(me.t, c, me.t1, 1).start()
    for copy in loads:
        copy.wait()
    a = PairLine(me, aown_ref, wa_ref, a_s, a_r)
    ch = PairLine(me, choice_ref, cho_ref, c_s, c_r)
    w = FullGather(me, wown_ref, wout_ref, w_s, w_f, w_r)
    a.start()
    ch.start()
    keep = [pltpu.make_async_copy(wown_ref, wout_ref.at[me.d, me.t], ls.at[0]), pltpu.make_async_copy(choice_ref, cho_ref.at[me.d], ls.at[1])]
    for copy in keep:
        copy.start()
    wa_ref[me.d] = aown_ref[...]
    early = max(1, me.line - 2)

    def hop(k, carry):
        a.hop(k)
        ch.hop(k)
        return carry
    lax.fori_loop(1, early + 1, hop, 0)
    w.start()

    def forward(c):
        xcopy(me.t2, c, me.t1, 2).wait_recv()
        xcopy(me.t2, c, me.t1, 2).start()

    for c in range(chunks // 2):
        forward(c)
    lax.fori_loop(early + 1, me.line, hop, 0)
    for c in range(chunks // 2, chunks):
        forward(c)
    a.pair_arrivals()
    ch.pair_arrivals()

    sel = spread_heads(wa_ref.shape[2], wp_ref.shape[2])
    bp_ref[...] = jnp.zeros_like(bp_ref)
    wrows = wa_ref.shape[1] // 3
    group = 16 // math.gcd(wrows, 16)
    for s in range(3):
        n = b_ref.shape[1]
        bp_ref[s, s * n:(s + 1) * n] = (0.5 * dot(b_ref[s], sel)).astype(BF16)
        for o in range(0, ndp, group):
            wp_ref[s, o * wrows:(o + group) * wrows] = jnp.concatenate(
                [dot(wa_ref[o + j, s * wrows:(s + 1) * wrows], sel) for j in range(group)], axis=0).astype(BF16)
    for c in range(chunks):
        xcopy(me.t1, c, me.t1, 2).wait_recv()
        xcopy(me.t3, c, me.t1, 2).wait_recv()
    w.firsts()
    nblk = xn_ref.shape[0] // BLK
    span = 2 * nblk - 3

    def upto(step):
        return 1 + jnp.minimum(step * (me.line - 1) // span, me.line - 1)

    def relay(step):
        lax.fori_loop(upto(step), upto(step + 1), lambda k, c: (w.hop(k), c)[1], 0)

    def project_step(b, c):
        project(b, xn_ref, wp_ref, at_ref, bp_ref, scale_ref, seg_ref, mq_ref, q_ref, qt_ref, k_ref, kt_ref, v_ref, vt_ref, rank_ref)
        relay(b)
        return c
    lax.fori_loop(0, nblk, project_step, 0)
    outs = [pltpu.make_async_copy(src, dst, os.at[n]) for n, (src, dst) in enumerate((
        (xn_ref, xno_ref), (q_ref, qo_ref), (k_ref, ko_ref), (kt_ref, kto_ref), (v_ref, vo_ref), (rank_ref, ranko_ref),
        (wp_ref, wpo_ref), (bp_ref, bpo_ref)))]
    for copy in outs:
        copy.start()
    per = tok // BLK

    def piece(i):
        rows = pl.ds(pl.multiple_of(i * BLK, BLK), BLK)
        return mix_ref.at[rows], mixed_ref.at[me.t, pl.ds(pl.multiple_of((i % per) * BLK, BLK), BLK)], i // per

    def attend_step(i, c):
        attend_block(i, qt_ref, k_ref, vt_ref, m_ref, acc_ref, mixt_ref, mix_ref)
        src, dst, t = piece(i)
        @pl.when(t == me.t)
        def _():
            pltpu.make_async_copy(src, dst, ms.at[i]).start()
        @pl.when(t != me.t)
        def _():
            remote(src, dst, ms.at[i], mr.at[me.t, i % per], me.d, t).start()
        relay(nblk + i)
        return c
    lax.fori_loop(0, nblk, attend_step, 0)
    late = [pltpu.make_async_copy(qt_ref, qto_ref, os.at[len(outs)]), pltpu.make_async_copy(mixt_ref, mixto_ref, os.at[len(outs) + 1])]
    for copy in late:
        copy.start()
    w.lasts()
    for t in (me.t1, me.t2, me.t3):
        for h in range(per):
            dst = mixed_ref.at[t, pl.ds(h * BLK, BLK)]
            remote(dst, dst, ms.at[0], mr.at[t, h], me.d, t).wait_recv()
    w.finish()
    a.sent()
    ch.sent()
    for c in range(chunks):
        for kind in range(3):
            xcopy(me.t, c, me.t1, kind).wait_send()

    def settle(i, c):
        src, dst, t = piece(i)
        @pl.when(t == me.t)
        def _():
            pltpu.make_async_copy(src, dst, ms.at[i]).wait()
        @pl.when(t != me.t)
        def _():
            remote(src, dst, ms.at[i], mr.at[me.t, i % per], me.d, t).wait_send()
        return c
    lax.fori_loop(0, nblk, settle, 0)
    for copy in keep + outs + late:
        copy.wait()


def swap_kernel(ndp, x_ref, o_ref, send, recv, ls):
    me = Place(ndp)
    greet(me, tensor=(me.t1, me.t2, me.t3))
    size = o_ref.shape[1]

    def copy(n, t):
        return remote(x_ref.at[pl.ds(pl.multiple_of(t * size, size), size)], o_ref.at[me.t], send.at[n], recv.at[me.t], me.d, t)

    own = pltpu.make_async_copy(x_ref.at[pl.ds(pl.multiple_of(me.t * size, size), size)], o_ref.at[me.t], ls.at[0])
    for n, t in enumerate((me.t3, me.t2, me.t1)):
        copy(n, t).start()
    own.start()
    for t in (me.t1, me.t2, me.t3):
        remote(o_ref.at[t], o_ref.at[t], send.at[0], recv.at[t], me.d, t).wait_recv()
    for n, t in enumerate((me.t3, me.t2, me.t1)):
        copy(n, t).wait_send()
    own.wait()


def sigmoid(v):
    return 1.0 / (1.0 + jnp.exp(-v))


def mid_kernel(x_ref, g_ref, mix4_ref, gain_ref, at_ref, b_ref, wall_ref, out_ref, dmid_ref, dmix_ref, grads_ref,
               mix_ref, mid_ref, hid_ref, up_ref, act_ref, f_ref, low_ref, w_ref, wb0_ref, wb1_ref, wb2_ref, ls):
    width = x_ref.shape[1]
    step = 256
    part = mix4_ref.shape[2]
    blocks = (wb0_ref, wb1_ref, wb2_ref)
    ndp, nt, wrows = wb0_ref.shape[:3]
    loads = [pltpu.make_async_copy(wall_ref.at[:, :, pl.ds(n * wrows, wrows)], blocks[n], ls.at[n]) for n in range(3)]
    for copy in loads:
        copy.start()

    def assemble(n):
        loads[n].wait()
        for o in range(ndp):
            for t in range(nt):
                w_ref[n, o * wrows:(o + 1) * wrows, t * part:(t + 1) * part] = blocks[n][o, t]

    for t in range(mix4_ref.shape[0]):
        mix_ref[:, t * part:(t + 1) * part] = mix4_ref[t]

    def cols(n):
        return pl.ds(pl.multiple_of(n * step, step), step)

    def each(fn):
        lax.fori_loop(0, width // step, lambda n, c: (fn(cols(n)), c)[1], 0)

    gain = gain_ref[1:2, :]
    r_out = dot_nt(mix_ref[...], at_ref[0]).astype(BF16)
    assemble(0)

    def project_out(n):
        attn = dot_nt(mix_ref[...], w_ref[0, n, :]) + 0.5 * dot(r_out, b_ref[0, :, n])
        mid_ref[:, n] = x_ref[:, n].astype(F32) + attn
    each(project_out)
    middle = mid_ref[...]
    r = lax.rsqrt(jnp.mean(middle * middle, axis=-1, keepdims=True) + EPS)
    hid_ref[...] = (middle * r * gain).astype(BF16)
    r_up = dot_nt(hid_ref[...], at_ref[1]).astype(BF16)
    assemble(1)

    def up_step(n):
        up = dot(hid_ref[...], w_ref[1, :, n]) + 0.5 * dot(r_up, b_ref[1, :, n])
        up_ref[:, n] = up
        act_ref[:, n] = (up * sigmoid(up)).astype(BF16)
    each(up_step)
    r_down = dot_nt(act_ref[...], at_ref[2]).astype(BF16)
    assemble(2)

    def down_step(n):
        down = dot_nt(act_ref[...], w_ref[2, n, :]) + 0.5 * dot(r_down, b_ref[2, :, n])
        out_ref[:, n] = (mid_ref[:, n] + down).astype(BF16)
    each(down_step)
    grads_ref[5] = 0.5 * dot_tn(r_down, g_ref[...])
    dz_down = (0.5 * dot_nt(g_ref[...], b_ref[2])).astype(BF16)
    grads_ref[3] = dot_tn(dz_down, act_ref[...])

    def act_back(n):
        d_act = dot(g_ref[...], w_ref[2, :, n]) + dot(dz_down, at_ref[2, :, n])
        up = up_ref[:, n]
        sg = sigmoid(up)
        low_ref[:, n] = (d_act * sg * (1.0 + up * (1.0 - sg))).astype(BF16)
    each(act_back)
    dz_up = (0.5 * dot_nt(low_ref[...], b_ref[1])).astype(BF16)
    grads_ref[1] = 0.5 * dot_tn(r_up, low_ref[...])
    grads_ref[0] = dot_tn(dz_up, hid_ref[...])

    def hidden_back(n):
        f_ref[:, n] = (dot_nt(low_ref[...], w_ref[1, n, :]) + dot(dz_up, at_ref[1, :, n])) * gain_ref[1:2, n]
    each(hidden_back)
    gd = f_ref[...]
    middle = mid_ref[...]
    s = jnp.mean(middle * gd, axis=-1, keepdims=True)
    d_mid = g_ref[...].astype(F32) + r * gd - middle * (r * r * r * s)
    dmid_ref[...] = d_mid
    low_ref[...] = d_mid.astype(BF16)
    dz_out = (0.5 * dot_nt(low_ref[...], b_ref[0])).astype(BF16)
    grads_ref[4] = 0.5 * dot_tn(r_out, low_ref[...])
    grads_ref[2] = dot_tn(dz_out, mix_ref[...])

    def mixed_back(n):
        act_ref[:, n] = (dot(low_ref[...], w_ref[0, :, n]) + dot(dz_out, at_ref[0, :, n])).astype(BF16)
    each(mixed_back)
    for t in range(dmix_ref.shape[0]):
        dmix_ref[t] = act_ref[:, t * part:(t + 1) * part]


def finish_kernel(ndp, chunks, dq_ref, dk_ref, dv_ref, wp_ref, bp_ref, at_ref, xn_ref, rank_ref, x_ref, dmid_ref, gain_ref, gmid_ref,
                  ig_ref, gall_ref,
                  dn_ref, r1_ref, s2_ref, r2_ref, ga_ref, gb_ref, gp_ref, gr_ref, g2_ref, gown_ref,
                  s1s, s1r, s2s, s2r, g1s, g1r, gs, gr, fs, fr, ls):
    me = Place(ndp)
    tok = x_ref.shape[0]
    greet(me, tensor=(me.t1, me.t2), pair=True, line=True)
    ga_ref[...] = jnp.zeros_like(ga_ref)
    gb_ref[...] = jnp.zeros_like(gb_ref)

    def shard(t, slot):
        def half(b, c):
            rows = pl.ds(pl.multiple_of(t * tok + b * BLK, BLK), BLK)
            ds = [ref[rows, :] for ref in (dq_ref, dk_ref, dv_ref)]
            dz = sum(dot_nt(ds[s], bp_ref[s]) for s in range(3)).astype(BF16)
            dn = sum(dot_nt(ds[s], wp_ref[s]) for s in range(3)) + dot(dz, at_ref[...])
            dn_ref[slot, pl.ds(pl.multiple_of(b * BLK, BLK), BLK), :] = dn.astype(BF16)
            ga_ref[...] += dot_tn(dz, xn_ref[rows, :])
            for s in range(3):
                gb_ref[s] += dot_tn(rank_ref[rows, :], ds[s])
            return c
        lax.fori_loop(0, tok // BLK, half, 0)

    def one(slot):
        return remote(dn_ref.at[slot], r1_ref.at[slot], s1s.at[slot], s1r.at[slot], me.d, me.t1)

    shard(me.t3, 0)
    one(0).start()
    shard(me.t2, 2)
    one(0).wait_recv()
    s2_ref[...] = (dn_ref[2].astype(F32) + r1_ref[0].astype(F32)).astype(BF16)
    size = tok // chunks

    def two(c):
        rows = pl.ds(c * size, size)
        return remote(s2_ref.at[rows], r2_ref.at[rows], s2s.at[c], s2r.at[c], me.d, me.t2)

    two(0).start()
    shard(me.t1, 1)
    one(1).start()
    shard(me.t, 3)
    hd = gb_ref.shape[2]
    heads_cols = (hd // 128) * HD
    l = lax.broadcasted_iota(jnp.int32, (hd, at_ref.shape[1]), 0)
    col = lax.broadcasted_iota(jnp.int32, (hd, at_ref.shape[1]), 1)
    put = ((l & 127) < HD) & (me.t * heads_cols + (l >> 7) * HD + (l & 127) == col)
    put = jnp.where(put, 1.0, 0.0).astype(BF16)
    n16 = gb_ref.shape[1] // 3
    n48 = 3 * n16
    gp_ref[0, :n48] = ga_ref[...].astype(BF16)
    for s in range(3):
        gp_ref[0, n48 + s * n16:n48 + (s + 1) * n16] = dot((0.5 * gb_ref[s, s * n16:(s + 1) * n16]).astype(BF16), put).astype(BF16)
    gp_ref[1] = gmid_ref[...].astype(BF16)

    g1 = remote(gp_ref.at[1 - me.c], gr_ref.at[0], g1s.at[0], g1r.at[0], me.d, me.t1)
    g1.start()
    g1.wait_recv()
    g2_ref[...] = (gp_ref[me.c].astype(F32) + gr_ref[0].astype(F32)).astype(BF16)
    g2 = remote(g2_ref, gr_ref.at[1], g1s.at[1], g1r.at[1], me.d, me.t2)
    g2.start()
    for c in range(1, chunks):
        two(c).start()
    g2.wait_recv()
    gown_ref[...] = (g2_ref[...].astype(F32) + gr_ref[1].astype(F32)).astype(BF16)
    g = PairLine(me, gown_ref, gall_ref.at[me.c], gs, gr)
    g.start()

    def relay(o, own=False):
        return remote(gown_ref if own else gall_ref.at[me.c, o], gall_ref.at[me.c, o], fs.at[o], fr.at[o], me.d, me.t1)

    relay(me.d, True).start()
    keep = pltpu.make_async_copy(gown_ref, gall_ref.at[me.c, me.d], ls.at[0])
    keep.start()
    lax.fori_loop(1, me.line, lambda k, c: (g.hop(k, lambda o: relay(o).start()), c)[1], 0)
    g.pair_arrivals(lambda o: relay(o).start())
    one(1).wait_recv()
    for c in range(chunks):
        two(c).wait_recv()
        rows = pl.ds(c * size, size)
        dn = dn_ref[3, rows, :].astype(F32) + r1_ref[1, rows, :].astype(F32) + r2_ref[rows, :].astype(F32)
        x = x_ref[rows, :].astype(F32)
        r = lax.rsqrt(jnp.mean(x * x, axis=-1, keepdims=True) + EPS)
        gd = gain_ref[0:1, :] * dn
        ig_ref[rows, :] = dmid_ref[rows, :] + r * gd - x * (r * r * r * jnp.mean(x * gd, axis=-1, keepdims=True))
    def settle(o, c):
        remote(gown_ref, gall_ref.at[1 - me.c, o], fs.at[o], fr.at[o], me.d, me.t1).wait_recv()
        remote(gown_ref, gall_ref.at[1 - me.c, o], fs.at[o], fr.at[o], me.d, me.t1).wait_send()
        return c
    lax.fori_loop(0, ndp, settle, 0)
    g.sent()
    keep.wait()
    for slot in range(2):
        one(slot).wait_send()
    for c in range(chunks):
        two(c).wait_send()
    g1.wait_send()
    g2.wait_send()


def place_kernel(e_ref, g_ref, ain_ref, bqkv_ref, bup_ref, aout_ref, adown_ref, bres_ref):
    ndp = g_ref.shape[1]
    for ref in (ain_ref, bqkv_ref, bup_ref, aout_ref, adown_ref, bres_ref):
        ref[...] = jnp.zeros_like(ref)

    def add(d, c):
        e = e_ref[d]
        for n in range(3):
            ain_ref[n, e] += g_ref[0, d, n * 16:(n + 1) * 16, :].astype(F32)
            bqkv_ref[n, e] += g_ref[0, d, (3 + n) * 16:(4 + n) * 16, :].astype(F32)
        ain_ref[3, e] += g_ref[1, d, 0:16, :].astype(F32)
        bup_ref[e] += g_ref[1, d, 16:32, :].astype(F32)
        aout_ref[e] += g_ref[1, d, 32:48, :].astype(F32)
        adown_ref[e] += g_ref[1, d, 48:64, :].astype(F32)
        bres_ref[0, e] += g_ref[1, d, 64:80, :].astype(F32)
        bres_ref[1, e] += g_ref[1, d, 80:96, :].astype(F32)
        return c
    lax.fori_loop(0, ndp, add, 0)


VMEM = pltpu.VMEM
DMA = pltpu.SemaphoreType.DMA
IN_VMEM = pl.BlockSpec(memory_space=pltpu.VMEM)
IN_SMEM = pl.BlockSpec(memory_space=pltpu.SMEM)
IN_ANY = pl.BlockSpec(memory_space=pl.ANY)


def shape(*dims, dtype=BF16):
    return jax.ShapeDtypeStruct(dims, dtype)


def params(cid=None, limit=60 << 20):
    if cid is None:
        return pltpu.CompilerParams(vmem_limit_bytes=limit)
    return pltpu.CompilerParams(collective_id=cid, has_side_effects=True, vmem_limit_bytes=limit)


def local(
    inputs, cotangent, adapter_choice_per_tree, segment_lengths, segment_parents, norm_gain_rows, query_dimension_scale,
    attention_weights, output_weight, feedforward_weights, adapter_first_input, adapter_second_attention, adapter_second_up,
    adapter_first_output, adapter_first_down, adapter_second_residual,
):
    ndp, nt = lax.axis_size("dp"), lax.axis_size("tensor")
    tpos = lax.axis_index("tensor")
    tok, width = inputs.shape
    tree = tok * nt
    wrows, hcols = output_weight.shape
    heads = hcols // HD
    pad = heads * 128
    segs = segment_lengths.shape[1]
    rank = adapter_first_input.shape[3]
    nblk = tree // BLK
    e = adapter_choice_per_tree[0]
    lens, parents = segment_lengths[0], segment_parents[0]

    def pick(table, axis):
        return lax.dynamic_index_in_dim(table, e, axis, keepdims=False)

    a_in = pick(jnp.swapaxes(adapter_first_input, 2, 3), 1)
    b_attn = lax.dynamic_slice_in_dim(pick(adapter_second_attention, 1), tpos * hcols, hcols, 2)
    b_res = pick(adapter_second_residual, 1)
    at_qkv = a_in[:3].reshape(3 * rank, width)
    at_mid = jnp.stack([pick(jnp.swapaxes(adapter_first_output, 1, 2), 0), a_in[3], pick(jnp.swapaxes(adapter_first_down, 1, 2), 0)])
    b_mid = jnp.stack([b_res[0], pick(adapter_second_up, 0), b_res[1]])
    ends = jnp.cumsum(lens)
    lane = jnp.arange(128, dtype=jnp.int32) - HD
    spot = (lane[None, :] == jnp.arange(segs, dtype=jnp.int32)[:, None])
    seg = jnp.stack([jnp.sum(jnp.where(spot, (ends - lens)[:, None], 0), 0), jnp.sum(jnp.where(spot, ends[:, None], 0), 0)]
                    + [jnp.zeros((128,), jnp.int32)] * 6).astype(F32)
    idx = jnp.arange(segs, dtype=jnp.int32)
    grand = jnp.sum(jnp.where(parents[:, None] == idx[None, :], parents[None, :], 0), axis=1)
    reach = (idx[:, None] == idx[None, :]) | (parents[:, None] == idx[None, :]) | (grand[:, None] == idx[None, :])
    mq = jnp.pad(jnp.where(reach, 0.0, -BIG).astype(BF16), ((HD, 128 - HD - segs), (HD, 128 - HD - segs)))
    scale = jnp.pad(jnp.broadcast_to(query_dimension_scale[None, :] / math.sqrt(HD), (heads, HD)), ((0, 0), (0, 128 - HD))).reshape(1, pad)

    chunks = 4
    choice = jnp.full((8, 128), e, F32)
    wr = wrows * 3
    tall = (heads, tree, 128)
    wall, choices, mixed, xn, q, qt, k, kt, v, ranks, mixt, wp, bp = pl.pallas_call(
        functools.partial(forward_kernel, ndp, chunks),
        out_shape=[shape(ndp, nt, wr, hcols), shape(ndp, 8, 128, dtype=F32), shape(nt, tok, hcols), shape(tree, width),
                   shape(*tall), shape(heads, 128, tree), shape(*tall), shape(heads, HD, tree), shape(*tall),
                   shape(tree, 3 * rank), shape(hcols, tree), shape(3, width, pad), shape(3, 3 * rank, pad)],
        in_specs=[IN_VMEM] * 8 + [IN_ANY] * 3, out_specs=[IN_ANY] * 13,
        scratch_shapes=[VMEM((wr, hcols), BF16), VMEM((wr, hcols), BF16), VMEM((tree, width), BF16), VMEM((ndp, wr, hcols), BF16),
                        VMEM((3, width, pad), BF16), VMEM((3, 3 * rank, pad), BF16), VMEM(tall, BF16), VMEM((heads, 128, tree), BF16),
                        VMEM(tall, BF16), VMEM((heads, HD, tree), BF16), VMEM(tall, BF16), VMEM((heads, HD + 16, tree), BF16),
                        VMEM((tree, 3 * rank), BF16), VMEM((hcols, tree), BF16), VMEM((tree, hcols), BF16),
                        VMEM((heads, 1, BLK), F32), VMEM((heads, HD + 16, BLK), F32), DMA((3,)), DMA((10,)),
                        DMA((3, chunks)), DMA((nt, chunks)), DMA((3, ndp)), DMA((ndp,)), DMA((3, ndp)), DMA((ndp,)),
                        DMA((2, ndp, nt, 4)), DMA((2,)), DMA((2, ndp, nt)), DMA((nblk,)), DMA((nt, tok // BLK))],
        compiler_params=params(1), name="forward",
    )(inputs, norm_gain_rows, choice, at_qkv, b_attn, scale, seg, mq, attention_weights.reshape(wr, hcols), output_weight,
      feedforward_weights.reshape(2 * wrows, hcols))

    def swap(x, cid):
        return pl.pallas_call(
            functools.partial(swap_kernel, ndp), out_shape=shape(nt, tok, hcols), in_specs=[IN_VMEM], out_specs=IN_ANY,
            scratch_shapes=[DMA((3,)), DMA((nt,)), DMA((1,))], compiler_params=params(cid), name="swap",
        )(x)

    output, d_mid, d_mix, g_mid = pl.pallas_call(
        mid_kernel,
        out_shape=[shape(tok, width), shape(tok, width, dtype=F32), shape(nt, tok, hcols), shape(6, rank, width, dtype=F32)],
        in_specs=[IN_VMEM] * 6 + [IN_ANY], out_specs=[IN_VMEM] * 4,
        scratch_shapes=[VMEM((tok, width), BF16), VMEM((tok, width), F32), VMEM((tok, width), BF16), VMEM((tok, width), F32),
                        VMEM((tok, width), BF16), VMEM((tok, width), F32), VMEM((tok, width), BF16), VMEM((3, width, width), BF16)]
        + [VMEM((ndp, nt, wrows, hcols), BF16)] * 3 + [DMA((3,))],
        compiler_params=params(), name="middle",
    )(inputs, cotangent, mixed, norm_gain_rows, at_mid, b_mid, wall)
    d_mixed = swap(d_mix.reshape(nt * tok, hcols), 3).reshape(tree, hcols)

    dq, dk, dv = pl.pallas_call(
        bwd_kernel, out_shape=[shape(tree, pad)] * 3, in_specs=[IN_SMEM] * 2 + [IN_VMEM] * 8, out_specs=[IN_VMEM] * 3,
        scratch_shapes=[VMEM((heads, tree, 128), BF16), VMEM((heads, 128, tree), BF16), VMEM((heads, HD, tree), F32),
                        VMEM((heads, tree, 128), F32), VMEM((heads, tree, 128), F32), pltpu.SMEM((nblk * nblk,), jnp.int32)],
        compiler_params=params(limit=62 << 20), name="attend_back",
    )(lens, parents, d_mixed, mixt, q, qt, k, kt, v, scale)

    gr = 6 * rank
    input_grad, gathered = pl.pallas_call(
        functools.partial(finish_kernel, ndp, chunks),
        out_shape=[shape(tok, width, dtype=F32), shape(2, ndp, gr, width)],
        in_specs=[IN_VMEM] * 12, out_specs=[IN_VMEM, IN_ANY],
        scratch_shapes=[VMEM((4, tok, width), BF16), VMEM((2, tok, width), BF16), VMEM((tok, width), BF16), VMEM((tok, width), BF16),
                        VMEM((3 * rank, width), F32), VMEM((3, 3 * rank, pad), F32), VMEM((2, gr, width), BF16), VMEM((2, gr, width), BF16),
                        VMEM((gr, width), BF16), VMEM((gr, width), BF16),
                        DMA((2,)), DMA((2,)), DMA((chunks,)), DMA((chunks,)), DMA((2,)), DMA((2,)), DMA((3, ndp)), DMA((ndp,)),
                        DMA((ndp,)), DMA((ndp,)), DMA((1,))],
        compiler_params=params(4, 62 << 20), name="finish",
    )(dq, dk, dv, wp, bp, at_qkv, xn, ranks, inputs, d_mid, norm_gain_rows, g_mid.reshape(gr, width))

    count = adapter_first_input.shape[1]
    ga_in, gb_qkv, gb_up, ga_out, ga_down, gb_res = pl.pallas_call(
        place_kernel,
        out_shape=[shape(4, count, rank, width, dtype=F32), shape(3, count, rank, width, dtype=F32), shape(count, rank, width, dtype=F32),
                   shape(count, rank, width, dtype=F32), shape(count, rank, width, dtype=F32), shape(2, count, rank, width, dtype=F32)],
        in_specs=[IN_SMEM, IN_VMEM], out_specs=[IN_VMEM] * 6, compiler_params=params(), name="place",
    )(choices[:, 0, 0].astype(jnp.int32), gathered)
    return (output, input_grad, jnp.swapaxes(ga_in, 2, 3), gb_qkv, gb_up, jnp.swapaxes(ga_out, 1, 2), jnp.swapaxes(ga_down, 1, 2), gb_res)


def solution(mesh):
    tokens, weights = P(("dp", "tensor"), None), P(None, "dp", "tensor")
    in_specs = (tokens, tokens, P("dp"), P("dp", None), P("dp", None), P(), P(), weights, P("dp", "tensor"), weights) + (P(),) * 6
    out_specs = (tokens, tokens) + (P(),) * 6
    return jax.shard_map(local, mesh=mesh, in_specs=in_specs, out_specs=out_specs, check_vma=False)
```

```python
import functools
import math

import jax
import jax.numpy as jnp
from jax import lax
from jax.experimental import pallas as pl
from jax.experimental.pallas import tpu as pltpu
from jax.sharding import PartitionSpec as P

F32, BF16 = jnp.float32, jnp.bfloat16
BIG = 1e30
BLK = 256
HD = 80

def dot(a, b):
    return lax.dot_general(a, b, (((1,), (0,)), ((), ())), preferred_element_type=F32)
def dot_nt(a, b):
    return lax.dot_general(a, b, (((1,), (1,)), ((), ())), preferred_element_type=F32)
def dot_tn(a, b):
    return lax.dot_general(a, b, (((0,), (0,)), ((), ())), preferred_element_type=F32)

def project(b, x_ref, wp_ref, a_ref, bp_ref, scale_ref, seg_ref, mq_ref, q_ref, qt_ref, k_ref, kt_ref, v_ref, vt_ref, rank_ref):
    rows = pl.ds(pl.multiple_of(b * BLK, BLK), BLK)
    xb = x_ref[rows, :]
    rank = dot_nt(xb, a_ref[...]).astype(BF16)
    rank_ref[rows, :] = rank
    lane = lax.broadcasted_iota(jnp.int32, (BLK, 128), 1)
    tok = (lax.broadcasted_iota(jnp.int32, (BLK, 128), 0) + b * BLK).astype(F32)
    hot = jnp.where((tok >= seg_ref[0:1, :]) & (tok < seg_ref[1:2, :]), 1.0, 0.0)
    qfeat = dot(hot.astype(BF16), mq_ref[...])
    kfeat = jnp.where((lane >= HD + 13) & (lane < HD + 16), 1.0, hot)
    vfeat = jnp.where(lane < HD + 2, 1.0, 0.0)
    heads = q_ref.shape[0]
    for s, (n_ref, t_ref, feat) in enumerate(((q_ref, qt_ref, qfeat), (k_ref, kt_ref, kfeat), (v_ref, vt_ref, vfeat))):
        y = dot(xb, wp_ref[s]) + dot(rank, bp_ref[s])
        if s == 0:
            y = y * scale_ref[...]
        for h in range(heads):
            yh = jnp.where(lane < HD, y[:, h * 128:(h + 1) * 128], feat)
            n_ref[h, rows, :] = yh.astype(BF16)
            yt = yh.T
            t_ref[h, :, rows] = yt[:t_ref.shape[1]].astype(BF16)

def attend_block(i, qt_ref, k_ref, vt_ref, m_ref, acc_ref, mixt_ref, mix_ref, count=None, jlist=None):
    heads = qt_ref.shape[0]
    cols = pl.ds(pl.multiple_of(i * BLK, BLK), BLK)
    m_ref[...] = jnp.full_like(m_ref, -3e38)
    acc_ref[...] = jnp.zeros_like(acc_ref)
    def step(j, diag):
        rows = pl.ds(pl.multiple_of(j * BLK, BLK), BLK)
        hs = range(heads)
        ss = [dot(k_ref[h, rows, :], qt_ref[h, :, cols]) for h in hs]
        if diag:
            low = lax.broadcasted_iota(jnp.int32, ss[0].shape, 0) <= lax.broadcasted_iota(jnp.int32, ss[0].shape, 1)
            ss = [jnp.where(low, s, -BIG) for s in ss]
        olds = [m_ref[h] for h in hs]
        news = [jnp.maximum(olds[h], jnp.max(ss[h], axis=0, keepdims=True)) for h in hs]
        ps = [jnp.exp(ss[h] - news[h]).astype(BF16) for h in hs]
        pv = [dot(vt_ref[h, :, rows], ps[h]) for h in hs]
        accs = [acc_ref[h] * jnp.exp(olds[h] - news[h]) + pv[h] for h in hs]
        for h in hs:
            acc_ref[h] = accs[h]
            m_ref[h] = news[h]
    if jlist is None:
        lax.fori_loop(0, i, lambda j, c: (step(j, False), c)[1], 0)
    else:
        lax.fori_loop(0, count, lambda n, c: (step(jlist(n), False), c)[1], 0)
    step(i, True)
    outs = []
    for h in range(heads):
        acc = acc_ref[h]
        l = acc[HD:HD + 1]
        o = acc[:HD] * (1.0 / l)
        lse = m_ref[h] + jnp.log(l)
        hi = (-lse).astype(BF16).astype(F32)
        mid = (-lse - hi).astype(BF16).astype(F32)
        lo = -lse - hi - mid
        r = lax.broadcasted_iota(jnp.int32, (16, BLK), 0)
        old = qt_ref[h, HD:HD + 16, cols].astype(F32)
        new = jnp.where(r == 13, hi, jnp.where(r == 14, mid, jnp.where(r == 15, lo, old)))
        qt_ref[h, HD:HD + 16, cols] = new.astype(BF16)
        outs.append(o)
    ot = jnp.concatenate(outs, axis=0)
    mixt_ref[:, cols] = ot.astype(BF16)
    mix_ref[cols, :] = ot.T.astype(BF16)

def spread_heads(hcols, pad):
    c = lax.broadcasted_iota(jnp.int32, (hcols, pad), 0)
    l = lax.broadcasted_iota(jnp.int32, (hcols, pad), 1)
    return jnp.where(((l & 127) < HD) & ((l >> 7) * HD + (l & 127) == c), 1.0, 0.0).astype(BF16)


def bwd_prep(b, dm_ref, mixt_ref, do_ref, dot_ref):
    rows = pl.ds(pl.multiple_of(b * BLK, BLK), BLK)
    heads = do_ref.shape[0]
    dt = dm_ref[rows, :].astype(F32).T
    prod = dt * mixt_ref[:, rows].astype(F32)
    r = lax.broadcasted_iota(jnp.int32, (16, BLK), 0)
    for h in range(heads):
        d = dt[h * HD:(h + 1) * HD]
        delta = -jnp.sum(prod[h * HD:(h + 1) * HD], axis=0, keepdims=True)
        hi = delta.astype(BF16).astype(F32)
        ext = jnp.where(r == 0, hi, jnp.where(r == 1, delta - hi, 0.0))
        full = jnp.concatenate([d, ext, jnp.zeros((32, BLK), F32)], axis=0)
        dot_ref[h, :, rows] = full.astype(BF16)
        do_ref[h, rows, :] = full.T.astype(BF16)

def bwd_pair(i, j, diag, q_ref, qt_ref, k_ref, kt_ref, v_ref, do_ref, dot_ref, dqt_ref, dk_ref, dv_ref):
    heads = q_ref.shape[0]
    cols = pl.ds(pl.multiple_of(i * BLK, BLK), BLK)
    rows = pl.ds(pl.multiple_of(j * BLK, BLK), BLK)
    hs = range(heads)
    ss = [dot(k_ref[h, rows, :], qt_ref[h, :, cols]) for h in hs]
    dps = [dot(v_ref[h, rows, :], dot_ref[h, :, cols]) for h in hs]
    if diag:
        low = lax.broadcasted_iota(jnp.int32, ss[0].shape, 0) <= lax.broadcasted_iota(jnp.int32, ss[0].shape, 1)
        ss = [jnp.where(low, s, -BIG) for s in ss]
    ps = [jnp.exp(s) for s in ss]
    dss = [(p * dp).astype(BF16) for p, dp in zip(ps, dps)]
    ps = [p.astype(BF16) for p in ps]
    dvs = [dot(ps[h], do_ref[h, cols, :]) for h in hs]
    dks = [dot(dss[h], q_ref[h, cols, :]) for h in hs]
    dqs = [dot(kt_ref[h, :, rows], dss[h]) for h in hs]
    for h in hs:
        dv_ref[h, rows, :] += dvs[h]
        dk_ref[h, rows, :] += dks[h]
        dqt_ref[h, :, cols] += dqs[h]

MESH = pl.DeviceIdType.MESH


class Place:
    def __init__(self, ndp):
        self.d, self.t = lax.axis_index("dp"), lax.axis_index("tensor")
        self.line = ndp // 2
        self.p, self.par = self.d // 2, self.d % 2
        self.dx = self.d + 1 - 2 * self.par
        self.c, self.y = self.t % 2, self.t // 2
        self.t1 = self.t + 1 - 2 * self.c
        self.t2 = (self.t + 2) % 4
        self.t3 = (self.t1 + 2) % 4
        self.has_left, self.has_right = self.p > 0, self.p < self.line - 1


def signal(sem, d, t):
    pl.semaphore_signal(sem, inc=1, device_id=(d, t), device_id_type=MESH)


def remote(src, dst, send_sem, recv_sem, d, t):
    return pltpu.make_async_remote_copy(src_ref=src, dst_ref=dst, send_sem=send_sem, recv_sem=recv_sem, device_id=(d, t), device_id_type=MESH)


def greet(me, tensor=(), pair=False, line=False):
    bar = pltpu.get_barrier_semaphore()
    count = len(tensor) + (1 if pair else 0)
    for t in tensor:
        signal(bar, me.d, t)
    if pair:
        signal(bar, me.dx, me.t)
    if line:
        @pl.when(me.has_left)
        def _():
            signal(bar, me.d - 2, me.t)
        @pl.when(me.has_right)
        def _():
            signal(bar, me.d + 2, me.t)
        count = count + jnp.where(me.has_left, 1, 0) + jnp.where(me.has_right, 1, 0)
    pl.semaphore_wait(bar, count)


class PairLine:
    def __init__(self, me, own, buf, send, recv):
        self.me, self.own, self.buf, self.send, self.recv = me, own, buf, send, recv

    def copy(self, o, src, d, kind):
        return remote(src, self.buf.at[o], self.send.at[kind, o], self.recv.at[o], d, self.me.t)

    def start(self):
        me = self.me
        @pl.when(me.has_left)
        def _():
            self.copy(me.d, self.own, me.d - 2, 0).start()
        @pl.when(me.has_right)
        def _():
            self.copy(me.d, self.own, me.d + 2, 1).start()
        self.copy(me.d, self.own, me.dx, 2).start()

    def hop(self, k, then=None):
        me = self.me
        @pl.when(me.p - k >= 0)
        def _():
            o = me.d - 2 * k
            self.copy(o, self.buf.at[o], me.dx, 2).wait_recv()
            @pl.when(me.has_right)
            def _():
                self.copy(o, self.buf.at[o], me.d + 2, 1).start()
            self.copy(o, self.buf.at[o], me.dx, 2).start()
            if then is not None:
                then(o)
        @pl.when(me.p + k < me.line)
        def _():
            o = me.d + 2 * k
            self.copy(o, self.buf.at[o], me.dx, 2).wait_recv()
            @pl.when(me.has_left)
            def _():
                self.copy(o, self.buf.at[o], me.d - 2, 0).start()
            self.copy(o, self.buf.at[o], me.dx, 2).start()
            if then is not None:
                then(o)

    def pair_arrivals(self, then=None):
        def one(q, c):
            o = 2 * q + 1 - self.me.par
            self.copy(o, self.buf.at[o], self.me.dx, 2).wait_recv()
            if then is not None:
                then(o)
            return c
        lax.fori_loop(0, self.me.line, one, 0)

    def sent(self):
        me = self.me
        def one(q, c):
            o = 2 * q + me.par
            self.copy(o, self.buf.at[o], me.dx, 2).wait_send()
            @pl.when((q >= me.p) & me.has_left)
            def _():
                self.copy(o, self.buf.at[o], me.dx, 0).wait_send()
            @pl.when((q <= me.p) & me.has_right)
            def _():
                self.copy(o, self.buf.at[o], me.dx, 1).wait_send()
            return c
        lax.fori_loop(0, me.line, one, 0)


class FullGather:
    def __init__(self, me, own, buf, send, first, recv):
        self.me, self.own, self.buf, self.send, self.first, self.recv = me, own, buf, send, first, recv
        cut = own.shape[0] // 32 * 16
        self.parts = (pl.ds(0, cut), pl.ds(cut, own.shape[0] - cut))

    def copy(self, h, o, t, d2, t2, kind, own=False):
        rows = self.parts[h]
        src = self.own.at[rows] if own else self.buf.at[o, t, rows]
        sem = self.first.at[h] if kind == 4 else self.send.at[h, o, t, kind]
        return remote(src, self.buf.at[o, t, rows], sem, self.recv.at[h, o, t], d2, t2)

    def last(self, h):
        me = self.me
        return (me.d, me.t2) if h == 0 else (me.dx, me.t)

    def spread(self, h, o, t, left, right, own=False):
        me = self.me
        @pl.when(left)
        def _():
            self.copy(h, o, t, me.d - 2, me.t, 0, own).start()
        @pl.when(right)
        def _():
            self.copy(h, o, t, me.d + 2, me.t, 1, own).start()
        self.copy(h, o, t, *self.last(h), 2, own).start()
        self.copy(h, o, t, me.d, me.t1, 3, own).start()

    def start(self):
        me = self.me
        self.copy(0, me.d, me.t, me.dx, me.t, 4, True).start()
        self.copy(1, me.d, me.t, me.d, me.t2, 4, True).start()
        for h in range(2):
            self.spread(h, me.d, me.t, me.has_left, me.has_right, True)

    def arrived(self, h, o, t):
        self.copy(h, o, t, self.me.d, self.me.t1, 3).wait_recv()

    def firsts(self):
        me = self.me
        self.arrived(0, me.dx, me.t)
        self.spread(0, me.dx, me.t, me.has_left, me.has_right)
        self.arrived(1, me.d, me.t2)
        self.spread(1, me.d, me.t2, me.has_left, me.has_right)

    def streams(self, q):
        me = self.me
        return ((0, 2 * q + me.par, me.t), (0, 2 * q + 1 - me.par, me.t), (1, 2 * q + me.par, me.t), (1, 2 * q + me.par, me.t2))

    def hop(self, k):
        me = self.me
        @pl.when(me.p - k >= 0)
        def _():
            for h, o, t in self.streams(me.p - k):
                self.arrived(h, o, t)
                self.spread(h, o, t, False, me.has_right)
        @pl.when(me.p + k < me.line)
        def _():
            for h, o, t in self.streams(me.p + k):
                self.arrived(h, o, t)
                self.spread(h, o, t, me.has_left, False)

    def lasts(self):
        me = self.me
        def one(q, c):
            for h, o, t in ((0, 2 * q, me.t2), (0, 2 * q + 1, me.t2), (1, 2 * q + 1 - me.par, me.t), (1, 2 * q + 1 - me.par, me.t2)):
                self.arrived(h, o, t)
                self.copy(h, o, t, me.d, me.t1, 3).start()
            return c
        lax.fori_loop(0, me.line, one, 0)

    def finish(self):
        me = self.me
        def one(o, c):
            for h in range(2):
                self.arrived(h, o, me.t1)
                self.arrived(h, o, me.t3)
                for t in (me.t, me.t2):
                    self.copy(h, o, t, me.d, me.t1, 3).wait_send()
            return c
        lax.fori_loop(0, 2 * me.line, one, 0)
        def two(q, c):
            for h, o, t in self.streams(q):
                self.copy(h, o, t, me.d, me.t1, 2).wait_send()
                @pl.when((q >= me.p) & me.has_left)
                def _():
                    self.copy(h, o, t, me.d, me.t1, 0).wait_send()
                @pl.when((q <= me.p) & me.has_right)
                def _():
                    self.copy(h, o, t, me.d, me.t1, 1).wait_send()
            return c
        lax.fori_loop(0, me.line, two, 0)
        for h in range(2):
            self.copy(h, me.d, me.t, me.d, me.t1, 4).wait_send()


EPS = 1e-6


def forward_kernel(ndp, chunks, x_ref, gain_ref, choice_ref, at_ref, b_ref, scale_ref, seg_ref, mq_ref, a_ref, wo_ref, wf_ref,
                   wout_ref, cho_ref, mixed_ref, xno_ref, qo_ref, qto_ref, ko_ref, kto_ref, vo_ref, ranko_ref, mixto_ref, wpo_ref, bpo_ref,
                   aown_ref, wown_ref, xn_ref, wa_ref, wp_ref, bp_ref, q_ref, qt_ref, k_ref, kt_ref, v_ref, vt_ref, rank_ref, mixt_ref,
                   mix_ref, m_ref, acc_ref, ls, os, xs, xr, a_s, a_r, c_s, c_r, w_s, w_f, w_r, ms, mr):
    me = Place(ndp)
    tok, width = x_ref.shape
    rows_o = wo_ref.shape[0]
    loads = [pltpu.make_async_copy(a_ref, aown_ref, ls.at[0]), pltpu.make_async_copy(wo_ref, wown_ref.at[pl.ds(0, rows_o)], ls.at[1]),
             pltpu.make_async_copy(wf_ref, wown_ref.at[pl.ds(rows_o, wf_ref.shape[0])], ls.at[2])]
    for copy in loads:
        copy.start()
    x = x_ref[...].astype(F32)
    mine = pl.ds(pl.multiple_of(me.t * tok, tok), tok)
    xn_ref[mine, :] = (x * lax.rsqrt(jnp.mean(x * x, axis=-1, keepdims=True) + EPS) * gain_ref[0:1, :]).astype(BF16)
    greet(me, tensor=(me.t1, me.t2, me.t3), pair=True, line=True)
    size = tok // chunks

    def xcopy(o, c, t, kind):
        rows = pl.ds(pl.multiple_of(o * tok + c * size, size), size)
        return remote(xn_ref.at[rows], xn_ref.at[rows], xs.at[kind, c], xr.at[o, c], me.d, t)

    for c in range(chunks):
        xcopy(me.t, c, me.t2, 0).start()
    for c in range(chunks):
        xcopy(me.t, c, me.t1, 1).start()
    for copy in loads:
        copy.wait()
    a = PairLine(me, aown_ref, wa_ref, a_s, a_r)
    ch = PairLine(me, choice_ref, cho_ref, c_s, c_r)
    w = FullGather(me, wown_ref, wout_ref, w_s, w_f, w_r)
    a.start()
    ch.start()
    keep = [pltpu.make_async_copy(wown_ref, wout_ref.at[me.d, me.t], ls.at[0]), pltpu.make_async_copy(choice_ref, cho_ref.at[me.d], ls.at[1])]
    for copy in keep:
        copy.start()
    wa_ref[me.d] = aown_ref[...]
    early = max(1, me.line - 2)

    def hop(k, carry):
        a.hop(k)
        ch.hop(k)
        return carry
    lax.fori_loop(1, early + 1, hop, 0)
    w.start()

    def forward(c):
        xcopy(me.t2, c, me.t1, 2).wait_recv()
        xcopy(me.t2, c, me.t1, 2).start()

    for c in range(chunks // 2):
        forward(c)
    lax.fori_loop(early + 1, me.line, hop, 0)
    for c in range(chunks // 2, chunks):
        forward(c)
    a.pair_arrivals()
    ch.pair_arrivals()

    sel = spread_heads(wa_ref.shape[2], wp_ref.shape[2])
    bp_ref[...] = jnp.zeros_like(bp_ref)
    wrows = wa_ref.shape[1] // 3
    group = 16 // math.gcd(wrows, 16)
    for s in range(3):
        n = b_ref.shape[1]
        bp_ref[s, s * n:(s + 1) * n] = (0.5 * dot(b_ref[s], sel)).astype(BF16)
        for o in range(0, ndp, group):
            wp_ref[s, o * wrows:(o + group) * wrows] = jnp.concatenate(
                [dot(wa_ref[o + j, s * wrows:(s + 1) * wrows], sel) for j in range(group)], axis=0).astype(BF16)
    for c in range(chunks):
        xcopy(me.t1, c, me.t1, 2).wait_recv()
        xcopy(me.t3, c, me.t1, 2).wait_recv()
    w.firsts()
    nblk = xn_ref.shape[0] // BLK
    span = 2 * nblk - 3

    def upto(step):
        return 1 + jnp.minimum(step * (me.line - 1) // span, me.line - 1)

    def relay(step):
        lax.fori_loop(upto(step), upto(step + 1), lambda k, c: (w.hop(k), c)[1], 0)

    def project_step(b, c):
        project(b, xn_ref, wp_ref, at_ref, bp_ref, scale_ref, seg_ref, mq_ref, q_ref, qt_ref, k_ref, kt_ref, v_ref, vt_ref, rank_ref)
        relay(b)
        return c
    lax.fori_loop(0, nblk, project_step, 0)
    outs = [pltpu.make_async_copy(src, dst, os.at[n]) for n, (src, dst) in enumerate((
        (xn_ref, xno_ref), (q_ref, qo_ref), (k_ref, ko_ref), (kt_ref, kto_ref), (v_ref, vo_ref), (rank_ref, ranko_ref),
        (wp_ref, wpo_ref), (bp_ref, bpo_ref)))]
    for copy in outs:
        copy.start()
    per = tok // BLK

    def piece(i):
        rows = pl.ds(pl.multiple_of(i * BLK, BLK), BLK)
        return mix_ref.at[rows], mixed_ref.at[me.t, pl.ds(pl.multiple_of((i % per) * BLK, BLK), BLK)], i // per

    def attend_step(i, c):
        attend_block(i, qt_ref, k_ref, vt_ref, m_ref, acc_ref, mixt_ref, mix_ref)
        src, dst, t = piece(i)
        @pl.when(t == me.t)
        def _():
            pltpu.make_async_copy(src, dst, ms.at[i]).start()
        @pl.when(t != me.t)
        def _():
            remote(src, dst, ms.at[i], mr.at[me.t, i % per], me.d, t).start()
        relay(nblk + i)
        return c
    lax.fori_loop(0, nblk, attend_step, 0)
    late = [pltpu.make_async_copy(qt_ref, qto_ref, os.at[len(outs)]), pltpu.make_async_copy(mixt_ref, mixto_ref, os.at[len(outs) + 1])]
    for copy in late:
        copy.start()
    w.lasts()
    for t in (me.t1, me.t2, me.t3):
        for h in range(per):
            dst = mixed_ref.at[t, pl.ds(h * BLK, BLK)]
            remote(dst, dst, ms.at[0], mr.at[t, h], me.d, t).wait_recv()
    w.finish()
    a.sent()
    ch.sent()
    for c in range(chunks):
        for kind in range(3):
            xcopy(me.t, c, me.t1, kind).wait_send()

    def settle(i, c):
        src, dst, t = piece(i)
        @pl.when(t == me.t)
        def _():
            pltpu.make_async_copy(src, dst, ms.at[i]).wait()
        @pl.when(t != me.t)
        def _():
            remote(src, dst, ms.at[i], mr.at[me.t, i % per], me.d, t).wait_send()
        return c
    lax.fori_loop(0, nblk, settle, 0)
    for copy in keep + outs + late:
        copy.wait()


def sigmoid(v):
    return 1.0 / (1.0 + jnp.exp(-v))


def mid_kernel(x_ref, g_ref, mix4_ref, gain_ref, at_ref, b_ref, wall_ref, out_ref, dmid_ref, dmix_ref, grads_ref,
               mix_ref, mid_ref, hid_ref, up_ref, act_ref, f_ref, low_ref, w_ref, wb0_ref, wb1_ref, wb2_ref, ls):
    width = x_ref.shape[1]
    step = 256
    part = mix4_ref.shape[2]
    blocks = (wb0_ref, wb1_ref, wb2_ref)
    ndp, nt, wrows = wb0_ref.shape[:3]
    loads = [pltpu.make_async_copy(wall_ref.at[:, :, pl.ds(n * wrows, wrows)], blocks[n], ls.at[n]) for n in range(3)]
    for copy in loads:
        copy.start()

    def assemble(n):
        loads[n].wait()
        for o in range(ndp):
            for t in range(nt):
                w_ref[n, o * wrows:(o + 1) * wrows, t * part:(t + 1) * part] = blocks[n][o, t]

    for t in range(mix4_ref.shape[0]):
        mix_ref[:, t * part:(t + 1) * part] = mix4_ref[t]

    def cols(n):
        return pl.ds(pl.multiple_of(n * step, step), step)

    def each(fn):
        lax.fori_loop(0, width // step, lambda n, c: (fn(cols(n)), c)[1], 0)

    gain = gain_ref[1:2, :]
    r_out = dot_nt(mix_ref[...], at_ref[0]).astype(BF16)
    assemble(0)

    def project_out(n):
        attn = dot_nt(mix_ref[...], w_ref[0, n, :]) + 0.5 * dot(r_out, b_ref[0, :, n])
        mid_ref[:, n] = x_ref[:, n].astype(F32) + attn
    each(project_out)
    middle = mid_ref[...]
    r = lax.rsqrt(jnp.mean(middle * middle, axis=-1, keepdims=True) + EPS)
    hid_ref[...] = (middle * r * gain).astype(BF16)
    r_up = dot_nt(hid_ref[...], at_ref[1]).astype(BF16)
    assemble(1)

    def up_step(n):
        up = dot(hid_ref[...], w_ref[1, :, n]) + 0.5 * dot(r_up, b_ref[1, :, n])
        up_ref[:, n] = up
        act_ref[:, n] = (up * sigmoid(up)).astype(BF16)
    each(up_step)
    r_down = dot_nt(act_ref[...], at_ref[2]).astype(BF16)
    assemble(2)

    def down_step(n):
        down = dot_nt(act_ref[...], w_ref[2, n, :]) + 0.5 * dot(r_down, b_ref[2, :, n])
        out_ref[:, n] = (mid_ref[:, n] + down).astype(BF16)
    each(down_step)
    grads_ref[5] = 0.5 * dot_tn(r_down, g_ref[...])
    dz_down = (0.5 * dot_nt(g_ref[...], b_ref[2])).astype(BF16)
    grads_ref[3] = dot_tn(dz_down, act_ref[...])

    def act_back(n):
        d_act = dot(g_ref[...], w_ref[2, :, n]) + dot(dz_down, at_ref[2, :, n])
        up = up_ref[:, n]
        sg = sigmoid(up)
        low_ref[:, n] = (d_act * sg * (1.0 + up * (1.0 - sg))).astype(BF16)
    each(act_back)
    dz_up = (0.5 * dot_nt(low_ref[...], b_ref[1])).astype(BF16)
    grads_ref[1] = 0.5 * dot_tn(r_up, low_ref[...])
    grads_ref[0] = dot_tn(dz_up, hid_ref[...])

    def hidden_back(n):
        f_ref[:, n] = (dot_nt(low_ref[...], w_ref[1, n, :]) + dot(dz_up, at_ref[1, :, n])) * gain_ref[1:2, n]
    each(hidden_back)
    gd = f_ref[...]
    middle = mid_ref[...]
    s = jnp.mean(middle * gd, axis=-1, keepdims=True)
    d_mid = g_ref[...].astype(F32) + r * gd - middle * (r * r * r * s)
    dmid_ref[...] = d_mid
    low_ref[...] = d_mid.astype(BF16)
    dz_out = (0.5 * dot_nt(low_ref[...], b_ref[0])).astype(BF16)
    grads_ref[4] = 0.5 * dot_tn(r_out, low_ref[...])
    grads_ref[2] = dot_tn(dz_out, mix_ref[...])

    def mixed_back(n):
        act_ref[:, n] = (dot(low_ref[...], w_ref[0, :, n]) + dot(dz_out, at_ref[0, :, n])).astype(BF16)
    each(mixed_back)
    for t in range(dmix_ref.shape[0]):
        dmix_ref[t] = act_ref[:, t * part:(t + 1) * part]


class GradSum:
    def __init__(self, me, gp, gr, g2, own, out, s, r, ls_, lr, fs, fr, keep):
        self.me, self.gp, self.gr, self.g2, self.own, self.out, self.s, self.r, self.fs, self.fr = me, gp, gr, g2, own, out, s, r, fs, fr
        self.line = PairLine(me, own, out.at[me.c], ls_, lr)
        self.keep = pltpu.make_async_copy(own, out.at[me.c, me.d], keep)

    def one(self):
        return remote(self.gp.at[1 - self.me.c], self.gr.at[0], self.s.at[0], self.r.at[0], self.me.d, self.me.t1)

    def two(self):
        return remote(self.g2, self.gr.at[1], self.s.at[1], self.r.at[1], self.me.d, self.me.t2)

    def second(self):
        self.one().wait_recv()
        self.g2[...] = (self.gp[self.me.c].astype(F32) + self.gr[0].astype(F32)).astype(BF16)
        self.two().start()

    def relay(self, o, own=False):
        src = self.own if own else self.out.at[self.me.c, o]
        return remote(src, self.out.at[self.me.c, o], self.fs.at[o], self.fr.at[o], self.me.d, self.me.t1)

    def gather(self):
        self.two().wait_recv()
        self.own[...] = (self.g2[...].astype(F32) + self.gr[1].astype(F32)).astype(BF16)
        self.line.start()
        self.relay(self.me.d, True).start()
        self.keep.start()

    def hop(self, k):
        self.line.hop(k, lambda o: self.relay(o).start())

    def arrivals(self):
        self.line.pair_arrivals(lambda o: self.relay(o).start())

    def settle(self, ndp):
        def one(o, c):
            self.relay(o, True).wait_send()
            remote(self.own, self.out.at[1 - self.me.c, o], self.fs.at[o], self.fr.at[o], self.me.d, self.me.t1).wait_recv()
            return c
        lax.fori_loop(0, ndp, one, 0)
        self.line.sent()
        self.keep.wait()
        self.one().wait_send()
        self.two().wait_send()


def back_kernel(ndp, dmix_ref, mixt_h, q_h, qt_h, k_h, kt_h, v_h, wp_h, xn_h, rank_h, x_h, dmid_h, scale_ref, bp_ref, at_ref, gain_ref, gmid_ref,
                ig_h, gm_h, ga_h,
                mixt_ref, q_ref, qt_ref, k_ref, kt_ref, v_ref, wp_ref, xn_ref, rank_ref, x_ref, dmid_ref, dm_ref, do_ref, dot_ref,
                dqt_ref, dk_ref, dv_ref, dn_ref, r1_ref, s2_ref, r2_ref, ro_ref, ga_ref, gb_ref, put_ref,
                gpm, grm, g2m, gom, gpa, gra, g2a, goa, lsem, dsem, drecv, es, er, s2s, r2r, ros, ror, igs,
                ms, mr, mls, mlr, mfs, mfr, mk, as_, ar, als, alr, afs, afr, ak):
    me = Place(ndp)
    tok = x_ref.shape[0]
    nblk = dm_ref.shape[0] // BLK
    per, half, hb = tok // BLK, nblk // 2, BLK // 2
    heads = q_ref.shape[0]
    loads = [pltpu.make_async_copy(src, dst, lsem.at[n]) for n, (src, dst) in enumerate((
        (mixt_h, mixt_ref), (q_h, q_ref), (qt_h, qt_ref), (k_h, k_ref), (kt_h, kt_ref), (v_h, v_ref),
        (wp_h, wp_ref), (xn_h, xn_ref), (rank_h, rank_ref), (x_h, x_ref), (dmid_h, dmid_ref)))]
    n48 = gpm.shape[1]
    for c in range(2):
        gpm[c] = gmid_ref[c * n48:(c + 1) * n48].astype(BF16)
    greet(me, tensor=(me.t1, me.t2, me.t3), pair=True, line=True)

    def token_rows(t):
        return pl.ds(pl.multiple_of(t * tok, tok), tok)

    def swap(n, t):
        return remote(dmix_ref.at[t], dm_ref.at[token_rows(me.t)], dsem.at[n], drecv.at[me.t], me.d, t)

    own = pltpu.make_async_copy(dmix_ref.at[me.t], dm_ref.at[token_rows(me.t)], dsem.at[3])
    for n, t in enumerate((me.t3, me.t2, me.t1)):
        swap(n, t).start()
    own.start()
    gm = GradSum(me, gpm, grm, g2m, gom, gm_h, ms, mr, mls, mlr, mfs, mfr, mk.at[0])
    ga = GradSum(me, gpa, gra, g2a, goa, ga_h, as_, ar, als, alr, afs, afr, ak.at[0])
    gm.one().start()
    for copy in loads:
        copy.start()
    for ref in (dqt_ref, dk_ref, dv_ref, ga_ref, gb_ref):
        ref[...] = jnp.zeros_like(ref)
    hd = gb_ref.shape[2]
    l = lax.broadcasted_iota(jnp.int32, put_ref.shape, 0)
    col = lax.broadcasted_iota(jnp.int32, put_ref.shape, 1)
    put = ((l & 127) < HD) & (me.t * (heads * HD) + (l >> 7) * HD + (l & 127) == col)
    put_ref[...] = jnp.where(put, 1.0, 0.0).astype(BF16)
    for copy in loads[:6]:
        copy.wait()

    def prep(t):
        lax.fori_loop(t * per, (t + 1) * per, lambda b, c: (bwd_prep(b, dm_ref, mixt_ref, do_ref, dot_ref), c)[1], 0)

    def arrived(t):
        remote(dmix_ref.at[t], dm_ref.at[token_rows(t)], dsem.at[0], drecv.at[t], me.d, t).wait_recv()

    own.wait()
    prep(me.t)
    arrived(me.t1)
    prep(me.t1)
    gm.second()
    arrived(me.t2)
    prep(me.t2)
    arrived(me.t3)
    prep(me.t3)
    for copy in loads[6:]:
        copy.wait()
    args = (q_ref, qt_ref, k_ref, kt_ref, v_ref, do_ref, dot_ref, dqt_ref, dk_ref, dv_ref)
    lane = lax.broadcasted_iota(jnp.int32, (BLK, 128), 1)

    def block(a):
        return (1 - me.y) * (nblk - 1 - a) + me.y * a

    def exchange(a):
        rows = pl.ds(pl.multiple_of((1 - me.c) * hb, hb), hb)
        return remote(dn_ref.at[a, rows], r1_ref.at[a], es.at[a], er.at[a], me.d, me.t1)

    def own_block(a):
        return remote(dn_ref.at[a], ro_ref.at[block(a) % per], ros.at[a % per], ror.at[block(a) % per], me.d, me.t1)

    def mine_rows():
        return pl.ds(pl.multiple_of(me.c * hb, hb), hb)

    def deliver(a):
        b = block(a)
        return remote(s2_ref.at[a], r2_ref.at[b % per, mine_rows()], s2s.at[a], r2r.at[b % per, me.c], me.d, b // per)

    def is_mine(a):
        return block(a) // per == me.t

    def pass_on(a):
        exchange(a).wait_recv()
        s2_ref[a] = (dn_ref[a, mine_rows(), :].astype(F32) + r1_ref[a].astype(F32)).astype(BF16)
        deliver(a).start()

    def final(a):
        rows = pl.ds(pl.multiple_of(block(a) * BLK, BLK), BLK)
        dq, dk, dv = [], [], []
        for h in range(heads):
            g = jnp.concatenate([dqt_ref[h, :, rows], jnp.zeros((48, BLK), F32)], axis=0).T
            dq.append((g * scale_ref[:, h * 128:(h + 1) * 128]).astype(BF16))
            dk.append(jnp.where(lane < HD, dk_ref[h, rows, :], 0.0).astype(BF16))
            dv.append(jnp.where(lane < HD, dv_ref[h, rows, :], 0.0).astype(BF16))
        ds = [jnp.concatenate(g, axis=1) for g in (dq, dk, dv)]
        dz = sum(dot_nt(ds[s], bp_ref[s]) for s in range(3)).astype(BF16)
        dn = sum(dot_nt(ds[s], wp_ref[s]) for s in range(3)) + dot(dz, at_ref[...])
        dn_ref[a] = dn.astype(BF16)
        ga_ref[...] += dot_tn(dz, xn_ref[rows, :])
        for s in range(3):
            gb_ref[s] += dot_tn(rank_ref[rows, :], ds[s])

    def upto(a):
        return 1 + jnp.minimum(a * (me.line - 1) // (nblk - 2), me.line - 1)

    def pairs(a):
        b = block(a)
        bwd_pair(b, b, True, *args)

        def other(n, c):
            bwd_pair(b + me.y * (1 + n), b - (1 - me.y) * (1 + n), False, *args)
            return c
        lax.fori_loop(0, nblk - 1 - a, other, 0)

    def far_step(a, c):
        pairs(a)
        @pl.when(a > 0)
        def _():
            pass_on(a - 1)
        final(a)
        exchange(a).start()
        @pl.when(a == 0)
        def _():
            gm.gather()
        lax.fori_loop(upto(a), upto(a + 1), lambda k, n: (gm.hop(k), n)[1], 0)
        return c
    lax.fori_loop(0, half, far_step, 0)

    def near_step(a, c):
        pairs(a)
        @pl.when(a == half)
        def _():
            pass_on(a - 1)
        final(a)
        @pl.when(jnp.logical_not(is_mine(a)))
        def _():
            own_block(a).start()
        lax.fori_loop(upto(a), upto(a + 1), lambda k, n: (gm.hop(k), n)[1], 0)
        return c
    lax.fori_loop(half, nblk, near_step, 0)
    n16 = n48 // 3
    gpa[0] = ga_ref[...].astype(BF16)
    gb = jnp.concatenate([gb_ref[s, s * n16:(s + 1) * n16] for s in range(3)], axis=0)
    gpa[1] = dot((0.5 * gb).astype(BF16), put_ref[...]).astype(BF16)
    ga.one().start()
    gm.arrivals()
    ga.second()

    def combine(i, c):
        b = me.t * per + i
        a = block(b)
        rows = pl.ds(pl.multiple_of(i * BLK, BLK), BLK)
        remote(dn_ref.at[a], ro_ref.at[i], ros.at[0], ror.at[i], me.d, me.t1).wait_recv()
        for h in range(2):
            remote(s2_ref.at[0], r2_ref.at[i, pl.ds(h * hb, hb)], s2s.at[0], r2r.at[i, h], me.d, me.t2).wait_recv()
        dn = dn_ref[a].astype(F32) + ro_ref[i].astype(F32) + r2_ref[i].astype(F32)
        x = x_ref[rows, :].astype(F32)
        r = lax.rsqrt(jnp.mean(x * x, axis=-1, keepdims=True) + EPS)
        gd = gain_ref[0:1, :] * dn
        dmid_ref[rows, :] = dmid_ref[rows, :] + r * gd - x * (r * r * r * jnp.mean(x * gd, axis=-1, keepdims=True))
        return c
    ga.gather()
    lax.fori_loop(0, per, combine, 0)
    put_ig = pltpu.make_async_copy(dmid_ref, ig_h, igs.at[0])
    put_ig.start()
    lax.fori_loop(1, me.line, lambda k, c: (ga.hop(k), c)[1], 0)
    ga.arrivals()
    ga.settle(ndp)
    gm.settle(ndp)

    def sent(a, c):
        exchange(a).wait_send()
        deliver(a).wait_send()
        return c
    lax.fori_loop(0, half, sent, 0)

    def own_sent(a, c):
        @pl.when(jnp.logical_not(is_mine(a)))
        def _():
            own_block(a).wait_send()
        return c
    lax.fori_loop(half, nblk, own_sent, 0)
    for n, t in enumerate((me.t3, me.t2, me.t1)):
        swap(n, t).wait_send()
    put_ig.wait()


def place_kernel(e_ref, gm_ref, ga_ref, ain_h, bqkv_h, bup_h, aout_h, adown_h, bres_h, out_ref, sem):
    ndp = gm_ref.shape[1]
    slots = ([(ga_ref, 0, n, ain_h.at[n]) for n in range(3)] + [(ga_ref, 1, n, bqkv_h.at[n]) for n in range(3)]
             + [(gm_ref, 0, 0, ain_h.at[3]), (gm_ref, 0, 1, bup_h), (gm_ref, 0, 2, aout_h),
                (gm_ref, 1, 0, adown_h), (gm_ref, 1, 1, bres_h.at[0]), (gm_ref, 1, 2, bres_h.at[1])])
    copies = []
    for n, (src, c, k, dst) in enumerate(slots):
        out_ref[n] = jnp.zeros(out_ref.shape[1:], F32)

        def add(d, carry):
            e = e_ref[d, 0, 0].astype(jnp.int32)
            out_ref[n, e] += src[c, d, k * 16:(k + 1) * 16, :].astype(F32)
            return carry
        lax.fori_loop(0, ndp, add, 0)
        copies.append(pltpu.make_async_copy(out_ref.at[n], dst, sem.at[n]))
        copies[-1].start()
    for copy in copies:
        copy.wait()


VMEM = pltpu.VMEM
DMA = pltpu.SemaphoreType.DMA
IN_VMEM = pl.BlockSpec(memory_space=pltpu.VMEM)
IN_SMEM = pl.BlockSpec(memory_space=pltpu.SMEM)
IN_ANY = pl.BlockSpec(memory_space=pl.ANY)


def shape(*dims, dtype=BF16):
    return jax.ShapeDtypeStruct(dims, dtype)


def params(cid=None, limit=60 << 20):
    if cid is None:
        return pltpu.CompilerParams(vmem_limit_bytes=limit)
    return pltpu.CompilerParams(collective_id=cid, has_side_effects=True, vmem_limit_bytes=limit)


def local(
    inputs, cotangent, adapter_choice_per_tree, segment_lengths, segment_parents, norm_gain_rows, query_dimension_scale,
    attention_weights, output_weight, feedforward_weights, adapter_first_input, adapter_second_attention, adapter_second_up,
    adapter_first_output, adapter_first_down, adapter_second_residual,
):
    ndp, nt = lax.axis_size("dp"), lax.axis_size("tensor")
    tpos = lax.axis_index("tensor")
    tok, width = inputs.shape
    tree = tok * nt
    wrows, hcols = output_weight.shape
    heads = hcols // HD
    pad = heads * 128
    segs = segment_lengths.shape[1]
    rank = adapter_first_input.shape[3]
    nblk = tree // BLK
    e = adapter_choice_per_tree[0]
    lens, parents = segment_lengths[0], segment_parents[0]

    def pick(table, axis):
        return lax.dynamic_index_in_dim(table, e, axis, keepdims=False)

    a_in = pick(jnp.swapaxes(adapter_first_input, 2, 3), 1)
    b_attn = lax.dynamic_slice_in_dim(pick(adapter_second_attention, 1), tpos * hcols, hcols, 2)
    b_res = pick(adapter_second_residual, 1)
    at_qkv = a_in[:3].reshape(3 * rank, width)
    at_mid = jnp.stack([pick(jnp.swapaxes(adapter_first_output, 1, 2), 0), a_in[3], pick(jnp.swapaxes(adapter_first_down, 1, 2), 0)])
    b_mid = jnp.stack([b_res[0], pick(adapter_second_up, 0), b_res[1]])
    ends = jnp.cumsum(lens)
    lane = jnp.arange(128, dtype=jnp.int32) - HD
    spot = (lane[None, :] == jnp.arange(segs, dtype=jnp.int32)[:, None])
    seg = jnp.stack([jnp.sum(jnp.where(spot, (ends - lens)[:, None], 0), 0), jnp.sum(jnp.where(spot, ends[:, None], 0), 0)]
                    + [jnp.zeros((128,), jnp.int32)] * 6).astype(F32)
    idx = jnp.arange(segs, dtype=jnp.int32)
    grand = jnp.sum(jnp.where(parents[:, None] == idx[None, :], parents[None, :], 0), axis=1)
    reach = (idx[:, None] == idx[None, :]) | (parents[:, None] == idx[None, :]) | (grand[:, None] == idx[None, :])
    mq = jnp.pad(jnp.where(reach, 0.0, -BIG).astype(BF16), ((HD, 128 - HD - segs), (HD, 128 - HD - segs)))
    scale = jnp.pad(jnp.broadcast_to(query_dimension_scale[None, :] / math.sqrt(HD), (heads, HD)), ((0, 0), (0, 128 - HD))).reshape(1, pad)

    chunks = 4
    choice = jnp.full((8, 128), e, F32)
    wr = wrows * 3
    tall = (heads, tree, 128)
    wall, choices, mixed, xn, q, qt, k, kt, v, ranks, mixt, wp, bp = pl.pallas_call(
        functools.partial(forward_kernel, ndp, chunks),
        out_shape=[shape(ndp, nt, wr, hcols), shape(ndp, 8, 128, dtype=F32), shape(nt, tok, hcols), shape(tree, width),
                   shape(*tall), shape(heads, 128, tree), shape(*tall), shape(heads, HD, tree), shape(*tall),
                   shape(tree, 3 * rank), shape(hcols, tree), shape(3, width, pad), shape(3, 3 * rank, pad)],
        in_specs=[IN_VMEM] * 8 + [IN_ANY] * 3, out_specs=[IN_ANY] * 13,
        scratch_shapes=[VMEM((wr, hcols), BF16), VMEM((wr, hcols), BF16), VMEM((tree, width), BF16), VMEM((ndp, wr, hcols), BF16),
                        VMEM((3, width, pad), BF16), VMEM((3, 3 * rank, pad), BF16), VMEM(tall, BF16), VMEM((heads, 128, tree), BF16),
                        VMEM(tall, BF16), VMEM((heads, HD, tree), BF16), VMEM(tall, BF16), VMEM((heads, HD + 16, tree), BF16),
                        VMEM((tree, 3 * rank), BF16), VMEM((hcols, tree), BF16), VMEM((tree, hcols), BF16),
                        VMEM((heads, 1, BLK), F32), VMEM((heads, HD + 16, BLK), F32), DMA((3,)), DMA((10,)),
                        DMA((3, chunks)), DMA((nt, chunks)), DMA((3, ndp)), DMA((ndp,)), DMA((3, ndp)), DMA((ndp,)),
                        DMA((2, ndp, nt, 4)), DMA((2,)), DMA((2, ndp, nt)), DMA((nblk,)), DMA((nt, tok // BLK))],
        compiler_params=params(1), name="forward",
    )(inputs, norm_gain_rows, choice, at_qkv, b_attn, scale, seg, mq, attention_weights.reshape(wr, hcols), output_weight,
      feedforward_weights.reshape(2 * wrows, hcols))

    output, d_mid, d_mix, g_mid = pl.pallas_call(
        mid_kernel,
        out_shape=[shape(tok, width), shape(tok, width, dtype=F32), shape(nt, tok, hcols), shape(6, rank, width, dtype=F32)],
        in_specs=[IN_VMEM] * 6 + [IN_ANY], out_specs=[IN_VMEM] * 4,
        scratch_shapes=[VMEM((tok, width), BF16), VMEM((tok, width), F32), VMEM((tok, width), BF16), VMEM((tok, width), F32),
                        VMEM((tok, width), BF16), VMEM((tok, width), F32), VMEM((tok, width), BF16), VMEM((3, width, width), BF16)]
        + [VMEM((ndp, nt, wrows, hcols), BF16)] * 3 + [DMA((3,))],
        compiler_params=params(), name="middle",
    )(inputs, cotangent, mixed, norm_gain_rows, at_mid, b_mid, wall)
    gr = 6 * rank
    half_rows = gr // 2
    half, hb, per = nblk // 2, BLK // 2, tok // BLK
    grad_bufs = [VMEM((2, half_rows, width), BF16), VMEM((2, half_rows, width), BF16), VMEM((half_rows, width), BF16), VMEM((half_rows, width), BF16)]
    grad_sems = [DMA((2,)), DMA((2,)), DMA((3, ndp)), DMA((ndp,)), DMA((ndp,)), DMA((ndp,)), DMA((1,))]
    input_grad, grads_mid, grads_attn = pl.pallas_call(
        functools.partial(back_kernel, ndp),
        out_shape=[shape(tok, width, dtype=F32), shape(2, ndp, half_rows, width), shape(2, ndp, half_rows, width)],
        in_specs=[IN_ANY] * 12 + [IN_VMEM] * 5, out_specs=[IN_ANY] * 3,
        scratch_shapes=[VMEM((hcols, tree), BF16), VMEM(tall, BF16), VMEM((heads, 128, tree), BF16), VMEM(tall, BF16), VMEM((heads, HD, tree), BF16),
                        VMEM(tall, BF16), VMEM((3, width, pad), BF16), VMEM((tree, width), BF16), VMEM((tree, 3 * rank), BF16),
                        VMEM((tok, width), BF16), VMEM((tok, width), F32), VMEM((tree, hcols), BF16), VMEM(tall, BF16), VMEM((heads, 128, tree), BF16),
                        VMEM((heads, HD, tree), F32), VMEM(tall, F32), VMEM(tall, F32), VMEM((nblk, BLK, width), BF16), VMEM((half, hb, width), BF16),
                        VMEM((half, hb, width), BF16), VMEM((per, BLK, width), BF16), VMEM((per, BLK, width), BF16),
                        VMEM((3 * rank, width), F32), VMEM((3, 3 * rank, pad), F32), VMEM((pad, width), BF16)]
        + grad_bufs + grad_bufs + [DMA((11,)), DMA((4,)), DMA((nt,)), DMA((half,)), DMA((half,)), DMA((half,)), DMA((per, 2)), DMA((per,)), DMA((per,)), DMA((1,))]
        + grad_sems + grad_sems,
        compiler_params=params(4, 62 << 20), name="back",
    )(d_mix, mixt, q, qt, k, kt, v, wp, xn, ranks, inputs, d_mid, scale, bp, at_qkv, norm_gain_rows, g_mid.reshape(gr, width))

    count = adapter_first_input.shape[1]
    table = shape(count, rank, width, dtype=F32)
    ga_in, gb_qkv, gb_up, ga_out, ga_down, gb_res = pl.pallas_call(
        place_kernel,
        out_shape=[shape(4, count, rank, width, dtype=F32), shape(3, count, rank, width, dtype=F32), table, table, table,
                   shape(2, count, rank, width, dtype=F32)],
        in_specs=[IN_SMEM] + [IN_VMEM] * 2, out_specs=[IN_ANY] * 6,
        scratch_shapes=[VMEM((12, count, rank, width), F32), DMA((12,))], compiler_params=params(), name="place",
    )(choices, grads_mid, grads_attn)
    return (output, input_grad, jnp.swapaxes(ga_in, 2, 3), gb_qkv, gb_up, jnp.swapaxes(ga_out, 1, 2), jnp.swapaxes(ga_down, 1, 2), gb_res)


def solution(mesh):
    tokens, weights = P(("dp", "tensor"), None), P(None, "dp", "tensor")
    in_specs = (tokens, tokens, P("dp"), P("dp", None), P("dp", None), P(), P(), weights, P("dp", "tensor"), weights) + (P(),) * 6
    out_specs = (tokens, tokens) + (P(),) * 6
    return jax.shard_map(local, mesh=mesh, in_specs=in_specs, out_specs=out_specs, check_vma=False)
```

```python
import functools
import math

import jax
import jax.numpy as jnp
from jax import lax
from jax.experimental import pallas as pl
from jax.experimental.pallas import tpu as pltpu
from jax.sharding import PartitionSpec as P

F32, BF16 = jnp.float32, jnp.bfloat16
BIG = 1e30
BLK = 256
HD = 80

def dot(a, b):
    return lax.dot_general(a, b, (((1,), (0,)), ((), ())), preferred_element_type=F32)
def dot_nt(a, b):
    return lax.dot_general(a, b, (((1,), (1,)), ((), ())), preferred_element_type=F32)
def dot_tn(a, b):
    return lax.dot_general(a, b, (((0,), (0,)), ((), ())), preferred_element_type=F32)

def project(b, s, x_ref, wp_ref, a_ref, bp_ref, scale_ref, seg_ref, mq_ref, n_ref, t_ref, rank_ref):
    rows = pl.ds(pl.multiple_of(b * BLK, BLK), BLK)
    xb = x_ref[rows, :]
    if s == 0:
        rank_ref[rows, :] = dot_nt(xb, a_ref[...]).astype(BF16)
    lane = lax.broadcasted_iota(jnp.int32, (BLK, 128), 1)
    if s == 2:
        feat = jnp.where(lane < HD + 2, 1.0, 0.0)
    else:
        tok = (lax.broadcasted_iota(jnp.int32, (BLK, 128), 0) + b * BLK).astype(F32)
        feat = jnp.where((tok >= seg_ref[0:1, :]) & (tok < seg_ref[1:2, :]), 1.0, 0.0)
        if s == 0:
            feat = dot(feat.astype(BF16), mq_ref[...])
        else:
            feat = jnp.where((lane >= HD + 13) & (lane < HD + 16), 1.0, feat)
    y = dot(xb, wp_ref[s]) + dot(rank_ref[rows, :], bp_ref[s])
    if s == 0:
        y = y * scale_ref[...]
    for h in range(n_ref.shape[0]):
        yh = jnp.where(lane < HD, y[:, h * 128:(h + 1) * 128], feat)
        n_ref[h, rows, :] = yh.astype(BF16)
        t_ref[h, :, rows] = yh.T[:t_ref.shape[1]].astype(BF16)

def attend_block(i, qt_ref, k_ref, vt_ref, m_ref, acc_ref, mixt_ref, mix_ref, count=None, jlist=None):
    heads = qt_ref.shape[0]
    cols = pl.ds(pl.multiple_of(i * BLK, BLK), BLK)
    m_ref[...] = jnp.full_like(m_ref, -3e38)
    acc_ref[...] = jnp.zeros_like(acc_ref)
    def step(j, diag):
        rows = pl.ds(pl.multiple_of(j * BLK, BLK), BLK)
        hs = range(heads)
        ss = [dot(k_ref[h, rows, :], qt_ref[h, :, cols]) for h in hs]
        if diag:
            low = lax.broadcasted_iota(jnp.int32, ss[0].shape, 0) <= lax.broadcasted_iota(jnp.int32, ss[0].shape, 1)
            ss = [jnp.where(low, s, -BIG) for s in ss]
        olds = [m_ref[h] for h in hs]
        news = [jnp.maximum(olds[h], jnp.max(ss[h], axis=0, keepdims=True)) for h in hs]
        ps = [jnp.exp(ss[h] - news[h]).astype(BF16) for h in hs]
        pv = [dot(vt_ref[h, :, rows], ps[h]) for h in hs]
        accs = [acc_ref[h] * jnp.exp(olds[h] - news[h]) + pv[h] for h in hs]
        for h in hs:
            acc_ref[h] = accs[h]
            m_ref[h] = news[h]
    if jlist is None:
        lax.fori_loop(0, i, lambda j, c: (step(j, False), c)[1], 0)
    else:
        lax.fori_loop(0, count, lambda n, c: (step(jlist(n), False), c)[1], 0)
    step(i, True)
    outs = []
    for h in range(heads):
        acc = acc_ref[h]
        l = acc[HD:HD + 1]
        o = acc[:HD] * (1.0 / l)
        lse = m_ref[h] + jnp.log(l)
        hi = (-lse).astype(BF16).astype(F32)
        mid = (-lse - hi).astype(BF16).astype(F32)
        lo = -lse - hi - mid
        r = lax.broadcasted_iota(jnp.int32, (16, BLK), 0)
        old = qt_ref[h, HD:HD + 16, cols].astype(F32)
        new = jnp.where(r == 13, hi, jnp.where(r == 14, mid, jnp.where(r == 15, lo, old)))
        qt_ref[h, HD:HD + 16, cols] = new.astype(BF16)
        outs.append(o)
    ot = jnp.concatenate(outs, axis=0)
    mixt_ref[:, cols] = ot.astype(BF16)
    mix_ref[cols, :] = ot.T.astype(BF16)

def spread_heads(hcols, pad):
    c = lax.broadcasted_iota(jnp.int32, (hcols, pad), 0)
    l = lax.broadcasted_iota(jnp.int32, (hcols, pad), 1)
    return jnp.where(((l & 127) < HD) & ((l >> 7) * HD + (l & 127) == c), 1.0, 0.0).astype(BF16)

def head_columns(me, pad, width):
    l = lax.broadcasted_iota(jnp.int32, (pad, width), 0)
    col = lax.broadcasted_iota(jnp.int32, (pad, width), 1)
    put = ((l & 127) < HD) & (me.t * (pad // 128 * HD) + (l >> 7) * HD + (l & 127) == col)
    return jnp.where(put, 1.0, 0.0).astype(BF16)

def tree_masks(len_ref, par_ref, seg_ref, mq_ref):
    segs = len_ref.shape[1]
    lane = lax.broadcasted_iota(jnp.int32, (1, 128), 1) - HD
    row = lax.broadcasted_iota(jnp.int32, (128, 1), 0) - HD
    lo = hi = jnp.zeros((1, 128), jnp.int32)
    up = grand = jnp.full((128, 1), -1, jnp.int32)
    start = 0
    for u in range(segs):
        end = start + len_ref[0, u]
        parent = par_ref[0, u]
        lo = jnp.where(lane == u, start, lo)
        hi = jnp.where(lane == u, end, hi)
        up = jnp.where(row == u, parent, up)
        grand = jnp.where(row == u, par_ref[0, parent], grand)
        start = end
    seg_ref[0:1, :] = lo.astype(F32)
    seg_ref[1:2, :] = hi.astype(F32)
    reach = (lane == row) | (lane == up) | (lane == grand)
    inside = (row >= 0) & (row < segs) & (lane >= 0) & (lane < segs)
    mq_ref[...] = jnp.where(inside & jnp.logical_not(reach), -BIG, 0.0).astype(BF16)

def bwd_prep(b, dm_ref, mixt_ref, do_ref, dot_ref):
    rows = pl.ds(pl.multiple_of(b * BLK, BLK), BLK)
    heads = do_ref.shape[0]
    dt = dm_ref[rows, :].astype(F32).T
    prod = dt * mixt_ref[:, rows].astype(F32)
    r = lax.broadcasted_iota(jnp.int32, (16, BLK), 0)
    for h in range(heads):
        d = dt[h * HD:(h + 1) * HD]
        delta = -jnp.sum(prod[h * HD:(h + 1) * HD], axis=0, keepdims=True)
        hi = delta.astype(BF16).astype(F32)
        ext = jnp.where(r == 0, hi, jnp.where(r == 1, delta - hi, 0.0))
        full = jnp.concatenate([d, ext, jnp.zeros((32, BLK), F32)], axis=0)
        dot_ref[h, :, rows] = full.astype(BF16)
        do_ref[h, rows, :] = full.T.astype(BF16)

def bwd_pair(i, j, diag, q_ref, qt_ref, k_ref, kt_ref, v_ref, do_ref, dot_ref, dqt_ref, dk_ref, dv_ref):
    heads = q_ref.shape[0]
    cols = pl.ds(pl.multiple_of(i * BLK, BLK), BLK)
    rows = pl.ds(pl.multiple_of(j * BLK, BLK), BLK)
    hs = range(heads)
    ss = [dot(k_ref[h, rows, :], qt_ref[h, :, cols]) for h in hs]
    dps = [dot(v_ref[h, rows, :], dot_ref[h, :, cols]) for h in hs]
    if diag:
        low = lax.broadcasted_iota(jnp.int32, ss[0].shape, 0) <= lax.broadcasted_iota(jnp.int32, ss[0].shape, 1)
        ss = [jnp.where(low, s, -BIG) for s in ss]
    ps = [jnp.exp(s) for s in ss]
    dss = [(p * dp).astype(BF16) for p, dp in zip(ps, dps)]
    ps = [p.astype(BF16) for p in ps]
    dvs = [dot(ps[h], do_ref[h, cols, :]) for h in hs]
    dks = [dot(dss[h], q_ref[h, cols, :]) for h in hs]
    dqs = [dot(kt_ref[h, :, rows], dss[h]) for h in hs]
    for h in hs:
        dv_ref[h, rows, :] += dvs[h]
        dk_ref[h, rows, :] += dks[h]
        dqt_ref[h, :, cols] += dqs[h]

MESH = pl.DeviceIdType.MESH


class Place:
    def __init__(self, ndp):
        self.d, self.t = lax.axis_index("dp"), lax.axis_index("tensor")
        self.line = ndp // 2
        self.p, self.par = self.d // 2, self.d % 2
        self.dx = self.d + 1 - 2 * self.par
        self.c, self.y = self.t % 2, self.t // 2
        self.t1 = self.t + 1 - 2 * self.c
        self.t2 = (self.t + 2) % 4
        self.t3 = (self.t1 + 2) % 4
        self.has_left, self.has_right = self.p > 0, self.p < self.line - 1


def signal(sem, d, t):
    pl.semaphore_signal(sem, inc=1, device_id=(d, t), device_id_type=MESH)


def remote(src, dst, send_sem, recv_sem, d, t):
    return pltpu.make_async_remote_copy(src_ref=src, dst_ref=dst, send_sem=send_sem, recv_sem=recv_sem, device_id=(d, t), device_id_type=MESH)


def greet(me, tensor=(), pair=False, line=False):
    bar = pltpu.get_barrier_semaphore()
    count = len(tensor) + (1 if pair else 0)
    for t in tensor:
        signal(bar, me.d, t)
    if pair:
        signal(bar, me.dx, me.t)
    if line:
        @pl.when(me.has_left)
        def _():
            signal(bar, me.d - 2, me.t)
        @pl.when(me.has_right)
        def _():
            signal(bar, me.d + 2, me.t)
        count = count + jnp.where(me.has_left, 1, 0) + jnp.where(me.has_right, 1, 0)
    pl.semaphore_wait(bar, count)


class PairLine:
    def __init__(self, me, own, buf, send, recv, part=None):
        self.me, self.own, self.buf, self.send, self.recv, self.part = me, own, buf, send, recv, part

    def slot(self, o):
        return self.buf.at[o] if self.part is None else self.buf.at[o, self.part]

    def copy(self, o, src, d, kind):
        send, recv = (self.send.at[kind, o], self.recv.at[o]) if self.part is None else (self.send.at[kind, o, self.part], self.recv.at[o, self.part])
        return remote(src, self.slot(o), send, recv, d, self.me.t)

    def start(self):
        me = self.me
        @pl.when(me.has_left)
        def _():
            self.copy(me.d, self.own, me.d - 2, 0).start()
        @pl.when(me.has_right)
        def _():
            self.copy(me.d, self.own, me.d + 2, 1).start()
        self.copy(me.d, self.own, me.dx, 2).start()

    def hop(self, k, then=None):
        me = self.me
        @pl.when(me.p - k >= 0)
        def _():
            o = me.d - 2 * k
            self.copy(o, self.slot(o), me.dx, 2).wait_recv()
            @pl.when(me.has_right)
            def _():
                self.copy(o, self.slot(o), me.d + 2, 1).start()
            self.copy(o, self.slot(o), me.dx, 2).start()
            if then is not None:
                then(o)
        @pl.when(me.p + k < me.line)
        def _():
            o = me.d + 2 * k
            self.copy(o, self.slot(o), me.dx, 2).wait_recv()
            @pl.when(me.has_left)
            def _():
                self.copy(o, self.slot(o), me.d - 2, 0).start()
            self.copy(o, self.slot(o), me.dx, 2).start()
            if then is not None:
                then(o)

    def pair_arrivals(self, then=None):
        def one(q, c):
            o = 2 * q + 1 - self.me.par
            self.copy(o, self.slot(o), self.me.dx, 2).wait_recv()
            if then is not None:
                then(o)
            return c
        lax.fori_loop(0, self.me.line, one, 0)

    def sent(self):
        me = self.me
        def one(q, c):
            o = 2 * q + me.par
            self.copy(o, self.slot(o), me.dx, 2).wait_send()
            @pl.when((q >= me.p) & me.has_left)
            def _():
                self.copy(o, self.slot(o), me.dx, 0).wait_send()
            @pl.when((q <= me.p) & me.has_right)
            def _():
                self.copy(o, self.slot(o), me.dx, 1).wait_send()
            return c
        lax.fori_loop(0, me.line, one, 0)


class FullGather:
    def __init__(self, me, own, buf, send, first, recv):
        self.me, self.own, self.buf, self.send, self.first, self.recv = me, own, buf, send, first, recv
        cut = own.shape[0] // 48 * 16
        self.parts = (pl.ds(0, cut), pl.ds(cut, own.shape[0] - cut))

    def copy(self, h, o, t, d2, t2, kind, own=False):
        rows = self.parts[h]
        src = self.own.at[rows] if own else self.buf.at[o, t, rows]
        sem = self.first.at[h] if kind == 4 else self.send.at[h, o, t, kind]
        return remote(src, self.buf.at[o, t, rows], sem, self.recv.at[h, o, t], d2, t2)

    def last(self, h):
        me = self.me
        return (me.d, me.t2) if h == 0 else (me.dx, me.t)

    def spread(self, h, o, t, left, right, own=False):
        me = self.me
        @pl.when(left)
        def _():
            self.copy(h, o, t, me.d - 2, me.t, 0, own).start()
        @pl.when(right)
        def _():
            self.copy(h, o, t, me.d + 2, me.t, 1, own).start()
        self.copy(h, o, t, *self.last(h), 2, own).start()
        self.copy(h, o, t, me.d, me.t1, 3, own).start()

    def start(self):
        me = self.me
        self.copy(0, me.d, me.t, me.dx, me.t, 4, True).start()
        self.copy(1, me.d, me.t, me.d, me.t2, 4, True).start()
        for h in (1, 0):
            self.spread(h, me.d, me.t, me.has_left, me.has_right, True)

    def arrived(self, h, o, t):
        self.copy(h, o, t, self.me.d, self.me.t1, 3).wait_recv()

    def firsts(self):
        me = self.me
        self.arrived(0, me.dx, me.t)
        self.spread(0, me.dx, me.t, me.has_left, me.has_right)
        self.arrived(1, me.d, me.t2)
        self.spread(1, me.d, me.t2, me.has_left, me.has_right)

    def streams(self, q):
        me = self.me
        return ((0, 2 * q + me.par, me.t), (0, 2 * q + 1 - me.par, me.t), (1, 2 * q + me.par, me.t), (1, 2 * q + me.par, me.t2))

    def hop(self, k):
        me = self.me
        @pl.when(me.p - k >= 0)
        def _():
            for h, o, t in self.streams(me.p - k):
                self.arrived(h, o, t)
                self.spread(h, o, t, False, me.has_right)
        @pl.when(me.p + k < me.line)
        def _():
            for h, o, t in self.streams(me.p + k):
                self.arrived(h, o, t)
                self.spread(h, o, t, me.has_left, False)

    def lasts(self, k):
        me = self.me

        def place(q):
            for h, o, t in ((0, 2 * q, me.t2), (0, 2 * q + 1, me.t2), (1, 2 * q + 1 - me.par, me.t), (1, 2 * q + 1 - me.par, me.t2)):
                self.arrived(h, o, t)
                self.copy(h, o, t, me.d, me.t1, 3).start()

        @pl.when(me.p - k >= 0)
        def _():
            place(me.p - k)
        @pl.when((me.p + k < me.line) & (k > 0))
        def _():
            place(me.p + k)

    def finish(self):
        me = self.me
        def one(o, c):
            for h in range(2):
                self.arrived(h, o, me.t1)
                self.arrived(h, o, me.t3)
                for t in (me.t, me.t2):
                    self.copy(h, o, t, me.d, me.t1, 3).wait_send()
            return c
        lax.fori_loop(0, 2 * me.line, one, 0)
        def two(q, c):
            for h, o, t in self.streams(q):
                self.copy(h, o, t, me.d, me.t1, 2).wait_send()
                @pl.when((q >= me.p) & me.has_left)
                def _():
                    self.copy(h, o, t, me.d, me.t1, 0).wait_send()
                @pl.when((q <= me.p) & me.has_right)
                def _():
                    self.copy(h, o, t, me.d, me.t1, 1).wait_send()
            return c
        lax.fori_loop(0, me.line, two, 0)
        for h in range(2):
            self.copy(h, me.d, me.t, me.d, me.t1, 4).wait_send()


EPS = 1e-6


def forward_kernel(ndp, chunks, choice_in, len_ref, par_ref, x_ref, gain_ref, qs_ref, ain_h, btab_h, a_ref, wo_ref, wf_ref,
                   wout_ref, cho_ref, mixed_ref, xno_ref, qo_ref, qto_ref, ko_ref, kto_ref, vo_ref, ranko_ref, mixto_ref, wpo_ref, bpo_ref, ato_ref, scaleo_ref,
                   ain_ref, btab_ref, choice_ref, at_ref, scale_ref, seg_ref, mq_ref, put_ref,
                   aown_ref, wown_ref, xn_ref, wa_ref, wp_ref, bp_ref, q_ref, qt_ref, k_ref, kt_ref, v_ref, vt_ref, rank_ref, mixt_ref,
                   mix_ref, m_ref, acc_ref, ls, os, xs, xr, a_s, a_r, c_s, c_r, w_s, w_f, w_r, ms, mr):
    me = Place(ndp)
    tok, width = x_ref.shape
    rows_o = wo_ref.shape[0]
    loads = [pltpu.make_async_copy(a_ref, aown_ref, ls.at[0]), pltpu.make_async_copy(wo_ref, wown_ref.at[pl.ds(0, rows_o)], ls.at[1]),
             pltpu.make_async_copy(wf_ref, wown_ref.at[pl.ds(rows_o, wf_ref.shape[0])], ls.at[2])]
    tables = [pltpu.make_async_copy(ain_h.at[pl.ds(0, 3)], ain_ref, ls.at[3]), pltpu.make_async_copy(btab_h, btab_ref, ls.at[4])]
    for copy in loads + tables:
        copy.start()
    e = choice_in[0]
    choice_ref[...] = jnp.zeros_like(choice_ref) + e.astype(F32)
    x = x_ref[...].astype(F32)
    mine = pl.ds(pl.multiple_of(me.t * tok, tok), tok)
    xn_ref[mine, :] = (x * lax.rsqrt(jnp.mean(x * x, axis=-1, keepdims=True) + EPS) * gain_ref[0:1, :]).astype(BF16)
    greet(me, tensor=(me.t1, me.t2, me.t3), pair=True, line=True)
    size = tok // chunks

    def xcopy(o, c, t, kind):
        rows = pl.ds(pl.multiple_of(o * tok + c * size, size), size)
        return remote(xn_ref.at[rows], xn_ref.at[rows], xs.at[kind, c], xr.at[o, c], me.d, t)

    for c in range(chunks):
        xcopy(me.t, c, me.t2, 0).start()
    for c in range(chunks):
        xcopy(me.t, c, me.t1, 1).start()
    for copy in loads:
        copy.wait()
    parts = [PairLine(me, aown_ref.at[n], wa_ref, a_s, a_r, n) for n in range(3)]
    ch = PairLine(me, choice_ref, cho_ref, c_s, c_r)
    w = FullGather(me, wown_ref, wout_ref, w_s, w_f, w_r)
    parts[0].start()
    parts[1].start()
    keep = [pltpu.make_async_copy(wown_ref, wout_ref.at[me.d, me.t], ls.at[0]), pltpu.make_async_copy(choice_ref, cho_ref.at[me.d], ls.at[1])]
    for copy in keep:
        copy.start()
    wa_ref[me.d] = aown_ref[...]
    tree_masks(len_ref, par_ref, seg_ref, mq_ref)
    scale_ref[...] = jnp.zeros_like(scale_ref)
    for h in range(q_ref.shape[0]):
        scale_ref[:, h * 128:h * 128 + HD] = qs_ref[...] * (1.0 / math.sqrt(HD))
    put_ref[...] = head_columns(me, *put_ref.shape)
    for copy in tables:
        copy.wait()
    parts[0].hop(1)
    parts[2].start()
    ch.start()

    def diagonal(n, carry):
        for part in range(3):
            k = n - part
            @pl.when((k >= 1) & (k < me.line))
            def _():
                parts[part].hop(k)
        return carry
    lax.fori_loop(2, me.line + 2, diagonal, 0)
    w.start()
    n16 = ain_ref.shape[2]
    for s in range(3):
        at_ref[s * n16:(s + 1) * n16] = ain_ref[s, e]
    picked = jnp.concatenate([btab_ref[s, e] for s in range(3)], axis=0)
    spread = (0.5 * dot_nt(picked, put_ref[...])).astype(BF16)
    bp_ref[...] = jnp.zeros_like(bp_ref)
    for s in range(3):
        bp_ref[s, s * n16:(s + 1) * n16] = spread[s * n16:(s + 1) * n16]

    def forward(c):
        xcopy(me.t2, c, me.t1, 2).wait_recv()
        xcopy(me.t2, c, me.t1, 2).start()

    for c in range(chunks // 2):
        forward(c)
    nblk = xn_ref.shape[0] // BLK
    near = nblk // 2
    wrows = wa_ref.shape[2]
    group = 16 // math.gcd(wrows, 16)
    sel = spread_heads(wa_ref.shape[3], wp_ref.shape[2])

    def project_blocks(first, s):
        n_ref, t_ref = ((q_ref, qt_ref), (k_ref, kt_ref), (v_ref, vt_ref))[s]
        lax.fori_loop(0, near, lambda n, c: (project(first + n, s, xn_ref, wp_ref, at_ref, bp_ref, scale_ref, seg_ref, mq_ref, n_ref, t_ref, rank_ref), c)[1], 0)

    for c in range(chunks):
        xcopy(me.t1, c, me.t1, 2).wait_recv()
    for s in range(3):
        parts[s].pair_arrivals()
        for o in range(0, ndp, group):
            wp_ref[s, o * wrows:(o + group) * wrows] = jnp.concatenate([dot(wa_ref[o + j, s], sel) for j in range(group)], axis=0).astype(BF16)
        project_blocks(me.y * near, s)
        if s < 2:
            forward(chunks // 2 + s)
    for c in range(chunks):
        xcopy(me.t3, c, me.t1, 2).wait_recv()
    w.firsts()
    for s in range(3):
        project_blocks((1 - me.y) * near, s)

    def hops(i):
        done = 1 + jnp.maximum((me.line - 2) * (i + 1) * (i + 2) + 2 * nblk, 0) // ((nblk - 1) * nblk)
        return jnp.minimum(done, me.line - 1)

    def relay(i):
        lax.fori_loop(hops(i - 1), hops(i), lambda k, c: (w.hop(k + 1), ch.hop(k + 1), c)[2], 0)
    w.hop(1)
    ch.hop(1)
    outs = [pltpu.make_async_copy(src, dst, os.at[n]) for n, (src, dst) in enumerate((
        (xn_ref, xno_ref), (q_ref, qo_ref), (k_ref, ko_ref), (kt_ref, kto_ref), (v_ref, vo_ref), (rank_ref, ranko_ref),
        (wp_ref, wpo_ref), (bp_ref, bpo_ref), (at_ref, ato_ref), (scale_ref, scaleo_ref)))]
    for copy in outs:
        copy.start()
    per = tok // BLK

    def piece(i):
        rows = pl.ds(pl.multiple_of(i * BLK, BLK), BLK)
        return mix_ref.at[rows], mixed_ref.at[me.t, pl.ds(pl.multiple_of((i % per) * BLK, BLK), BLK)], i // per

    def attend_step(i, c):
        attend_block(i, qt_ref, k_ref, vt_ref, m_ref, acc_ref, mixt_ref, mix_ref)
        src, dst, t = piece(i)
        @pl.when(t == me.t)
        def _():
            pltpu.make_async_copy(src, dst, ms.at[i]).start()
        @pl.when(t != me.t)
        def _():
            remote(src, dst, ms.at[i], mr.at[me.t, i % per], me.d, t).start()
        relay(i)
        lax.fori_loop(jnp.where(i == 0, 0, hops(i - 2)), hops(i - 1), lambda k, n: (w.lasts(k), n)[1], 0)
        return c
    lax.fori_loop(0, nblk, attend_step, 0)
    late = [pltpu.make_async_copy(qt_ref, qto_ref, os.at[len(outs)]), pltpu.make_async_copy(mixt_ref, mixto_ref, os.at[len(outs) + 1])]
    for copy in late:
        copy.start()
    lax.fori_loop(hops(nblk - 2), me.line, lambda k, c: (w.lasts(k), c)[1], 0)
    ch.pair_arrivals()
    for t in (me.t1, me.t2, me.t3):
        for h in range(per):
            dst = mixed_ref.at[t, pl.ds(h * BLK, BLK)]
            remote(dst, dst, ms.at[0], mr.at[t, h], me.d, t).wait_recv()
    w.finish()
    for part in parts:
        part.sent()
    ch.sent()
    for c in range(chunks):
        for kind in range(3):
            xcopy(me.t, c, me.t1, kind).wait_send()

    def settle(i, c):
        src, dst, t = piece(i)
        @pl.when(t == me.t)
        def _():
            pltpu.make_async_copy(src, dst, ms.at[i]).wait()
        @pl.when(t != me.t)
        def _():
            remote(src, dst, ms.at[i], mr.at[me.t, i % per], me.d, t).wait_send()
        return c
    lax.fori_loop(0, nblk, settle, 0)
    for copy in keep + outs + late:
        copy.wait()


def sigmoid(v):
    return 1.0 / (1.0 + jnp.exp(-v))


def mid_kernel(e_ref, x_ref, g_ref, mix4_ref, gain_ref, wall_ref, aout_h, ain_h, adown_h, bup_h, bres_h, out_ref, dmid_ref, dmix_ref, grads_ref,
               at_ref, b_ref, ts, mix_ref, mid_ref, hid_ref, up_ref, act_ref, f_ref, low_ref, w_ref, wb0_ref, wb1_ref, wb2_ref, ls):
    width = x_ref.shape[1]
    step = 256
    part = mix4_ref.shape[2]
    blocks = (wb0_ref, wb1_ref, wb2_ref)
    ndp, nt, wrows = wb0_ref.shape[:3]
    loads = [pltpu.make_async_copy(wall_ref.at[:, :, pl.ds(n * wrows, wrows)], blocks[n], ls.at[n]) for n in range(3)]
    e = e_ref[0]
    tables = [pltpu.make_async_copy(src, dst, ts.at[n]) for n, (src, dst) in enumerate((
        (aout_h.at[e], at_ref.at[0]), (ain_h.at[3, e], at_ref.at[1]), (adown_h.at[e], at_ref.at[2]),
        (bres_h.at[0, e], b_ref.at[0]), (bup_h.at[e], b_ref.at[1]), (bres_h.at[1, e], b_ref.at[2])))]
    for copy in tables + loads:
        copy.start()
    for copy in tables:
        copy.wait()

    def assemble(n):
        loads[n].wait()
        for o in range(ndp):
            for t in range(nt):
                w_ref[n, o * wrows:(o + 1) * wrows, t * part:(t + 1) * part] = blocks[n][o, t]

    for t in range(mix4_ref.shape[0]):
        mix_ref[:, t * part:(t + 1) * part] = mix4_ref[t]

    def cols(n):
        return pl.ds(pl.multiple_of(n * step, step), step)

    def each(fn):
        lax.fori_loop(0, width // step, lambda n, c: (fn(cols(n)), c)[1], 0)

    gain = gain_ref[1:2, :]
    r_out = dot_nt(mix_ref[...], at_ref[0]).astype(BF16)
    assemble(0)

    def project_out(n):
        attn = dot_nt(mix_ref[...], w_ref[0, n, :]) + 0.5 * dot(r_out, b_ref[0, :, n])
        mid_ref[:, n] = x_ref[:, n].astype(F32) + attn
    each(project_out)
    middle = mid_ref[...]
    r = lax.rsqrt(jnp.mean(middle * middle, axis=-1, keepdims=True) + EPS)
    hid_ref[...] = (middle * r * gain).astype(BF16)
    r_up = dot_nt(hid_ref[...], at_ref[1]).astype(BF16)
    assemble(1)

    def up_step(n):
        up = dot(hid_ref[...], w_ref[1, :, n]) + 0.5 * dot(r_up, b_ref[1, :, n])
        up_ref[:, n] = up
        act_ref[:, n] = (up * sigmoid(up)).astype(BF16)
    each(up_step)
    r_down = dot_nt(act_ref[...], at_ref[2]).astype(BF16)
    assemble(2)

    def down_step(n):
        down = dot_nt(act_ref[...], w_ref[2, n, :]) + 0.5 * dot(r_down, b_ref[2, :, n])
        out_ref[:, n] = (mid_ref[:, n] + down).astype(BF16)
    each(down_step)
    grads_ref[5] = 0.5 * dot_tn(r_down, g_ref[...])
    dz_down = (0.5 * dot_nt(g_ref[...], b_ref[2])).astype(BF16)
    grads_ref[3] = dot_tn(dz_down, act_ref[...])

    def act_back(n):
        d_act = dot(g_ref[...], w_ref[2, :, n]) + dot(dz_down, at_ref[2, :, n])
        up = up_ref[:, n]
        sg = sigmoid(up)
        low_ref[:, n] = (d_act * sg * (1.0 + up * (1.0 - sg))).astype(BF16)
    each(act_back)
    dz_up = (0.5 * dot_nt(low_ref[...], b_ref[1])).astype(BF16)
    grads_ref[1] = 0.5 * dot_tn(r_up, low_ref[...])
    grads_ref[0] = dot_tn(dz_up, hid_ref[...])

    def hidden_back(n):
        f_ref[:, n] = (dot_nt(low_ref[...], w_ref[1, n, :]) + dot(dz_up, at_ref[1, :, n])) * gain_ref[1:2, n]
    each(hidden_back)
    gd = f_ref[...]
    middle = mid_ref[...]
    s = jnp.mean(middle * gd, axis=-1, keepdims=True)
    d_mid = g_ref[...].astype(F32) + r * gd - middle * (r * r * r * s)
    dmid_ref[...] = d_mid
    low_ref[...] = d_mid.astype(BF16)
    dz_out = (0.5 * dot_nt(low_ref[...], b_ref[0])).astype(BF16)
    grads_ref[4] = 0.5 * dot_tn(r_out, low_ref[...])
    grads_ref[2] = dot_tn(dz_out, mix_ref[...])

    def mixed_back(n):
        act_ref[:, n] = (dot(low_ref[...], w_ref[0, :, n]) + dot(dz_out, at_ref[0, :, n])).astype(BF16)
    each(mixed_back)
    for t in range(dmix_ref.shape[0]):
        dmix_ref[t] = act_ref[:, t * part:(t + 1) * part]


class GradSum:
    def __init__(self, me, gp, gr, g2, own, out, s, r, ls_, lr, fs, fr, keep):
        self.me, self.gp, self.gr, self.g2, self.own, self.out, self.s, self.r, self.fs, self.fr = me, gp, gr, g2, own, out, s, r, fs, fr
        self.line = PairLine(me, own, out.at[me.c], ls_, lr)
        self.keep = pltpu.make_async_copy(own, out.at[me.c, me.d], keep)

    def one(self):
        return remote(self.gp.at[1 - self.me.c], self.gr.at[0], self.s.at[0], self.r.at[0], self.me.d, self.me.t1)

    def two(self):
        return remote(self.g2, self.gr.at[1], self.s.at[1], self.r.at[1], self.me.d, self.me.t2)

    def second(self):
        self.one().wait_recv()
        self.g2[...] = (self.gp[self.me.c].astype(F32) + self.gr[0].astype(F32)).astype(BF16)
        self.two().start()

    def relay(self, o, own=False):
        src = self.own if own else self.out.at[self.me.c, o]
        return remote(src, self.out.at[self.me.c, o], self.fs.at[o], self.fr.at[o], self.me.d, self.me.t1)

    def gather(self):
        self.two().wait_recv()
        self.own[...] = (self.g2[...].astype(F32) + self.gr[1].astype(F32)).astype(BF16)
        self.line.start()
        self.relay(self.me.d, True).start()
        self.keep.start()

    def hop(self, k):
        self.line.hop(k, lambda o: self.relay(o).start())

    def arrivals(self):
        self.line.pair_arrivals(lambda o: self.relay(o).start())

    def settle(self, ndp):
        def one(o, c):
            self.relay(o, True).wait_send()
            remote(self.own, self.out.at[1 - self.me.c, o], self.fs.at[o], self.fr.at[o], self.me.d, self.me.t1).wait_recv()
            return c
        lax.fori_loop(0, ndp, one, 0)
        self.line.sent()
        self.keep.wait()
        self.one().wait_send()
        self.two().wait_send()


def back_kernel(ndp, dmix_ref, mixt_h, q_h, qt_h, k_h, kt_h, v_h, wp_h, xn_h, rank_h, x_h, dmid_h, scale_ref, bp_ref, at_ref, gain_ref, gmid_ref,
                ig_h, gm_h, ga_h,
                mixt_ref, q_ref, qt_ref, k_ref, kt_ref, v_ref, wp_ref, xn_ref, rank_ref, x_ref, dmid_ref, dm_ref, do_ref, dot_ref,
                dqt_ref, dk_ref, dv_ref, dn_ref, r1_ref, s2_ref, r2_ref, ro_ref, ga_ref, gb_ref, put_ref,
                gpm, grm, g2m, gom, gpa, gra, g2a, goa, lsem, dsem, drecv, es, er, s2s, r2r, ros, ror, igs,
                ms, mr, mls, mlr, mfs, mfr, mk, as_, ar, als, alr, afs, afr, ak):
    me = Place(ndp)
    tok = x_ref.shape[0]
    nblk = dm_ref.shape[0] // BLK
    per, half, hb = tok // BLK, nblk // 2, BLK // 2
    heads = q_ref.shape[0]
    loads = [pltpu.make_async_copy(src, dst, lsem.at[n]) for n, (src, dst) in enumerate((
        (mixt_h, mixt_ref), (q_h, q_ref), (qt_h, qt_ref), (k_h, k_ref), (kt_h, kt_ref), (v_h, v_ref),
        (wp_h, wp_ref), (xn_h, xn_ref), (rank_h, rank_ref), (x_h, x_ref), (dmid_h, dmid_ref)))]
    n48 = gpm.shape[1]
    for c in range(2):
        gpm[c] = gmid_ref[c * n48:(c + 1) * n48].astype(BF16)
    greet(me, tensor=(me.t1, me.t2, me.t3), pair=True, line=True)

    def token_rows(t):
        return pl.ds(pl.multiple_of(t * tok, tok), tok)

    def swap(n, t):
        return remote(dmix_ref.at[t], dm_ref.at[token_rows(me.t)], dsem.at[n], drecv.at[me.t], me.d, t)

    own = pltpu.make_async_copy(dmix_ref.at[me.t], dm_ref.at[token_rows(me.t)], dsem.at[3])
    for n, t in enumerate((me.t3, me.t2, me.t1)):
        swap(n, t).start()
    own.start()
    gm = GradSum(me, gpm, grm, g2m, gom, gm_h, ms, mr, mls, mlr, mfs, mfr, mk.at[0])
    ga = GradSum(me, gpa, gra, g2a, goa, ga_h, as_, ar, als, alr, afs, afr, ak.at[0])
    gm.one().start()
    for copy in loads:
        copy.start()
    for ref in (dqt_ref, dk_ref, dv_ref, ga_ref, gb_ref):
        ref[...] = jnp.zeros_like(ref)
    put_ref[...] = head_columns(me, *put_ref.shape)
    for copy in loads[:6]:
        copy.wait()

    def prep(t):
        lax.fori_loop(t * per, (t + 1) * per, lambda b, c: (bwd_prep(b, dm_ref, mixt_ref, do_ref, dot_ref), c)[1], 0)

    def arrived(t):
        remote(dmix_ref.at[t], dm_ref.at[token_rows(t)], dsem.at[0], drecv.at[t], me.d, t).wait_recv()

    own.wait()
    prep(me.t)
    arrived(me.t1)
    prep(me.t1)
    gm.second()
    arrived(me.t2)
    prep(me.t2)
    arrived(me.t3)
    prep(me.t3)
    for copy in loads[6:]:
        copy.wait()
    args = (q_ref, qt_ref, k_ref, kt_ref, v_ref, do_ref, dot_ref, dqt_ref, dk_ref, dv_ref)
    lane = lax.broadcasted_iota(jnp.int32, (BLK, 128), 1)

    def block(a):
        return (1 - me.y) * (nblk - 1 - a) + me.y * a

    def exchange(a):
        rows = pl.ds(pl.multiple_of((1 - me.c) * hb, hb), hb)
        return remote(dn_ref.at[a, rows], r1_ref.at[a], es.at[a], er.at[a], me.d, me.t1)

    def own_block(a):
        return remote(dn_ref.at[a], ro_ref.at[block(a) % per], ros.at[a % per], ror.at[block(a) % per], me.d, me.t1)

    def mine_rows():
        return pl.ds(pl.multiple_of(me.c * hb, hb), hb)

    def deliver(a):
        b = block(a)
        return remote(s2_ref.at[a], r2_ref.at[b % per, mine_rows()], s2s.at[a], r2r.at[b % per, me.c], me.d, b // per)

    def is_mine(a):
        return block(a) // per == me.t

    def pass_on(a):
        exchange(a).wait_recv()
        s2_ref[a] = (dn_ref[a, mine_rows(), :].astype(F32) + r1_ref[a].astype(F32)).astype(BF16)
        deliver(a).start()

    def final(a):
        rows = pl.ds(pl.multiple_of(block(a) * BLK, BLK), BLK)
        dq, dk, dv = [], [], []
        for h in range(heads):
            g = jnp.concatenate([dqt_ref[h, :, rows], jnp.zeros((48, BLK), F32)], axis=0).T
            dq.append((g * scale_ref[:, h * 128:(h + 1) * 128]).astype(BF16))
            dk.append(jnp.where(lane < HD, dk_ref[h, rows, :], 0.0).astype(BF16))
            dv.append(jnp.where(lane < HD, dv_ref[h, rows, :], 0.0).astype(BF16))
        ds = [jnp.concatenate(g, axis=1) for g in (dq, dk, dv)]
        dz = sum(dot_nt(ds[s], bp_ref[s]) for s in range(3)).astype(BF16)
        dn = sum(dot_nt(ds[s], wp_ref[s]) for s in range(3)) + dot(dz, at_ref[...])
        dn_ref[a] = dn.astype(BF16)
        ga_ref[...] += dot_tn(dz, xn_ref[rows, :])
        for s in range(3):
            gb_ref[s] += dot_tn(rank_ref[rows, :], ds[s])

    def upto(a):
        return 1 + jnp.minimum(a * (me.line - 1) // (nblk - 2), me.line - 1)

    def pairs(a):
        b = block(a)
        bwd_pair(b, b, True, *args)

        def other(n, c):
            bwd_pair(b + me.y * (1 + n), b - (1 - me.y) * (1 + n), False, *args)
            return c
        lax.fori_loop(0, nblk - 1 - a, other, 0)

    def far_step(a, c):
        pairs(a)
        @pl.when(a > 0)
        def _():
            pass_on(a - 1)
        final(a)
        exchange(a).start()
        @pl.when(a == 0)
        def _():
            gm.gather()
        lax.fori_loop(upto(a), upto(a + 1), lambda k, n: (gm.hop(k), n)[1], 0)
        return c
    lax.fori_loop(0, half, far_step, 0)

    def near_step(a, c):
        pairs(a)
        @pl.when(a == half)
        def _():
            pass_on(a - 1)
        final(a)
        @pl.when(jnp.logical_not(is_mine(a)))
        def _():
            own_block(a).start()
        lax.fori_loop(upto(a), upto(a + 1), lambda k, n: (gm.hop(k), n)[1], 0)
        return c
    lax.fori_loop(half, nblk, near_step, 0)
    n16 = n48 // 3
    gpa[0] = ga_ref[...].astype(BF16)
    gb = jnp.concatenate([gb_ref[s, s * n16:(s + 1) * n16] for s in range(3)], axis=0)
    gpa[1] = dot((0.5 * gb).astype(BF16), put_ref[...]).astype(BF16)
    ga.one().start()
    gm.arrivals()
    ga.second()

    def combine(i, c):
        b = me.t * per + i
        a = block(b)
        rows = pl.ds(pl.multiple_of(i * BLK, BLK), BLK)
        remote(dn_ref.at[a], ro_ref.at[i], ros.at[0], ror.at[i], me.d, me.t1).wait_recv()
        for h in range(2):
            remote(s2_ref.at[0], r2_ref.at[i, pl.ds(h * hb, hb)], s2s.at[0], r2r.at[i, h], me.d, me.t2).wait_recv()
        dn = dn_ref[a].astype(F32) + ro_ref[i].astype(F32) + r2_ref[i].astype(F32)
        x = x_ref[rows, :].astype(F32)
        r = lax.rsqrt(jnp.mean(x * x, axis=-1, keepdims=True) + EPS)
        gd = gain_ref[0:1, :] * dn
        dmid_ref[rows, :] = dmid_ref[rows, :] + r * gd - x * (r * r * r * jnp.mean(x * gd, axis=-1, keepdims=True))
        return c
    ga.gather()
    lax.fori_loop(0, per, combine, 0)
    put_ig = pltpu.make_async_copy(dmid_ref, ig_h, igs.at[0])
    put_ig.start()
    lax.fori_loop(1, me.line, lambda k, c: (ga.hop(k), c)[1], 0)
    ga.arrivals()
    ga.settle(ndp)
    gm.settle(ndp)

    def sent(a, c):
        exchange(a).wait_send()
        deliver(a).wait_send()
        return c
    lax.fori_loop(0, half, sent, 0)

    def own_sent(a, c):
        @pl.when(jnp.logical_not(is_mine(a)))
        def _():
            own_block(a).wait_send()
        return c
    lax.fori_loop(half, nblk, own_sent, 0)
    for n, t in enumerate((me.t3, me.t2, me.t1)):
        swap(n, t).wait_send()
    put_ig.wait()


def place_kernel(e_ref, gm_ref, ga_ref, ig_in, ain_h, bqkv_h, bup_h, aout_h, adown_h, bres_h, ig_out, out_ref, sem):
    ndp = gm_ref.shape[1]
    slots = ([(ga_ref, 0, n, ain_h.at[n]) for n in range(3)] + [(ga_ref, 1, n, bqkv_h.at[n]) for n in range(3)]
             + [(gm_ref, 0, 0, ain_h.at[3]), (gm_ref, 0, 1, bup_h), (gm_ref, 0, 2, aout_h),
                (gm_ref, 1, 0, adown_h), (gm_ref, 1, 1, bres_h.at[0]), (gm_ref, 1, 2, bres_h.at[1])])
    copies = [pltpu.make_async_copy(ig_in, ig_out, sem.at[len(slots)])]
    copies[0].start()
    for n, (src, c, k, dst) in enumerate(slots):
        out_ref[n] = jnp.zeros(out_ref.shape[1:], F32)

        def add(d, carry):
            e = e_ref[d, 0, 0].astype(jnp.int32)
            out_ref[n, e] += src[c, d, k * 16:(k + 1) * 16, :].astype(F32)
            return carry
        lax.fori_loop(0, ndp, add, 0)
        copies.append(pltpu.make_async_copy(out_ref.at[n], dst, sem.at[n]))
        copies[-1].start()
    for copy in copies:
        copy.wait()


VMEM = pltpu.VMEM
DMA = pltpu.SemaphoreType.DMA
IN_VMEM = pl.BlockSpec(memory_space=pltpu.VMEM)
IN_SMEM = pl.BlockSpec(memory_space=pltpu.SMEM)
IN_ANY = pl.BlockSpec(memory_space=pl.ANY)


def shape(*dims, dtype=BF16):
    return jax.ShapeDtypeStruct(dims, dtype)


def params(cid=None, limit=60 << 20):
    if cid is None:
        return pltpu.CompilerParams(vmem_limit_bytes=limit)
    return pltpu.CompilerParams(collective_id=cid, has_side_effects=True, vmem_limit_bytes=limit)


def local(
    inputs, cotangent, adapter_choice_per_tree, segment_lengths, segment_parents, norm_gain_rows, query_dimension_scale,
    attention_weights, output_weight, feedforward_weights, adapter_first_input, adapter_second_attention, adapter_second_up,
    adapter_first_output, adapter_first_down, adapter_second_residual,
):
    ndp, nt = lax.axis_size("dp"), lax.axis_size("tensor")
    tok, width = inputs.shape
    tree = tok * nt
    wrows, hcols = output_weight.shape
    heads = hcols // HD
    pad = heads * 128
    rank = adapter_first_input.shape[3]
    nblk = tree // BLK
    a_in, a_out, a_down = (jnp.swapaxes(table, -1, -2) for table in (adapter_first_input, adapter_first_output, adapter_first_down))

    chunks = 4
    count = a_in.shape[1]
    wr = wrows * 3
    tall = (heads, tree, 128)
    wall, choices, mixed, xn, q, qt, k, kt, v, ranks, mixt, wp, bp, at_qkv, scale = pl.pallas_call(
        functools.partial(forward_kernel, ndp, chunks),
        out_shape=[shape(ndp, nt, wr, hcols), shape(ndp, 8, 128, dtype=F32), shape(nt, tok, hcols), shape(tree, width),
                   shape(*tall), shape(heads, 128, tree), shape(*tall), shape(heads, HD, tree), shape(*tall),
                   shape(tree, 3 * rank), shape(hcols, tree), shape(3, width, pad), shape(3, 3 * rank, pad), shape(3 * rank, width),
                   shape(1, pad, dtype=F32)],
        in_specs=[IN_SMEM] * 3 + [IN_VMEM] * 3 + [IN_ANY] * 5, out_specs=[IN_ANY] * 15,
        scratch_shapes=[VMEM((3, count, rank, width), BF16), VMEM((3, count, rank, width), BF16), VMEM((8, 128), F32), VMEM((3 * rank, width), BF16),
                        VMEM((1, pad), F32), VMEM((8, 128), F32), VMEM((128, 128), BF16), VMEM((pad, width), BF16),
                        VMEM((3, wrows, hcols), BF16), VMEM((wr, hcols), BF16), VMEM((tree, width), BF16), VMEM((ndp, 3, wrows, hcols), BF16),
                        VMEM((3, width, pad), BF16), VMEM((3, 3 * rank, pad), BF16), VMEM(tall, BF16), VMEM((heads, 128, tree), BF16),
                        VMEM(tall, BF16), VMEM((heads, HD, tree), BF16), VMEM(tall, BF16), VMEM((heads, HD + 16, tree), BF16),
                        VMEM((tree, 3 * rank), BF16), VMEM((hcols, tree), BF16), VMEM((tree, hcols), BF16),
                        VMEM((heads, 1, BLK), F32), VMEM((heads, HD + 16, BLK), F32), DMA((5,)), DMA((12,)),
                        DMA((3, chunks)), DMA((nt, chunks)), DMA((3, ndp, 3)), DMA((ndp, 3)), DMA((3, ndp)), DMA((ndp,)),
                        DMA((2, ndp, nt, 4)), DMA((2,)), DMA((2, ndp, nt)), DMA((nblk,)), DMA((nt, tok // BLK))],
        compiler_params=params(1), name="forward",
    )(adapter_choice_per_tree, segment_lengths, segment_parents, inputs, norm_gain_rows, query_dimension_scale[None, :], a_in,
      adapter_second_attention, attention_weights, output_weight,
      feedforward_weights.reshape(2 * wrows, hcols))

    output, d_mid, d_mix, g_mid = pl.pallas_call(
        mid_kernel,
        out_shape=[shape(tok, width), shape(tok, width, dtype=F32), shape(nt, tok, hcols), shape(6, rank, width, dtype=F32)],
        in_specs=[IN_SMEM] + [IN_VMEM] * 4 + [IN_ANY] * 6, out_specs=[IN_VMEM] * 4,
        scratch_shapes=[VMEM((3, rank, width), BF16), VMEM((3, rank, width), BF16), DMA((6,)), VMEM((tok, width), BF16), VMEM((tok, width), F32), VMEM((tok, width), BF16), VMEM((tok, width), F32),
                        VMEM((tok, width), BF16), VMEM((tok, width), F32), VMEM((tok, width), BF16), VMEM((3, width, width), BF16)]
        + [VMEM((ndp, nt, wrows, hcols), BF16)] * 3 + [DMA((3,))],
        compiler_params=params(), name="middle",
    )(adapter_choice_per_tree, inputs, cotangent, mixed, norm_gain_rows, wall, a_out, a_in, a_down, adapter_second_up, adapter_second_residual)
    gr = 6 * rank
    half_rows = gr // 2
    half, hb, per = nblk // 2, BLK // 2, tok // BLK
    grad_bufs = [VMEM((2, half_rows, width), BF16), VMEM((2, half_rows, width), BF16), VMEM((half_rows, width), BF16), VMEM((half_rows, width), BF16)]
    grad_sems = [DMA((2,)), DMA((2,)), DMA((3, ndp)), DMA((ndp,)), DMA((ndp,)), DMA((ndp,)), DMA((1,))]
    input_grad, grads_mid, grads_attn = pl.pallas_call(
        functools.partial(back_kernel, ndp),
        out_shape=[shape(tok, width, dtype=F32), shape(2, ndp, half_rows, width), shape(2, ndp, half_rows, width)],
        in_specs=[IN_ANY] * 12 + [IN_VMEM] * 5, out_specs=[IN_ANY] * 3,
        scratch_shapes=[VMEM((hcols, tree), BF16), VMEM(tall, BF16), VMEM((heads, 128, tree), BF16), VMEM(tall, BF16), VMEM((heads, HD, tree), BF16),
                        VMEM(tall, BF16), VMEM((3, width, pad), BF16), VMEM((tree, width), BF16), VMEM((tree, 3 * rank), BF16),
                        VMEM((tok, width), BF16), VMEM((tok, width), F32), VMEM((tree, hcols), BF16), VMEM(tall, BF16), VMEM((heads, 128, tree), BF16),
                        VMEM((heads, HD, tree), F32), VMEM(tall, F32), VMEM(tall, F32), VMEM((nblk, BLK, width), BF16), VMEM((half, hb, width), BF16),
                        VMEM((half, hb, width), BF16), VMEM((per, BLK, width), BF16), VMEM((per, BLK, width), BF16),
                        VMEM((3 * rank, width), F32), VMEM((3, 3 * rank, pad), F32), VMEM((pad, width), BF16)]
        + grad_bufs + grad_bufs + [DMA((11,)), DMA((4,)), DMA((nt,)), DMA((half,)), DMA((half,)), DMA((half,)), DMA((per, 2)), DMA((per,)), DMA((per,)), DMA((1,))]
        + grad_sems + grad_sems,
        compiler_params=params(4, 62 << 20), name="back",
    )(d_mix, mixt, q, qt, k, kt, v, wp, xn, ranks, inputs, d_mid, scale, bp, at_qkv, norm_gain_rows, g_mid.reshape(gr, width))

    table = shape(count, rank, width, dtype=F32)
    ga_in, gb_qkv, gb_up, ga_out, ga_down, gb_res, input_grad = pl.pallas_call(
        place_kernel,
        out_shape=[shape(4, count, rank, width, dtype=F32), shape(3, count, rank, width, dtype=F32), table, table, table,
                   shape(2, count, rank, width, dtype=F32), shape(tok, width, dtype=F32)],
        in_specs=[IN_SMEM] + [IN_VMEM] * 2 + [IN_ANY], out_specs=[IN_ANY] * 7,
        scratch_shapes=[VMEM((12, count, rank, width), F32), DMA((13,))], compiler_params=params(), name="place",
    )(choices, grads_mid, grads_attn, input_grad)
    return (output, input_grad, jnp.swapaxes(ga_in, 2, 3), gb_qkv, gb_up, jnp.swapaxes(ga_out, 1, 2), jnp.swapaxes(ga_down, 1, 2), gb_res)


def solution(mesh):
    tokens, weights = P(("dp", "tensor"), None), P(None, "dp", "tensor")
    in_specs = (tokens, tokens, P("dp"), P("dp", None), P("dp", None), P(), P(), weights, P("dp", "tensor"), weights) + (P(),) * 6
    out_specs = (tokens, tokens) + (P(),) * 6
    return jax.shard_map(local, mesh=mesh, in_specs=in_specs, out_specs=out_specs, check_vma=False)
```

```python
import functools
import math

import jax
import jax.numpy as jnp
from jax import lax
from jax.experimental import pallas as pl
from jax.experimental.pallas import tpu as pltpu
from jax.sharding import PartitionSpec as P

F32, BF16 = jnp.float32, jnp.bfloat16
BIG = 1e30
BLK = 256
HD = 80

def dot(a, b):
    return lax.dot_general(a, b, (((1,), (0,)), ((), ())), preferred_element_type=F32)
def dot_nt(a, b):
    return lax.dot_general(a, b, (((1,), (1,)), ((), ())), preferred_element_type=F32)
def dot_tn(a, b):
    return lax.dot_general(a, b, (((0,), (0,)), ((), ())), preferred_element_type=F32)

def project(b, s, x_ref, wp_ref, a_ref, bp_ref, scale_ref, seg_ref, mq_ref, n_ref, t_ref, rank_ref):
    rows = pl.ds(pl.multiple_of(b * BLK, BLK), BLK)
    xb = x_ref[rows, :]
    if s == 0:
        rank_ref[rows, :] = dot_nt(xb, a_ref[...]).astype(BF16)
    lane = lax.broadcasted_iota(jnp.int32, (BLK, 128), 1)
    if s == 2:
        feat = jnp.where(lane < HD + 2, 1.0, 0.0)
    else:
        tok = (lax.broadcasted_iota(jnp.int32, (BLK, 128), 0) + b * BLK).astype(F32)
        feat = jnp.where((tok >= seg_ref[0:1, :]) & (tok < seg_ref[1:2, :]), 1.0, 0.0)
        if s == 0:
            feat = dot(feat.astype(BF16), mq_ref[...])
        else:
            feat = jnp.where((lane >= HD + 13) & (lane < HD + 16), 1.0, feat)
    y = dot(xb, wp_ref[s]) + dot(rank_ref[rows, :], bp_ref[s])
    if s == 0:
        y = y * scale_ref[...]
    for h in range(n_ref.shape[0]):
        yh = jnp.where(lane < HD, y[:, h * 128:(h + 1) * 128], feat)
        n_ref[h, rows, :] = yh.astype(BF16)
        t_ref[h, :, rows] = yh.T[:t_ref.shape[1]].astype(BF16)

def attend_block(i, qt_ref, k_ref, vt_ref, m_ref, acc_ref, mixt_ref, mix_ref, count=None, jlist=None):
    heads = qt_ref.shape[0]
    cols = pl.ds(pl.multiple_of(i * BLK, BLK), BLK)
    m_ref[...] = jnp.full_like(m_ref, -3e38)
    acc_ref[...] = jnp.zeros_like(acc_ref)
    def step(j, diag):
        rows = pl.ds(pl.multiple_of(j * BLK, BLK), BLK)
        hs = range(heads)
        ss = [dot(k_ref[h, rows, :], qt_ref[h, :, cols]) for h in hs]
        if diag:
            low = lax.broadcasted_iota(jnp.int32, ss[0].shape, 0) <= lax.broadcasted_iota(jnp.int32, ss[0].shape, 1)
            ss = [jnp.where(low, s, -BIG) for s in ss]
        olds = [m_ref[h] for h in hs]
        news = [jnp.maximum(olds[h], jnp.max(ss[h], axis=0, keepdims=True)) for h in hs]
        ps = [jnp.exp(ss[h] - news[h]).astype(BF16) for h in hs]
        pv = [dot(vt_ref[h, :, rows], ps[h]) for h in hs]
        accs = [acc_ref[h] * jnp.exp(olds[h] - news[h]) + pv[h] for h in hs]
        for h in hs:
            acc_ref[h] = accs[h]
            m_ref[h] = news[h]
    if jlist is None:
        lax.fori_loop(0, i, lambda j, c: (step(j, False), c)[1], 0)
    else:
        lax.fori_loop(0, count, lambda n, c: (step(jlist(n), False), c)[1], 0)
    step(i, True)
    outs = []
    for h in range(heads):
        acc = acc_ref[h]
        l = acc[HD:HD + 1]
        o = acc[:HD] * (1.0 / l)
        lse = m_ref[h] + jnp.log(l)
        hi = (-lse).astype(BF16).astype(F32)
        mid = (-lse - hi).astype(BF16).astype(F32)
        lo = -lse - hi - mid
        r = lax.broadcasted_iota(jnp.int32, (16, BLK), 0)
        old = qt_ref[h, HD:HD + 16, cols].astype(F32)
        new = jnp.where(r == 13, hi, jnp.where(r == 14, mid, jnp.where(r == 15, lo, old)))
        qt_ref[h, HD:HD + 16, cols] = new.astype(BF16)
        outs.append(o)
    ot = jnp.concatenate(outs, axis=0)
    mixt_ref[:, cols] = ot.astype(BF16)
    mix_ref[cols, :] = ot.T.astype(BF16)

def row_parts(rows):
    return 2 if rows % 32 == 0 else 1

def third_lanes(j, part, c):
    return (j >> 6) == (part + c) % 2, (j & 63) + 256 * (1 - c)

def pack_block(block, c, store):
    rows, cols = block.shape
    parts = row_parts(rows)
    size = rows // parts
    src = lax.broadcasted_iota(jnp.int32, (cols, 256), 0)
    dst = lax.broadcasted_iota(jnp.int32, (cols, 256), 1)
    full = dot(block, jnp.where(src == dst + 64 * c, 1.0, 0.0).astype(BF16)).astype(BF16)
    rest = jnp.zeros((size, 128), F32)
    for r in range(parts):
        store(r, full[r * size:(r + 1) * size, :128])
        store(parts + r, full[r * size:(r + 1) * size, 128:])
        held, col = third_lanes(dst[:, :128], r, c)
        rest = rest + dot(block[r * size:(r + 1) * size], jnp.where(held & (src[:, :128] == col), 1.0, 0.0).astype(BF16))
    store(2 * parts, rest.astype(BF16))

def spread_heads(c, parts, pad):
    def matrix(k, held, col):
        l = lax.broadcasted_iota(jnp.int32, (k, pad), 1)
        return jnp.where(held & ((l & 127) < HD) & ((l >> 7) * HD + (l & 127) == col), 1.0, 0.0).astype(BF16)
    lane = lax.broadcasted_iota(jnp.int32, (256, 1), 0)
    rest = lax.broadcasted_iota(jnp.int32, (128, 1), 0)
    return matrix(256, lane >= 0, lane + 64 * c), [matrix(128, *third_lanes(rest, r, c)) for r in range(parts)]

def head_columns(me, pad, width):
    l = lax.broadcasted_iota(jnp.int32, (pad, width), 0)
    col = lax.broadcasted_iota(jnp.int32, (pad, width), 1)
    put = ((l & 127) < HD) & (me.t * (pad // 128 * HD) + (l >> 7) * HD + (l & 127) == col)
    return jnp.where(put, 1.0, 0.0).astype(BF16)

def tree_masks(len_ref, par_ref, seg_ref, mq_ref):
    segs = len_ref.shape[1]
    lane = lax.broadcasted_iota(jnp.int32, (1, 128), 1) - HD
    row = lax.broadcasted_iota(jnp.int32, (128, 1), 0) - HD
    lo = hi = jnp.zeros((1, 128), jnp.int32)
    up = grand = jnp.full((128, 1), -1, jnp.int32)
    start = 0
    for u in range(segs):
        end = start + len_ref[0, u]
        parent = par_ref[0, u]
        lo = jnp.where(lane == u, start, lo)
        hi = jnp.where(lane == u, end, hi)
        up = jnp.where(row == u, parent, up)
        grand = jnp.where(row == u, par_ref[0, parent], grand)
        start = end
    seg_ref[0:1, :] = lo.astype(F32)
    seg_ref[1:2, :] = hi.astype(F32)
    reach = (lane == row) | (lane == up) | (lane == grand)
    inside = (row >= 0) & (row < segs) & (lane >= 0) & (lane < segs)
    mq_ref[...] = jnp.where(inside & jnp.logical_not(reach), -BIG, 0.0).astype(BF16)

def bwd_prep(b, dm_ref, mixt_ref, do_ref, dot_ref):
    rows = pl.ds(pl.multiple_of(b * BLK, BLK), BLK)
    heads = do_ref.shape[0]
    dt = dm_ref[rows, :].astype(F32).T
    prod = dt * mixt_ref[:, rows].astype(F32)
    r = lax.broadcasted_iota(jnp.int32, (16, BLK), 0)
    for h in range(heads):
        d = dt[h * HD:(h + 1) * HD]
        delta = -jnp.sum(prod[h * HD:(h + 1) * HD], axis=0, keepdims=True)
        hi = delta.astype(BF16).astype(F32)
        ext = jnp.where(r == 0, hi, jnp.where(r == 1, delta - hi, 0.0))
        full = jnp.concatenate([d, ext, jnp.zeros((32, BLK), F32)], axis=0)
        dot_ref[h, :, rows] = full.astype(BF16)
        do_ref[h, rows, :] = full.T.astype(BF16)

def bwd_pair(i, j, diag, q_ref, qt_ref, k_ref, kt_ref, v_ref, do_ref, dot_ref, dqt_ref, dk_ref, dv_ref):
    heads = q_ref.shape[0]
    cols = pl.ds(pl.multiple_of(i * BLK, BLK), BLK)
    rows = pl.ds(pl.multiple_of(j * BLK, BLK), BLK)
    hs = range(heads)
    ss = [dot(k_ref[h, rows, :], qt_ref[h, :, cols]) for h in hs]
    dps = [dot(v_ref[h, rows, :], dot_ref[h, :, cols]) for h in hs]
    if diag:
        low = lax.broadcasted_iota(jnp.int32, ss[0].shape, 0) <= lax.broadcasted_iota(jnp.int32, ss[0].shape, 1)
        ss = [jnp.where(low, s, -BIG) for s in ss]
    ps = [jnp.exp(s) for s in ss]
    dss = [(p * dp).astype(BF16) for p, dp in zip(ps, dps)]
    ps = [p.astype(BF16) for p in ps]
    dvs = [dot(ps[h], do_ref[h, cols, :]) for h in hs]
    dks = [dot(dss[h], q_ref[h, cols, :]) for h in hs]
    dqs = [dot(kt_ref[h, :, rows], dss[h]) for h in hs]
    for h in hs:
        dv_ref[h, rows, :] += dvs[h]
        dk_ref[h, rows, :] += dks[h]
        dqt_ref[h, :, cols] += dqs[h]

MESH = pl.DeviceIdType.MESH


class Place:
    def __init__(self, ndp):
        self.d, self.t = lax.axis_index("dp"), lax.axis_index("tensor")
        self.line = ndp // 2
        self.p, self.par = self.d // 2, self.d % 2
        self.dx = self.d + 1 - 2 * self.par
        self.c, self.y = self.t % 2, self.t // 2
        self.t1 = self.t + 1 - 2 * self.c
        self.t2 = (self.t + 2) % 4
        self.t3 = (self.t1 + 2) % 4
        self.has_left, self.has_right = self.p > 0, self.p < self.line - 1


def signal(sem, d, t):
    pl.semaphore_signal(sem, inc=1, device_id=(d, t), device_id_type=MESH)


def remote(src, dst, send_sem, recv_sem, d, t):
    return pltpu.make_async_remote_copy(src_ref=src, dst_ref=dst, send_sem=send_sem, recv_sem=recv_sem, device_id=(d, t), device_id_type=MESH)


def greet(me, tensor=(), pair=False, line=False):
    bar = pltpu.get_barrier_semaphore()
    count = len(tensor) + (1 if pair else 0)
    for t in tensor:
        signal(bar, me.d, t)
    if pair:
        signal(bar, me.dx, me.t)
    if line:
        @pl.when(me.has_left)
        def _():
            signal(bar, me.d - 2, me.t)
        @pl.when(me.has_right)
        def _():
            signal(bar, me.d + 2, me.t)
        count = count + jnp.where(me.has_left, 1, 0) + jnp.where(me.has_right, 1, 0)
    pl.semaphore_wait(bar, count)


class PairLine:
    def __init__(self, me, own, buf, send, recv, part=None):
        self.me, self.own, self.buf, self.send, self.recv, self.part = me, own, buf, send, recv, part

    def slot(self, o):
        return self.buf.at[o] if self.part is None else self.buf.at[o, self.part]

    def copy(self, o, src, d, kind):
        send, recv = (self.send.at[kind, o], self.recv.at[o]) if self.part is None else (self.send.at[kind, o, self.part], self.recv.at[o, self.part])
        return remote(src, self.slot(o), send, recv, d, self.me.t)

    def start(self):
        me = self.me
        @pl.when(me.has_left)
        def _():
            self.copy(me.d, self.own, me.d - 2, 0).start()
        @pl.when(me.has_right)
        def _():
            self.copy(me.d, self.own, me.d + 2, 1).start()
        self.copy(me.d, self.own, me.dx, 2).start()

    def hop(self, k, then=None):
        me = self.me
        @pl.when(me.p - k >= 0)
        def _():
            o = me.d - 2 * k
            self.copy(o, self.slot(o), me.dx, 2).wait_recv()
            @pl.when(me.has_right)
            def _():
                self.copy(o, self.slot(o), me.d + 2, 1).start()
            self.copy(o, self.slot(o), me.dx, 2).start()
            if then is not None:
                then(o)
        @pl.when(me.p + k < me.line)
        def _():
            o = me.d + 2 * k
            self.copy(o, self.slot(o), me.dx, 2).wait_recv()
            @pl.when(me.has_left)
            def _():
                self.copy(o, self.slot(o), me.d - 2, 0).start()
            self.copy(o, self.slot(o), me.dx, 2).start()
            if then is not None:
                then(o)

    def pair_arrivals(self, then=None):
        def one(q, c):
            o = 2 * q + 1 - self.me.par
            self.copy(o, self.slot(o), self.me.dx, 2).wait_recv()
            if then is not None:
                then(o)
            return c
        lax.fori_loop(0, self.me.line, one, 0)

    def sent(self):
        me = self.me
        def one(q, c):
            o = 2 * q + me.par
            self.copy(o, self.slot(o), me.dx, 2).wait_send()
            @pl.when((q >= me.p) & me.has_left)
            def _():
                self.copy(o, self.slot(o), me.dx, 0).wait_send()
            @pl.when((q <= me.p) & me.has_right)
            def _():
                self.copy(o, self.slot(o), me.dx, 1).wait_send()
            return c
        lax.fori_loop(0, me.line, one, 0)


class FullGather:
    def __init__(self, me, own, buf, send, first, recv):
        self.me, self.own, self.buf, self.send, self.first, self.recv = me, own, buf, send, first, recv
        cut = own.shape[0] // 3
        self.parts = (pl.ds(0, cut), pl.ds(cut, own.shape[0] - cut))

    def copy(self, h, o, t, d2, t2, kind, own=False):
        rows = self.parts[h]
        src = self.own.at[rows] if own else self.buf.at[o, t, rows]
        sem = self.first.at[h] if kind == 4 else self.send.at[h, o, t, kind]
        return remote(src, self.buf.at[o, t, rows], sem, self.recv.at[h, o, t], d2, t2)

    def last(self, h):
        me = self.me
        return (me.d, me.t2) if h == 0 else (me.dx, me.t)

    def spread(self, h, o, t, left, right, own=False):
        me = self.me
        @pl.when(left)
        def _():
            self.copy(h, o, t, me.d - 2, me.t, 0, own).start()
        @pl.when(right)
        def _():
            self.copy(h, o, t, me.d + 2, me.t, 1, own).start()
        self.copy(h, o, t, *self.last(h), 2, own).start()
        self.copy(h, o, t, me.d, me.t1, 3, own).start()

    def start(self):
        me = self.me
        self.copy(0, me.d, me.t, me.dx, me.t, 4, True).start()
        self.copy(1, me.d, me.t, me.d, me.t2, 4, True).start()
        for h in (1, 0):
            self.spread(h, me.d, me.t, me.has_left, me.has_right, True)

    def arrived(self, h, o, t):
        self.copy(h, o, t, self.me.d, self.me.t1, 3).wait_recv()

    def firsts(self):
        me = self.me
        self.arrived(0, me.dx, me.t)
        self.spread(0, me.dx, me.t, me.has_left, me.has_right)
        self.arrived(1, me.d, me.t2)
        self.spread(1, me.d, me.t2, me.has_left, me.has_right)

    def streams(self, q):
        me = self.me
        return ((0, 2 * q + me.par, me.t), (0, 2 * q + 1 - me.par, me.t), (1, 2 * q + me.par, me.t), (1, 2 * q + me.par, me.t2))

    def hop(self, k):
        me = self.me
        @pl.when(me.p - k >= 0)
        def _():
            for h, o, t in self.streams(me.p - k):
                self.arrived(h, o, t)
                self.spread(h, o, t, False, me.has_right)
        @pl.when(me.p + k < me.line)
        def _():
            for h, o, t in self.streams(me.p + k):
                self.arrived(h, o, t)
                self.spread(h, o, t, me.has_left, False)

    def lasts(self, k):
        me = self.me

        def place(q):
            for h, o, t in ((0, 2 * q, me.t2), (0, 2 * q + 1, me.t2), (1, 2 * q + 1 - me.par, me.t), (1, 2 * q + 1 - me.par, me.t2)):
                self.arrived(h, o, t)
                self.copy(h, o, t, me.d, me.t1, 3).start()

        @pl.when(me.p - k >= 0)
        def _():
            place(me.p - k)
        @pl.when((me.p + k < me.line) & (k > 0))
        def _():
            place(me.p + k)

    def finish(self):
        me = self.me
        def one(o, c):
            for h in range(2):
                self.arrived(h, o, me.t1)
                self.arrived(h, o, me.t3)
                for t in (me.t, me.t2):
                    self.copy(h, o, t, me.d, me.t1, 3).wait_send()
            return c
        lax.fori_loop(0, 2 * me.line, one, 0)
        def two(q, c):
            for h, o, t in self.streams(q):
                self.copy(h, o, t, me.d, me.t1, 2).wait_send()
                @pl.when((q >= me.p) & me.has_left)
                def _():
                    self.copy(h, o, t, me.d, me.t1, 0).wait_send()
                @pl.when((q <= me.p) & me.has_right)
                def _():
                    self.copy(h, o, t, me.d, me.t1, 1).wait_send()
            return c
        lax.fori_loop(0, me.line, two, 0)
        for h in range(2):
            self.copy(h, me.d, me.t, me.d, me.t1, 4).wait_send()


EPS = 1e-6


def forward_kernel(ndp, chunks, choice_in, len_ref, par_ref, x_ref, gain_ref, qs_ref, ain_h, btab_h, a_ref, wo_ref, wf_ref,
                   wout_ref, cho_ref, mixed_ref, xno_ref, qo_ref, qto_ref, ko_ref, kto_ref, vo_ref, ranko_ref, mixto_ref, wpo_ref, bpo_ref, ato_ref, scaleo_ref,
                   ain_ref, btab_ref, choice_ref, at_ref, scale_ref, seg_ref, mq_ref, put_ref,
                   araw_ref, wraw_ref, aown_ref, wown_ref, xn_ref, wa_ref, wp_ref, bp_ref, q_ref, qt_ref, k_ref, kt_ref, v_ref, vt_ref, rank_ref, mixt_ref,
                   mix_ref, m_ref, acc_ref, ls, os, xs, xr, a_s, a_r, c_s, c_r, w_s, w_f, w_r, ms, mr):
    me = Place(ndp)
    tok, width = x_ref.shape
    loads = [pltpu.make_async_copy(a_ref, araw_ref, ls.at[0]), pltpu.make_async_copy(wo_ref, wraw_ref.at[0], ls.at[1]),
             pltpu.make_async_copy(wf_ref, wraw_ref.at[pl.ds(1, 2)], ls.at[2])]
    tables = [pltpu.make_async_copy(ain_h.at[pl.ds(0, 3)], ain_ref, ls.at[3]), pltpu.make_async_copy(btab_h, btab_ref, ls.at[4])]
    for copy in loads + tables:
        copy.start()
    e = choice_in[0]
    choice_ref[...] = jnp.zeros_like(choice_ref) + e.astype(F32)
    x = x_ref[...].astype(F32)
    mine = pl.ds(pl.multiple_of(me.t * tok, tok), tok)
    xn_ref[mine, :] = (x * lax.rsqrt(jnp.mean(x * x, axis=-1, keepdims=True) + EPS) * gain_ref[0:1, :]).astype(BF16)
    greet(me, tensor=(me.t1, me.t2, me.t3), pair=True, line=True)
    size = tok // chunks

    def xcopy(o, c, t, kind):
        rows = pl.ds(pl.multiple_of(o * tok + c * size, size), size)
        return remote(xn_ref.at[rows], xn_ref.at[rows], xs.at[kind, c], xr.at[o, c], me.d, t)

    for c in range(chunks):
        xcopy(me.t, c, me.t2, 0).start()
    for c in range(chunks):
        xcopy(me.t, c, me.t1, 1).start()
    for copy in loads:
        copy.wait()
    pieces = aown_ref.shape[1]

    def pack(raw_ref, own_ref, n, index):
        def store(k, v):
            own_ref[index(n, k)] = v
        pack_block(raw_ref[n], me.c, store)
    for n in range(3):
        pack(araw_ref, aown_ref, n, lambda n, k: (n, k))
    parts = [PairLine(me, aown_ref.at[n], wa_ref, a_s, a_r, n) for n in range(3)]
    ch = PairLine(me, choice_ref, cho_ref, c_s, c_r)
    w = FullGather(me, wown_ref, wout_ref, w_s, w_f, w_r)
    parts[0].start()
    parts[1].start()
    for n in range(3):
        pack(wraw_ref, wown_ref, n, lambda n, k: n * pieces + k)
    keep = [pltpu.make_async_copy(wown_ref, wout_ref.at[me.d, me.t], ls.at[0]), pltpu.make_async_copy(choice_ref, cho_ref.at[me.d], ls.at[1])]
    for copy in keep:
        copy.start()
    wa_ref[me.d] = aown_ref[...]
    tree_masks(len_ref, par_ref, seg_ref, mq_ref)
    scale_ref[...] = jnp.zeros_like(scale_ref)
    for h in range(q_ref.shape[0]):
        scale_ref[:, h * 128:h * 128 + HD] = qs_ref[...] * (1.0 / math.sqrt(HD))
    put_ref[...] = head_columns(me, *put_ref.shape)
    for copy in tables:
        copy.wait()
    parts[0].hop(1)
    parts[2].start()
    ch.start()

    def diagonal(n, carry):
        for part in range(3):
            k = n - part
            @pl.when((k >= 1) & (k < me.line))
            def _():
                parts[part].hop(k)
        return carry
    lax.fori_loop(2, me.line + 2, diagonal, 0)
    w.start()
    n16 = ain_ref.shape[2]
    for s in range(3):
        at_ref[s * n16:(s + 1) * n16] = ain_ref[s, e]
    picked = jnp.concatenate([btab_ref[s, e] for s in range(3)], axis=0)
    spread = (0.5 * dot_nt(picked, put_ref[...])).astype(BF16)
    bp_ref[...] = jnp.zeros_like(bp_ref)
    for s in range(3):
        bp_ref[s, s * n16:(s + 1) * n16] = spread[s * n16:(s + 1) * n16]

    def forward(c):
        xcopy(me.t2, c, me.t1, 2).wait_recv()
        xcopy(me.t2, c, me.t1, 2).start()

    for c in range(chunks // 2):
        forward(c)
    nblk = xn_ref.shape[0] // BLK
    near = nblk // 2
    half_rows = wa_ref.shape[3]
    sides = pieces // 2
    wrows = half_rows * sides
    sel, sel_rest = spread_heads(me.c, sides, wp_ref.shape[2])

    def spread_weights(s):
        if sides == 1:
            group = 16 // math.gcd(wrows, 16)
            for o in range(0, ndp, group):
                wp_ref[s, o * wrows:(o + group) * wrows] = jnp.concatenate([
                    dot(jnp.concatenate([wa_ref[o + j, s, 0], wa_ref[o + j, s, 1]], axis=1), sel) + dot(wa_ref[o + j, s, 2], sel_rest[0])
                    for j in range(group)], axis=0).astype(BF16)
            return
        flat = [wa_ref[:, s, k].reshape(ndp * half_rows, 128) for k in range(pieces)]
        for r in range(sides):
            y = (dot(jnp.concatenate([flat[r], flat[sides + r]], axis=1), sel) + dot(flat[2 * sides], sel_rest[r])).astype(BF16)
            for o in range(ndp):
                wp_ref[s, o * wrows + r * half_rows:o * wrows + (r + 1) * half_rows] = y[o * half_rows:(o + 1) * half_rows]

    def project_blocks(first, s):
        n_ref, t_ref = ((q_ref, qt_ref), (k_ref, kt_ref), (v_ref, vt_ref))[s]
        lax.fori_loop(0, near, lambda n, c: (project(first + n, s, xn_ref, wp_ref, at_ref, bp_ref, scale_ref, seg_ref, mq_ref, n_ref, t_ref, rank_ref), c)[1], 0)

    for c in range(chunks):
        xcopy(me.t1, c, me.t1, 2).wait_recv()
    for s in range(3):
        parts[s].pair_arrivals()
        spread_weights(s)
        project_blocks(me.y * near, s)
        if s < 2:
            forward(chunks // 2 + s)
    for c in range(chunks):
        xcopy(me.t3, c, me.t1, 2).wait_recv()
    w.firsts()
    for s in range(3):
        project_blocks((1 - me.y) * near, s)

    def hops(i):
        done = 1 + jnp.maximum((me.line - 2) * (i + 1) * (i + 2) + 2 * nblk, 0) // ((nblk - 1) * nblk)
        return jnp.minimum(done, me.line - 1)

    def relay(i):
        lax.fori_loop(hops(i - 1), hops(i), lambda k, c: (w.hop(k + 1), ch.hop(k + 1), c)[2], 0)
    w.hop(1)
    ch.hop(1)
    outs = [pltpu.make_async_copy(src, dst, os.at[n]) for n, (src, dst) in enumerate((
        (xn_ref, xno_ref), (q_ref, qo_ref), (k_ref, ko_ref), (kt_ref, kto_ref), (v_ref, vo_ref), (rank_ref, ranko_ref),
        (wp_ref, wpo_ref), (bp_ref, bpo_ref), (at_ref, ato_ref), (scale_ref, scaleo_ref)))]
    for copy in outs:
        copy.start()
    per = tok // BLK

    def piece(i):
        rows = pl.ds(pl.multiple_of(i * BLK, BLK), BLK)
        return mix_ref.at[rows], mixed_ref.at[me.t, pl.ds(pl.multiple_of((i % per) * BLK, BLK), BLK)], i // per

    def attend_step(i, c):
        attend_block(i, qt_ref, k_ref, vt_ref, m_ref, acc_ref, mixt_ref, mix_ref)
        src, dst, t = piece(i)
        @pl.when(t == me.t)
        def _():
            pltpu.make_async_copy(src, dst, ms.at[i]).start()
        @pl.when(t != me.t)
        def _():
            remote(src, dst, ms.at[i], mr.at[me.t, i % per], me.d, t).start()
        relay(i)
        lax.fori_loop(jnp.where(i == 0, 0, hops(i - 2)), hops(i - 1), lambda k, n: (w.lasts(k), n)[1], 0)
        return c
    lax.fori_loop(0, nblk, attend_step, 0)
    late = [pltpu.make_async_copy(qt_ref, qto_ref, os.at[len(outs)]), pltpu.make_async_copy(mixt_ref, mixto_ref, os.at[len(outs) + 1])]
    for copy in late:
        copy.start()
    lax.fori_loop(hops(nblk - 2), me.line, lambda k, c: (w.lasts(k), c)[1], 0)
    ch.pair_arrivals()
    for t in (me.t1, me.t2, me.t3):
        for h in range(per):
            dst = mixed_ref.at[t, pl.ds(h * BLK, BLK)]
            remote(dst, dst, ms.at[0], mr.at[t, h], me.d, t).wait_recv()
    w.finish()
    for part in parts:
        part.sent()
    ch.sent()
    for c in range(chunks):
        for kind in range(3):
            xcopy(me.t, c, me.t1, kind).wait_send()

    def settle(i, c):
        src, dst, t = piece(i)
        @pl.when(t == me.t)
        def _():
            pltpu.make_async_copy(src, dst, ms.at[i]).wait()
        @pl.when(t != me.t)
        def _():
            remote(src, dst, ms.at[i], mr.at[me.t, i % per], me.d, t).wait_send()
        return c
    lax.fori_loop(0, nblk, settle, 0)
    for copy in keep + outs + late:
        copy.wait()


def sigmoid(v):
    return 1.0 / (1.0 + jnp.exp(-v))


def mid_kernel(e_ref, x_ref, g_ref, mix4_ref, gain_ref, wall_ref, aout_h, ain_h, adown_h, bup_h, bres_h, out_ref, dmid_ref, dmix_ref, grads_ref,
               at_ref, b_ref, ts, mix_ref, mid_ref, hid_ref, up_ref, act_ref, f_ref, low_ref, w_ref, wb0_ref, wb1_ref, wb2_ref, ls):
    width = x_ref.shape[1]
    step = 256
    part = mix4_ref.shape[2]
    blocks = (wb0_ref, wb1_ref, wb2_ref)
    ndp, nt, pieces, size = wb0_ref.shape[:4]
    sides = pieces // 2
    loads = [pltpu.make_async_copy(wall_ref.at[:, :, pl.ds(n * pieces, pieces)], blocks[n], ls.at[n]) for n in range(3)]
    e = e_ref[0]
    tables = [pltpu.make_async_copy(src, dst, ts.at[n]) for n, (src, dst) in enumerate((
        (aout_h.at[e], at_ref.at[0]), (ain_h.at[3, e], at_ref.at[1]), (adown_h.at[e], at_ref.at[2]),
        (bres_h.at[0, e], b_ref.at[0]), (bup_h.at[e], b_ref.at[1]), (bres_h.at[1, e], b_ref.at[2])))]
    for copy in tables + loads:
        copy.start()
    for copy in tables:
        copy.wait()

    def assemble(n):
        loads[n].wait()
        low_lane = lax.broadcasted_iota(jnp.int32, (size, 128), 1) < 64

        def block(o, y, even, odd):
            for r in range(sides):
                rows = pl.ds((o * sides + r) * size, size)
                base = 2 * part * y
                w_ref[n, rows, base:base + 128] = even[r]
                w_ref[n, rows, base + 128:base + 256] = even[sides + r]
                first, second = (even, odd) if r == 0 else (odd, even)
                both = jnp.where(low_lane, first[2 * sides].astype(F32), second[2 * sides].astype(F32))
                w_ref[n, rows, base + 256:base + 384] = (both if r == 0 else pltpu.roll(both, 64, 1)).astype(BF16)
                w_ref[n, rows, base + 384:base + 512] = odd[r]
                w_ref[n, rows, base + 512:base + 640] = odd[sides + r]
        for o in range(ndp):
            for y in range(nt // 2):
                block(o, y, blocks[n].at[o, 2 * y], blocks[n].at[o, 2 * y + 1])

    for t in range(mix4_ref.shape[0]):
        mix_ref[:, t * part:(t + 1) * part] = mix4_ref[t]

    def cols(n):
        return pl.ds(pl.multiple_of(n * step, step), step)

    def each(fn):
        lax.fori_loop(0, width // step, lambda n, c: (fn(cols(n)), c)[1], 0)

    gain = gain_ref[1:2, :]
    r_out = dot_nt(mix_ref[...], at_ref[0]).astype(BF16)
    assemble(0)

    def project_out(n):
        attn = dot_nt(mix_ref[...], w_ref[0, n, :]) + 0.5 * dot(r_out, b_ref[0, :, n])
        mid_ref[:, n] = x_ref[:, n].astype(F32) + attn
    each(project_out)
    middle = mid_ref[...]
    r = lax.rsqrt(jnp.mean(middle * middle, axis=-1, keepdims=True) + EPS)
    hid_ref[...] = (middle * r * gain).astype(BF16)
    r_up = dot_nt(hid_ref[...], at_ref[1]).astype(BF16)
    assemble(1)

    def up_step(n):
        up = dot(hid_ref[...], w_ref[1, :, n]) + 0.5 * dot(r_up, b_ref[1, :, n])
        up_ref[:, n] = up
        act_ref[:, n] = (up * sigmoid(up)).astype(BF16)
    each(up_step)
    r_down = dot_nt(act_ref[...], at_ref[2]).astype(BF16)
    assemble(2)

    def down_step(n):
        down = dot_nt(act_ref[...], w_ref[2, n, :]) + 0.5 * dot(r_down, b_ref[2, :, n])
        out_ref[:, n] = (mid_ref[:, n] + down).astype(BF16)
    each(down_step)
    grads_ref[5] = 0.5 * dot_tn(r_down, g_ref[...])
    dz_down = (0.5 * dot_nt(g_ref[...], b_ref[2])).astype(BF16)
    grads_ref[3] = dot_tn(dz_down, act_ref[...])

    def act_back(n):
        d_act = dot(g_ref[...], w_ref[2, :, n]) + dot(dz_down, at_ref[2, :, n])
        up = up_ref[:, n]
        sg = sigmoid(up)
        low_ref[:, n] = (d_act * sg * (1.0 + up * (1.0 - sg))).astype(BF16)
    each(act_back)
    dz_up = (0.5 * dot_nt(low_ref[...], b_ref[1])).astype(BF16)
    grads_ref[1] = 0.5 * dot_tn(r_up, low_ref[...])
    grads_ref[0] = dot_tn(dz_up, hid_ref[...])

    def hidden_back(n):
        f_ref[:, n] = (dot_nt(low_ref[...], w_ref[1, n, :]) + dot(dz_up, at_ref[1, :, n])) * gain_ref[1:2, n]
    each(hidden_back)
    gd = f_ref[...]
    middle = mid_ref[...]
    s = jnp.mean(middle * gd, axis=-1, keepdims=True)
    d_mid = g_ref[...].astype(F32) + r * gd - middle * (r * r * r * s)
    dmid_ref[...] = d_mid
    low_ref[...] = d_mid.astype(BF16)
    dz_out = (0.5 * dot_nt(low_ref[...], b_ref[0])).astype(BF16)
    grads_ref[4] = 0.5 * dot_tn(r_out, low_ref[...])
    grads_ref[2] = dot_tn(dz_out, mix_ref[...])

    def mixed_back(n):
        act_ref[:, n] = (dot(low_ref[...], w_ref[0, :, n]) + dot(dz_out, at_ref[0, :, n])).astype(BF16)
    each(mixed_back)
    for t in range(dmix_ref.shape[0]):
        dmix_ref[t] = act_ref[:, t * part:(t + 1) * part]


class GradSum:
    def __init__(self, me, gp, gr, g2, own, out, s, r, ls_, lr, fs, fr, keep):
        self.me, self.gp, self.gr, self.g2, self.own, self.out, self.s, self.r, self.fs, self.fr = me, gp, gr, g2, own, out, s, r, fs, fr
        self.line = PairLine(me, own, out.at[me.c], ls_, lr)
        self.keep = pltpu.make_async_copy(own, out.at[me.c, me.d], keep)

    def one(self):
        return remote(self.gp.at[1 - self.me.c], self.gr.at[0], self.s.at[0], self.r.at[0], self.me.d, self.me.t1)

    def two(self):
        return remote(self.g2, self.gr.at[1], self.s.at[1], self.r.at[1], self.me.d, self.me.t2)

    def second(self):
        self.one().wait_recv()
        self.g2[...] = (self.gp[self.me.c].astype(F32) + self.gr[0].astype(F32)).astype(BF16)
        self.two().start()

    def relay(self, o, own=False):
        src = self.own if own else self.out.at[self.me.c, o]
        return remote(src, self.out.at[self.me.c, o], self.fs.at[o], self.fr.at[o], self.me.d, self.me.t1)

    def gather(self):
        self.two().wait_recv()
        self.own[...] = (self.g2[...].astype(F32) + self.gr[1].astype(F32)).astype(BF16)
        self.line.start()
        self.relay(self.me.d, True).start()
        self.keep.start()

    def hop(self, k):
        self.line.hop(k, lambda o: self.relay(o).start())

    def arrivals(self):
        self.line.pair_arrivals(lambda o: self.relay(o).start())

    def settle(self, ndp):
        def one(o, c):
            self.relay(o, True).wait_send()
            remote(self.own, self.out.at[1 - self.me.c, o], self.fs.at[o], self.fr.at[o], self.me.d, self.me.t1).wait_recv()
            return c
        lax.fori_loop(0, ndp, one, 0)
        self.line.sent()
        self.keep.wait()
        self.one().wait_send()
        self.two().wait_send()


def back_kernel(ndp, dmix_ref, mixt_h, q_h, qt_h, k_h, kt_h, v_h, wp_h, xn_h, rank_h, x_h, dmid_h, scale_ref, bp_ref, at_ref, gain_ref, gmid_ref,
                ig_h, gm_h, ga_h,
                mixt_ref, q_ref, qt_ref, k_ref, kt_ref, v_ref, wp_ref, xn_ref, rank_ref, x_ref, dmid_ref, dm_ref, do_ref, dot_ref,
                dqt_ref, dk_ref, dv_ref, dn_ref, r1_ref, s2_ref, r2_ref, ro_ref, ga_ref, gb_ref, put_ref,
                gpm, grm, g2m, gom, gpa, gra, g2a, goa, lsem, dsem, drecv, es, er, s2s, r2r, ros, ror, igs,
                ms, mr, mls, mlr, mfs, mfr, mk, as_, ar, als, alr, afs, afr, ak):
    me = Place(ndp)
    tok = x_ref.shape[0]
    nblk = dm_ref.shape[0] // BLK
    per, half, hb = tok // BLK, nblk // 2, BLK // 2
    heads = q_ref.shape[0]
    loads = [pltpu.make_async_copy(src, dst, lsem.at[n]) for n, (src, dst) in enumerate((
        (mixt_h, mixt_ref), (q_h, q_ref), (qt_h, qt_ref), (k_h, k_ref), (kt_h, kt_ref), (v_h, v_ref),
        (wp_h, wp_ref), (xn_h, xn_ref), (rank_h, rank_ref), (x_h, x_ref), (dmid_h, dmid_ref)))]
    n48 = gpm.shape[1]
    for c in range(2):
        gpm[c] = gmid_ref[c * n48:(c + 1) * n48].astype(BF16)
    greet(me, tensor=(me.t1, me.t2, me.t3), pair=True, line=True)

    def token_rows(t):
        return pl.ds(pl.multiple_of(t * tok, tok), tok)

    def swap(n, t):
        return remote(dmix_ref.at[t], dm_ref.at[token_rows(me.t)], dsem.at[n], drecv.at[me.t], me.d, t)

    own = pltpu.make_async_copy(dmix_ref.at[me.t], dm_ref.at[token_rows(me.t)], dsem.at[3])
    for n, t in enumerate((me.t3, me.t2, me.t1)):
        swap(n, t).start()
    own.start()
    gm = GradSum(me, gpm, grm, g2m, gom, gm_h, ms, mr, mls, mlr, mfs, mfr, mk.at[0])
    ga = GradSum(me, gpa, gra, g2a, goa, ga_h, as_, ar, als, alr, afs, afr, ak.at[0])
    gm.one().start()
    for copy in loads:
        copy.start()
    for ref in (dqt_ref, dk_ref, dv_ref, ga_ref, gb_ref):
        ref[...] = jnp.zeros_like(ref)
    put_ref[...] = head_columns(me, *put_ref.shape)
    for copy in loads[:6]:
        copy.wait()

    def prep(t):
        lax.fori_loop(t * per, (t + 1) * per, lambda b, c: (bwd_prep(b, dm_ref, mixt_ref, do_ref, dot_ref), c)[1], 0)

    def arrived(t):
        remote(dmix_ref.at[t], dm_ref.at[token_rows(t)], dsem.at[0], drecv.at[t], me.d, t).wait_recv()

    own.wait()
    prep(me.t)
    arrived(me.t1)
    prep(me.t1)
    gm.second()
    arrived(me.t2)
    prep(me.t2)
    arrived(me.t3)
    prep(me.t3)
    for copy in loads[6:]:
        copy.wait()
    args = (q_ref, qt_ref, k_ref, kt_ref, v_ref, do_ref, dot_ref, dqt_ref, dk_ref, dv_ref)
    lane = lax.broadcasted_iota(jnp.int32, (BLK, 128), 1)

    def block(a):
        return (1 - me.y) * (nblk - 1 - a) + me.y * a

    def exchange(a):
        rows = pl.ds(pl.multiple_of((1 - me.c) * hb, hb), hb)
        return remote(dn_ref.at[a, rows], r1_ref.at[a], es.at[a], er.at[a], me.d, me.t1)

    def own_block(a):
        return remote(dn_ref.at[a], ro_ref.at[block(a) % per], ros.at[a % per], ror.at[block(a) % per], me.d, me.t1)

    def mine_rows():
        return pl.ds(pl.multiple_of(me.c * hb, hb), hb)

    def deliver(a):
        b = block(a)
        return remote(s2_ref.at[a], r2_ref.at[b % per, mine_rows()], s2s.at[a], r2r.at[b % per, me.c], me.d, b // per)

    def is_mine(a):
        return block(a) // per == me.t

    def pass_on(a):
        exchange(a).wait_recv()
        s2_ref[a] = (dn_ref[a, mine_rows(), :].astype(F32) + r1_ref[a].astype(F32)).astype(BF16)
        deliver(a).start()

    def final(a):
        rows = pl.ds(pl.multiple_of(block(a) * BLK, BLK), BLK)
        dq, dk, dv = [], [], []
        for h in range(heads):
            g = jnp.concatenate([dqt_ref[h, :, rows], jnp.zeros((48, BLK), F32)], axis=0).T
            dq.append((g * scale_ref[:, h * 128:(h + 1) * 128]).astype(BF16))
            dk.append(jnp.where(lane < HD, dk_ref[h, rows, :], 0.0).astype(BF16))
            dv.append(jnp.where(lane < HD, dv_ref[h, rows, :], 0.0).astype(BF16))
        ds = [jnp.concatenate(g, axis=1) for g in (dq, dk, dv)]
        dz = sum(dot_nt(ds[s], bp_ref[s]) for s in range(3)).astype(BF16)
        dn = sum(dot_nt(ds[s], wp_ref[s]) for s in range(3)) + dot(dz, at_ref[...])
        dn_ref[a] = dn.astype(BF16)
        ga_ref[...] += dot_tn(dz, xn_ref[rows, :])
        for s in range(3):
            gb_ref[s] += dot_tn(rank_ref[rows, :], ds[s])

    def upto(a):
        return 1 + jnp.minimum(a * (me.line - 1) // (nblk - 2), me.line - 1)

    def pairs(a):
        b = block(a)
        bwd_pair(b, b, True, *args)

        def other(n, c):
            bwd_pair(b + me.y * (1 + n), b - (1 - me.y) * (1 + n), False, *args)
            return c
        lax.fori_loop(0, nblk - 1 - a, other, 0)

    def far_step(a, c):
        pairs(a)
        @pl.when(a > 0)
        def _():
            pass_on(a - 1)
        final(a)
        exchange(a).start()
        @pl.when(a == 0)
        def _():
            gm.gather()
        lax.fori_loop(upto(a), upto(a + 1), lambda k, n: (gm.hop(k), n)[1], 0)
        return c
    lax.fori_loop(0, half, far_step, 0)

    def near_step(a, c):
        pairs(a)
        @pl.when(a == half)
        def _():
            pass_on(a - 1)
        final(a)
        @pl.when(jnp.logical_not(is_mine(a)))
        def _():
            own_block(a).start()
        lax.fori_loop(upto(a), upto(a + 1), lambda k, n: (gm.hop(k), n)[1], 0)
        return c
    lax.fori_loop(half, nblk, near_step, 0)
    n16 = n48 // 3
    gpa[0] = ga_ref[...].astype(BF16)
    gb = jnp.concatenate([gb_ref[s, s * n16:(s + 1) * n16] for s in range(3)], axis=0)
    gpa[1] = dot((0.5 * gb).astype(BF16), put_ref[...]).astype(BF16)
    ga.one().start()
    gm.arrivals()
    ga.second()

    def combine(i, c):
        b = me.t * per + i
        a = block(b)
        rows = pl.ds(pl.multiple_of(i * BLK, BLK), BLK)
        remote(dn_ref.at[a], ro_ref.at[i], ros.at[0], ror.at[i], me.d, me.t1).wait_recv()
        for h in range(2):
            remote(s2_ref.at[0], r2_ref.at[i, pl.ds(h * hb, hb)], s2s.at[0], r2r.at[i, h], me.d, me.t2).wait_recv()
        dn = dn_ref[a].astype(F32) + ro_ref[i].astype(F32) + r2_ref[i].astype(F32)
        x = x_ref[rows, :].astype(F32)
        r = lax.rsqrt(jnp.mean(x * x, axis=-1, keepdims=True) + EPS)
        gd = gain_ref[0:1, :] * dn
        dmid_ref[rows, :] = dmid_ref[rows, :] + r * gd - x * (r * r * r * jnp.mean(x * gd, axis=-1, keepdims=True))
        return c
    ga.gather()
    lax.fori_loop(0, per, combine, 0)
    put_ig = pltpu.make_async_copy(dmid_ref, ig_h, igs.at[0])
    put_ig.start()
    lax.fori_loop(1, me.line, lambda k, c: (ga.hop(k), c)[1], 0)
    ga.arrivals()
    ga.settle(ndp)
    gm.settle(ndp)

    def sent(a, c):
        exchange(a).wait_send()
        deliver(a).wait_send()
        return c
    lax.fori_loop(0, half, sent, 0)

    def own_sent(a, c):
        @pl.when(jnp.logical_not(is_mine(a)))
        def _():
            own_block(a).wait_send()
        return c
    lax.fori_loop(half, nblk, own_sent, 0)
    for n, t in enumerate((me.t3, me.t2, me.t1)):
        swap(n, t).wait_send()
    put_ig.wait()


def place_kernel(e_ref, gm_ref, ga_ref, ain_h, bqkv_h, bup_h, aout_h, adown_h, bres_h, out_ref, sem):
    ndp = gm_ref.shape[1]
    slots = ([(ga_ref, 0, n, ain_h.at[n]) for n in range(3)] + [(ga_ref, 1, n, bqkv_h.at[n]) for n in range(3)]
             + [(gm_ref, 0, 0, ain_h.at[3]), (gm_ref, 0, 1, bup_h), (gm_ref, 0, 2, aout_h),
                (gm_ref, 1, 0, adown_h), (gm_ref, 1, 1, bres_h.at[0]), (gm_ref, 1, 2, bres_h.at[1])])
    copies = []
    for n, (src, c, k, dst) in enumerate(slots):
        out_ref[n] = jnp.zeros(out_ref.shape[1:], F32)

        def add(d, carry):
            e = e_ref[d, 0, 0].astype(jnp.int32)
            out_ref[n, e] += src[c, d, k * 16:(k + 1) * 16, :].astype(F32)
            return carry
        lax.fori_loop(0, ndp, add, 0)
        copies.append(pltpu.make_async_copy(out_ref.at[n], dst, sem.at[n]))
        copies[-1].start()
    for copy in copies:
        copy.wait()


VMEM = pltpu.VMEM
DMA = pltpu.SemaphoreType.DMA
IN_VMEM = pl.BlockSpec(memory_space=pltpu.VMEM)
IN_SMEM = pl.BlockSpec(memory_space=pltpu.SMEM)
IN_ANY = pl.BlockSpec(memory_space=pl.ANY)


def shape(*dims, dtype=BF16):
    return jax.ShapeDtypeStruct(dims, dtype)


def params(cid=None, limit=60 << 20):
    if cid is None:
        return pltpu.CompilerParams(vmem_limit_bytes=limit)
    return pltpu.CompilerParams(collective_id=cid, has_side_effects=True, vmem_limit_bytes=limit)


def local(
    inputs, cotangent, adapter_choice_per_tree, segment_lengths, segment_parents, norm_gain_rows, query_dimension_scale,
    attention_weights, output_weight, feedforward_weights, adapter_first_input, adapter_second_attention, adapter_second_up,
    adapter_first_output, adapter_first_down, adapter_second_residual,
):
    ndp, nt = lax.axis_size("dp"), lax.axis_size("tensor")
    tok, width = inputs.shape
    tree = tok * nt
    wrows, hcols = output_weight.shape
    heads = hcols // HD
    pad = heads * 128
    rank = adapter_first_input.shape[3]
    nblk = tree // BLK
    a_in, a_out, a_down = (jnp.swapaxes(table, -1, -2) for table in (adapter_first_input, adapter_first_output, adapter_first_down))

    chunks = 4
    count = a_in.shape[1]
    sides = row_parts(wrows)
    packed = (2 * sides + 1, wrows // sides, 128)
    flat = (3 * packed[0],) + packed[1:]
    tall = (heads, tree, 128)
    wall, choices, mixed, xn, q, qt, k, kt, v, ranks, mixt, wp, bp, at_qkv, scale = pl.pallas_call(
        functools.partial(forward_kernel, ndp, chunks),
        out_shape=[shape(ndp, nt, *flat), shape(ndp, 8, 128, dtype=F32), shape(nt, tok, hcols), shape(tree, width),
                   shape(*tall), shape(heads, 128, tree), shape(*tall), shape(heads, HD, tree), shape(*tall),
                   shape(tree, 3 * rank), shape(hcols, tree), shape(3, width, pad), shape(3, 3 * rank, pad), shape(3 * rank, width),
                   shape(1, pad, dtype=F32)],
        in_specs=[IN_SMEM] * 3 + [IN_VMEM] * 3 + [IN_ANY] * 5, out_specs=[IN_ANY] * 15,
        scratch_shapes=[VMEM((3, count, rank, width), BF16), VMEM((3, count, rank, width), BF16), VMEM((8, 128), F32), VMEM((3 * rank, width), BF16),
                        VMEM((1, pad), F32), VMEM((8, 128), F32), VMEM((128, 128), BF16), VMEM((pad, width), BF16),
                        VMEM((3, wrows, hcols), BF16), VMEM((3, wrows, hcols), BF16), VMEM((3, *packed), BF16), VMEM(flat, BF16), VMEM((tree, width), BF16),
                        VMEM((ndp, 3, *packed), BF16),
                        VMEM((3, width, pad), BF16), VMEM((3, 3 * rank, pad), BF16), VMEM(tall, BF16), VMEM((heads, 128, tree), BF16),
                        VMEM(tall, BF16), VMEM((heads, HD, tree), BF16), VMEM(tall, BF16), VMEM((heads, HD + 16, tree), BF16),
                        VMEM((tree, 3 * rank), BF16), VMEM((hcols, tree), BF16), VMEM((tree, hcols), BF16),
                        VMEM((heads, 1, BLK), F32), VMEM((heads, HD + 16, BLK), F32), DMA((5,)), DMA((12,)),
                        DMA((3, chunks)), DMA((nt, chunks)), DMA((3, ndp, 3)), DMA((ndp, 3)), DMA((3, ndp)), DMA((ndp,)),
                        DMA((2, ndp, nt, 4)), DMA((2,)), DMA((2, ndp, nt)), DMA((nblk,)), DMA((nt, tok // BLK))],
        compiler_params=params(1), name="forward",
    )(adapter_choice_per_tree, segment_lengths, segment_parents, inputs, norm_gain_rows, query_dimension_scale[None, :], a_in,
      adapter_second_attention, attention_weights, output_weight,
      feedforward_weights)

    output, d_mid, d_mix, g_mid = pl.pallas_call(
        mid_kernel,
        out_shape=[shape(tok, width), shape(tok, width, dtype=F32), shape(nt, tok, hcols), shape(6, rank, width, dtype=F32)],
        in_specs=[IN_SMEM] + [IN_VMEM] * 4 + [IN_ANY] * 6, out_specs=[IN_VMEM] * 4,
        scratch_shapes=[VMEM((3, rank, width), BF16), VMEM((3, rank, width), BF16), DMA((6,)), VMEM((tok, width), BF16), VMEM((tok, width), F32), VMEM((tok, width), BF16), VMEM((tok, width), F32),
                        VMEM((tok, width), BF16), VMEM((tok, width), F32), VMEM((tok, width), BF16), VMEM((3, width, width), BF16)]
        + [VMEM((ndp, nt, *packed), BF16)] * 3 + [DMA((3,))],
        compiler_params=params(), name="middle",
    )(adapter_choice_per_tree, inputs, cotangent, mixed, norm_gain_rows, wall, a_out, a_in, a_down, adapter_second_up, adapter_second_residual)
    gr = 6 * rank
    half_rows = gr // 2
    half, hb, per = nblk // 2, BLK // 2, tok // BLK
    grad_bufs = [VMEM((2, half_rows, width), BF16), VMEM((2, half_rows, width), BF16), VMEM((half_rows, width), BF16), VMEM((half_rows, width), BF16)]
    grad_sems = [DMA((2,)), DMA((2,)), DMA((3, ndp)), DMA((ndp,)), DMA((ndp,)), DMA((ndp,)), DMA((1,))]
    input_grad, grads_mid, grads_attn = pl.pallas_call(
        functools.partial(back_kernel, ndp),
        out_shape=[shape(tok, width, dtype=F32), shape(2, ndp, half_rows, width), shape(2, ndp, half_rows, width)],
        in_specs=[IN_ANY] * 12 + [IN_VMEM] * 5, out_specs=[IN_ANY] * 3,
        scratch_shapes=[VMEM((hcols, tree), BF16), VMEM(tall, BF16), VMEM((heads, 128, tree), BF16), VMEM(tall, BF16), VMEM((heads, HD, tree), BF16),
                        VMEM(tall, BF16), VMEM((3, width, pad), BF16), VMEM((tree, width), BF16), VMEM((tree, 3 * rank), BF16),
                        VMEM((tok, width), BF16), VMEM((tok, width), F32), VMEM((tree, hcols), BF16), VMEM(tall, BF16), VMEM((heads, 128, tree), BF16),
                        VMEM((heads, HD, tree), F32), VMEM(tall, F32), VMEM(tall, F32), VMEM((nblk, BLK, width), BF16), VMEM((half, hb, width), BF16),
                        VMEM((half, hb, width), BF16), VMEM((per, BLK, width), BF16), VMEM((per, BLK, width), BF16),
                        VMEM((3 * rank, width), F32), VMEM((3, 3 * rank, pad), F32), VMEM((pad, width), BF16)]
        + grad_bufs + grad_bufs + [DMA((11,)), DMA((4,)), DMA((nt,)), DMA((half,)), DMA((half,)), DMA((half,)), DMA((per, 2)), DMA((per,)), DMA((per,)), DMA((1,))]
        + grad_sems + grad_sems,
        compiler_params=params(4, 62 << 20), name="back",
    )(d_mix, mixt, q, qt, k, kt, v, wp, xn, ranks, inputs, d_mid, scale, bp, at_qkv, norm_gain_rows, g_mid.reshape(gr, width))

    table = shape(count, rank, width, dtype=F32)
    ga_in, gb_qkv, gb_up, ga_out, ga_down, gb_res = pl.pallas_call(
        place_kernel,
        out_shape=[shape(4, count, rank, width, dtype=F32), shape(3, count, rank, width, dtype=F32), table, table, table,
                   shape(2, count, rank, width, dtype=F32)],
        in_specs=[IN_SMEM] + [IN_VMEM] * 2, out_specs=[IN_ANY] * 6,
        scratch_shapes=[VMEM((12, count, rank, width), F32), DMA((12,))], compiler_params=params(), name="place",
    )(choices, grads_mid, grads_attn)
    return (output, input_grad, jnp.swapaxes(ga_in, 2, 3), gb_qkv, gb_up, jnp.swapaxes(ga_out, 1, 2), jnp.swapaxes(ga_down, 1, 2), gb_res)


def solution(mesh):
    tokens, weights = P(("dp", "tensor"), None), P(None, "dp", "tensor")
    in_specs = (tokens, tokens, P("dp"), P("dp", None), P("dp", None), P(), P(), weights, P("dp", "tensor"), weights) + (P(),) * 6
    out_specs = (tokens, tokens) + (P(),) * 6
    return jax.shard_map(local, mesh=mesh, in_specs=in_specs, out_specs=out_specs, check_vma=False)
```

```python
import functools
import math

import jax
import jax.numpy as jnp
from jax import lax
from jax.experimental import pallas as pl
from jax.experimental.pallas import tpu as pltpu
from jax.sharding import PartitionSpec as P

F32, BF16 = jnp.float32, jnp.bfloat16
BIG = 1e30
BLK = 256
HD = 80

def dot(a, b):
    return lax.dot_general(a, b, (((1,), (0,)), ((), ())), preferred_element_type=F32)
def dot_nt(a, b):
    return lax.dot_general(a, b, (((1,), (1,)), ((), ())), preferred_element_type=F32)
def dot_tn(a, b):
    return lax.dot_general(a, b, (((0,), (0,)), ((), ())), preferred_element_type=F32)

def project(b, s, x_ref, wp_ref, a_ref, bp_ref, scale_ref, seg_ref, mq_ref, n_ref, t_ref, rank_ref):
    rows = pl.ds(pl.multiple_of(b * BLK, BLK), BLK)
    xb = x_ref[rows, :]
    if s == 0:
        rank_ref[rows, :] = dot_nt(xb, a_ref[...]).astype(BF16)
    lane = lax.broadcasted_iota(jnp.int32, (BLK, 128), 1)
    if s == 2:
        feat = jnp.where(lane < HD + 2, 1.0, 0.0)
    else:
        tok = (lax.broadcasted_iota(jnp.int32, (BLK, 128), 0) + b * BLK).astype(F32)
        feat = jnp.where((tok >= seg_ref[0:1, :]) & (tok < seg_ref[1:2, :]), 1.0, 0.0)
        if s == 0:
            feat = dot(feat.astype(BF16), mq_ref[...])
        else:
            feat = jnp.where((lane >= HD + 13) & (lane < HD + 16), 1.0, feat)
    y = dot(xb, wp_ref[s]) + dot(rank_ref[rows, :], bp_ref[s])
    if s == 0:
        y = y * scale_ref[...]
    for h in range(n_ref.shape[0]):
        yh = jnp.where(lane < HD, y[:, h * 128:(h + 1) * 128], feat)
        n_ref[h, rows, :] = yh.astype(BF16)
        t_ref[h, :, rows] = yh.T[:t_ref.shape[1]].astype(BF16)

def attend_block(i, c, qt_ref, k_ref, vt_ref, m_ref, acc_ref, mixt_ref, mix_ref):
    heads = qt_ref.shape[0]
    cols = pl.ds(pl.multiple_of(i * BLK, BLK), BLK)
    m_ref[...] = jnp.full_like(m_ref, -3e38)
    acc_ref[...] = jnp.zeros_like(acc_ref)
    def step(j, diag):
        rows = pl.ds(pl.multiple_of(j * BLK, BLK), BLK)
        hs = range(heads)
        ss = [dot(k_ref[h, rows, :], qt_ref[h, :, cols]) for h in hs]
        if diag:
            low = lax.broadcasted_iota(jnp.int32, ss[0].shape, 0) <= lax.broadcasted_iota(jnp.int32, ss[0].shape, 1)
            ss = [jnp.where(low, s, -BIG) for s in ss]
        olds = [m_ref[h] for h in hs]
        news = [jnp.maximum(olds[h], jnp.max(ss[h], axis=0, keepdims=True)) for h in hs]
        ps = [jnp.exp(ss[h] - news[h]).astype(BF16) for h in hs]
        pv = [dot(vt_ref[h, :, rows], ps[h]) for h in hs]
        accs = [acc_ref[h] * jnp.exp(olds[h] - news[h]) + pv[h] for h in hs]
        for h in hs:
            acc_ref[h] = accs[h]
            m_ref[h] = news[h]
    lax.fori_loop(0, i, lambda j, n: (step(j, False), n)[1], 0)
    step(i, True)
    outs = []
    for h in range(heads):
        acc = acc_ref[h]
        l = acc[HD:HD + 1]
        o = acc[:HD] * (1.0 / l)
        lse = m_ref[h] + jnp.log(l)
        hi = (-lse).astype(BF16).astype(F32)
        mid = (-lse - hi).astype(BF16).astype(F32)
        lo = -lse - hi - mid
        r = lax.broadcasted_iota(jnp.int32, (16, BLK), 0)
        old = qt_ref[h, HD:HD + 16, cols].astype(F32)
        new = jnp.where(r == 13, hi, jnp.where(r == 14, mid, jnp.where(r == 15, lo, old)))
        qt_ref[h, HD:HD + 16, cols] = new.astype(BF16)
        outs.append(o)
    ot = jnp.concatenate(outs, axis=0)
    mixt_ref[:, cols] = ot.astype(BF16)
    half = BLK // 2
    full = jnp.where(c == 0, ot[:256], ot[64:]).T.astype(BF16)
    rest = jnp.where(c == 0, ot[256:], ot[:64])
    first, second = rest[:, :half], rest[:, half:]
    for r in range(2):
        for k in range(2):
            mix_ref[i, 2 * k + r] = full[r * half:(r + 1) * half, k * 128:(k + 1) * 128]
    mix_ref[i, 4] = jnp.concatenate([jnp.where(c == 0, first, second), jnp.where(c == 0, second, first)], axis=0).T.astype(BF16)

def row_parts(rows):
    return 2 if rows % 32 == 0 else 1

def third_lanes(j, part, c):
    return (j >> 6) == (part + c) % 2, (j & 63) + 256 * (1 - c)

def pack_block(block, c, store):
    rows, cols = block.shape
    parts = row_parts(rows)
    size = rows // parts
    src = lax.broadcasted_iota(jnp.int32, (cols, 256), 0)
    dst = lax.broadcasted_iota(jnp.int32, (cols, 256), 1)
    full = dot(block, jnp.where(src == dst + 64 * c, 1.0, 0.0).astype(BF16)).astype(BF16)
    rest = jnp.zeros((size, 128), F32)
    for r in range(parts):
        store(r, full[r * size:(r + 1) * size, :128])
        store(parts + r, full[r * size:(r + 1) * size, 128:])
        held, col = third_lanes(dst[:, :128], r, c)
        rest = rest + dot(block[r * size:(r + 1) * size], jnp.where(held & (src[:, :128] == col), 1.0, 0.0).astype(BF16))
    store(2 * parts, rest.astype(BF16))

def spread_heads(c, parts, pad):
    def matrix(k, held, col):
        l = lax.broadcasted_iota(jnp.int32, (k, pad), 1)
        return jnp.where(held & ((l & 127) < HD) & ((l >> 7) * HD + (l & 127) == col), 1.0, 0.0).astype(BF16)
    lane = lax.broadcasted_iota(jnp.int32, (256, 1), 0)
    rest = lax.broadcasted_iota(jnp.int32, (128, 1), 0)
    return matrix(256, lane >= 0, lane + 64 * c), [matrix(128, *third_lanes(rest, r, c)) for r in range(parts)]

def head_columns(me, pad, width):
    l = lax.broadcasted_iota(jnp.int32, (pad, width), 0)
    col = lax.broadcasted_iota(jnp.int32, (pad, width), 1)
    put = ((l & 127) < HD) & (me.t * (pad // 128 * HD) + (l >> 7) * HD + (l & 127) == col)
    return jnp.where(put, 1.0, 0.0).astype(BF16)

def tree_masks(len_ref, par_ref, seg_ref, mq_ref):
    segs = len_ref.shape[1]
    lane = lax.broadcasted_iota(jnp.int32, (1, 128), 1) - HD
    row = lax.broadcasted_iota(jnp.int32, (128, 1), 0) - HD
    lo = hi = jnp.zeros((1, 128), jnp.int32)
    up = grand = jnp.full((128, 1), -1, jnp.int32)
    start = 0
    for u in range(segs):
        end = start + len_ref[0, u]
        parent = par_ref[0, u]
        lo = jnp.where(lane == u, start, lo)
        hi = jnp.where(lane == u, end, hi)
        up = jnp.where(row == u, parent, up)
        grand = jnp.where(row == u, par_ref[0, parent], grand)
        start = end
    seg_ref[0:1, :] = lo.astype(F32)
    seg_ref[1:2, :] = hi.astype(F32)
    reach = (lane == row) | (lane == up) | (lane == grand)
    inside = (row >= 0) & (row < segs) & (lane >= 0) & (lane < segs)
    mq_ref[...] = jnp.where(inside & jnp.logical_not(reach), -BIG, 0.0).astype(BF16)

def bwd_prep(b, c, dm_ref, mixt_ref, do_ref, dot_ref):
    rows = pl.ds(pl.multiple_of(b * BLK, BLK), BLK)
    heads = do_ref.shape[0]
    t, i = b // dm_ref.shape[1], b % dm_ref.shape[1]
    full = [jnp.concatenate([dm_ref[t, i, 2 * k + r].astype(F32).T for r in range(2)], axis=1) for k in range(2)]
    rest = dm_ref[t, i, 4].astype(F32).T
    low, high = rest[:64], rest[64:]
    rest = jnp.concatenate([jnp.where(c == 0, low, high), jnp.where(c == 0, high, low)], axis=1)
    dt = jnp.where(c == 0, jnp.concatenate(full + [rest], axis=0), jnp.concatenate([rest] + full, axis=0))
    prod = dt * mixt_ref[:, rows].astype(F32)
    r = lax.broadcasted_iota(jnp.int32, (16, BLK), 0)
    for h in range(heads):
        d = dt[h * HD:(h + 1) * HD]
        delta = -jnp.sum(prod[h * HD:(h + 1) * HD], axis=0, keepdims=True)
        hi = delta.astype(BF16).astype(F32)
        ext = jnp.where(r == 0, hi, jnp.where(r == 1, delta - hi, 0.0))
        full = jnp.concatenate([d, ext, jnp.zeros((32, BLK), F32)], axis=0)
        dot_ref[h, :, rows] = full.astype(BF16)
        do_ref[h, rows, :] = full.T.astype(BF16)

def bwd_pair(i, j, diag, q_ref, qt_ref, k_ref, kt_ref, v_ref, do_ref, dot_ref, dqt_ref, dk_ref, dv_ref):
    heads = q_ref.shape[0]
    cols = pl.ds(pl.multiple_of(i * BLK, BLK), BLK)
    rows = pl.ds(pl.multiple_of(j * BLK, BLK), BLK)
    hs = range(heads)
    ss = [dot(k_ref[h, rows, :], qt_ref[h, :, cols]) for h in hs]
    dps = [dot(v_ref[h, rows, :], dot_ref[h, :, cols]) for h in hs]
    if diag:
        low = lax.broadcasted_iota(jnp.int32, ss[0].shape, 0) <= lax.broadcasted_iota(jnp.int32, ss[0].shape, 1)
        ss = [jnp.where(low, s, -BIG) for s in ss]
    ps = [jnp.exp(s) for s in ss]
    dss = [(p * dp).astype(BF16) for p, dp in zip(ps, dps)]
    ps = [p.astype(BF16) for p in ps]
    dvs = [dot(ps[h], do_ref[h, cols, :]) for h in hs]
    dks = [dot(dss[h], q_ref[h, cols, :]) for h in hs]
    dqs = [dot(kt_ref[h, :, rows], dss[h]) for h in hs]
    for h in hs:
        dv_ref[h, rows, :] += dvs[h]
        dk_ref[h, rows, :] += dks[h]
        dqt_ref[h, :, cols] += dqs[h]

MESH = pl.DeviceIdType.MESH


class Place:
    def __init__(self, ndp):
        self.d, self.t = lax.axis_index("dp"), lax.axis_index("tensor")
        self.line = ndp // 2
        self.p, self.par = self.d // 2, self.d % 2
        self.dx = self.d + 1 - 2 * self.par
        self.c, self.y = self.t % 2, self.t // 2
        self.t1 = self.t + 1 - 2 * self.c
        self.t2 = (self.t + 2) % 4
        self.t3 = (self.t1 + 2) % 4
        self.has_left, self.has_right = self.p > 0, self.p < self.line - 1


def signal(sem, d, t):
    pl.semaphore_signal(sem, inc=1, device_id=(d, t), device_id_type=MESH)


def remote(src, dst, send_sem, recv_sem, d, t):
    return pltpu.make_async_remote_copy(src_ref=src, dst_ref=dst, send_sem=send_sem, recv_sem=recv_sem, device_id=(d, t), device_id_type=MESH)


def greet(me, tensor=(), pair=False, line=False):
    bar = pltpu.get_barrier_semaphore()
    count = len(tensor) + (1 if pair else 0)
    for t in tensor:
        signal(bar, me.d, t)
    if pair:
        signal(bar, me.dx, me.t)
    if line:
        @pl.when(me.has_left)
        def _():
            signal(bar, me.d - 2, me.t)
        @pl.when(me.has_right)
        def _():
            signal(bar, me.d + 2, me.t)
        count = count + jnp.where(me.has_left, 1, 0) + jnp.where(me.has_right, 1, 0)
    pl.semaphore_wait(bar, count)


class PairLine:
    def __init__(self, me, own, buf, send, recv, part=None):
        self.me, self.own, self.buf, self.send, self.recv, self.part = me, own, buf, send, recv, part

    def slot(self, o):
        return self.buf.at[o] if self.part is None else self.buf.at[o, self.part]

    def copy(self, o, src, d, kind):
        send, recv = (self.send.at[kind, o], self.recv.at[o]) if self.part is None else (self.send.at[kind, o, self.part], self.recv.at[o, self.part])
        return remote(src, self.slot(o), send, recv, d, self.me.t)

    def start(self):
        me = self.me
        @pl.when(me.has_left)
        def _():
            self.copy(me.d, self.own, me.d - 2, 0).start()
        @pl.when(me.has_right)
        def _():
            self.copy(me.d, self.own, me.d + 2, 1).start()
        self.copy(me.d, self.own, me.dx, 2).start()

    def hop(self, k, then=None):
        me = self.me
        @pl.when(me.p - k >= 0)
        def _():
            o = me.d - 2 * k
            self.copy(o, self.slot(o), me.dx, 2).wait_recv()
            @pl.when(me.has_right)
            def _():
                self.copy(o, self.slot(o), me.d + 2, 1).start()
            self.copy(o, self.slot(o), me.dx, 2).start()
            if then is not None:
                then(o)
        @pl.when(me.p + k < me.line)
        def _():
            o = me.d + 2 * k
            self.copy(o, self.slot(o), me.dx, 2).wait_recv()
            @pl.when(me.has_left)
            def _():
                self.copy(o, self.slot(o), me.d - 2, 0).start()
            self.copy(o, self.slot(o), me.dx, 2).start()
            if then is not None:
                then(o)

    def pair_arrivals(self, then=None):
        def one(q, c):
            o = 2 * q + 1 - self.me.par
            self.copy(o, self.slot(o), self.me.dx, 2).wait_recv()
            if then is not None:
                then(o)
            return c
        lax.fori_loop(0, self.me.line, one, 0)

    def sent(self):
        me = self.me
        def one(q, c):
            o = 2 * q + me.par
            self.copy(o, self.slot(o), me.dx, 2).wait_send()
            @pl.when((q >= me.p) & me.has_left)
            def _():
                self.copy(o, self.slot(o), me.dx, 0).wait_send()
            @pl.when((q <= me.p) & me.has_right)
            def _():
                self.copy(o, self.slot(o), me.dx, 1).wait_send()
            return c
        lax.fori_loop(0, me.line, one, 0)


class FullGather:
    def __init__(self, me, own, buf, send, first, recv):
        self.me, self.own, self.buf, self.send, self.first, self.recv = me, own, buf, send, first, recv
        cut = own.shape[0] // 3
        self.parts = (pl.ds(0, cut), pl.ds(cut, own.shape[0] - cut))

    def copy(self, h, o, t, d2, t2, kind, own=False):
        rows = self.parts[h]
        src = self.own.at[rows] if own else self.buf.at[o, t, rows]
        sem = self.first.at[h] if kind == 4 else self.send.at[h, o, t, kind]
        return remote(src, self.buf.at[o, t, rows], sem, self.recv.at[h, o, t], d2, t2)

    def last(self, h):
        me = self.me
        return (me.d, me.t2) if h == 0 else (me.dx, me.t)

    def spread(self, h, o, t, left, right, own=False):
        me = self.me
        @pl.when(left)
        def _():
            self.copy(h, o, t, me.d - 2, me.t, 0, own).start()
        @pl.when(right)
        def _():
            self.copy(h, o, t, me.d + 2, me.t, 1, own).start()
        self.copy(h, o, t, *self.last(h), 2, own).start()
        self.copy(h, o, t, me.d, me.t1, 3, own).start()

    def start(self):
        me = self.me
        self.copy(0, me.d, me.t, me.dx, me.t, 4, True).start()
        self.copy(1, me.d, me.t, me.d, me.t2, 4, True).start()
        for h in (1, 0):
            self.spread(h, me.d, me.t, me.has_left, me.has_right, True)

    def arrived(self, h, o, t):
        self.copy(h, o, t, self.me.d, self.me.t1, 3).wait_recv()

    def firsts(self):
        me = self.me
        self.arrived(0, me.dx, me.t)
        self.spread(0, me.dx, me.t, me.has_left, me.has_right)
        self.arrived(1, me.d, me.t2)
        self.spread(1, me.d, me.t2, me.has_left, me.has_right)

    def streams(self, q):
        me = self.me
        return ((0, 2 * q + me.par, me.t), (0, 2 * q + 1 - me.par, me.t), (1, 2 * q + me.par, me.t), (1, 2 * q + me.par, me.t2))

    def hop(self, k):
        me = self.me
        @pl.when(me.p - k >= 0)
        def _():
            for h, o, t in self.streams(me.p - k):
                self.arrived(h, o, t)
                self.spread(h, o, t, False, me.has_right)
        @pl.when(me.p + k < me.line)
        def _():
            for h, o, t in self.streams(me.p + k):
                self.arrived(h, o, t)
                self.spread(h, o, t, me.has_left, False)

    def lasts(self, k):
        me = self.me

        def place(q):
            for h, o, t in ((0, 2 * q, me.t2), (0, 2 * q + 1, me.t2), (1, 2 * q + 1 - me.par, me.t), (1, 2 * q + 1 - me.par, me.t2)):
                self.arrived(h, o, t)
                self.copy(h, o, t, me.d, me.t1, 3).start()

        @pl.when(me.p - k >= 0)
        def _():
            place(me.p - k)
        @pl.when((me.p + k < me.line) & (k > 0))
        def _():
            place(me.p + k)

    def finish(self):
        me = self.me
        def one(o, c):
            for h in range(2):
                self.arrived(h, o, me.t1)
                self.arrived(h, o, me.t3)
                for t in (me.t, me.t2):
                    self.copy(h, o, t, me.d, me.t1, 3).wait_send()
            return c
        lax.fori_loop(0, 2 * me.line, one, 0)
        def two(q, c):
            for h, o, t in self.streams(q):
                self.copy(h, o, t, me.d, me.t1, 2).wait_send()
                @pl.when((q >= me.p) & me.has_left)
                def _():
                    self.copy(h, o, t, me.d, me.t1, 0).wait_send()
                @pl.when((q <= me.p) & me.has_right)
                def _():
                    self.copy(h, o, t, me.d, me.t1, 1).wait_send()
            return c
        lax.fori_loop(0, me.line, two, 0)
        for h in range(2):
            self.copy(h, me.d, me.t, me.d, me.t1, 4).wait_send()


EPS = 1e-6


def forward_kernel(ndp, chunks, choice_in, len_ref, par_ref, x_ref, gain_ref, qs_ref, ain_h, btab_h, a_ref, wo_ref, wf_ref,
                   wout_ref, cho_ref, mixed_ref, xno_ref, qo_ref, qto_ref, ko_ref, kto_ref, vo_ref, ranko_ref, mixto_ref, wpo_ref, bpo_ref, ato_ref, scaleo_ref,
                   ain_ref, btab_ref, choice_ref, at_ref, scale_ref, seg_ref, mq_ref, put_ref,
                   araw_ref, wraw_ref, aown_ref, wown_ref, xn_ref, wa_ref, wp_ref, bp_ref, q_ref, qt_ref, k_ref, kt_ref, v_ref, vt_ref, rank_ref, mixt_ref,
                   mix_ref, m_ref, acc_ref, ls, os, xs, xr, a_s, a_r, c_s, c_r, w_s, w_f, w_r, ms, mr):
    me = Place(ndp)
    tok, width = x_ref.shape
    loads = [pltpu.make_async_copy(a_ref, araw_ref, ls.at[0]), pltpu.make_async_copy(wo_ref, wraw_ref.at[0], ls.at[1]),
             pltpu.make_async_copy(wf_ref, wraw_ref.at[pl.ds(1, 2)], ls.at[2])]
    tables = [pltpu.make_async_copy(ain_h.at[pl.ds(0, 3)], ain_ref, ls.at[3]), pltpu.make_async_copy(btab_h, btab_ref, ls.at[4])]
    for copy in loads + tables:
        copy.start()
    e = choice_in[0]
    choice_ref[...] = jnp.zeros_like(choice_ref) + e.astype(F32)
    x = x_ref[...].astype(F32)
    mine = pl.ds(pl.multiple_of(me.t * tok, tok), tok)
    xn_ref[mine, :] = (x * lax.rsqrt(jnp.mean(x * x, axis=-1, keepdims=True) + EPS) * gain_ref[0:1, :]).astype(BF16)
    greet(me, tensor=(me.t1, me.t2, me.t3), pair=True, line=True)
    size = tok // chunks

    def xcopy(o, c, t, kind):
        rows = pl.ds(pl.multiple_of(o * tok + c * size, size), size)
        return remote(xn_ref.at[rows], xn_ref.at[rows], xs.at[kind, c], xr.at[o, c], me.d, t)

    for c in range(chunks):
        xcopy(me.t, c, me.t2, 0).start()
    for c in range(chunks):
        xcopy(me.t, c, me.t1, 1).start()
    for copy in loads:
        copy.wait()
    pieces = aown_ref.shape[1]

    def pack(raw_ref, own_ref, n, index):
        def store(k, v):
            own_ref[index(n, k)] = v
        pack_block(raw_ref[n], me.c, store)
    for n in range(3):
        pack(araw_ref, aown_ref, n, lambda n, k: (n, k))
    parts = [PairLine(me, aown_ref.at[n], wa_ref, a_s, a_r, n) for n in range(3)]
    ch = PairLine(me, choice_ref, cho_ref, c_s, c_r)
    w = FullGather(me, wown_ref, wout_ref, w_s, w_f, w_r)
    parts[0].start()
    parts[1].start()
    for n in range(3):
        pack(wraw_ref, wown_ref, n, lambda n, k: n * pieces + k)
    keep = [pltpu.make_async_copy(wown_ref, wout_ref.at[me.d, me.t], ls.at[0]), pltpu.make_async_copy(choice_ref, cho_ref.at[me.d], ls.at[1])]
    for copy in keep:
        copy.start()
    wa_ref[me.d] = aown_ref[...]
    tree_masks(len_ref, par_ref, seg_ref, mq_ref)
    scale_ref[...] = jnp.zeros_like(scale_ref)
    for h in range(q_ref.shape[0]):
        scale_ref[:, h * 128:h * 128 + HD] = qs_ref[...] * (1.0 / math.sqrt(HD))
    put_ref[...] = head_columns(me, *put_ref.shape)
    for copy in tables:
        copy.wait()
    parts[0].hop(1)
    parts[2].start()
    ch.start()

    def diagonal(n, carry):
        for part in range(3):
            k = n - part
            @pl.when((k >= 1) & (k < me.line))
            def _():
                parts[part].hop(k)
        return carry
    lax.fori_loop(2, me.line + 2, diagonal, 0)
    w.start()
    n16 = ain_ref.shape[2]
    for s in range(3):
        at_ref[s * n16:(s + 1) * n16] = ain_ref[s, e]
    picked = jnp.concatenate([btab_ref[s, e] for s in range(3)], axis=0)
    spread = (0.5 * dot_nt(picked, put_ref[...])).astype(BF16)
    bp_ref[...] = jnp.zeros_like(bp_ref)
    for s in range(3):
        bp_ref[s, s * n16:(s + 1) * n16] = spread[s * n16:(s + 1) * n16]

    def forward(c):
        xcopy(me.t2, c, me.t1, 2).wait_recv()
        xcopy(me.t2, c, me.t1, 2).start()

    for c in range(chunks // 2):
        forward(c)
    nblk = xn_ref.shape[0] // BLK
    near = nblk // 2
    half_rows = wa_ref.shape[3]
    sides = pieces // 2
    wrows = half_rows * sides
    sel, sel_rest = spread_heads(me.c, sides, wp_ref.shape[2])

    def spread_weights(s):
        if sides == 1:
            group = 16 // math.gcd(wrows, 16)
            for o in range(0, ndp, group):
                wp_ref[s, o * wrows:(o + group) * wrows] = jnp.concatenate([
                    dot(jnp.concatenate([wa_ref[o + j, s, 0], wa_ref[o + j, s, 1]], axis=1), sel) + dot(wa_ref[o + j, s, 2], sel_rest[0])
                    for j in range(group)], axis=0).astype(BF16)
            return
        flat = [wa_ref[:, s, k].reshape(ndp * half_rows, 128) for k in range(pieces)]
        for r in range(sides):
            y = (dot(jnp.concatenate([flat[r], flat[sides + r]], axis=1), sel) + dot(flat[2 * sides], sel_rest[r])).astype(BF16)
            for o in range(ndp):
                wp_ref[s, o * wrows + r * half_rows:o * wrows + (r + 1) * half_rows] = y[o * half_rows:(o + 1) * half_rows]

    def project_blocks(first, s):
        n_ref, t_ref = ((q_ref, qt_ref), (k_ref, kt_ref), (v_ref, vt_ref))[s]
        lax.fori_loop(0, near, lambda n, c: (project(first + n, s, xn_ref, wp_ref, at_ref, bp_ref, scale_ref, seg_ref, mq_ref, n_ref, t_ref, rank_ref), c)[1], 0)

    for c in range(chunks):
        xcopy(me.t1, c, me.t1, 2).wait_recv()
    for s in range(3):
        parts[s].pair_arrivals()
        spread_weights(s)
        project_blocks(me.y * near, s)
        if s < 2:
            forward(chunks // 2 + s)
    for c in range(chunks):
        xcopy(me.t3, c, me.t1, 2).wait_recv()
    w.firsts()
    for s in range(3):
        project_blocks((1 - me.y) * near, s)

    def hops(i):
        done = 1 + jnp.maximum((me.line - 2) * (i + 1) * (i + 2) + 2 * nblk, 0) // ((nblk - 1) * nblk)
        return jnp.minimum(done, me.line - 1)

    def relay(i):
        lax.fori_loop(hops(i - 1), hops(i), lambda k, c: (w.hop(k + 1), ch.hop(k + 1), c)[2], 0)
    w.hop(1)
    ch.hop(1)
    outs = [pltpu.make_async_copy(src, dst, os.at[n]) for n, (src, dst) in enumerate((
        (xn_ref, xno_ref), (q_ref, qo_ref), (k_ref, ko_ref), (kt_ref, kto_ref), (v_ref, vo_ref), (rank_ref, ranko_ref),
        (wp_ref, wpo_ref), (bp_ref, bpo_ref), (at_ref, ato_ref), (scale_ref, scaleo_ref)))]
    for copy in outs:
        copy.start()
    per = tok // BLK

    def piece(i):
        return mix_ref.at[i], mixed_ref.at[me.t, i % per], i // per

    def attend_step(i, c):
        attend_block(i, me.c, qt_ref, k_ref, vt_ref, m_ref, acc_ref, mixt_ref, mix_ref)
        src, dst, t = piece(i)
        @pl.when(t == me.t)
        def _():
            pltpu.make_async_copy(src, dst, ms.at[i]).start()
        @pl.when(t != me.t)
        def _():
            remote(src, dst, ms.at[i], mr.at[me.t, i % per], me.d, t).start()
        relay(i)
        lax.fori_loop(jnp.where(i == 0, 0, hops(i - 2)), hops(i - 1), lambda k, n: (w.lasts(k), n)[1], 0)
        return c
    lax.fori_loop(0, nblk, attend_step, 0)
    late = [pltpu.make_async_copy(qt_ref, qto_ref, os.at[len(outs)]), pltpu.make_async_copy(mixt_ref, mixto_ref, os.at[len(outs) + 1])]
    for copy in late:
        copy.start()
    lax.fori_loop(hops(nblk - 2), me.line, lambda k, c: (w.lasts(k), c)[1], 0)
    ch.pair_arrivals()
    for t in (me.t1, me.t2, me.t3):
        for h in range(per):
            dst = mixed_ref.at[t, h]
            remote(dst, dst, ms.at[0], mr.at[t, h], me.d, t).wait_recv()
    w.finish()
    for part in parts:
        part.sent()
    ch.sent()
    for c in range(chunks):
        for kind in range(3):
            xcopy(me.t, c, me.t1, kind).wait_send()

    def settle(i, c):
        src, dst, t = piece(i)
        @pl.when(t == me.t)
        def _():
            pltpu.make_async_copy(src, dst, ms.at[i]).wait()
        @pl.when(t != me.t)
        def _():
            remote(src, dst, ms.at[i], mr.at[me.t, i % per], me.d, t).wait_send()
        return c
    lax.fori_loop(0, nblk, settle, 0)
    for copy in keep + outs + late:
        copy.wait()


def sigmoid(v):
    return 1.0 / (1.0 + jnp.exp(-v))


def mid_kernel(e_ref, x_ref, g_ref, mix4_ref, gain_ref, wall_ref, aout_h, ain_h, adown_h, bup_h, bres_h, out_ref, dmid_ref, dmix_ref, grads_ref,
               at_ref, b_ref, ts, mix_ref, mid_ref, hid_ref, up_ref, act_ref, f_ref, low_ref, w_ref, wb0_ref, wb1_ref, wb2_ref, ls):
    width = x_ref.shape[1]
    step = 256
    part = width // mix4_ref.shape[0]
    blocks = (wb0_ref, wb1_ref, wb2_ref)
    ndp, nt, pieces, size = wb0_ref.shape[:4]
    sides = pieces // 2
    loads = [pltpu.make_async_copy(wall_ref.at[:, :, pl.ds(n * pieces, pieces)], blocks[n], ls.at[n]) for n in range(3)]
    e = e_ref[0]
    tables = [pltpu.make_async_copy(src, dst, ts.at[n]) for n, (src, dst) in enumerate((
        (aout_h.at[e], at_ref.at[0]), (ain_h.at[3, e], at_ref.at[1]), (adown_h.at[e], at_ref.at[2]),
        (bres_h.at[0, e], b_ref.at[0]), (bup_h.at[e], b_ref.at[1]), (bres_h.at[1, e], b_ref.at[2])))]
    for copy in tables + loads:
        copy.start()
    for copy in tables:
        copy.wait()

    def join(dst_ref, first_part, y, even, odd):
        pieces, size = even.shape[:2]
        sides = pieces // 2
        low_lane = lax.broadcasted_iota(jnp.int32, (size, 128), 1) < 64
        base = 2 * part * y
        for r in range(sides):
            rows = pl.ds((first_part + r) * size, size)
            dst_ref[rows, base:base + 128] = even[r]
            dst_ref[rows, base + 128:base + 256] = even[sides + r]
            first, second = (even, odd) if r == 0 else (odd, even)
            both = jnp.where(low_lane, first[2 * sides].astype(F32), second[2 * sides].astype(F32))
            dst_ref[rows, base + 256:base + 384] = (both if r == 0 else pltpu.roll(both, 64, 1)).astype(BF16)
            dst_ref[rows, base + 384:base + 512] = odd[r]
            dst_ref[rows, base + 512:base + 640] = odd[sides + r]

    def assemble(n):
        loads[n].wait()
        dst = w_ref.at[n]
        for o in range(ndp):
            for y in range(nt // 2):
                join(dst, o * sides, y, blocks[n].at[o, 2 * y], blocks[n].at[o, 2 * y + 1])

    for y in range(nt // 2):
        for i in range(mix4_ref.shape[1]):
            join(mix_ref, 2 * i, y, mix4_ref.at[2 * y, i], mix4_ref.at[2 * y + 1, i])

    def cols(n):
        return pl.ds(pl.multiple_of(n * step, step), step)

    def each(fn):
        lax.fori_loop(0, width // step, lambda n, c: (fn(cols(n)), c)[1], 0)

    gain = gain_ref[1:2, :]
    r_out = dot_nt(mix_ref[...], at_ref[0]).astype(BF16)
    assemble(0)

    def project_out(n):
        attn = dot_nt(mix_ref[...], w_ref[0, n, :]) + 0.5 * dot(r_out, b_ref[0, :, n])
        mid_ref[:, n] = x_ref[:, n].astype(F32) + attn
    each(project_out)
    middle = mid_ref[...]
    r = lax.rsqrt(jnp.mean(middle * middle, axis=-1, keepdims=True) + EPS)
    hid_ref[...] = (middle * r * gain).astype(BF16)
    r_up = dot_nt(hid_ref[...], at_ref[1]).astype(BF16)
    assemble(1)

    def up_step(n):
        up = dot(hid_ref[...], w_ref[1, :, n]) + 0.5 * dot(r_up, b_ref[1, :, n])
        up_ref[:, n] = up
        act_ref[:, n] = (up * sigmoid(up)).astype(BF16)
    each(up_step)
    r_down = dot_nt(act_ref[...], at_ref[2]).astype(BF16)
    assemble(2)

    def down_step(n):
        down = dot_nt(act_ref[...], w_ref[2, n, :]) + 0.5 * dot(r_down, b_ref[2, :, n])
        out_ref[:, n] = (mid_ref[:, n] + down).astype(BF16)
    each(down_step)
    grads_ref[5] = 0.5 * dot_tn(r_down, g_ref[...])
    dz_down = (0.5 * dot_nt(g_ref[...], b_ref[2])).astype(BF16)
    grads_ref[3] = dot_tn(dz_down, act_ref[...])

    def act_back(n):
        d_act = dot(g_ref[...], w_ref[2, :, n]) + dot(dz_down, at_ref[2, :, n])
        up = up_ref[:, n]
        sg = sigmoid(up)
        low_ref[:, n] = (d_act * sg * (1.0 + up * (1.0 - sg))).astype(BF16)
    each(act_back)
    dz_up = (0.5 * dot_nt(low_ref[...], b_ref[1])).astype(BF16)
    grads_ref[1] = 0.5 * dot_tn(r_up, low_ref[...])
    grads_ref[0] = dot_tn(dz_up, hid_ref[...])

    def hidden_back(n):
        f_ref[:, n] = (dot_nt(low_ref[...], w_ref[1, n, :]) + dot(dz_up, at_ref[1, :, n])) * gain_ref[1:2, n]
    each(hidden_back)
    gd = f_ref[...]
    middle = mid_ref[...]
    s = jnp.mean(middle * gd, axis=-1, keepdims=True)
    d_mid = g_ref[...].astype(F32) + r * gd - middle * (r * r * r * s)
    dmid_ref[...] = d_mid
    low_ref[...] = d_mid.astype(BF16)
    dz_out = (0.5 * dot_nt(low_ref[...], b_ref[0])).astype(BF16)
    grads_ref[4] = 0.5 * dot_tn(r_out, low_ref[...])
    grads_ref[2] = dot_tn(dz_out, mix_ref[...])

    def mixed_back(n):
        act_ref[:, n] = (dot(low_ref[...], w_ref[0, :, n]) + dot(dz_out, at_ref[0, :, n])).astype(BF16)
    each(mixed_back)
    half = dmix_ref.shape[3]
    low_lane = lax.broadcasted_iota(jnp.int32, (half, 128), 1) < 64
    for y in range(nt // 2):
        base = 2 * part * y
        for i in range(dmix_ref.shape[1]):
            halves = [pl.ds((2 * i + r) * half, half) for r in range(2)]
            for r in range(2):
                dmix_ref[2 * y, i, r] = act_ref[halves[r], base:base + 128]
                dmix_ref[2 * y, i, 2 + r] = act_ref[halves[r], base + 128:base + 256]
                dmix_ref[2 * y + 1, i, r] = act_ref[halves[r], base + 384:base + 512]
                dmix_ref[2 * y + 1, i, 2 + r] = act_ref[halves[r], base + 512:base + 640]
            top = act_ref[halves[0], base + 256:base + 384].astype(F32)
            turned = pltpu.roll(act_ref[halves[1], base + 256:base + 384].astype(F32), 64, 1)
            dmix_ref[2 * y, i, 4] = jnp.where(low_lane, top, turned).astype(BF16)
            dmix_ref[2 * y + 1, i, 4] = jnp.where(low_lane, turned, top).astype(BF16)


class GradSum:
    def __init__(self, me, gp, gr, g2, own, out, s, r, ls_, lr, fs, fr, keep):
        self.me, self.gp, self.gr, self.g2, self.own, self.out, self.s, self.r, self.fs, self.fr = me, gp, gr, g2, own, out, s, r, fs, fr
        self.line = PairLine(me, own, out.at[me.c], ls_, lr)
        self.keep = pltpu.make_async_copy(own, out.at[me.c, me.d], keep)

    def one(self):
        return remote(self.gp.at[1 - self.me.c], self.gr.at[0], self.s.at[0], self.r.at[0], self.me.d, self.me.t1)

    def two(self):
        return remote(self.g2, self.gr.at[1], self.s.at[1], self.r.at[1], self.me.d, self.me.t2)

    def second(self):
        self.one().wait_recv()
        self.g2[...] = (self.gp[self.me.c].astype(F32) + self.gr[0].astype(F32)).astype(BF16)
        self.two().start()

    def relay(self, o, own=False):
        src = self.own if own else self.out.at[self.me.c, o]
        return remote(src, self.out.at[self.me.c, o], self.fs.at[o], self.fr.at[o], self.me.d, self.me.t1)

    def gather(self):
        self.two().wait_recv()
        self.own[...] = (self.g2[...].astype(F32) + self.gr[1].astype(F32)).astype(BF16)
        self.line.start()
        self.relay(self.me.d, True).start()
        self.keep.start()

    def hop(self, k):
        self.line.hop(k, lambda o: self.relay(o).start())

    def arrivals(self):
        self.line.pair_arrivals(lambda o: self.relay(o).start())

    def settle(self, ndp):
        def one(o, c):
            self.relay(o, True).wait_send()
            remote(self.own, self.out.at[1 - self.me.c, o], self.fs.at[o], self.fr.at[o], self.me.d, self.me.t1).wait_recv()
            return c
        lax.fori_loop(0, ndp, one, 0)
        self.line.sent()
        self.keep.wait()
        self.one().wait_send()
        self.two().wait_send()


def back_kernel(ndp, dmix_ref, mixt_h, q_h, qt_h, k_h, kt_h, v_h, wp_h, xn_h, rank_h, x_h, dmid_h, scale_ref, bp_ref, at_ref, gain_ref, gmid_ref,
                ig_h, gm_h, ga_h,
                mixt_ref, q_ref, qt_ref, k_ref, kt_ref, v_ref, wp_ref, xn_ref, rank_ref, x_ref, dmid_ref, dm_ref, do_ref, dot_ref,
                dqt_ref, dk_ref, dv_ref, dn_ref, r1_ref, s2_ref, r2_ref, ro_ref, ga_ref, gb_ref, put_ref,
                gpm, grm, g2m, gom, gpa, gra, g2a, goa, lsem, dsem, drecv, es, er, s2s, r2r, ros, ror, igs,
                ms, mr, mls, mlr, mfs, mfr, mk, as_, ar, als, alr, afs, afr, ak):
    me = Place(ndp)
    tok = x_ref.shape[0]
    per, hb = tok // BLK, BLK // 2
    nblk = per * dm_ref.shape[0]
    half = nblk // 2
    heads = q_ref.shape[0]
    loads = [pltpu.make_async_copy(src, dst, lsem.at[n]) for n, (src, dst) in enumerate((
        (mixt_h, mixt_ref), (q_h, q_ref), (qt_h, qt_ref), (k_h, k_ref), (kt_h, kt_ref), (v_h, v_ref),
        (wp_h, wp_ref), (xn_h, xn_ref), (rank_h, rank_ref), (x_h, x_ref), (dmid_h, dmid_ref)))]
    n48 = gpm.shape[1]
    for c in range(2):
        gpm[c] = gmid_ref[c * n48:(c + 1) * n48].astype(BF16)
    greet(me, tensor=(me.t1, me.t2, me.t3), pair=True, line=True)

    def swap(n, t):
        return remote(dmix_ref.at[t], dm_ref.at[me.t], dsem.at[n], drecv.at[me.t], me.d, t)

    own = pltpu.make_async_copy(dmix_ref.at[me.t], dm_ref.at[me.t], dsem.at[3])
    for n, t in enumerate((me.t3, me.t2, me.t1)):
        swap(n, t).start()
    own.start()
    gm = GradSum(me, gpm, grm, g2m, gom, gm_h, ms, mr, mls, mlr, mfs, mfr, mk.at[0])
    ga = GradSum(me, gpa, gra, g2a, goa, ga_h, as_, ar, als, alr, afs, afr, ak.at[0])
    gm.one().start()
    for copy in loads:
        copy.start()
    for ref in (dqt_ref, dk_ref, dv_ref, ga_ref, gb_ref):
        ref[...] = jnp.zeros_like(ref)
    put_ref[...] = head_columns(me, *put_ref.shape)
    for copy in loads[:6]:
        copy.wait()

    def prep(t):
        lax.fori_loop(t * per, (t + 1) * per, lambda b, c: (bwd_prep(b, me.c, dm_ref, mixt_ref, do_ref, dot_ref), c)[1], 0)

    args = (q_ref, qt_ref, k_ref, kt_ref, v_ref, do_ref, dot_ref, dqt_ref, dk_ref, dv_ref)

    def block(a):
        return (1 - me.y) * (nblk - 1 - a) + me.y * a

    def pairs(a):
        b = block(a)
        bwd_pair(b, b, True, *args)

        def other(n, c):
            bwd_pair(b + me.y * (1 + n), b - (1 - me.y) * (1 + n), False, *args)
            return c
        lax.fori_loop(0, nblk - 1 - a, other, 0)

    def arrived(t):
        remote(dmix_ref.at[t], dm_ref.at[t], dsem.at[0], drecv.at[t], me.d, t).wait_recv()

    own.wait()
    prep(me.t)
    arrived(me.t1)
    prep(me.t1)
    gm.second()
    lax.fori_loop(half, nblk, lambda a, c: (pairs(a), c)[1], 0)
    arrived(me.t2)
    prep(me.t2)
    arrived(me.t3)
    prep(me.t3)
    for copy in loads[6:]:
        copy.wait()
    lane = lax.broadcasted_iota(jnp.int32, (BLK, 128), 1)

    def exchange(a):
        rows = pl.ds(pl.multiple_of((1 - me.c) * hb, hb), hb)
        return remote(dn_ref.at[a, rows], r1_ref.at[a], es.at[a], er.at[a], me.d, me.t1)

    def own_block(a):
        return remote(dn_ref.at[a], ro_ref.at[block(a) % per], ros.at[a % per], ror.at[block(a) % per], me.d, me.t1)

    def mine_rows():
        return pl.ds(pl.multiple_of(me.c * hb, hb), hb)

    def deliver(a):
        b = block(a)
        return remote(s2_ref.at[a], r2_ref.at[b % per, mine_rows()], s2s.at[a], r2r.at[b % per, me.c], me.d, b // per)

    def is_mine(a):
        return block(a) // per == me.t

    def pass_on(a):
        exchange(a).wait_recv()
        s2_ref[a] = (dn_ref[a, mine_rows(), :].astype(F32) + r1_ref[a].astype(F32)).astype(BF16)
        deliver(a).start()

    def final(a):
        rows = pl.ds(pl.multiple_of(block(a) * BLK, BLK), BLK)
        dq, dk, dv = [], [], []
        for h in range(heads):
            g = jnp.concatenate([dqt_ref[h, :, rows], jnp.zeros((48, BLK), F32)], axis=0).T
            dq.append((g * scale_ref[:, h * 128:(h + 1) * 128]).astype(BF16))
            dk.append(jnp.where(lane < HD, dk_ref[h, rows, :], 0.0).astype(BF16))
            dv.append(jnp.where(lane < HD, dv_ref[h, rows, :], 0.0).astype(BF16))
        ds = [jnp.concatenate(g, axis=1) for g in (dq, dk, dv)]
        dz = sum(dot_nt(ds[s], bp_ref[s]) for s in range(3)).astype(BF16)
        dn = sum(dot_nt(ds[s], wp_ref[s]) for s in range(3)) + dot(dz, at_ref[...])
        dn_ref[a] = dn.astype(BF16)
        ga_ref[...] += dot_tn(dz, xn_ref[rows, :])
        for s in range(3):
            gb_ref[s] += dot_tn(rank_ref[rows, :], ds[s])

    def upto(a):
        return 1 + jnp.minimum(a * (me.line - 1) // (nblk - 2), me.line - 1)

    def far_step(a, c):
        pairs(a)
        @pl.when(a > 0)
        def _():
            pass_on(a - 1)
        final(a)
        exchange(a).start()
        @pl.when(a == 0)
        def _():
            gm.gather()
        lax.fori_loop(upto(a), upto(a + 1), lambda k, n: (gm.hop(k), n)[1], 0)
        return c
    lax.fori_loop(0, half, far_step, 0)

    def near_step(a, c):
        final(a)
        @pl.when(a == half)
        def _():
            pass_on(a - 1)
        @pl.when(jnp.logical_not(is_mine(a)))
        def _():
            own_block(a).start()
        lax.fori_loop(upto(a), upto(a + 1), lambda k, n: (gm.hop(k), n)[1], 0)
        return c
    lax.fori_loop(half, nblk, near_step, 0)
    n16 = n48 // 3
    gpa[0] = ga_ref[...].astype(BF16)
    gb = jnp.concatenate([gb_ref[s, s * n16:(s + 1) * n16] for s in range(3)], axis=0)
    gpa[1] = dot((0.5 * gb).astype(BF16), put_ref[...]).astype(BF16)
    ga.one().start()
    gm.arrivals()
    ga.second()

    def combine(i, c):
        b = me.t * per + i
        a = block(b)
        rows = pl.ds(pl.multiple_of(i * BLK, BLK), BLK)
        remote(dn_ref.at[a], ro_ref.at[i], ros.at[0], ror.at[i], me.d, me.t1).wait_recv()
        for h in range(2):
            remote(s2_ref.at[0], r2_ref.at[i, pl.ds(h * hb, hb)], s2s.at[0], r2r.at[i, h], me.d, me.t2).wait_recv()
        dn = dn_ref[a].astype(F32) + ro_ref[i].astype(F32) + r2_ref[i].astype(F32)
        x = x_ref[rows, :].astype(F32)
        r = lax.rsqrt(jnp.mean(x * x, axis=-1, keepdims=True) + EPS)
        gd = gain_ref[0:1, :] * dn
        dmid_ref[rows, :] = dmid_ref[rows, :] + r * gd - x * (r * r * r * jnp.mean(x * gd, axis=-1, keepdims=True))
        return c
    ga.gather()
    lax.fori_loop(0, per, combine, 0)
    put_ig = pltpu.make_async_copy(dmid_ref, ig_h, igs.at[0])
    put_ig.start()
    lax.fori_loop(1, me.line, lambda k, c: (ga.hop(k), c)[1], 0)
    ga.arrivals()
    ga.settle(ndp)
    gm.settle(ndp)

    def sent(a, c):
        exchange(a).wait_send()
        deliver(a).wait_send()
        return c
    lax.fori_loop(0, half, sent, 0)

    def own_sent(a, c):
        @pl.when(jnp.logical_not(is_mine(a)))
        def _():
            own_block(a).wait_send()
        return c
    lax.fori_loop(half, nblk, own_sent, 0)
    for n, t in enumerate((me.t3, me.t2, me.t1)):
        swap(n, t).wait_send()
    put_ig.wait()


def place_kernel(e_ref, gm_ref, ga_ref, ain_h, bqkv_h, bup_h, aout_h, adown_h, bres_h, out_ref, sem):
    ndp = gm_ref.shape[1]
    slots = ([(ga_ref, 0, n, ain_h.at[n]) for n in range(3)] + [(ga_ref, 1, n, bqkv_h.at[n]) for n in range(3)]
             + [(gm_ref, 0, 0, ain_h.at[3]), (gm_ref, 0, 1, bup_h), (gm_ref, 0, 2, aout_h),
                (gm_ref, 1, 0, adown_h), (gm_ref, 1, 1, bres_h.at[0]), (gm_ref, 1, 2, bres_h.at[1])])
    copies = []
    for n, (src, c, k, dst) in enumerate(slots):
        out_ref[n] = jnp.zeros(out_ref.shape[1:], F32)

        def add(d, carry):
            e = e_ref[d, 0, 0].astype(jnp.int32)
            out_ref[n, e] += src[c, d, k * 16:(k + 1) * 16, :].astype(F32)
            return carry
        lax.fori_loop(0, ndp, add, 0)
        copies.append(pltpu.make_async_copy(out_ref.at[n], dst, sem.at[n]))
        copies[-1].start()
    for copy in copies:
        copy.wait()


VMEM = pltpu.VMEM
DMA = pltpu.SemaphoreType.DMA
IN_VMEM = pl.BlockSpec(memory_space=pltpu.VMEM)
IN_SMEM = pl.BlockSpec(memory_space=pltpu.SMEM)
IN_ANY = pl.BlockSpec(memory_space=pl.ANY)


def shape(*dims, dtype=BF16):
    return jax.ShapeDtypeStruct(dims, dtype)


def params(cid=None, limit=60 << 20):
    if cid is None:
        return pltpu.CompilerParams(vmem_limit_bytes=limit)
    return pltpu.CompilerParams(collective_id=cid, has_side_effects=True, vmem_limit_bytes=limit)


def local(
    inputs, cotangent, adapter_choice_per_tree, segment_lengths, segment_parents, norm_gain_rows, query_dimension_scale,
    attention_weights, output_weight, feedforward_weights, adapter_first_input, adapter_second_attention, adapter_second_up,
    adapter_first_output, adapter_first_down, adapter_second_residual,
):
    ndp, nt = lax.axis_size("dp"), lax.axis_size("tensor")
    tok, width = inputs.shape
    tree = tok * nt
    wrows, hcols = output_weight.shape
    heads = hcols // HD
    pad = heads * 128
    rank = adapter_first_input.shape[3]
    nblk = tree // BLK
    a_in, a_out, a_down = (jnp.swapaxes(table, -1, -2) for table in (adapter_first_input, adapter_first_output, adapter_first_down))

    chunks = 4
    halves = (5, BLK // 2, 128)
    swapped = (nt, tok // BLK) + halves
    count = a_in.shape[1]
    sides = row_parts(wrows)
    packed = (2 * sides + 1, wrows // sides, 128)
    flat = (3 * packed[0],) + packed[1:]
    tall = (heads, tree, 128)
    wall, choices, mixed, xn, q, qt, k, kt, v, ranks, mixt, wp, bp, at_qkv, scale = pl.pallas_call(
        functools.partial(forward_kernel, ndp, chunks),
        out_shape=[shape(ndp, nt, *flat), shape(ndp, 8, 128, dtype=F32), shape(*swapped), shape(tree, width),
                   shape(*tall), shape(heads, 128, tree), shape(*tall), shape(heads, HD, tree), shape(*tall),
                   shape(tree, 3 * rank), shape(hcols, tree), shape(3, width, pad), shape(3, 3 * rank, pad), shape(3 * rank, width),
                   shape(1, pad, dtype=F32)],
        in_specs=[IN_SMEM] * 3 + [IN_VMEM] * 3 + [IN_ANY] * 5, out_specs=[IN_ANY] * 15,
        scratch_shapes=[VMEM((3, count, rank, width), BF16), VMEM((3, count, rank, width), BF16), VMEM((8, 128), F32), VMEM((3 * rank, width), BF16),
                        VMEM((1, pad), F32), VMEM((8, 128), F32), VMEM((128, 128), BF16), VMEM((pad, width), BF16),
                        VMEM((3, wrows, hcols), BF16), VMEM((3, wrows, hcols), BF16), VMEM((3, *packed), BF16), VMEM(flat, BF16), VMEM((tree, width), BF16),
                        VMEM((ndp, 3, *packed), BF16),
                        VMEM((3, width, pad), BF16), VMEM((3, 3 * rank, pad), BF16), VMEM(tall, BF16), VMEM((heads, 128, tree), BF16),
                        VMEM(tall, BF16), VMEM((heads, HD, tree), BF16), VMEM(tall, BF16), VMEM((heads, HD + 16, tree), BF16),
                        VMEM((tree, 3 * rank), BF16), VMEM((hcols, tree), BF16), VMEM((nblk, *halves), BF16),
                        VMEM((heads, 1, BLK), F32), VMEM((heads, HD + 16, BLK), F32), DMA((5,)), DMA((12,)),
                        DMA((3, chunks)), DMA((nt, chunks)), DMA((3, ndp, 3)), DMA((ndp, 3)), DMA((3, ndp)), DMA((ndp,)),
                        DMA((2, ndp, nt, 4)), DMA((2,)), DMA((2, ndp, nt)), DMA((nblk,)), DMA((nt, tok // BLK))],
        compiler_params=params(1), name="forward",
    )(adapter_choice_per_tree, segment_lengths, segment_parents, inputs, norm_gain_rows, query_dimension_scale[None, :], a_in,
      adapter_second_attention, attention_weights, output_weight,
      feedforward_weights)

    output, d_mid, d_mix, g_mid = pl.pallas_call(
        mid_kernel,
        out_shape=[shape(tok, width), shape(tok, width, dtype=F32), shape(*swapped), shape(6, rank, width, dtype=F32)],
        in_specs=[IN_SMEM] + [IN_VMEM] * 4 + [IN_ANY] * 6, out_specs=[IN_VMEM] * 4,
        scratch_shapes=[VMEM((3, rank, width), BF16), VMEM((3, rank, width), BF16), DMA((6,)), VMEM((tok, width), BF16), VMEM((tok, width), F32), VMEM((tok, width), BF16), VMEM((tok, width), F32),
                        VMEM((tok, width), BF16), VMEM((tok, width), F32), VMEM((tok, width), BF16), VMEM((3, width, width), BF16)]
        + [VMEM((ndp, nt, *packed), BF16)] * 3 + [DMA((3,))],
        compiler_params=params(), name="middle",
    )(adapter_choice_per_tree, inputs, cotangent, mixed, norm_gain_rows, wall, a_out, a_in, a_down, adapter_second_up, adapter_second_residual)
    gr = 6 * rank
    half_rows = gr // 2
    half, hb, per = nblk // 2, BLK // 2, tok // BLK
    grad_bufs = [VMEM((2, half_rows, width), BF16), VMEM((2, half_rows, width), BF16), VMEM((half_rows, width), BF16), VMEM((half_rows, width), BF16)]
    grad_sems = [DMA((2,)), DMA((2,)), DMA((3, ndp)), DMA((ndp,)), DMA((ndp,)), DMA((ndp,)), DMA((1,))]
    input_grad, grads_mid, grads_attn = pl.pallas_call(
        functools.partial(back_kernel, ndp),
        out_shape=[shape(tok, width, dtype=F32), shape(2, ndp, half_rows, width), shape(2, ndp, half_rows, width)],
        in_specs=[IN_ANY] * 12 + [IN_VMEM] * 5, out_specs=[IN_ANY] * 3,
        scratch_shapes=[VMEM((hcols, tree), BF16), VMEM(tall, BF16), VMEM((heads, 128, tree), BF16), VMEM(tall, BF16), VMEM((heads, HD, tree), BF16),
                        VMEM(tall, BF16), VMEM((3, width, pad), BF16), VMEM((tree, width), BF16), VMEM((tree, 3 * rank), BF16),
                        VMEM((tok, width), BF16), VMEM((tok, width), F32), VMEM(swapped, BF16), VMEM(tall, BF16), VMEM((heads, 128, tree), BF16),
                        VMEM((heads, HD, tree), F32), VMEM(tall, F32), VMEM(tall, F32), VMEM((nblk, BLK, width), BF16), VMEM((half, hb, width), BF16),
                        VMEM((half, hb, width), BF16), VMEM((per, BLK, width), BF16), VMEM((per, BLK, width), BF16),
                        VMEM((3 * rank, width), F32), VMEM((3, 3 * rank, pad), F32), VMEM((pad, width), BF16)]
        + grad_bufs + grad_bufs + [DMA((11,)), DMA((4,)), DMA((nt,)), DMA((half,)), DMA((half,)), DMA((half,)), DMA((per, 2)), DMA((per,)), DMA((per,)), DMA((1,))]
        + grad_sems + grad_sems,
        compiler_params=params(4, 62 << 20), name="back",
    )(d_mix, mixt, q, qt, k, kt, v, wp, xn, ranks, inputs, d_mid, scale, bp, at_qkv, norm_gain_rows, g_mid.reshape(gr, width))

    table = shape(count, rank, width, dtype=F32)
    ga_in, gb_qkv, gb_up, ga_out, ga_down, gb_res = pl.pallas_call(
        place_kernel,
        out_shape=[shape(4, count, rank, width, dtype=F32), shape(3, count, rank, width, dtype=F32), table, table, table,
                   shape(2, count, rank, width, dtype=F32)],
        in_specs=[IN_SMEM] + [IN_VMEM] * 2, out_specs=[IN_ANY] * 6,
        scratch_shapes=[VMEM((12, count, rank, width), F32), DMA((12,))], compiler_params=params(), name="place",
    )(choices, grads_mid, grads_attn)
    return (output, input_grad, jnp.swapaxes(ga_in, 2, 3), gb_qkv, gb_up, jnp.swapaxes(ga_out, 1, 2), jnp.swapaxes(ga_down, 1, 2), gb_res)


def solution(mesh):
    tokens, weights = P(("dp", "tensor"), None), P(None, "dp", "tensor")
    in_specs = (tokens, tokens, P("dp"), P("dp", None), P("dp", None), P(), P(), weights, P("dp", "tensor"), weights) + (P(),) * 6
    out_specs = (tokens, tokens) + (P(),) * 6
    return jax.shard_map(local, mesh=mesh, in_specs=in_specs, out_specs=out_specs, check_vma=False)
```

```python
import functools
import math

import jax
import jax.numpy as jnp
from jax import lax
from jax.experimental import pallas as pl
from jax.experimental.pallas import tpu as pltpu
from jax.sharding import PartitionSpec as P

F32, BF16 = jnp.float32, jnp.bfloat16
BIG = 1e30
BLK = 256
HD = 80

def dot(a, b):
    return lax.dot_general(a, b, (((1,), (0,)), ((), ())), preferred_element_type=F32)
def dot_nt(a, b):
    return lax.dot_general(a, b, (((1,), (1,)), ((), ())), preferred_element_type=F32)
def dot_tn(a, b):
    return lax.dot_general(a, b, (((0,), (0,)), ((), ())), preferred_element_type=F32)

def project(b, s, x_ref, wp_ref, a_ref, bp_ref, scale_ref, seg_ref, mq_ref, n_ref, t_ref, rank_ref):
    rows = pl.ds(pl.multiple_of(b * BLK, BLK), BLK)
    xb = x_ref[rows, :]
    if s == 0:
        rank_ref[rows, :] = dot_nt(xb, a_ref[...]).astype(BF16)
    lane = lax.broadcasted_iota(jnp.int32, (BLK, 128), 1)
    if s == 2:
        feat = jnp.where(lane < HD + 2, 1.0, 0.0)
    else:
        tok = (lax.broadcasted_iota(jnp.int32, (BLK, 128), 0) + b * BLK).astype(F32)
        feat = jnp.where((tok >= seg_ref[0:1, :]) & (tok < seg_ref[1:2, :]), 1.0, 0.0)
        if s == 0:
            feat = dot(feat.astype(BF16), mq_ref[...])
        else:
            feat = jnp.where((lane >= HD + 13) & (lane < HD + 16), 1.0, feat)
    y = dot(xb, wp_ref[s]) + dot(rank_ref[rows, :], bp_ref[s])
    if s == 0:
        y = y * scale_ref[...]
    for h in range(n_ref.shape[0]):
        yh = jnp.where(lane < HD, y[:, h * 128:(h + 1) * 128], feat)
        n_ref[h, rows, :] = yh.astype(BF16)
        t_ref[h, :, rows] = yh.T[:t_ref.shape[1]].astype(BF16)

def attend_block(i, c, qt_ref, k_ref, vt_ref, m_ref, acc_ref, mixt_ref, mix_ref):
    heads = qt_ref.shape[0]
    cols = pl.ds(pl.multiple_of(i * BLK, BLK), BLK)
    m_ref[...] = jnp.full_like(m_ref, -3e38)
    acc_ref[...] = jnp.zeros_like(acc_ref)
    def step(j, diag):
        rows = pl.ds(pl.multiple_of(j * BLK, BLK), BLK)
        hs = range(heads)
        ss = [dot(k_ref[h, rows, :], qt_ref[h, :, cols]) for h in hs]
        if diag:
            low = lax.broadcasted_iota(jnp.int32, ss[0].shape, 0) <= lax.broadcasted_iota(jnp.int32, ss[0].shape, 1)
            ss = [jnp.where(low, s, -BIG) for s in ss]
        olds = [m_ref[h] for h in hs]
        news = [jnp.maximum(olds[h], jnp.max(ss[h], axis=0, keepdims=True)) for h in hs]
        ps = [jnp.exp(ss[h] - news[h]).astype(BF16) for h in hs]
        pv = [dot(vt_ref[h, :, rows], ps[h]) for h in hs]
        accs = [acc_ref[h] * jnp.exp(olds[h] - news[h]) + pv[h] for h in hs]
        for h in hs:
            acc_ref[h] = accs[h]
            m_ref[h] = news[h]
    lax.fori_loop(0, i, lambda j, n: (step(j, False), n)[1], 0)
    step(i, True)
    outs = []
    for h in range(heads):
        acc = acc_ref[h]
        l = acc[HD:HD + 1]
        o = acc[:HD] * (1.0 / l)
        lse = m_ref[h] + jnp.log(l)
        hi = (-lse).astype(BF16).astype(F32)
        mid = (-lse - hi).astype(BF16).astype(F32)
        lo = -lse - hi - mid
        r = lax.broadcasted_iota(jnp.int32, (16, BLK), 0)
        old = qt_ref[h, HD:HD + 16, cols].astype(F32)
        new = jnp.where(r == 13, hi, jnp.where(r == 14, mid, jnp.where(r == 15, lo, old)))
        qt_ref[h, HD:HD + 16, cols] = new.astype(BF16)
        outs.append(o)
    ot = jnp.concatenate(outs, axis=0)
    mixt_ref[:, cols] = ot.astype(BF16)
    half = BLK // 2
    full = jnp.where(c == 0, ot[:256], ot[64:]).T.astype(BF16)
    rest = jnp.where(c == 0, ot[256:], ot[:64])
    first, second = rest[:, :half], rest[:, half:]
    for r in range(2):
        for k in range(2):
            mix_ref[i, 2 * k + r] = full[r * half:(r + 1) * half, k * 128:(k + 1) * 128]
    mix_ref[i, 4] = jnp.concatenate([jnp.where(c == 0, first, second), jnp.where(c == 0, second, first)], axis=0).T.astype(BF16)

def row_parts(rows):
    return 2 if rows % 32 == 0 else 1

def third_lanes(j, part, c):
    return (j >> 6) == (part + c) % 2, (j & 63) + 256 * (1 - c)

def pack_block(block, c, store):
    rows, cols = block.shape
    parts = row_parts(rows)
    size = rows // parts
    src = lax.broadcasted_iota(jnp.int32, (cols, 256), 0)
    dst = lax.broadcasted_iota(jnp.int32, (cols, 256), 1)
    full = dot(block, jnp.where(src == dst + 64 * c, 1.0, 0.0).astype(BF16)).astype(BF16)
    rest = jnp.zeros((size, 128), F32)
    for r in range(parts):
        store(r, full[r * size:(r + 1) * size, :128])
        store(parts + r, full[r * size:(r + 1) * size, 128:])
        held, col = third_lanes(dst[:, :128], r, c)
        rest = rest + dot(block[r * size:(r + 1) * size], jnp.where(held & (src[:, :128] == col), 1.0, 0.0).astype(BF16))
    store(2 * parts, rest.astype(BF16))

def spread_heads(c, parts, pad):
    def matrix(k, held, col):
        l = lax.broadcasted_iota(jnp.int32, (k, pad), 1)
        return jnp.where(held & ((l & 127) < HD) & ((l >> 7) * HD + (l & 127) == col), 1.0, 0.0).astype(BF16)
    lane = lax.broadcasted_iota(jnp.int32, (256, 1), 0)
    rest = lax.broadcasted_iota(jnp.int32, (128, 1), 0)
    return matrix(256, lane >= 0, lane + 64 * c), [matrix(128, *third_lanes(rest, r, c)) for r in range(parts)]

def head_columns(me, pad, width):
    l = lax.broadcasted_iota(jnp.int32, (pad, width), 0)
    col = lax.broadcasted_iota(jnp.int32, (pad, width), 1)
    put = ((l & 127) < HD) & (me.t * (pad // 128 * HD) + (l >> 7) * HD + (l & 127) == col)
    return jnp.where(put, 1.0, 0.0).astype(BF16)

def tree_masks(len_ref, par_ref, seg_ref, mq_ref):
    segs = len_ref.shape[1]
    lane = lax.broadcasted_iota(jnp.int32, (1, 128), 1) - HD
    row = lax.broadcasted_iota(jnp.int32, (128, 1), 0) - HD
    lo = hi = jnp.zeros((1, 128), jnp.int32)
    up = grand = jnp.full((128, 1), -1, jnp.int32)
    start = 0
    for u in range(segs):
        end = start + len_ref[0, u]
        parent = par_ref[0, u]
        lo = jnp.where(lane == u, start, lo)
        hi = jnp.where(lane == u, end, hi)
        up = jnp.where(row == u, parent, up)
        grand = jnp.where(row == u, par_ref[0, parent], grand)
        start = end
    seg_ref[0:1, :] = lo.astype(F32)
    seg_ref[1:2, :] = hi.astype(F32)
    reach = (lane == row) | (lane == up) | (lane == grand)
    inside = (row >= 0) & (row < segs) & (lane >= 0) & (lane < segs)
    mq_ref[...] = jnp.where(inside & jnp.logical_not(reach), -BIG, 0.0).astype(BF16)

def bwd_prep(b, c, dm_ref, mixt_ref, do_ref, dot_ref):
    rows = pl.ds(pl.multiple_of(b * BLK, BLK), BLK)
    heads = do_ref.shape[0]
    t, i = b // dm_ref.shape[1], b % dm_ref.shape[1]
    full = [jnp.concatenate([dm_ref[t, i, 2 * k + r].astype(F32).T for r in range(2)], axis=1) for k in range(2)]
    rest = dm_ref[t, i, 4].astype(F32).T
    low, high = rest[:64], rest[64:]
    rest = jnp.concatenate([jnp.where(c == 0, low, high), jnp.where(c == 0, high, low)], axis=1)
    dt = jnp.where(c == 0, jnp.concatenate(full + [rest], axis=0), jnp.concatenate([rest] + full, axis=0))
    prod = dt * mixt_ref[:, rows].astype(F32)
    r = lax.broadcasted_iota(jnp.int32, (16, BLK), 0)
    for h in range(heads):
        d = dt[h * HD:(h + 1) * HD]
        delta = -jnp.sum(prod[h * HD:(h + 1) * HD], axis=0, keepdims=True)
        hi = delta.astype(BF16).astype(F32)
        ext = jnp.where(r == 0, hi, jnp.where(r == 1, delta - hi, 0.0))
        full = jnp.concatenate([d, ext, jnp.zeros((32, BLK), F32)], axis=0)
        dot_ref[h, :, rows] = full.astype(BF16)
        do_ref[h, rows, :] = full.T.astype(BF16)

def bwd_pair(i, j, diag, q_ref, qt_ref, k_ref, kt_ref, v_ref, do_ref, dot_ref, dqt_ref, dk_ref, dv_ref):
    heads = q_ref.shape[0]
    cols = pl.ds(pl.multiple_of(i * BLK, BLK), BLK)
    rows = pl.ds(pl.multiple_of(j * BLK, BLK), BLK)
    hs = range(heads)
    ss = [dot(k_ref[h, rows, :], qt_ref[h, :, cols]) for h in hs]
    dps = [dot(v_ref[h, rows, :], dot_ref[h, :, cols]) for h in hs]
    if diag:
        low = lax.broadcasted_iota(jnp.int32, ss[0].shape, 0) <= lax.broadcasted_iota(jnp.int32, ss[0].shape, 1)
        ss = [jnp.where(low, s, -BIG) for s in ss]
    ps = [jnp.exp(s) for s in ss]
    dss = [(p * dp).astype(BF16) for p, dp in zip(ps, dps)]
    ps = [p.astype(BF16) for p in ps]
    dvs = [dot(ps[h], do_ref[h, cols, :]) for h in hs]
    dks = [dot(dss[h], q_ref[h, cols, :]) for h in hs]
    dqs = [dot(kt_ref[h, :, rows], dss[h]) for h in hs]
    for h in hs:
        dv_ref[h, rows, :] += dvs[h]
        dk_ref[h, rows, :] += dks[h]
        dqt_ref[h, :, cols] += dqs[h]

MESH = pl.DeviceIdType.MESH


class Place:
    def __init__(self, ndp):
        self.d, self.t = lax.axis_index("dp"), lax.axis_index("tensor")
        self.line = ndp // 2
        self.p, self.par = self.d // 2, self.d % 2
        self.dx = self.d + 1 - 2 * self.par
        self.c, self.y = self.t % 2, self.t // 2
        self.t1 = self.t + 1 - 2 * self.c
        self.t2 = (self.t + 2) % 4
        self.t3 = (self.t1 + 2) % 4
        self.has_left, self.has_right = self.p > 0, self.p < self.line - 1


def signal(sem, d, t):
    pl.semaphore_signal(sem, inc=1, device_id=(d, t), device_id_type=MESH)


def remote(src, dst, send_sem, recv_sem, d, t):
    return pltpu.make_async_remote_copy(src_ref=src, dst_ref=dst, send_sem=send_sem, recv_sem=recv_sem, device_id=(d, t), device_id_type=MESH)


def greet(me, tensor=(), pair=False, line=False):
    bar = pltpu.get_barrier_semaphore()
    count = len(tensor) + (1 if pair else 0)
    for t in tensor:
        signal(bar, me.d, t)
    if pair:
        signal(bar, me.dx, me.t)
    if line:
        @pl.when(me.has_left)
        def _():
            signal(bar, me.d - 2, me.t)
        @pl.when(me.has_right)
        def _():
            signal(bar, me.d + 2, me.t)
        count = count + jnp.where(me.has_left, 1, 0) + jnp.where(me.has_right, 1, 0)
    pl.semaphore_wait(bar, count)


class PairLine:
    def __init__(self, me, own, buf, send, recv, part=None):
        self.me, self.own, self.buf, self.send, self.recv, self.part = me, own, buf, send, recv, part

    def slot(self, o):
        return self.buf.at[o] if self.part is None else self.buf.at[o, self.part]

    def copy(self, o, src, d, kind):
        send, recv = (self.send.at[kind, o], self.recv.at[o]) if self.part is None else (self.send.at[kind, o, self.part], self.recv.at[o, self.part])
        return remote(src, self.slot(o), send, recv, d, self.me.t)

    def start(self):
        me = self.me
        @pl.when(me.has_left)
        def _():
            self.copy(me.d, self.own, me.d - 2, 0).start()
        @pl.when(me.has_right)
        def _():
            self.copy(me.d, self.own, me.d + 2, 1).start()
        self.copy(me.d, self.own, me.dx, 2).start()

    def hop(self, k, then=None):
        me = self.me
        @pl.when(me.p - k >= 0)
        def _():
            o = me.d - 2 * k
            self.copy(o, self.slot(o), me.dx, 2).wait_recv()
            @pl.when(me.has_right)
            def _():
                self.copy(o, self.slot(o), me.d + 2, 1).start()
            self.copy(o, self.slot(o), me.dx, 2).start()
            if then is not None:
                then(o)
        @pl.when(me.p + k < me.line)
        def _():
            o = me.d + 2 * k
            self.copy(o, self.slot(o), me.dx, 2).wait_recv()
            @pl.when(me.has_left)
            def _():
                self.copy(o, self.slot(o), me.d - 2, 0).start()
            self.copy(o, self.slot(o), me.dx, 2).start()
            if then is not None:
                then(o)

    def pair_arrivals(self, then=None):
        def one(q, c):
            o = 2 * q + 1 - self.me.par
            self.copy(o, self.slot(o), self.me.dx, 2).wait_recv()
            if then is not None:
                then(o)
            return c
        lax.fori_loop(0, self.me.line, one, 0)

    def sent(self):
        me = self.me
        def one(q, c):
            o = 2 * q + me.par
            self.copy(o, self.slot(o), me.dx, 2).wait_send()
            @pl.when((q >= me.p) & me.has_left)
            def _():
                self.copy(o, self.slot(o), me.dx, 0).wait_send()
            @pl.when((q <= me.p) & me.has_right)
            def _():
                self.copy(o, self.slot(o), me.dx, 1).wait_send()
            return c
        lax.fori_loop(0, me.line, one, 0)


class FullGather:
    def __init__(self, me, own, buf, send, first, recv):
        self.me, self.own, self.buf, self.send, self.first, self.recv = me, own, buf, send, first, recv
        cut = own.shape[0] // 3
        self.parts = (pl.ds(0, cut), pl.ds(cut, own.shape[0] - cut))

    def copy(self, h, o, t, d2, t2, kind, own=False):
        rows = self.parts[h]
        src = self.own.at[rows] if own else self.buf.at[o, t, rows]
        sem = self.first.at[h] if kind == 4 else self.send.at[h, o, t, kind]
        return remote(src, self.buf.at[o, t, rows], sem, self.recv.at[h, o, t], d2, t2)

    def last(self, h):
        me = self.me
        return (me.d, me.t2) if h == 0 else (me.dx, me.t)

    def spread(self, h, o, t, left, right, own=False):
        me = self.me
        @pl.when(left)
        def _():
            self.copy(h, o, t, me.d - 2, me.t, 0, own).start()
        @pl.when(right)
        def _():
            self.copy(h, o, t, me.d + 2, me.t, 1, own).start()
        self.copy(h, o, t, *self.last(h), 2, own).start()
        self.copy(h, o, t, me.d, me.t1, 3, own).start()

    def start(self):
        me = self.me
        self.copy(0, me.d, me.t, me.dx, me.t, 4, True).start()
        self.copy(1, me.d, me.t, me.d, me.t2, 4, True).start()
        for h in (1, 0):
            self.spread(h, me.d, me.t, me.has_left, me.has_right, True)

    def arrived(self, h, o, t):
        self.copy(h, o, t, self.me.d, self.me.t1, 3).wait_recv()

    def firsts(self):
        me = self.me
        self.arrived(0, me.dx, me.t)
        self.spread(0, me.dx, me.t, me.has_left, me.has_right)
        self.arrived(1, me.d, me.t2)
        self.spread(1, me.d, me.t2, me.has_left, me.has_right)

    def streams(self, q):
        me = self.me
        return ((0, 2 * q + me.par, me.t), (0, 2 * q + 1 - me.par, me.t), (1, 2 * q + me.par, me.t), (1, 2 * q + me.par, me.t2))

    def hop(self, k):
        me = self.me
        @pl.when(me.p - k >= 0)
        def _():
            for h, o, t in self.streams(me.p - k):
                self.arrived(h, o, t)
                self.spread(h, o, t, False, me.has_right)
        @pl.when(me.p + k < me.line)
        def _():
            for h, o, t in self.streams(me.p + k):
                self.arrived(h, o, t)
                self.spread(h, o, t, me.has_left, False)

    def lasts(self, k):
        me = self.me

        def place(q):
            for h, o, t in ((0, 2 * q, me.t2), (0, 2 * q + 1, me.t2), (1, 2 * q + 1 - me.par, me.t), (1, 2 * q + 1 - me.par, me.t2)):
                self.arrived(h, o, t)
                self.copy(h, o, t, me.d, me.t1, 3).start()

        @pl.when(me.p - k >= 0)
        def _():
            place(me.p - k)
        @pl.when((me.p + k < me.line) & (k > 0))
        def _():
            place(me.p + k)

    def finish(self):
        me = self.me
        def one(o, c):
            for h in range(2):
                self.arrived(h, o, me.t1)
                self.arrived(h, o, me.t3)
                for t in (me.t, me.t2):
                    self.copy(h, o, t, me.d, me.t1, 3).wait_send()
            return c
        lax.fori_loop(0, 2 * me.line, one, 0)
        def two(q, c):
            for h, o, t in self.streams(q):
                self.copy(h, o, t, me.d, me.t1, 2).wait_send()
                @pl.when((q >= me.p) & me.has_left)
                def _():
                    self.copy(h, o, t, me.d, me.t1, 0).wait_send()
                @pl.when((q <= me.p) & me.has_right)
                def _():
                    self.copy(h, o, t, me.d, me.t1, 1).wait_send()
            return c
        lax.fori_loop(0, me.line, two, 0)
        for h in range(2):
            self.copy(h, me.d, me.t, me.d, me.t1, 4).wait_send()


EPS = 1e-6


def forward_kernel(ndp, chunks, choice_in, len_ref, par_ref, x_ref, gain_ref, qs_ref, ain_h, btab_h, a_ref, wo_ref, wf_ref,
                   wout_ref, cho_ref, mixed_ref, xno_ref, qo_ref, qto_ref, ko_ref, kto_ref, vo_ref, ranko_ref, mixto_ref, wpo_ref, bpo_ref, ato_ref, scaleo_ref,
                   ain_ref, btab_ref, choice_ref, at_ref, scale_ref, seg_ref, mq_ref, put_ref,
                   araw_ref, wraw_ref, aown_ref, wown_ref, xn_ref, wa_ref, wp_ref, bp_ref, q_ref, qt_ref, k_ref, kt_ref, v_ref, vt_ref, rank_ref, mixt_ref,
                   mix_ref, m_ref, acc_ref, ls, os, xs, xr, a_s, a_r, c_s, c_r, w_s, w_f, w_r, ms, mr):
    me = Place(ndp)
    tok, width = x_ref.shape
    loads = [pltpu.make_async_copy(a_ref, araw_ref, ls.at[0]), pltpu.make_async_copy(wo_ref, wraw_ref.at[0], ls.at[1]),
             pltpu.make_async_copy(wf_ref, wraw_ref.at[pl.ds(1, 2)], ls.at[2])]
    tables = [pltpu.make_async_copy(ain_h.at[pl.ds(0, 3)], ain_ref, ls.at[3]), pltpu.make_async_copy(btab_h, btab_ref, ls.at[4])]
    for copy in loads + tables:
        copy.start()
    e = choice_in[0]
    choice_ref[...] = jnp.zeros_like(choice_ref) + e.astype(F32)
    x = x_ref[...].astype(F32)
    mine = pl.ds(pl.multiple_of(me.t * tok, tok), tok)
    xn_ref[mine, :] = (x * lax.rsqrt(jnp.mean(x * x, axis=-1, keepdims=True) + EPS) * gain_ref[0:1, :]).astype(BF16)
    greet(me, tensor=(me.t1, me.t2, me.t3), pair=True, line=True)
    size = tok // chunks

    def xcopy(o, c, t, kind):
        rows = pl.ds(pl.multiple_of(o * tok + c * size, size), size)
        return remote(xn_ref.at[rows], xn_ref.at[rows], xs.at[kind, c], xr.at[o, c], me.d, t)

    for c in range(chunks):
        xcopy(me.t, c, me.t2, 0).start()
    for c in range(chunks):
        xcopy(me.t, c, me.t1, 1).start()
    for copy in loads:
        copy.wait()
    pieces = aown_ref.shape[1]

    def pack(raw_ref, own_ref, n, index):
        def store(k, v):
            own_ref[index(n, k)] = v
        pack_block(raw_ref[n], me.c, store)
    for n in range(3):
        pack(araw_ref, aown_ref, n, lambda n, k: (n, k))
    parts = [PairLine(me, aown_ref.at[n], wa_ref, a_s, a_r, n) for n in range(3)]
    ch = PairLine(me, choice_ref, cho_ref, c_s, c_r)
    w = FullGather(me, wown_ref, wout_ref, w_s, w_f, w_r)
    parts[0].start()
    parts[1].start()
    for n in range(3):
        pack(wraw_ref, wown_ref, n, lambda n, k: n * pieces + k)
    keep = [pltpu.make_async_copy(wown_ref, wout_ref.at[me.d, me.t], ls.at[0]), pltpu.make_async_copy(choice_ref, cho_ref.at[me.d], ls.at[1])]
    for copy in keep:
        copy.start()
    wa_ref[me.d] = aown_ref[...]
    tree_masks(len_ref, par_ref, seg_ref, mq_ref)
    scale_ref[...] = jnp.zeros_like(scale_ref)
    for h in range(q_ref.shape[0]):
        scale_ref[:, h * 128:h * 128 + HD] = qs_ref[...] * (1.0 / math.sqrt(HD))
    put_ref[...] = head_columns(me, *put_ref.shape)
    for copy in tables:
        copy.wait()
    parts[0].hop(1)
    parts[2].start()
    ch.start()

    def diagonal(n, carry):
        for part in range(3):
            k = n - part
            @pl.when((k >= 1) & (k < me.line))
            def _():
                parts[part].hop(k)
        return carry
    lax.fori_loop(2, me.line + 2, diagonal, 0)
    w.start()
    n16 = ain_ref.shape[2]
    for s in range(3):
        at_ref[s * n16:(s + 1) * n16] = ain_ref[s, e]
    picked = jnp.concatenate([btab_ref[s, e] for s in range(3)], axis=0)
    spread = (0.5 * dot_nt(picked, put_ref[...])).astype(BF16)
    bp_ref[...] = jnp.zeros_like(bp_ref)
    for s in range(3):
        bp_ref[s, s * n16:(s + 1) * n16] = spread[s * n16:(s + 1) * n16]

    def forward(c):
        xcopy(me.t2, c, me.t1, 2).wait_recv()
        xcopy(me.t2, c, me.t1, 2).start()

    for c in range(chunks // 2):
        forward(c)
    nblk = xn_ref.shape[0] // BLK
    near = nblk // 2
    half_rows = wa_ref.shape[3]
    sides = pieces // 2
    wrows = half_rows * sides
    sel, sel_rest = spread_heads(me.c, sides, wp_ref.shape[2])

    def spread_weights(s):
        if sides == 1:
            group = 16 // math.gcd(wrows, 16)
            for o in range(0, ndp, group):
                wp_ref[s, o * wrows:(o + group) * wrows] = jnp.concatenate([
                    dot(jnp.concatenate([wa_ref[o + j, s, 0], wa_ref[o + j, s, 1]], axis=1), sel) + dot(wa_ref[o + j, s, 2], sel_rest[0])
                    for j in range(group)], axis=0).astype(BF16)
            return
        flat = [wa_ref[:, s, k].reshape(ndp * half_rows, 128) for k in range(pieces)]
        for r in range(sides):
            y = (dot(jnp.concatenate([flat[r], flat[sides + r]], axis=1), sel) + dot(flat[2 * sides], sel_rest[r])).astype(BF16)
            for o in range(ndp):
                wp_ref[s, o * wrows + r * half_rows:o * wrows + (r + 1) * half_rows] = y[o * half_rows:(o + 1) * half_rows]

    def project_blocks(first, s):
        n_ref, t_ref = ((q_ref, qt_ref), (k_ref, kt_ref), (v_ref, vt_ref))[s]
        lax.fori_loop(0, near, lambda n, c: (project(first + n, s, xn_ref, wp_ref, at_ref, bp_ref, scale_ref, seg_ref, mq_ref, n_ref, t_ref, rank_ref), c)[1], 0)

    for c in range(chunks):
        xcopy(me.t1, c, me.t1, 2).wait_recv()
    for s in range(3):
        parts[s].pair_arrivals()
        spread_weights(s)
        project_blocks(me.y * near, s)
        if s < 2:
            forward(chunks // 2 + s)
    for c in range(chunks):
        xcopy(me.t3, c, me.t1, 2).wait_recv()
    w.firsts()
    for s in range(3):
        project_blocks((1 - me.y) * near, s)

    def hops(i):
        done = 1 + jnp.maximum((me.line - 2) * (i + 1) * (i + 2) + 2 * nblk, 0) // ((nblk - 1) * nblk)
        return jnp.minimum(done, me.line - 1)

    def relay(i):
        lax.fori_loop(hops(i - 1), hops(i), lambda k, c: (w.hop(k + 1), ch.hop(k + 1), c)[2], 0)
    w.hop(1)
    ch.hop(1)
    outs = [pltpu.make_async_copy(src, dst, os.at[n]) for n, (src, dst) in enumerate((
        (xn_ref, xno_ref), (q_ref, qo_ref), (k_ref, ko_ref), (kt_ref, kto_ref), (v_ref, vo_ref), (rank_ref, ranko_ref),
        (wp_ref, wpo_ref), (bp_ref, bpo_ref), (at_ref, ato_ref), (scale_ref, scaleo_ref)))]
    for copy in outs:
        copy.start()
    per = tok // BLK

    def piece(i):
        return mix_ref.at[i], mixed_ref.at[me.t, i % per], i // per

    def attend_step(i, c):
        attend_block(i, me.c, qt_ref, k_ref, vt_ref, m_ref, acc_ref, mixt_ref, mix_ref)
        src, dst, t = piece(i)
        @pl.when(t == me.t)
        def _():
            pltpu.make_async_copy(src, dst, ms.at[i]).start()
        @pl.when(t != me.t)
        def _():
            remote(src, dst, ms.at[i], mr.at[me.t, i % per], me.d, t).start()
        relay(i)
        lax.fori_loop(jnp.where(i == 0, 0, hops(i - 2)), hops(i - 1), lambda k, n: (w.lasts(k), n)[1], 0)
        return c
    lax.fori_loop(0, nblk, attend_step, 0)
    late = [pltpu.make_async_copy(qt_ref, qto_ref, os.at[len(outs)]), pltpu.make_async_copy(mixt_ref, mixto_ref, os.at[len(outs) + 1])]
    for copy in late:
        copy.start()
    lax.fori_loop(hops(nblk - 2), me.line, lambda k, c: (w.lasts(k), c)[1], 0)
    ch.pair_arrivals()
    for t in (me.t1, me.t2, me.t3):
        for h in range(per):
            dst = mixed_ref.at[t, h]
            remote(dst, dst, ms.at[0], mr.at[t, h], me.d, t).wait_recv()
    w.finish()
    for part in parts:
        part.sent()
    ch.sent()
    for c in range(chunks):
        for kind in range(3):
            xcopy(me.t, c, me.t1, kind).wait_send()

    def settle(i, c):
        src, dst, t = piece(i)
        @pl.when(t == me.t)
        def _():
            pltpu.make_async_copy(src, dst, ms.at[i]).wait()
        @pl.when(t != me.t)
        def _():
            remote(src, dst, ms.at[i], mr.at[me.t, i % per], me.d, t).wait_send()
        return c
    lax.fori_loop(0, nblk, settle, 0)
    for copy in keep + outs + late:
        copy.wait()


def sigmoid(v):
    return 1.0 / (1.0 + jnp.exp(-v))


def mid_kernel(e_ref, x_ref, g_ref, mix4_ref, gain_ref, wall_ref, aout_h, ain_h, adown_h, bup_h, bres_h, out_ref, dmid_ref, dmix_ref, grads_ref,
               at_ref, b_ref, ts, mix_ref, mid_ref, hid_ref, up_ref, act_ref, f_ref, low_ref, w_ref, wb0_ref, wb1_ref, wb2_ref, ls):
    width = x_ref.shape[1]
    step = 256
    part = width // mix4_ref.shape[0]
    blocks = (wb0_ref, wb1_ref, wb2_ref)
    ndp, nt, pieces, size = wb0_ref.shape[:4]
    sides = pieces // 2
    loads = [pltpu.make_async_copy(wall_ref.at[:, :, pl.ds(n * pieces, pieces)], blocks[n], ls.at[n]) for n in range(3)]
    e = e_ref[0]
    tables = [pltpu.make_async_copy(src, dst, ts.at[n]) for n, (src, dst) in enumerate((
        (aout_h.at[e], at_ref.at[0]), (ain_h.at[3, e], at_ref.at[1]), (adown_h.at[e], at_ref.at[2]),
        (bres_h.at[0, e], b_ref.at[0]), (bup_h.at[e], b_ref.at[1]), (bres_h.at[1, e], b_ref.at[2])))]
    for copy in tables + loads:
        copy.start()
    for copy in tables:
        copy.wait()

    def join(dst_ref, first_part, y, even, odd):
        pieces, size = even.shape[:2]
        sides = pieces // 2
        low_lane = lax.broadcasted_iota(jnp.int32, (size, 128), 1) < 64
        base = 2 * part * y
        for r in range(sides):
            rows = pl.ds((first_part + r) * size, size)
            dst_ref[rows, base:base + 128] = even[r]
            dst_ref[rows, base + 128:base + 256] = even[sides + r]
            first, second = (even, odd) if r == 0 else (odd, even)
            both = jnp.where(low_lane, first[2 * sides].astype(F32), second[2 * sides].astype(F32))
            dst_ref[rows, base + 256:base + 384] = (both if r == 0 else pltpu.roll(both, 64, 1)).astype(BF16)
            dst_ref[rows, base + 384:base + 512] = odd[r]
            dst_ref[rows, base + 512:base + 640] = odd[sides + r]

    def assemble(n):
        loads[n].wait()
        dst = w_ref.at[n]
        for o in range(ndp):
            for y in range(nt // 2):
                join(dst, o * sides, y, blocks[n].at[o, 2 * y], blocks[n].at[o, 2 * y + 1])

    for y in range(nt // 2):
        for i in range(mix4_ref.shape[1]):
            join(mix_ref, 2 * i, y, mix4_ref.at[2 * y, i], mix4_ref.at[2 * y + 1, i])

    def cols(n):
        return pl.ds(pl.multiple_of(n * step, step), step)

    def each(fn):
        lax.fori_loop(0, width // step, lambda n, c: (fn(cols(n)), c)[1], 0)

    gain = gain_ref[1:2, :]
    r_out = dot_nt(mix_ref[...], at_ref[0]).astype(BF16)
    assemble(0)

    def project_out(n):
        attn = dot_nt(mix_ref[...], w_ref[0, n, :]) + 0.5 * dot(r_out, b_ref[0, :, n])
        mid_ref[:, n] = x_ref[:, n].astype(F32) + attn
    each(project_out)
    middle = mid_ref[...]
    r = lax.rsqrt(jnp.mean(middle * middle, axis=-1, keepdims=True) + EPS)
    hid_ref[...] = (middle * r * gain).astype(BF16)
    r_up = dot_nt(hid_ref[...], at_ref[1]).astype(BF16)
    assemble(1)

    def up_step(n):
        up = dot(hid_ref[...], w_ref[1, :, n]) + 0.5 * dot(r_up, b_ref[1, :, n])
        up_ref[:, n] = up
        act_ref[:, n] = (up * sigmoid(up)).astype(BF16)
    each(up_step)
    r_down = dot_nt(act_ref[...], at_ref[2]).astype(BF16)
    assemble(2)

    def down_step(n):
        down = dot_nt(act_ref[...], w_ref[2, n, :]) + 0.5 * dot(r_down, b_ref[2, :, n])
        out_ref[:, n] = (mid_ref[:, n] + down).astype(BF16)
    each(down_step)
    grads_ref[5] = 0.5 * dot_tn(r_down, g_ref[...])
    dz_down = (0.5 * dot_nt(g_ref[...], b_ref[2])).astype(BF16)
    grads_ref[3] = dot_tn(dz_down, act_ref[...])

    def act_back(n):
        d_act = dot(g_ref[...], w_ref[2, :, n]) + dot(dz_down, at_ref[2, :, n])
        up = up_ref[:, n]
        sg = sigmoid(up)
        low_ref[:, n] = (d_act * sg * (1.0 + up * (1.0 - sg))).astype(BF16)
    each(act_back)
    dz_up = (0.5 * dot_nt(low_ref[...], b_ref[1])).astype(BF16)
    grads_ref[1] = 0.5 * dot_tn(r_up, low_ref[...])
    grads_ref[0] = dot_tn(dz_up, hid_ref[...])

    def hidden_back(n):
        f_ref[:, n] = (dot_nt(low_ref[...], w_ref[1, n, :]) + dot(dz_up, at_ref[1, :, n])) * gain_ref[1:2, n]
    each(hidden_back)
    gd = f_ref[...]
    middle = mid_ref[...]
    s = jnp.mean(middle * gd, axis=-1, keepdims=True)
    d_mid = g_ref[...].astype(F32) + r * gd - middle * (r * r * r * s)
    dmid_ref[...] = d_mid
    low_ref[...] = d_mid.astype(BF16)
    dz_out = (0.5 * dot_nt(low_ref[...], b_ref[0])).astype(BF16)
    grads_ref[4] = 0.5 * dot_tn(r_out, low_ref[...])
    grads_ref[2] = dot_tn(dz_out, mix_ref[...])

    def mixed_back(n):
        act_ref[:, n] = (dot(low_ref[...], w_ref[0, :, n]) + dot(dz_out, at_ref[0, :, n])).astype(BF16)
    each(mixed_back)
    half = dmix_ref.shape[3]
    low_lane = lax.broadcasted_iota(jnp.int32, (half, 128), 1) < 64
    for y in range(nt // 2):
        base = 2 * part * y
        for i in range(dmix_ref.shape[1]):
            halves = [pl.ds((2 * i + r) * half, half) for r in range(2)]
            for r in range(2):
                dmix_ref[2 * y, i, r] = act_ref[halves[r], base:base + 128]
                dmix_ref[2 * y, i, 2 + r] = act_ref[halves[r], base + 128:base + 256]
                dmix_ref[2 * y + 1, i, r] = act_ref[halves[r], base + 384:base + 512]
                dmix_ref[2 * y + 1, i, 2 + r] = act_ref[halves[r], base + 512:base + 640]
            top = act_ref[halves[0], base + 256:base + 384].astype(F32)
            turned = pltpu.roll(act_ref[halves[1], base + 256:base + 384].astype(F32), 64, 1)
            dmix_ref[2 * y, i, 4] = jnp.where(low_lane, top, turned).astype(BF16)
            dmix_ref[2 * y + 1, i, 4] = jnp.where(low_lane, turned, top).astype(BF16)


class GradSum:
    def __init__(self, me, gp, gr, g2, own, out, s, r, ls_, lr, fs, fr, keep):
        self.me, self.gp, self.gr, self.g2, self.own, self.out, self.s, self.r, self.fs, self.fr = me, gp, gr, g2, own, out, s, r, fs, fr
        self.lines = [PairLine(me, own.at[n], out.at[me.c], ls_, lr, n) for n in range(3)]
        self.keep = pltpu.make_async_copy(own, out.at[me.c, me.d], keep)

    def one(self):
        return remote(self.gp.at[1 - self.me.c], self.gr.at[0], self.s.at[0], self.r.at[0], self.me.d, self.me.t1)

    def two(self):
        return remote(self.g2, self.gr.at[1], self.s.at[1], self.r.at[1], self.me.d, self.me.t2)

    def second(self):
        self.one().wait_recv()
        self.g2[...] = (self.gp[self.me.c].astype(F32) + self.gr[0].astype(F32)).astype(BF16)
        self.two().start()

    def relay(self, o, n, own=False):
        src = self.own.at[n] if own else self.out.at[self.me.c, o, n]
        return remote(src, self.out.at[self.me.c, o, n], self.fs.at[o, n], self.fr.at[o, n], self.me.d, self.me.t1)

    def gather(self):
        self.two().wait_recv()
        total = (self.g2[...].astype(F32) + self.gr[1].astype(F32)).astype(BF16)
        size = self.own.shape[1]
        for n in range(3):
            self.own[n] = total[n * size:(n + 1) * size]
        for n in range(3):
            self.lines[n].start()
        for n in range(3):
            self.relay(self.me.d, n, True).start()
        self.keep.start()

    def hop(self, k):
        for n in range(3):
            self.lines[n].hop(k, lambda o: self.relay(o, n).start())

    def arrivals(self):
        for n in range(3):
            self.lines[n].pair_arrivals(lambda o: self.relay(o, n).start())

    def settle(self, ndp):
        def one(o, c):
            for n in range(3):
                self.relay(o, n, True).wait_send()
                remote(self.own.at[n], self.out.at[1 - self.me.c, o, n], self.fs.at[o, n], self.fr.at[o, n], self.me.d, self.me.t1).wait_recv()
            return c
        lax.fori_loop(0, ndp, one, 0)
        for line in self.lines:
            line.sent()
        self.keep.wait()
        self.one().wait_send()
        self.two().wait_send()


def back_kernel(ndp, dmix_ref, mixt_h, q_h, qt_h, k_h, kt_h, v_h, wp_h, xn_h, rank_h, x_h, dmid_h, scale_ref, bp_ref, at_ref, gain_ref, gmid_ref,
                ig_h, gm_h, ga_h,
                mixt_ref, q_ref, qt_ref, k_ref, kt_ref, v_ref, wp_ref, xn_ref, rank_ref, x_ref, dmid_ref, dm_ref, do_ref, dot_ref,
                dqt_ref, dk_ref, dv_ref, dn_ref, r1_ref, s2_ref, r2_ref, ro_ref, ga_ref, gb_ref, put_ref,
                gpm, grm, g2m, gom, gpa, gra, g2a, goa, lsem, dsem, drecv, es, er, s2s, r2r, ros, ror, igs,
                ms, mr, mls, mlr, mfs, mfr, mk, as_, ar, als, alr, afs, afr, ak):
    me = Place(ndp)
    tok = x_ref.shape[0]
    per, hb = tok // BLK, BLK // 2
    nblk = per * dm_ref.shape[0]
    half = nblk // 2
    heads = q_ref.shape[0]
    loads = [pltpu.make_async_copy(src, dst, lsem.at[n]) for n, (src, dst) in enumerate((
        (mixt_h, mixt_ref), (q_h, q_ref), (qt_h, qt_ref), (k_h, k_ref), (kt_h, kt_ref), (v_h, v_ref),
        (wp_h, wp_ref), (xn_h, xn_ref), (rank_h, rank_ref), (x_h, x_ref), (dmid_h, dmid_ref)))]
    n48 = gpm.shape[1]
    for c in range(2):
        gpm[c] = gmid_ref[c * n48:(c + 1) * n48].astype(BF16)
    greet(me, tensor=(me.t1, me.t2, me.t3), pair=True, line=True)

    def swap(n, t):
        return remote(dmix_ref.at[t], dm_ref.at[me.t], dsem.at[n], drecv.at[me.t], me.d, t)

    own = pltpu.make_async_copy(dmix_ref.at[me.t], dm_ref.at[me.t], dsem.at[3])
    for n, t in enumerate((me.t3, me.t2, me.t1)):
        swap(n, t).start()
    own.start()
    gm = GradSum(me, gpm, grm, g2m, gom, gm_h, ms, mr, mls, mlr, mfs, mfr, mk.at[0])
    ga = GradSum(me, gpa, gra, g2a, goa, ga_h, as_, ar, als, alr, afs, afr, ak.at[0])
    gm.one().start()
    for copy in loads:
        copy.start()
    for ref in (dqt_ref, dk_ref, dv_ref, ga_ref, gb_ref):
        ref[...] = jnp.zeros_like(ref)
    put_ref[...] = head_columns(me, *put_ref.shape)
    for copy in loads[:6]:
        copy.wait()

    def prep(t):
        lax.fori_loop(t * per, (t + 1) * per, lambda b, c: (bwd_prep(b, me.c, dm_ref, mixt_ref, do_ref, dot_ref), c)[1], 0)

    args = (q_ref, qt_ref, k_ref, kt_ref, v_ref, do_ref, dot_ref, dqt_ref, dk_ref, dv_ref)

    def block(a):
        return (1 - me.y) * (nblk - 1 - a) + me.y * a

    def others(a, first, last):
        b = block(a)

        def other(n, c):
            bwd_pair(b + me.y * (1 + n), b - (1 - me.y) * (1 + n), False, *args)
            return c
        lax.fori_loop(first, last, other, 0)

    def arrived(t):
        remote(dmix_ref.at[t], dm_ref.at[t], dsem.at[0], drecv.at[t], me.d, t).wait_recv()

    own.wait()
    prep(me.t)
    arrived(me.t1)
    prep(me.t1)
    gm.second()
    lax.fori_loop(half, nblk, lambda a, c: (bwd_pair(block(a), block(a), True, *args), others(a, 0, nblk - 1 - a), c)[2], 0)
    arrived(me.t2)
    prep(me.t2)
    arrived(me.t3)
    prep(me.t3)
    for copy in loads[6:]:
        copy.wait()
    lane = lax.broadcasted_iota(jnp.int32, (BLK, 128), 1)

    def exchange(a):
        rows = pl.ds(pl.multiple_of((1 - me.c) * hb, hb), hb)
        return remote(dn_ref.at[a, rows], r1_ref.at[a], es.at[a], er.at[a], me.d, me.t1)

    def own_block(a):
        return remote(dn_ref.at[a], ro_ref.at[block(a) % per], ros.at[a % per], ror.at[block(a) % per], me.d, me.t1)

    def mine_rows():
        return pl.ds(pl.multiple_of(me.c * hb, hb), hb)

    def deliver(a):
        b = block(a)
        return remote(s2_ref.at[a], r2_ref.at[b % per, mine_rows()], s2s.at[a], r2r.at[b % per, me.c], me.d, b // per)

    def is_mine(a):
        return block(a) // per == me.t

    def pass_on(a):
        exchange(a).wait_recv()
        s2_ref[a] = (dn_ref[a, mine_rows(), :].astype(F32) + r1_ref[a].astype(F32)).astype(BF16)
        deliver(a).start()

    def gradients(a):
        rows = pl.ds(pl.multiple_of(block(a) * BLK, BLK), BLK)
        dq, dk, dv = [], [], []
        for h in range(heads):
            g = jnp.concatenate([dqt_ref[h, :, rows], jnp.zeros((48, BLK), F32)], axis=0).T
            dq.append((g * scale_ref[:, h * 128:(h + 1) * 128]).astype(BF16))
            dk.append(jnp.where(lane < HD, dk_ref[h, rows, :], 0.0).astype(BF16))
            dv.append(jnp.where(lane < HD, dv_ref[h, rows, :], 0.0).astype(BF16))
        ds = [jnp.concatenate(g, axis=1) for g in (dq, dk, dv)]
        return rows, ds, sum(dot_nt(ds[s], bp_ref[s]) for s in range(3)).astype(BF16)

    def adapters(rows, ds, dz):
        ga_ref[...] += dot_tn(dz, xn_ref[rows, :])
        for s in range(3):
            gb_ref[s] += dot_tn(rank_ref[rows, :], ds[s])

    def normed_gradient(a, ds, dz):
        dn = sum(dot_nt(ds[s], wp_ref[s]) for s in range(3)) + dot(dz, at_ref[...])
        dn_ref[a] = dn.astype(BF16)

    def upto(a):
        return 1 + jnp.minimum(a * (me.line - 1) // (nblk - 2), me.line - 1)

    def far_step(a, c):
        bwd_pair(block(a), block(a), True, *args)
        others(a, 0, 2)
        @pl.when(a > 0)
        def _():
            pass_on(a - 1)
        others(a, 2, nblk - 1 - a)
        rows, ds, dz = gradients(a)
        normed_gradient(a, ds, dz)
        exchange(a).start()
        adapters(rows, ds, dz)
        @pl.when(a == 0)
        def _():
            gm.gather()
        lax.fori_loop(upto(a), upto(a + 1), lambda k, n: (gm.hop(k), n)[1], 0)
        return c
    lax.fori_loop(0, half, far_step, 0)

    def near_adapters(a, c):
        adapters(*gradients(a))
        return c
    lax.fori_loop(half, nblk, near_adapters, 0)
    n16 = n48 // 3
    gpa[0] = ga_ref[...].astype(BF16)
    gb = jnp.concatenate([gb_ref[s, s * n16:(s + 1) * n16] for s in range(3)], axis=0)
    gpa[1] = dot((0.5 * gb).astype(BF16), put_ref[...]).astype(BF16)
    ga.one().start()

    def near_step(a, c):
        _, ds, dz = gradients(a)
        normed_gradient(a, ds, dz)
        @pl.when(jnp.logical_not(is_mine(a)))
        def _():
            own_block(a).start()
        @pl.when(a == half)
        def _():
            ga.second()
            pass_on(a - 1)
        lax.fori_loop(upto(a), upto(a + 1), lambda k, n: (gm.hop(k), n)[1], 0)
        return c
    lax.fori_loop(half, nblk, near_step, 0)
    gm.arrivals()
    ga.gather()

    def combine(i, c):
        b = me.t * per + i
        a = block(b)
        rows = pl.ds(pl.multiple_of(i * BLK, BLK), BLK)
        remote(dn_ref.at[a], ro_ref.at[i], ros.at[0], ror.at[i], me.d, me.t1).wait_recv()
        for h in range(2):
            remote(s2_ref.at[0], r2_ref.at[i, pl.ds(h * hb, hb)], s2s.at[0], r2r.at[i, h], me.d, me.t2).wait_recv()
        dn = dn_ref[a].astype(F32) + ro_ref[i].astype(F32) + r2_ref[i].astype(F32)
        x = x_ref[rows, :].astype(F32)
        r = lax.rsqrt(jnp.mean(x * x, axis=-1, keepdims=True) + EPS)
        gd = gain_ref[0:1, :] * dn
        dmid_ref[rows, :] = dmid_ref[rows, :] + r * gd - x * (r * r * r * jnp.mean(x * gd, axis=-1, keepdims=True))
        return c
    lax.fori_loop(1, me.line, lambda k, c: (ga.hop(k), c)[1], 0)
    lax.fori_loop(0, per, combine, 0)
    put_ig = pltpu.make_async_copy(dmid_ref, ig_h, igs.at[0])
    put_ig.start()
    ga.arrivals()
    ga.settle(ndp)
    gm.settle(ndp)

    def sent(a, c):
        exchange(a).wait_send()
        deliver(a).wait_send()
        return c
    lax.fori_loop(0, half, sent, 0)

    def own_sent(a, c):
        @pl.when(jnp.logical_not(is_mine(a)))
        def _():
            own_block(a).wait_send()
        return c
    lax.fori_loop(half, nblk, own_sent, 0)
    for n, t in enumerate((me.t3, me.t2, me.t1)):
        swap(n, t).wait_send()
    put_ig.wait()


def place_kernel(e_ref, gm_ref, ga_ref, ain_h, bqkv_h, bup_h, aout_h, adown_h, bres_h, out_ref, sem):
    ndp = gm_ref.shape[1]
    slots = ([(ga_ref, 0, n, ain_h.at[n]) for n in range(3)] + [(ga_ref, 1, n, bqkv_h.at[n]) for n in range(3)]
             + [(gm_ref, 0, 0, ain_h.at[3]), (gm_ref, 0, 1, bup_h), (gm_ref, 0, 2, aout_h),
                (gm_ref, 1, 0, adown_h), (gm_ref, 1, 1, bres_h.at[0]), (gm_ref, 1, 2, bres_h.at[1])])
    copies = []
    for n, (src, c, k, dst) in enumerate(slots):
        out_ref[n] = jnp.zeros(out_ref.shape[1:], F32)

        def add(d, carry):
            e = e_ref[d, 0, 0].astype(jnp.int32)
            out_ref[n, e] += src[c, d, k].astype(F32)
            return carry
        lax.fori_loop(0, ndp, add, 0)
        copies.append(pltpu.make_async_copy(out_ref.at[n], dst, sem.at[n]))
        copies[-1].start()
    for copy in copies:
        copy.wait()


VMEM = pltpu.VMEM
DMA = pltpu.SemaphoreType.DMA
IN_VMEM = pl.BlockSpec(memory_space=pltpu.VMEM)
IN_SMEM = pl.BlockSpec(memory_space=pltpu.SMEM)
IN_ANY = pl.BlockSpec(memory_space=pl.ANY)


def shape(*dims, dtype=BF16):
    return jax.ShapeDtypeStruct(dims, dtype)


def params(cid=None, limit=60 << 20):
    if cid is None:
        return pltpu.CompilerParams(vmem_limit_bytes=limit)
    return pltpu.CompilerParams(collective_id=cid, has_side_effects=True, vmem_limit_bytes=limit)


def local(
    inputs, cotangent, adapter_choice_per_tree, segment_lengths, segment_parents, norm_gain_rows, query_dimension_scale,
    attention_weights, output_weight, feedforward_weights, adapter_first_input, adapter_second_attention, adapter_second_up,
    adapter_first_output, adapter_first_down, adapter_second_residual,
):
    ndp, nt = lax.axis_size("dp"), lax.axis_size("tensor")
    tok, width = inputs.shape
    tree = tok * nt
    wrows, hcols = output_weight.shape
    heads = hcols // HD
    pad = heads * 128
    rank = adapter_first_input.shape[3]
    nblk = tree // BLK
    a_in, a_out, a_down = (jnp.swapaxes(table, -1, -2) for table in (adapter_first_input, adapter_first_output, adapter_first_down))

    chunks = 4
    halves = (5, BLK // 2, 128)
    swapped = (nt, tok // BLK) + halves
    count = a_in.shape[1]
    sides = row_parts(wrows)
    packed = (2 * sides + 1, wrows // sides, 128)
    flat = (3 * packed[0],) + packed[1:]
    tall = (heads, tree, 128)
    wall, choices, mixed, xn, q, qt, k, kt, v, ranks, mixt, wp, bp, at_qkv, scale = pl.pallas_call(
        functools.partial(forward_kernel, ndp, chunks),
        out_shape=[shape(ndp, nt, *flat), shape(ndp, 8, 128, dtype=F32), shape(*swapped), shape(tree, width),
                   shape(*tall), shape(heads, 128, tree), shape(*tall), shape(heads, HD, tree), shape(*tall),
                   shape(tree, 3 * rank), shape(hcols, tree), shape(3, width, pad), shape(3, 3 * rank, pad), shape(3 * rank, width),
                   shape(1, pad, dtype=F32)],
        in_specs=[IN_SMEM] * 3 + [IN_VMEM] * 3 + [IN_ANY] * 5, out_specs=[IN_ANY] * 15,
        scratch_shapes=[VMEM((3, count, rank, width), BF16), VMEM((3, count, rank, width), BF16), VMEM((8, 128), F32), VMEM((3 * rank, width), BF16),
                        VMEM((1, pad), F32), VMEM((8, 128), F32), VMEM((128, 128), BF16), VMEM((pad, width), BF16),
                        VMEM((3, wrows, hcols), BF16), VMEM((3, wrows, hcols), BF16), VMEM((3, *packed), BF16), VMEM(flat, BF16), VMEM((tree, width), BF16),
                        VMEM((ndp, 3, *packed), BF16),
                        VMEM((3, width, pad), BF16), VMEM((3, 3 * rank, pad), BF16), VMEM(tall, BF16), VMEM((heads, 128, tree), BF16),
                        VMEM(tall, BF16), VMEM((heads, HD, tree), BF16), VMEM(tall, BF16), VMEM((heads, HD + 16, tree), BF16),
                        VMEM((tree, 3 * rank), BF16), VMEM((hcols, tree), BF16), VMEM((nblk, *halves), BF16),
                        VMEM((heads, 1, BLK), F32), VMEM((heads, HD + 16, BLK), F32), DMA((5,)), DMA((12,)),
                        DMA((3, chunks)), DMA((nt, chunks)), DMA((3, ndp, 3)), DMA((ndp, 3)), DMA((3, ndp)), DMA((ndp,)),
                        DMA((2, ndp, nt, 4)), DMA((2,)), DMA((2, ndp, nt)), DMA((nblk,)), DMA((nt, tok // BLK))],
        compiler_params=params(1), name="forward",
    )(adapter_choice_per_tree, segment_lengths, segment_parents, inputs, norm_gain_rows, query_dimension_scale[None, :], a_in,
      adapter_second_attention, attention_weights, output_weight,
      feedforward_weights)

    output, d_mid, d_mix, g_mid = pl.pallas_call(
        mid_kernel,
        out_shape=[shape(tok, width), shape(tok, width, dtype=F32), shape(*swapped), shape(6, rank, width, dtype=F32)],
        in_specs=[IN_SMEM] + [IN_VMEM] * 4 + [IN_ANY] * 6, out_specs=[IN_VMEM] * 4,
        scratch_shapes=[VMEM((3, rank, width), BF16), VMEM((3, rank, width), BF16), DMA((6,)), VMEM((tok, width), BF16), VMEM((tok, width), F32), VMEM((tok, width), BF16), VMEM((tok, width), F32),
                        VMEM((tok, width), BF16), VMEM((tok, width), F32), VMEM((tok, width), BF16), VMEM((3, width, width), BF16)]
        + [VMEM((ndp, nt, *packed), BF16)] * 3 + [DMA((3,))],
        compiler_params=params(), name="middle",
    )(adapter_choice_per_tree, inputs, cotangent, mixed, norm_gain_rows, wall, a_out, a_in, a_down, adapter_second_up, adapter_second_residual)
    gr = 6 * rank
    half_rows = gr // 2
    half, hb, per = nblk // 2, BLK // 2, tok // BLK
    grad_bufs = [VMEM((2, half_rows, width), BF16), VMEM((2, half_rows, width), BF16), VMEM((half_rows, width), BF16), VMEM((3, rank, width), BF16)]
    grad_sems = [DMA((2,)), DMA((2,)), DMA((3, ndp, 3)), DMA((ndp, 3)), DMA((ndp, 3)), DMA((ndp, 3)), DMA((1,))]
    input_grad, grads_mid, grads_attn = pl.pallas_call(
        functools.partial(back_kernel, ndp),
        out_shape=[shape(tok, width, dtype=F32), shape(2, ndp, 3, rank, width), shape(2, ndp, 3, rank, width)],
        in_specs=[IN_ANY] * 12 + [IN_VMEM] * 5, out_specs=[IN_ANY] * 3,
        scratch_shapes=[VMEM((hcols, tree), BF16), VMEM(tall, BF16), VMEM((heads, 128, tree), BF16), VMEM(tall, BF16), VMEM((heads, HD, tree), BF16),
                        VMEM(tall, BF16), VMEM((3, width, pad), BF16), VMEM((tree, width), BF16), VMEM((tree, 3 * rank), BF16),
                        VMEM((tok, width), BF16), VMEM((tok, width), F32), VMEM(swapped, BF16), VMEM(tall, BF16), VMEM((heads, 128, tree), BF16),
                        VMEM((heads, HD, tree), F32), VMEM(tall, F32), VMEM(tall, F32), VMEM((nblk, BLK, width), BF16), VMEM((half, hb, width), BF16),
                        VMEM((half, hb, width), BF16), VMEM((per, BLK, width), BF16), VMEM((per, BLK, width), BF16),
                        VMEM((3 * rank, width), F32), VMEM((3, 3 * rank, pad), F32), VMEM((pad, width), BF16)]
        + grad_bufs + grad_bufs + [DMA((11,)), DMA((4,)), DMA((nt,)), DMA((half,)), DMA((half,)), DMA((half,)), DMA((per, 2)), DMA((per,)), DMA((per,)), DMA((1,))]
        + grad_sems + grad_sems,
        compiler_params=params(4, 62 << 20), name="back",
    )(d_mix, mixt, q, qt, k, kt, v, wp, xn, ranks, inputs, d_mid, scale, bp, at_qkv, norm_gain_rows, g_mid.reshape(gr, width))

    table = shape(count, rank, width, dtype=F32)
    ga_in, gb_qkv, gb_up, ga_out, ga_down, gb_res = pl.pallas_call(
        place_kernel,
        out_shape=[shape(4, count, rank, width, dtype=F32), shape(3, count, rank, width, dtype=F32), table, table, table,
                   shape(2, count, rank, width, dtype=F32)],
        in_specs=[IN_SMEM] + [IN_VMEM] * 2, out_specs=[IN_ANY] * 6,
        scratch_shapes=[VMEM((12, count, rank, width), F32), DMA((12,))], compiler_params=params(), name="place",
    )(choices, grads_mid, grads_attn)
    return (output, input_grad, jnp.swapaxes(ga_in, 2, 3), gb_qkv, gb_up, jnp.swapaxes(ga_out, 1, 2), jnp.swapaxes(ga_down, 1, 2), gb_res)


def solution(mesh):
    tokens, weights = P(("dp", "tensor"), None), P(None, "dp", "tensor")
    in_specs = (tokens, tokens, P("dp"), P("dp", None), P("dp", None), P(), P(), weights, P("dp", "tensor"), weights) + (P(),) * 6
    out_specs = (tokens, tokens) + (P(),) * 6
    return jax.shard_map(local, mesh=mesh, in_specs=in_specs, out_specs=out_specs, check_vma=False)
```

```python
import functools
import math

import jax
import jax.numpy as jnp
from jax import lax
from jax.experimental import pallas as pl
from jax.experimental.pallas import tpu as pltpu
from jax.sharding import PartitionSpec as P

F32, BF16 = jnp.float32, jnp.bfloat16
BIG = 1e30
BLK = 256
HD = 80

def dot(a, b):
    return lax.dot_general(a, b, (((1,), (0,)), ((), ())), preferred_element_type=F32)
def dot_nt(a, b):
    return lax.dot_general(a, b, (((1,), (1,)), ((), ())), preferred_element_type=F32)
def dot_tn(a, b):
    return lax.dot_general(a, b, (((0,), (0,)), ((), ())), preferred_element_type=F32)

def project(b, s, x_ref, wp_ref, a_ref, bp_ref, scale_ref, seg_ref, mq_ref, n_ref, t_ref, rank_ref):
    rows = pl.ds(pl.multiple_of(b * BLK, BLK), BLK)
    xb = x_ref[rows, :]
    if s == 0:
        rank_ref[rows, :] = dot_nt(xb, a_ref[...]).astype(BF16)
    lane = lax.broadcasted_iota(jnp.int32, (BLK, 128), 1)
    if s == 2:
        feat = jnp.where(lane < HD + 2, 1.0, 0.0)
    else:
        tok = (lax.broadcasted_iota(jnp.int32, (BLK, 128), 0) + b * BLK).astype(F32)
        feat = jnp.where((tok >= seg_ref[0:1, :]) & (tok < seg_ref[1:2, :]), 1.0, 0.0)
        if s == 0:
            feat = dot(feat.astype(BF16), mq_ref[...])
        else:
            feat = jnp.where((lane >= HD + 13) & (lane < HD + 16), 1.0, feat)
    y = dot(xb, wp_ref[s]) + dot(rank_ref[rows, :], bp_ref[s])
    if s == 0:
        y = y * scale_ref[...]
    for h in range(n_ref.shape[0]):
        yh = jnp.where(lane < HD, y[:, h * 128:(h + 1) * 128], feat)
        n_ref[h, rows, :] = yh.astype(BF16)
        t_ref[h, :, rows] = yh.T[:t_ref.shape[1]].astype(BF16)

def attend_block(i, c, qt_ref, k_ref, vt_ref, m_ref, acc_ref, mixt_ref, mix_ref):
    heads = qt_ref.shape[0]
    cols = pl.ds(pl.multiple_of(i * BLK, BLK), BLK)
    m_ref[...] = jnp.full_like(m_ref, -3e38)
    acc_ref[...] = jnp.zeros_like(acc_ref)
    def step(j, diag):
        rows = pl.ds(pl.multiple_of(j * BLK, BLK), BLK)
        hs = range(heads)
        ss = [dot(k_ref[h, rows, :], qt_ref[h, :, cols]) for h in hs]
        if diag:
            low = lax.broadcasted_iota(jnp.int32, ss[0].shape, 0) <= lax.broadcasted_iota(jnp.int32, ss[0].shape, 1)
            ss = [jnp.where(low, s, -BIG) for s in ss]
        olds = [m_ref[h] for h in hs]
        news = [jnp.maximum(olds[h], jnp.max(ss[h], axis=0, keepdims=True)) for h in hs]
        ps = [jnp.exp(ss[h] - news[h]).astype(BF16) for h in hs]
        pv = [dot(vt_ref[h, :, rows], ps[h]) for h in hs]
        accs = [acc_ref[h] * jnp.exp(olds[h] - news[h]) + pv[h] for h in hs]
        for h in hs:
            acc_ref[h] = accs[h]
            m_ref[h] = news[h]
    lax.fori_loop(0, i, lambda j, n: (step(j, False), n)[1], 0)
    step(i, True)
    outs = []
    for h in range(heads):
        acc = acc_ref[h]
        l = acc[HD:HD + 1]
        o = acc[:HD] * (1.0 / l)
        lse = m_ref[h] + jnp.log(l)
        hi = (-lse).astype(BF16).astype(F32)
        mid = (-lse - hi).astype(BF16).astype(F32)
        lo = -lse - hi - mid
        r = lax.broadcasted_iota(jnp.int32, (16, BLK), 0)
        old = qt_ref[h, HD:HD + 16, cols].astype(F32)
        new = jnp.where(r == 13, hi, jnp.where(r == 14, mid, jnp.where(r == 15, lo, old)))
        qt_ref[h, HD:HD + 16, cols] = new.astype(BF16)
        outs.append(o)
    ot = jnp.concatenate(outs, axis=0)
    mixt_ref[:, cols] = ot.astype(BF16)
    half = BLK // 2
    full = jnp.where(c == 0, ot[:256], ot[64:]).T.astype(BF16)
    rest = jnp.where(c == 0, ot[256:], ot[:64])
    first, second = rest[:, :half], rest[:, half:]
    for r in range(2):
        for k in range(2):
            mix_ref[i, 2 * k + r] = full[r * half:(r + 1) * half, k * 128:(k + 1) * 128]
    mix_ref[i, 4] = jnp.concatenate([jnp.where(c == 0, first, second), jnp.where(c == 0, second, first)], axis=0).T.astype(BF16)

def row_parts(rows):
    return 2 if rows % 32 == 0 else 1

def third_lanes(j, part, c):
    return (j >> 6) == (part + c) % 2, (j & 63) + 256 * (1 - c)

def pack_block(block, c, store):
    rows, cols = block.shape
    parts = row_parts(rows)
    size = rows // parts
    src = lax.broadcasted_iota(jnp.int32, (cols, 256), 0)
    dst = lax.broadcasted_iota(jnp.int32, (cols, 256), 1)
    full = dot(block, jnp.where(src == dst + 64 * c, 1.0, 0.0).astype(BF16)).astype(BF16)
    rest = jnp.zeros((size, 128), F32)
    for r in range(parts):
        store(r, full[r * size:(r + 1) * size, :128])
        store(parts + r, full[r * size:(r + 1) * size, 128:])
        held, col = third_lanes(dst[:, :128], r, c)
        rest = rest + dot(block[r * size:(r + 1) * size], jnp.where(held & (src[:, :128] == col), 1.0, 0.0).astype(BF16))
    store(2 * parts, rest.astype(BF16))

def spread_heads(c, parts, pad):
    def matrix(k, held, col):
        l = lax.broadcasted_iota(jnp.int32, (k, pad), 1)
        return jnp.where(held & ((l & 127) < HD) & ((l >> 7) * HD + (l & 127) == col), 1.0, 0.0).astype(BF16)
    lane = lax.broadcasted_iota(jnp.int32, (256, 1), 0)
    rest = lax.broadcasted_iota(jnp.int32, (128, 1), 0)
    return matrix(256, lane >= 0, lane + 64 * c), [matrix(128, *third_lanes(rest, r, c)) for r in range(parts)]

def head_columns(me, pad, width):
    l = lax.broadcasted_iota(jnp.int32, (pad, width), 0)
    col = lax.broadcasted_iota(jnp.int32, (pad, width), 1)
    put = ((l & 127) < HD) & (me.t * (pad // 128 * HD) + (l >> 7) * HD + (l & 127) == col)
    return jnp.where(put, 1.0, 0.0).astype(BF16)

def tree_masks(len_ref, par_ref, seg_ref, mq_ref):
    segs = len_ref.shape[1]
    lane = lax.broadcasted_iota(jnp.int32, (1, 128), 1) - HD
    row = lax.broadcasted_iota(jnp.int32, (128, 1), 0) - HD
    lo = hi = jnp.zeros((1, 128), jnp.int32)
    up = grand = jnp.full((128, 1), -1, jnp.int32)
    start = 0
    for u in range(segs):
        end = start + len_ref[0, u]
        parent = par_ref[0, u]
        lo = jnp.where(lane == u, start, lo)
        hi = jnp.where(lane == u, end, hi)
        up = jnp.where(row == u, parent, up)
        grand = jnp.where(row == u, par_ref[0, parent], grand)
        start = end
    seg_ref[0:1, :] = lo.astype(F32)
    seg_ref[1:2, :] = hi.astype(F32)
    reach = (lane == row) | (lane == up) | (lane == grand)
    inside = (row >= 0) & (row < segs) & (lane >= 0) & (lane < segs)
    mq_ref[...] = jnp.where(inside & jnp.logical_not(reach), -BIG, 0.0).astype(BF16)

def bwd_prep(b, c, dm_ref, mixt_ref, do_ref, dot_ref):
    rows = pl.ds(pl.multiple_of(b * BLK, BLK), BLK)
    heads = do_ref.shape[0]
    t, i = b // dm_ref.shape[1], b % dm_ref.shape[1]
    full = [jnp.concatenate([dm_ref[t, i, 2 * k + r].astype(F32).T for r in range(2)], axis=1) for k in range(2)]
    rest = dm_ref[t, i, 4].astype(F32).T
    low, high = rest[:64], rest[64:]
    rest = jnp.concatenate([jnp.where(c == 0, low, high), jnp.where(c == 0, high, low)], axis=1)
    dt = jnp.where(c == 0, jnp.concatenate(full + [rest], axis=0), jnp.concatenate([rest] + full, axis=0))
    prod = dt * mixt_ref[:, rows].astype(F32)
    r = lax.broadcasted_iota(jnp.int32, (16, BLK), 0)
    for h in range(heads):
        d = dt[h * HD:(h + 1) * HD]
        delta = -jnp.sum(prod[h * HD:(h + 1) * HD], axis=0, keepdims=True)
        hi = delta.astype(BF16).astype(F32)
        ext = jnp.where(r == 0, hi, jnp.where(r == 1, delta - hi, 0.0))
        full = jnp.concatenate([d, ext, jnp.zeros((32, BLK), F32)], axis=0)
        dot_ref[h, :, rows] = full.astype(BF16)
        do_ref[h, rows, :] = full.T.astype(BF16)

def bwd_pair(i, j, diag, q_ref, qt_ref, k_ref, kt_ref, v_ref, do_ref, dot_ref, dqt_ref, dk_ref, dv_ref):
    heads = q_ref.shape[0]
    cols = pl.ds(pl.multiple_of(i * BLK, BLK), BLK)
    rows = pl.ds(pl.multiple_of(j * BLK, BLK), BLK)
    hs = range(heads)
    ss = [dot(k_ref[h, rows, :], qt_ref[h, :, cols]) for h in hs]
    dps = [dot(v_ref[h, rows, :], dot_ref[h, :, cols]) for h in hs]
    if diag:
        low = lax.broadcasted_iota(jnp.int32, ss[0].shape, 0) <= lax.broadcasted_iota(jnp.int32, ss[0].shape, 1)
        ss = [jnp.where(low, s, -BIG) for s in ss]
    ps = [jnp.exp(s) for s in ss]
    dss = [(p * dp).astype(BF16) for p, dp in zip(ps, dps)]
    ps = [p.astype(BF16) for p in ps]
    dvs = [dot(ps[h], do_ref[h, cols, :]) for h in hs]
    dks = [dot(dss[h], q_ref[h, cols, :]) for h in hs]
    dqs = [dot(kt_ref[h, :, rows], dss[h]) for h in hs]
    for h in hs:
        dv_ref[h, rows, :] += dvs[h]
        dk_ref[h, rows, :] += dks[h]
        dqt_ref[h, :, cols] += dqs[h]

MESH = pl.DeviceIdType.MESH


class Place:
    def __init__(self, ndp):
        self.d, self.t = lax.axis_index("dp"), lax.axis_index("tensor")
        self.line = ndp // 2
        self.p, self.par = self.d // 2, self.d % 2
        self.dx = self.d + 1 - 2 * self.par
        self.c, self.y = self.t % 2, self.t // 2
        self.t1 = self.t + 1 - 2 * self.c
        self.t2 = (self.t + 2) % 4
        self.t3 = (self.t1 + 2) % 4
        self.has_left, self.has_right = self.p > 0, self.p < self.line - 1


def signal(sem, d, t):
    pl.semaphore_signal(sem, inc=1, device_id=(d, t), device_id_type=MESH)


def remote(src, dst, send_sem, recv_sem, d, t):
    return pltpu.make_async_remote_copy(src_ref=src, dst_ref=dst, send_sem=send_sem, recv_sem=recv_sem, device_id=(d, t), device_id_type=MESH)


def greet(me, tensor=(), pair=False, line=False):
    bar = pltpu.get_barrier_semaphore()
    count = len(tensor) + (1 if pair else 0)
    for t in tensor:
        signal(bar, me.d, t)
    if pair:
        signal(bar, me.dx, me.t)
    if line:
        @pl.when(me.has_left)
        def _():
            signal(bar, me.d - 2, me.t)
        @pl.when(me.has_right)
        def _():
            signal(bar, me.d + 2, me.t)
        count = count + jnp.where(me.has_left, 1, 0) + jnp.where(me.has_right, 1, 0)
    pl.semaphore_wait(bar, count)


class PairLine:
    def __init__(self, me, own, buf, send, recv, part=None):
        self.me, self.own, self.buf, self.send, self.recv, self.part = me, own, buf, send, recv, part

    def slot(self, o):
        return self.buf.at[o] if self.part is None else self.buf.at[o, self.part]

    def copy(self, o, src, d, kind):
        send, recv = (self.send.at[kind, o], self.recv.at[o]) if self.part is None else (self.send.at[kind, o, self.part], self.recv.at[o, self.part])
        return remote(src, self.slot(o), send, recv, d, self.me.t)

    def start(self):
        me = self.me
        @pl.when(me.has_left)
        def _():
            self.copy(me.d, self.own, me.d - 2, 0).start()
        @pl.when(me.has_right)
        def _():
            self.copy(me.d, self.own, me.d + 2, 1).start()
        self.copy(me.d, self.own, me.dx, 2).start()

    def hop(self, k, then=None):
        me = self.me
        @pl.when(me.p - k >= 0)
        def _():
            o = me.d - 2 * k
            self.copy(o, self.slot(o), me.dx, 2).wait_recv()
            @pl.when(me.has_right)
            def _():
                self.copy(o, self.slot(o), me.d + 2, 1).start()
            self.copy(o, self.slot(o), me.dx, 2).start()
            if then is not None:
                then(o)
        @pl.when(me.p + k < me.line)
        def _():
            o = me.d + 2 * k
            self.copy(o, self.slot(o), me.dx, 2).wait_recv()
            @pl.when(me.has_left)
            def _():
                self.copy(o, self.slot(o), me.d - 2, 0).start()
            self.copy(o, self.slot(o), me.dx, 2).start()
            if then is not None:
                then(o)

    def pair_arrivals(self, then=None):
        def one(q, c):
            o = 2 * q + 1 - self.me.par
            self.copy(o, self.slot(o), self.me.dx, 2).wait_recv()
            if then is not None:
                then(o)
            return c
        lax.fori_loop(0, self.me.line, one, 0)

    def sent(self):
        me = self.me
        def one(q, c):
            o = 2 * q + me.par
            self.copy(o, self.slot(o), me.dx, 2).wait_send()
            @pl.when((q >= me.p) & me.has_left)
            def _():
                self.copy(o, self.slot(o), me.dx, 0).wait_send()
            @pl.when((q <= me.p) & me.has_right)
            def _():
                self.copy(o, self.slot(o), me.dx, 1).wait_send()
            return c
        lax.fori_loop(0, me.line, one, 0)


class FullGather:
    def __init__(self, me, own, buf, send, first, recv):
        self.me, self.own, self.buf, self.send, self.first, self.recv = me, own, buf, send, first, recv
        cut = own.shape[0] // 3
        self.parts = (pl.ds(0, cut), pl.ds(cut, own.shape[0] - cut))

    def copy(self, h, o, t, d2, t2, kind, own=False):
        rows = self.parts[h]
        src = self.own.at[rows] if own else self.buf.at[o, t, rows]
        sem = self.first.at[h] if kind == 4 else self.send.at[h, o, t, kind]
        return remote(src, self.buf.at[o, t, rows], sem, self.recv.at[h, o, t], d2, t2)

    def last(self, h):
        me = self.me
        return (me.d, me.t2) if h == 0 else (me.dx, me.t)

    def spread(self, h, o, t, left, right, own=False):
        me = self.me
        @pl.when(left)
        def _():
            self.copy(h, o, t, me.d - 2, me.t, 0, own).start()
        @pl.when(right)
        def _():
            self.copy(h, o, t, me.d + 2, me.t, 1, own).start()
        self.copy(h, o, t, *self.last(h), 2, own).start()
        self.copy(h, o, t, me.d, me.t1, 3, own).start()

    def start(self):
        me = self.me
        self.copy(0, me.d, me.t, me.dx, me.t, 4, True).start()
        self.copy(1, me.d, me.t, me.d, me.t2, 4, True).start()
        for h in (1, 0):
            self.spread(h, me.d, me.t, me.has_left, me.has_right, True)

    def arrived(self, h, o, t):
        self.copy(h, o, t, self.me.d, self.me.t1, 3).wait_recv()

    def firsts(self):
        me = self.me
        self.arrived(0, me.dx, me.t)
        self.spread(0, me.dx, me.t, me.has_left, me.has_right)
        self.arrived(1, me.d, me.t2)
        self.spread(1, me.d, me.t2, me.has_left, me.has_right)

    def streams(self, q):
        me = self.me
        return ((0, 2 * q + me.par, me.t), (0, 2 * q + 1 - me.par, me.t), (1, 2 * q + me.par, me.t), (1, 2 * q + me.par, me.t2))

    def hop(self, k):
        me = self.me
        @pl.when(me.p - k >= 0)
        def _():
            for h, o, t in self.streams(me.p - k):
                self.arrived(h, o, t)
                self.spread(h, o, t, False, me.has_right)
        @pl.when(me.p + k < me.line)
        def _():
            for h, o, t in self.streams(me.p + k):
                self.arrived(h, o, t)
                self.spread(h, o, t, me.has_left, False)

    def lasts(self, k):
        me = self.me

        def place(q):
            for h, o, t in ((0, 2 * q, me.t2), (0, 2 * q + 1, me.t2), (1, 2 * q + 1 - me.par, me.t), (1, 2 * q + 1 - me.par, me.t2)):
                self.arrived(h, o, t)
                self.copy(h, o, t, me.d, me.t1, 3).start()

        @pl.when(me.p - k >= 0)
        def _():
            place(me.p - k)
        @pl.when((me.p + k < me.line) & (k > 0))
        def _():
            place(me.p + k)

    def finish(self):
        me = self.me
        def one(o, c):
            for h in range(2):
                self.arrived(h, o, me.t1)
                self.arrived(h, o, me.t3)
                for t in (me.t, me.t2):
                    self.copy(h, o, t, me.d, me.t1, 3).wait_send()
            return c
        lax.fori_loop(0, 2 * me.line, one, 0)
        def two(q, c):
            for h, o, t in self.streams(q):
                self.copy(h, o, t, me.d, me.t1, 2).wait_send()
                @pl.when((q >= me.p) & me.has_left)
                def _():
                    self.copy(h, o, t, me.d, me.t1, 0).wait_send()
                @pl.when((q <= me.p) & me.has_right)
                def _():
                    self.copy(h, o, t, me.d, me.t1, 1).wait_send()
            return c
        lax.fori_loop(0, me.line, two, 0)
        for h in range(2):
            self.copy(h, me.d, me.t, me.d, me.t1, 4).wait_send()


EPS = 1e-6


def forward_kernel(ndp, chunks, choice_in, len_ref, par_ref, x_ref, gain_ref, qs_ref, ain_h, btab_h, a_ref, wo_ref, wf_ref,
                   wout_ref, cho_ref, mixed_ref, xno_ref, qo_ref, qto_ref, ko_ref, kto_ref, vo_ref, ranko_ref, mixto_ref, wpo_ref, bpo_ref, ato_ref, scaleo_ref,
                   ain_ref, btab_ref, choice_ref, at_ref, scale_ref, seg_ref, mq_ref, put_ref,
                   araw_ref, wraw_ref, aown_ref, wown_ref, xn_ref, wa_ref, wp_ref, bp_ref, q_ref, qt_ref, k_ref, kt_ref, v_ref, vt_ref, rank_ref, mixt_ref,
                   mix_ref, m_ref, acc_ref, ls, os, xs, xr, a_s, a_r, c_s, c_r, w_s, w_f, w_r, ms, mr):
    me = Place(ndp)
    tok, width = x_ref.shape
    loads = [pltpu.make_async_copy(a_ref, araw_ref, ls.at[0]), pltpu.make_async_copy(wo_ref, wraw_ref.at[0], ls.at[1]),
             pltpu.make_async_copy(wf_ref, wraw_ref.at[pl.ds(1, 2)], ls.at[2])]
    tables = [pltpu.make_async_copy(ain_h.at[pl.ds(0, 3)], ain_ref, ls.at[3]), pltpu.make_async_copy(btab_h, btab_ref, ls.at[4])]
    for copy in loads + tables:
        copy.start()
    e = choice_in[0]
    choice_ref[...] = jnp.zeros_like(choice_ref) + e.astype(F32)
    x = x_ref[...].astype(F32)
    mine = pl.ds(pl.multiple_of(me.t * tok, tok), tok)
    xn_ref[mine, :] = (x * lax.rsqrt(jnp.mean(x * x, axis=-1, keepdims=True) + EPS) * gain_ref[0:1, :]).astype(BF16)
    greet(me, tensor=(me.t1, me.t2, me.t3), pair=True, line=True)
    size = tok // chunks

    def xcopy(o, c, t, kind):
        rows = pl.ds(pl.multiple_of(o * tok + c * size, size), size)
        return remote(xn_ref.at[rows], xn_ref.at[rows], xs.at[kind, c], xr.at[o, c], me.d, t)

    for c in range(chunks):
        xcopy(me.t, c, me.t2, 0).start()
    for c in range(chunks):
        xcopy(me.t, c, me.t1, 1).start()
    for copy in loads:
        copy.wait()
    pieces = aown_ref.shape[1]

    def pack(raw_ref, own_ref, n, index):
        def store(k, v):
            own_ref[index(n, k)] = v
        pack_block(raw_ref[n], me.c, store)
    for n in range(3):
        pack(araw_ref, aown_ref, n, lambda n, k: (n, k))
    parts = [PairLine(me, aown_ref.at[n], wa_ref, a_s, a_r, n) for n in range(3)]
    ch = PairLine(me, choice_ref, cho_ref, c_s, c_r)
    w = FullGather(me, wown_ref, wout_ref, w_s, w_f, w_r)
    parts[0].start()
    parts[1].start()
    for n in range(3):
        pack(wraw_ref, wown_ref, n, lambda n, k: n * pieces + k)
    keep = [pltpu.make_async_copy(wown_ref, wout_ref.at[me.d, me.t], ls.at[0]), pltpu.make_async_copy(choice_ref, cho_ref.at[me.d], ls.at[1])]
    for copy in keep:
        copy.start()
    wa_ref[me.d] = aown_ref[...]
    tree_masks(len_ref, par_ref, seg_ref, mq_ref)
    scale_ref[...] = jnp.zeros_like(scale_ref)
    for h in range(q_ref.shape[0]):
        scale_ref[:, h * 128:h * 128 + HD] = qs_ref[...] * (1.0 / math.sqrt(HD))
    put_ref[...] = head_columns(me, *put_ref.shape)
    for copy in tables:
        copy.wait()
    parts[0].hop(1)
    parts[2].start()
    ch.start()

    def diagonal(n, carry):
        for part in range(3):
            k = n - part
            @pl.when((k >= 1) & (k < me.line))
            def _():
                parts[part].hop(k)
        return carry
    lax.fori_loop(2, me.line + 2, diagonal, 0)
    w.start()
    n16 = ain_ref.shape[2]
    for s in range(3):
        at_ref[s * n16:(s + 1) * n16] = ain_ref[s, e]
    picked = jnp.concatenate([btab_ref[s, e] for s in range(3)], axis=0)
    spread = (0.5 * dot_nt(picked, put_ref[...])).astype(BF16)
    bp_ref[...] = jnp.zeros_like(bp_ref)
    for s in range(3):
        bp_ref[s, s * n16:(s + 1) * n16] = spread[s * n16:(s + 1) * n16]

    def forward(c):
        xcopy(me.t2, c, me.t1, 2).wait_recv()
        xcopy(me.t2, c, me.t1, 2).start()

    for c in range(chunks // 2):
        forward(c)
    nblk = xn_ref.shape[0] // BLK
    near = nblk // 2
    half_rows = wa_ref.shape[3]
    sides = pieces // 2
    wrows = half_rows * sides
    sel, sel_rest = spread_heads(me.c, sides, wp_ref.shape[2])

    def spread_weights(s):
        if sides == 1:
            group = 16 // math.gcd(wrows, 16)
            for o in range(0, ndp, group):
                wp_ref[s, o * wrows:(o + group) * wrows] = jnp.concatenate([
                    dot(jnp.concatenate([wa_ref[o + j, s, 0], wa_ref[o + j, s, 1]], axis=1), sel) + dot(wa_ref[o + j, s, 2], sel_rest[0])
                    for j in range(group)], axis=0).astype(BF16)
            return
        flat = [wa_ref[:, s, k].reshape(ndp * half_rows, 128) for k in range(pieces)]
        for r in range(sides):
            y = (dot(jnp.concatenate([flat[r], flat[sides + r]], axis=1), sel) + dot(flat[2 * sides], sel_rest[r])).astype(BF16)
            for o in range(ndp):
                wp_ref[s, o * wrows + r * half_rows:o * wrows + (r + 1) * half_rows] = y[o * half_rows:(o + 1) * half_rows]

    def project_blocks(first, s):
        n_ref, t_ref = ((q_ref, qt_ref), (k_ref, kt_ref), (v_ref, vt_ref))[s]
        lax.fori_loop(0, near, lambda n, c: (project(first + n, s, xn_ref, wp_ref, at_ref, bp_ref, scale_ref, seg_ref, mq_ref, n_ref, t_ref, rank_ref), c)[1], 0)

    for c in range(chunks):
        xcopy(me.t1, c, me.t1, 2).wait_recv()
    for s in range(3):
        parts[s].pair_arrivals()
        spread_weights(s)
        project_blocks(me.y * near, s)
        if s < 2:
            forward(chunks // 2 + s)
    for c in range(chunks):
        xcopy(me.t3, c, me.t1, 2).wait_recv()
    w.firsts()
    for s in range(3):
        project_blocks((1 - me.y) * near, s)

    def hops(i):
        done = 1 + jnp.maximum((me.line - 2) * (i + 1) * (i + 2) + 2 * nblk, 0) // ((nblk - 1) * nblk)
        return jnp.minimum(done, me.line - 1)

    def relay(i):
        lax.fori_loop(hops(i - 1), hops(i), lambda k, c: (w.hop(k + 1), ch.hop(k + 1), c)[2], 0)
    w.hop(1)
    ch.hop(1)
    outs = [pltpu.make_async_copy(src, dst, os.at[n]) for n, (src, dst) in enumerate((
        (xn_ref, xno_ref), (q_ref, qo_ref), (k_ref, ko_ref), (kt_ref, kto_ref), (v_ref, vo_ref), (rank_ref, ranko_ref),
        (wp_ref, wpo_ref), (bp_ref, bpo_ref), (at_ref, ato_ref), (scale_ref, scaleo_ref)))]
    for copy in outs:
        copy.start()
    per = tok // BLK

    def piece(i):
        return mix_ref.at[i], mixed_ref.at[me.t, i % per], i // per

    def attend_step(i, c):
        attend_block(i, me.c, qt_ref, k_ref, vt_ref, m_ref, acc_ref, mixt_ref, mix_ref)
        src, dst, t = piece(i)
        @pl.when(t == me.t)
        def _():
            pltpu.make_async_copy(src, dst, ms.at[i]).start()
        @pl.when(t != me.t)
        def _():
            remote(src, dst, ms.at[i], mr.at[me.t, i % per], me.d, t).start()
        relay(i)
        lax.fori_loop(jnp.where(i == 0, 0, hops(i - 2)), hops(i - 1), lambda k, n: (w.lasts(k), n)[1], 0)
        return c
    lax.fori_loop(0, nblk, attend_step, 0)
    late = [pltpu.make_async_copy(qt_ref, qto_ref, os.at[len(outs)]), pltpu.make_async_copy(mixt_ref, mixto_ref, os.at[len(outs) + 1])]
    for copy in late:
        copy.start()
    lax.fori_loop(hops(nblk - 2), me.line, lambda k, c: (w.lasts(k), c)[1], 0)
    ch.pair_arrivals()
    for t in (me.t1, me.t2, me.t3):
        for h in range(per):
            dst = mixed_ref.at[t, h]
            remote(dst, dst, ms.at[0], mr.at[t, h], me.d, t).wait_recv()
    w.finish()
    for part in parts:
        part.sent()
    ch.sent()
    for c in range(chunks):
        for kind in range(3):
            xcopy(me.t, c, me.t1, kind).wait_send()

    def settle(i, c):
        src, dst, t = piece(i)
        @pl.when(t == me.t)
        def _():
            pltpu.make_async_copy(src, dst, ms.at[i]).wait()
        @pl.when(t != me.t)
        def _():
            remote(src, dst, ms.at[i], mr.at[me.t, i % per], me.d, t).wait_send()
        return c
    lax.fori_loop(0, nblk, settle, 0)
    for copy in keep + outs + late:
        copy.wait()


def sigmoid(v):
    return 1.0 / (1.0 + jnp.exp(-v))


def mid_kernel(e_ref, x_ref, g_ref, mix4_ref, gain_ref, wall_ref, aout_h, ain_h, adown_h, bup_h, bres_h, out_ref, dmid_ref, dmix_ref, grads_ref,
               at_ref, b_ref, ts, mix_ref, mid_ref, hid_ref, up_ref, act_ref, f_ref, low_ref, w_ref, wb0_ref, wb1_ref, wb2_ref, ls):
    width = x_ref.shape[1]
    step = 256
    part = width // mix4_ref.shape[0]
    blocks = (wb0_ref, wb1_ref, wb2_ref)
    ndp, nt, pieces, size = wb0_ref.shape[:4]
    sides = pieces // 2
    loads = [pltpu.make_async_copy(wall_ref.at[:, :, pl.ds(n * pieces, pieces)], blocks[n], ls.at[n]) for n in range(3)]
    e = e_ref[0]
    tables = [pltpu.make_async_copy(src, dst, ts.at[n]) for n, (src, dst) in enumerate((
        (aout_h.at[e], at_ref.at[0]), (ain_h.at[3, e], at_ref.at[1]), (adown_h.at[e], at_ref.at[2]),
        (bres_h.at[0, e], b_ref.at[0]), (bup_h.at[e], b_ref.at[1]), (bres_h.at[1, e], b_ref.at[2])))]
    for copy in tables + loads:
        copy.start()
    for copy in tables:
        copy.wait()

    def join(dst_ref, first_part, y, even, odd):
        pieces, size = even.shape[:2]
        sides = pieces // 2
        low_lane = lax.broadcasted_iota(jnp.int32, (size, 128), 1) < 64
        base = 2 * part * y
        for r in range(sides):
            rows = pl.ds((first_part + r) * size, size)
            dst_ref[rows, base:base + 128] = even[r]
            dst_ref[rows, base + 128:base + 256] = even[sides + r]
            first, second = (even, odd) if r == 0 else (odd, even)
            both = jnp.where(low_lane, first[2 * sides].astype(F32), second[2 * sides].astype(F32))
            dst_ref[rows, base + 256:base + 384] = (both if r == 0 else pltpu.roll(both, 64, 1)).astype(BF16)
            dst_ref[rows, base + 384:base + 512] = odd[r]
            dst_ref[rows, base + 512:base + 640] = odd[sides + r]

    def assemble(n):
        loads[n].wait()
        dst = w_ref.at[n]
        for o in range(ndp):
            for y in range(nt // 2):
                join(dst, o * sides, y, blocks[n].at[o, 2 * y], blocks[n].at[o, 2 * y + 1])

    for y in range(nt // 2):
        for i in range(mix4_ref.shape[1]):
            join(mix_ref, 2 * i, y, mix4_ref.at[2 * y, i], mix4_ref.at[2 * y + 1, i])

    def cols(n):
        return pl.ds(pl.multiple_of(n * step, step), step)

    def each(fn):
        lax.fori_loop(0, width // step, lambda n, c: (fn(cols(n)), c)[1], 0)

    gain = gain_ref[1:2, :]
    r_out = dot_nt(mix_ref[...], at_ref[0]).astype(BF16)
    assemble(0)

    def project_out(n):
        attn = dot_nt(mix_ref[...], w_ref[0, n, :]) + 0.5 * dot(r_out, b_ref[0, :, n])
        mid_ref[:, n] = x_ref[:, n].astype(F32) + attn
    each(project_out)
    middle = mid_ref[...]
    r = lax.rsqrt(jnp.mean(middle * middle, axis=-1, keepdims=True) + EPS)
    hid_ref[...] = (middle * r * gain).astype(BF16)
    r_up = dot_nt(hid_ref[...], at_ref[1]).astype(BF16)
    assemble(1)

    def up_step(n):
        up = dot(hid_ref[...], w_ref[1, :, n]) + 0.5 * dot(r_up, b_ref[1, :, n])
        up_ref[:, n] = up
        act_ref[:, n] = (up * sigmoid(up)).astype(BF16)
    each(up_step)
    r_down = dot_nt(act_ref[...], at_ref[2]).astype(BF16)
    assemble(2)

    def down_step(n):
        down = dot_nt(act_ref[...], w_ref[2, n, :]) + 0.5 * dot(r_down, b_ref[2, :, n])
        out_ref[:, n] = (mid_ref[:, n] + down).astype(BF16)
    each(down_step)
    grads_ref[5] = 0.5 * dot_tn(r_down, g_ref[...])
    dz_down = (0.5 * dot_nt(g_ref[...], b_ref[2])).astype(BF16)
    grads_ref[3] = dot_tn(dz_down, act_ref[...])

    def act_back(n):
        d_act = dot(g_ref[...], w_ref[2, :, n]) + dot(dz_down, at_ref[2, :, n])
        up = up_ref[:, n]
        sg = sigmoid(up)
        low_ref[:, n] = (d_act * sg * (1.0 + up * (1.0 - sg))).astype(BF16)
    each(act_back)
    dz_up = (0.5 * dot_nt(low_ref[...], b_ref[1])).astype(BF16)
    grads_ref[1] = 0.5 * dot_tn(r_up, low_ref[...])
    grads_ref[0] = dot_tn(dz_up, hid_ref[...])

    def hidden_back(n):
        f_ref[:, n] = (dot_nt(low_ref[...], w_ref[1, n, :]) + dot(dz_up, at_ref[1, :, n])) * gain_ref[1:2, n]
    each(hidden_back)
    gd = f_ref[...]
    middle = mid_ref[...]
    s = jnp.mean(middle * gd, axis=-1, keepdims=True)
    d_mid = g_ref[...].astype(F32) + r * gd - middle * (r * r * r * s)
    dmid_ref[...] = d_mid
    low_ref[...] = d_mid.astype(BF16)
    dz_out = (0.5 * dot_nt(low_ref[...], b_ref[0])).astype(BF16)
    grads_ref[4] = 0.5 * dot_tn(r_out, low_ref[...])
    grads_ref[2] = dot_tn(dz_out, mix_ref[...])

    def mixed_back(n):
        act_ref[:, n] = (dot(low_ref[...], w_ref[0, :, n]) + dot(dz_out, at_ref[0, :, n])).astype(BF16)
    each(mixed_back)
    half = dmix_ref.shape[3]
    low_lane = lax.broadcasted_iota(jnp.int32, (half, 128), 1) < 64
    for y in range(nt // 2):
        base = 2 * part * y
        for i in range(dmix_ref.shape[1]):
            halves = [pl.ds((2 * i + r) * half, half) for r in range(2)]
            for r in range(2):
                dmix_ref[2 * y, i, r] = act_ref[halves[r], base:base + 128]
                dmix_ref[2 * y, i, 2 + r] = act_ref[halves[r], base + 128:base + 256]
                dmix_ref[2 * y + 1, i, r] = act_ref[halves[r], base + 384:base + 512]
                dmix_ref[2 * y + 1, i, 2 + r] = act_ref[halves[r], base + 512:base + 640]
            top = act_ref[halves[0], base + 256:base + 384].astype(F32)
            turned = pltpu.roll(act_ref[halves[1], base + 256:base + 384].astype(F32), 64, 1)
            dmix_ref[2 * y, i, 4] = jnp.where(low_lane, top, turned).astype(BF16)
            dmix_ref[2 * y + 1, i, 4] = jnp.where(low_lane, turned, top).astype(BF16)


class GradSum:
    def __init__(self, me, gp, gr, g2, own, out, s, r, ls_, lr, fs, fr, keep):
        self.me, self.gp, self.gr, self.g2, self.own, self.out, self.s, self.r, self.fs, self.fr = me, gp, gr, g2, own, out, s, r, fs, fr
        self.lines = [PairLine(me, own.at[n], out.at[me.c], ls_, lr, n) for n in range(3)]
        self.keep = pltpu.make_async_copy(own, out.at[me.c, me.d], keep)

    def one(self):
        return remote(self.gp.at[1 - self.me.c], self.gr.at[0], self.s.at[0], self.r.at[0], self.me.d, self.me.t1)

    def two(self):
        return remote(self.g2, self.gr.at[1], self.s.at[1], self.r.at[1], self.me.d, self.me.t2)

    def second(self):
        self.one().wait_recv()
        self.g2[...] = (self.gp[self.me.c].astype(F32) + self.gr[0].astype(F32)).astype(BF16)
        self.two().start()

    def relay(self, o, n, own=False):
        src = self.own.at[n] if own else self.out.at[self.me.c, o, n]
        return remote(src, self.out.at[self.me.c, o, n], self.fs.at[o, n], self.fr.at[o, n], self.me.d, self.me.t1)

    def gather(self):
        self.two().wait_recv()
        total = (self.g2[...].astype(F32) + self.gr[1].astype(F32)).astype(BF16)
        size = self.own.shape[1]
        for n in range(3):
            self.own[n] = total[n * size:(n + 1) * size]
        for n in range(3):
            self.lines[n].start()
        for n in range(3):
            self.relay(self.me.d, n, True).start()
        self.keep.start()

    def hop(self, k):
        for n in range(3):
            self.lines[n].hop(k, lambda o: self.relay(o, n).start())

    def arrivals(self):
        for n in range(3):
            self.lines[n].pair_arrivals(lambda o: self.relay(o, n).start())

    def settle(self, ndp):
        def one(o, c):
            for n in range(3):
                self.relay(o, n, True).wait_send()
                remote(self.own.at[n], self.out.at[1 - self.me.c, o, n], self.fs.at[o, n], self.fr.at[o, n], self.me.d, self.me.t1).wait_recv()
            return c
        lax.fori_loop(0, ndp, one, 0)
        for line in self.lines:
            line.sent()
        self.keep.wait()
        self.one().wait_send()
        self.two().wait_send()


def back_kernel(ndp, dmix_ref, mixt_h, q_h, qt_h, k_h, kt_h, v_h, wp_h, xn_h, rank_h, x_h, dmid_h, scale_ref, bp_ref, at_ref, gain_ref, gmid_ref,
                ig_h, gm_h, ga_h,
                mixt_ref, q_ref, qt_ref, k_ref, kt_ref, v_ref, wp_ref, xn_ref, rank_ref, x_ref, dmid_ref, dm_ref, do_ref, dot_ref,
                dqt_ref, dk_ref, dv_ref, dn_ref, r1_ref, s2_ref, r2_ref, ro_ref, ga_ref, gb_ref, put_ref,
                gpm, grm, g2m, gom, gpa, gra, g2a, goa, lsem, dsem, drecv, es, er, s2s, r2r, ros, ror, igs,
                ms, mr, mls, mlr, mfs, mfr, mk, as_, ar, als, alr, afs, afr, ak):
    me = Place(ndp)
    tok = x_ref.shape[0]
    per, hb = tok // BLK, BLK // 2
    nblk = per * dm_ref.shape[0]
    half = nblk // 2
    heads = q_ref.shape[0]
    loads = [pltpu.make_async_copy(src, dst, lsem.at[n]) for n, (src, dst) in enumerate((
        (mixt_h, mixt_ref), (q_h, q_ref), (qt_h, qt_ref), (k_h, k_ref), (kt_h, kt_ref), (v_h, v_ref),
        (wp_h, wp_ref), (xn_h, xn_ref), (rank_h, rank_ref), (x_h, x_ref), (dmid_h, dmid_ref)))]
    n48 = gpm.shape[1]
    for c in range(2):
        gpm[c] = gmid_ref[c * n48:(c + 1) * n48].astype(BF16)
    greet(me, tensor=(me.t1, me.t2, me.t3), pair=True, line=True)

    def swap(n, t):
        return remote(dmix_ref.at[t], dm_ref.at[me.t], dsem.at[n], drecv.at[me.t], me.d, t)

    own = pltpu.make_async_copy(dmix_ref.at[me.t], dm_ref.at[me.t], dsem.at[3])
    for n, t in enumerate((me.t3, me.t2, me.t1)):
        swap(n, t).start()
    own.start()
    gm = GradSum(me, gpm, grm, g2m, gom, gm_h, ms, mr, mls, mlr, mfs, mfr, mk.at[0])
    ga = GradSum(me, gpa, gra, g2a, goa, ga_h, as_, ar, als, alr, afs, afr, ak.at[0])
    gm.one().start()
    for copy in loads:
        copy.start()
    for ref in (dqt_ref, dk_ref, dv_ref, ga_ref, gb_ref):
        ref[...] = jnp.zeros_like(ref)
    put_ref[...] = head_columns(me, *put_ref.shape)
    for copy in loads[:6]:
        copy.wait()

    def prep(t):
        lax.fori_loop(t * per, (t + 1) * per, lambda b, c: (bwd_prep(b, me.c, dm_ref, mixt_ref, do_ref, dot_ref), c)[1], 0)

    args = (q_ref, qt_ref, k_ref, kt_ref, v_ref, do_ref, dot_ref, dqt_ref, dk_ref, dv_ref)

    def block(a):
        return (1 - me.y) * (nblk - 1 - a) + me.y * a

    def others(a, first, last):
        b = block(a)

        def other(n, c):
            bwd_pair(b + me.y * (1 + n), b - (1 - me.y) * (1 + n), False, *args)
            return c
        lax.fori_loop(first, last, other, 0)

    def arrived(t):
        remote(dmix_ref.at[t], dm_ref.at[t], dsem.at[0], drecv.at[t], me.d, t).wait_recv()

    own.wait()
    prep(me.t)
    arrived(me.t1)
    prep(me.t1)
    gm.second()
    lax.fori_loop(half, nblk, lambda a, c: (bwd_pair(block(a), block(a), True, *args), others(a, 0, nblk - 1 - a), c)[2], 0)
    arrived(me.t2)
    prep(me.t2)
    arrived(me.t3)
    prep(me.t3)
    for copy in loads[6:]:
        copy.wait()
    lane = lax.broadcasted_iota(jnp.int32, (BLK, 128), 1)

    def exchange(a):
        rows = pl.ds(pl.multiple_of((1 - me.c) * hb, hb), hb)
        return remote(dn_ref.at[a, rows], r1_ref.at[a], es.at[a], er.at[a], me.d, me.t1)

    def own_block(a):
        return remote(dn_ref.at[a], ro_ref.at[block(a) % per], ros.at[a % per], ror.at[block(a) % per], me.d, me.t1)

    def mine_rows():
        return pl.ds(pl.multiple_of(me.c * hb, hb), hb)

    def deliver(a):
        b = block(a)
        return remote(s2_ref.at[a], r2_ref.at[b % per, mine_rows()], s2s.at[a], r2r.at[b % per, me.c], me.d, b // per)

    def is_mine(a):
        return block(a) // per == me.t

    def pass_on(a):
        exchange(a).wait_recv()
        s2_ref[a] = (dn_ref[a, mine_rows(), :].astype(F32) + r1_ref[a].astype(F32)).astype(BF16)
        deliver(a).start()

    def gradients(a):
        rows = pl.ds(pl.multiple_of(block(a) * BLK, BLK), BLK)
        dq, dk, dv = [], [], []
        for h in range(heads):
            g = jnp.concatenate([dqt_ref[h, :, rows], jnp.zeros((48, BLK), F32)], axis=0).T
            dq.append((g * scale_ref[:, h * 128:(h + 1) * 128]).astype(BF16))
            dk.append(jnp.where(lane < HD, dk_ref[h, rows, :], 0.0).astype(BF16))
            dv.append(jnp.where(lane < HD, dv_ref[h, rows, :], 0.0).astype(BF16))
        ds = [jnp.concatenate(g, axis=1) for g in (dq, dk, dv)]
        return rows, ds, sum(dot_nt(ds[s], bp_ref[s]) for s in range(3)).astype(BF16)

    def adapters(rows, ds, dz):
        ga_ref[...] += dot_tn(dz, xn_ref[rows, :])
        for s in range(3):
            gb_ref[s] += dot_tn(rank_ref[rows, :], ds[s])

    def normed_gradient(a, ds, dz):
        dn = sum(dot_nt(ds[s], wp_ref[s]) for s in range(3)) + dot(dz, at_ref[...])
        dn_ref[a] = dn.astype(BF16)

    def upto(a):
        return 1 + jnp.minimum(a * (me.line - 1) // (nblk - 2), me.line - 1)

    def far_step(a, c):
        bwd_pair(block(a), block(a), True, *args)
        others(a, 0, 2)
        @pl.when(a > 0)
        def _():
            pass_on(a - 1)
        others(a, 2, nblk - 1 - a)
        rows, ds, dz = gradients(a)
        normed_gradient(a, ds, dz)
        exchange(a).start()
        adapters(rows, ds, dz)
        @pl.when(a == 0)
        def _():
            gm.gather()
        lax.fori_loop(upto(a), upto(a + 1), lambda k, n: (gm.hop(k), n)[1], 0)
        return c
    lax.fori_loop(0, half, far_step, 0)

    def near_adapters(a, c):
        adapters(*gradients(a))
        return c
    lax.fori_loop(half, nblk, near_adapters, 0)
    n16 = n48 // 3
    gpa[0] = ga_ref[...].astype(BF16)
    gb = jnp.concatenate([gb_ref[s, s * n16:(s + 1) * n16] for s in range(3)], axis=0)
    gpa[1] = dot((0.5 * gb).astype(BF16), put_ref[...]).astype(BF16)
    ga.one().start()

    def near_step(a, c):
        _, ds, dz = gradients(a)
        normed_gradient(a, ds, dz)
        @pl.when(jnp.logical_not(is_mine(a)))
        def _():
            own_block(a).start()
        @pl.when(a == half)
        def _():
            ga.second()
            pass_on(a - 1)
        lax.fori_loop(upto(a), upto(a + 1), lambda k, n: (gm.hop(k), n)[1], 0)
        return c
    lax.fori_loop(half, nblk, near_step, 0)
    gm.arrivals()
    ga.gather()

    def combine(i, c):
        b = me.t * per + i
        a = block(b)
        rows = pl.ds(pl.multiple_of(i * BLK, BLK), BLK)
        remote(dn_ref.at[a], ro_ref.at[i], ros.at[0], ror.at[i], me.d, me.t1).wait_recv()
        for h in range(2):
            remote(s2_ref.at[0], r2_ref.at[i, pl.ds(h * hb, hb)], s2s.at[0], r2r.at[i, h], me.d, me.t2).wait_recv()
        dn = dn_ref[a].astype(F32) + ro_ref[i].astype(F32) + r2_ref[i].astype(F32)
        x = x_ref[rows, :].astype(F32)
        r = lax.rsqrt(jnp.mean(x * x, axis=-1, keepdims=True) + EPS)
        gd = gain_ref[0:1, :] * dn
        dmid_ref[rows, :] = dmid_ref[rows, :] + r * gd - x * (r * r * r * jnp.mean(x * gd, axis=-1, keepdims=True))
        return c
    lax.fori_loop(1, me.line, lambda k, c: (ga.hop(k), c)[1], 0)
    lax.fori_loop(0, per, combine, 0)
    put_ig = pltpu.make_async_copy(dmid_ref, ig_h, igs.at[0])
    put_ig.start()
    ga.arrivals()
    ga.settle(ndp)
    gm.settle(ndp)

    def sent(a, c):
        exchange(a).wait_send()
        deliver(a).wait_send()
        return c
    lax.fori_loop(0, half, sent, 0)

    def own_sent(a, c):
        @pl.when(jnp.logical_not(is_mine(a)))
        def _():
            own_block(a).wait_send()
        return c
    lax.fori_loop(half, nblk, own_sent, 0)
    for n, t in enumerate((me.t3, me.t2, me.t1)):
        swap(n, t).wait_send()
    put_ig.wait()


def place_kernel(e_ref, gm_ref, ga_ref, ig_in, ain_h, bqkv_h, bup_h, aout_h, adown_h, bres_h, ig_out, out_ref, ig_ref, sem):
    ndp = gm_ref.shape[1]
    slots = ([(ga_ref, 0, n, ain_h.at[n]) for n in range(3)] + [(ga_ref, 1, n, bqkv_h.at[n]) for n in range(3)]
             + [(gm_ref, 0, 0, ain_h.at[3]), (gm_ref, 0, 1, bup_h), (gm_ref, 0, 2, aout_h),
                (gm_ref, 1, 0, adown_h), (gm_ref, 1, 1, bres_h.at[0]), (gm_ref, 1, 2, bres_h.at[1])])
    fetch = pltpu.make_async_copy(ig_in, ig_ref, sem.at[len(slots)])
    fetch.start()
    copies = []
    for n, (src, c, k, dst) in enumerate(slots):
        out_ref[n] = jnp.zeros(out_ref.shape[1:], F32)

        def add(d, carry):
            e = e_ref[d, 0, 0].astype(jnp.int32)
            out_ref[n, e] += src[c, d, k].astype(F32)
            return carry
        lax.fori_loop(0, ndp, add, 0)
        copies.append(pltpu.make_async_copy(out_ref.at[n], dst, sem.at[n]))
        copies[-1].start()
        if n == 3:
            fetch.wait()
            keep = pltpu.make_async_copy(ig_ref, ig_out, sem.at[len(slots) + 1])
            keep.start()
    for copy in copies + [keep]:
        copy.wait()


VMEM = pltpu.VMEM
DMA = pltpu.SemaphoreType.DMA
IN_VMEM = pl.BlockSpec(memory_space=pltpu.VMEM)
IN_SMEM = pl.BlockSpec(memory_space=pltpu.SMEM)
IN_ANY = pl.BlockSpec(memory_space=pl.ANY)


def shape(*dims, dtype=BF16):
    return jax.ShapeDtypeStruct(dims, dtype)


def params(cid=None, limit=60 << 20):
    if cid is None:
        return pltpu.CompilerParams(vmem_limit_bytes=limit)
    return pltpu.CompilerParams(collective_id=cid, has_side_effects=True, vmem_limit_bytes=limit)


def local(
    inputs, cotangent, adapter_choice_per_tree, segment_lengths, segment_parents, norm_gain_rows, query_dimension_scale,
    attention_weights, output_weight, feedforward_weights, adapter_first_input, adapter_second_attention, adapter_second_up,
    adapter_first_output, adapter_first_down, adapter_second_residual,
):
    ndp, nt = lax.axis_size("dp"), lax.axis_size("tensor")
    tok, width = inputs.shape
    tree = tok * nt
    wrows, hcols = output_weight.shape
    heads = hcols // HD
    pad = heads * 128
    rank = adapter_first_input.shape[3]
    nblk = tree // BLK
    a_in, a_out, a_down = (jnp.swapaxes(table, -1, -2) for table in (adapter_first_input, adapter_first_output, adapter_first_down))

    chunks = 4
    halves = (5, BLK // 2, 128)
    swapped = (nt, tok // BLK) + halves
    count = a_in.shape[1]
    sides = row_parts(wrows)
    packed = (2 * sides + 1, wrows // sides, 128)
    flat = (3 * packed[0],) + packed[1:]
    tall = (heads, tree, 128)
    wall, choices, mixed, xn, q, qt, k, kt, v, ranks, mixt, wp, bp, at_qkv, scale = pl.pallas_call(
        functools.partial(forward_kernel, ndp, chunks),
        out_shape=[shape(ndp, nt, *flat), shape(ndp, 8, 128, dtype=F32), shape(*swapped), shape(tree, width),
                   shape(*tall), shape(heads, 128, tree), shape(*tall), shape(heads, HD, tree), shape(*tall),
                   shape(tree, 3 * rank), shape(hcols, tree), shape(3, width, pad), shape(3, 3 * rank, pad), shape(3 * rank, width),
                   shape(1, pad, dtype=F32)],
        in_specs=[IN_SMEM] * 3 + [IN_VMEM] * 3 + [IN_ANY] * 5, out_specs=[IN_ANY] * 15,
        scratch_shapes=[VMEM((3, count, rank, width), BF16), VMEM((3, count, rank, width), BF16), VMEM((8, 128), F32), VMEM((3 * rank, width), BF16),
                        VMEM((1, pad), F32), VMEM((8, 128), F32), VMEM((128, 128), BF16), VMEM((pad, width), BF16),
                        VMEM((3, wrows, hcols), BF16), VMEM((3, wrows, hcols), BF16), VMEM((3, *packed), BF16), VMEM(flat, BF16), VMEM((tree, width), BF16),
                        VMEM((ndp, 3, *packed), BF16),
                        VMEM((3, width, pad), BF16), VMEM((3, 3 * rank, pad), BF16), VMEM(tall, BF16), VMEM((heads, 128, tree), BF16),
                        VMEM(tall, BF16), VMEM((heads, HD, tree), BF16), VMEM(tall, BF16), VMEM((heads, HD + 16, tree), BF16),
                        VMEM((tree, 3 * rank), BF16), VMEM((hcols, tree), BF16), VMEM((nblk, *halves), BF16),
                        VMEM((heads, 1, BLK), F32), VMEM((heads, HD + 16, BLK), F32), DMA((5,)), DMA((12,)),
                        DMA((3, chunks)), DMA((nt, chunks)), DMA((3, ndp, 3)), DMA((ndp, 3)), DMA((3, ndp)), DMA((ndp,)),
                        DMA((2, ndp, nt, 4)), DMA((2,)), DMA((2, ndp, nt)), DMA((nblk,)), DMA((nt, tok // BLK))],
        compiler_params=params(1), name="forward",
    )(adapter_choice_per_tree, segment_lengths, segment_parents, inputs, norm_gain_rows, query_dimension_scale[None, :], a_in,
      adapter_second_attention, attention_weights, output_weight,
      feedforward_weights)

    output, d_mid, d_mix, g_mid = pl.pallas_call(
        mid_kernel,
        out_shape=[shape(tok, width), shape(tok, width, dtype=F32), shape(*swapped), shape(6, rank, width, dtype=F32)],
        in_specs=[IN_SMEM] + [IN_VMEM] * 4 + [IN_ANY] * 6, out_specs=[IN_VMEM] * 4,
        scratch_shapes=[VMEM((3, rank, width), BF16), VMEM((3, rank, width), BF16), DMA((6,)), VMEM((tok, width), BF16), VMEM((tok, width), F32), VMEM((tok, width), BF16), VMEM((tok, width), F32),
                        VMEM((tok, width), BF16), VMEM((tok, width), F32), VMEM((tok, width), BF16), VMEM((3, width, width), BF16)]
        + [VMEM((ndp, nt, *packed), BF16)] * 3 + [DMA((3,))],
        compiler_params=params(), name="middle",
    )(adapter_choice_per_tree, inputs, cotangent, mixed, norm_gain_rows, wall, a_out, a_in, a_down, adapter_second_up, adapter_second_residual)
    gr = 6 * rank
    half_rows = gr // 2
    half, hb, per = nblk // 2, BLK // 2, tok // BLK
    grad_bufs = [VMEM((2, half_rows, width), BF16), VMEM((2, half_rows, width), BF16), VMEM((half_rows, width), BF16), VMEM((3, rank, width), BF16)]
    grad_sems = [DMA((2,)), DMA((2,)), DMA((3, ndp, 3)), DMA((ndp, 3)), DMA((ndp, 3)), DMA((ndp, 3)), DMA((1,))]
    input_grad, grads_mid, grads_attn = pl.pallas_call(
        functools.partial(back_kernel, ndp),
        out_shape=[shape(tok, width, dtype=F32), shape(2, ndp, 3, rank, width), shape(2, ndp, 3, rank, width)],
        in_specs=[IN_ANY] * 12 + [IN_VMEM] * 5, out_specs=[IN_ANY] * 3,
        scratch_shapes=[VMEM((hcols, tree), BF16), VMEM(tall, BF16), VMEM((heads, 128, tree), BF16), VMEM(tall, BF16), VMEM((heads, HD, tree), BF16),
                        VMEM(tall, BF16), VMEM((3, width, pad), BF16), VMEM((tree, width), BF16), VMEM((tree, 3 * rank), BF16),
                        VMEM((tok, width), BF16), VMEM((tok, width), F32), VMEM(swapped, BF16), VMEM(tall, BF16), VMEM((heads, 128, tree), BF16),
                        VMEM((heads, HD, tree), F32), VMEM(tall, F32), VMEM(tall, F32), VMEM((nblk, BLK, width), BF16), VMEM((half, hb, width), BF16),
                        VMEM((half, hb, width), BF16), VMEM((per, BLK, width), BF16), VMEM((per, BLK, width), BF16),
                        VMEM((3 * rank, width), F32), VMEM((3, 3 * rank, pad), F32), VMEM((pad, width), BF16)]
        + grad_bufs + grad_bufs + [DMA((11,)), DMA((4,)), DMA((nt,)), DMA((half,)), DMA((half,)), DMA((half,)), DMA((per, 2)), DMA((per,)), DMA((per,)), DMA((1,))]
        + grad_sems + grad_sems,
        compiler_params=params(4, 62 << 20), name="back",
    )(d_mix, mixt, q, qt, k, kt, v, wp, xn, ranks, inputs, d_mid, scale, bp, at_qkv, norm_gain_rows, g_mid.reshape(gr, width))

    table = shape(count, rank, width, dtype=F32)
    ga_in, gb_qkv, gb_up, ga_out, ga_down, gb_res, input_grad = pl.pallas_call(
        place_kernel,
        out_shape=[shape(4, count, rank, width, dtype=F32), shape(3, count, rank, width, dtype=F32), table, table, table,
                   shape(2, count, rank, width, dtype=F32), shape(tok, width, dtype=F32)],
        in_specs=[IN_SMEM] + [IN_VMEM] * 2 + [IN_ANY], out_specs=[IN_ANY] * 7,
        scratch_shapes=[VMEM((12, count, rank, width), F32), VMEM((tok, width), F32), DMA((14,))], compiler_params=params(), name="place",
    )(choices, grads_mid, grads_attn, input_grad)
    return (output, input_grad, jnp.swapaxes(ga_in, 2, 3), gb_qkv, gb_up, jnp.swapaxes(ga_out, 1, 2), jnp.swapaxes(ga_down, 1, 2), gb_res)


def solution(mesh):
    tokens, weights = P(("dp", "tensor"), None), P(None, "dp", "tensor")
    in_specs = (tokens, tokens, P("dp"), P("dp", None), P("dp", None), P(), P(), weights, P("dp", "tensor"), weights) + (P(),) * 6
    out_specs = (tokens, tokens) + (P(),) * 6
    return jax.shard_map(local, mesh=mesh, in_specs=in_specs, out_specs=out_specs, check_vma=False)
```
